32 devices in a mesh: dp: 8 (over y, x, core), seq: 4 (over z).
Axes of the slice: x: 2, y: 2, z: 4, core: 2. Of those that a mesh axis runs over, the one named last changes fastest.
Arguments:
- byte_ids: int32 [16, 2048], P('dp', 'seq'), may hold values from 0 to 255
- segments: int32 [16, 2048], P('dp', 'seq'), may hold values from 0 to 7, never falling along the last dimension, each value on 1 to 1024 neighbouring positions
- embed_table: bfloat16 [256, 768], P(('dp', 'seq')), may hold values from -6 to 6
- conv_weight: bfloat16 [768, 5], P(('dp', 'seq')), may hold values from -2.5 to 2.5
- score_vector: bfloat16 [768], P(('dp', 'seq')), may hold values from -0.4375 to 0.4375
- first_gain: bfloat16 [768], P(('dp', 'seq')), may hold values from 0.25 to 1.75
- w_query: bfloat16 [768, 768], P(('dp', 'seq')), may hold values from -0.21875 to 0.21875
- w_key: bfloat16 [768, 768], P(('dp', 'seq')), may hold values from -0.21875 to 0.21875
- w_value: bfloat16 [768, 768], P(('dp', 'seq')), may hold values from -0.21875 to 0.21875
- w_output: bfloat16 [768, 768], P(('dp', 'seq')), may hold values from -1.5 to 1.5
- second_gain: bfloat16 [768], P(('dp', 'seq')), may hold values from 0.25 to 1.75
- w_gate: bfloat16 [768, 2048], P(('dp', 'seq')), may hold values from -0.21875 to 0.21875
- w_up: bfloat16 [768, 2048], P(('dp', 'seq')), may hold values from -0.21875 to 0.21875
- w_down: bfloat16 [2048, 768], P(('dp', 'seq')), may hold values from -0.125 to 0.125
- out_grad: bfloat16 [16, 1024, 768], P('dp', 'seq'), may hold values from -6 to 6
Outputs:
- layer_output: bfloat16 [16, 1024, 768], P('dp', 'seq')
- grad_embed_table: float32 [256, 768], P(('dp', 'seq'))
- grad_conv_weight: float32 [768, 5], P(('dp', 'seq'))
- grad_score_vector: float32 [768], P(('dp', 'seq'))
- grad_first_gain: float32 [768], P(('dp', 'seq'))
- grad_w_query: float32 [768, 768], P(('dp', 'seq'))
- grad_w_key: float32 [768, 768], P(('dp', 'seq'))
- grad_w_value: float32 [768, 768], P(('dp', 'seq'))
- grad_w_output: float32 [768, 768], P(('dp', 'seq'))
- grad_second_gain: float32 [768], P(('dp', 'seq'))
- grad_w_gate: float32 [768, 2048], P(('dp', 'seq'))
- grad_w_up: float32 [768, 2048], P(('dp', 'seq'))
- grad_w_down: float32 [2048, 768], P(('dp', 'seq'))
The draws below stay inside these ranges and needn't reach their ends.
Inputs may be any that keep to these rules, and one draw needn't show every extreme that they name: `segments`: within each sequence the document numbers never fall; each document holds 1 to 1024 bytes.
All inputs are finite; a program needn't handle non-finite values.
Results may differ from the reference program's by a relative error of at most 0.014.
Values may be sent and summed in bfloat16 or wider, within the bound.
A program may use at most 192 MiB of HBM per device.

```python
import math
import jax
import jax.numpy as jnp
import numpy as np
from jax import lax

D = 768
HEADS = 12
HEAD_DIM = 64
FF = 2048
VOCAB = 256
MAXBLOCK = 4
KW = 5
DOCS = 8
SEQ_LEN = 2048
TOK_SEQ = 1024
SEQS = 16
MOST_DOC = 1024


def set_ends(entries, own_key, smallest, top_value):
    place = [jax.random.randint(jax.random.fold_in(own_key, axis), (), 0, length) for axis, length in enumerate(entries.shape)]
    widest = entries.shape.index(max(entries.shape))
    neighbour = place[:widest] + [(place[widest] + 1) % entries.shape[widest]] + place[widest + 1:]
    return entries.at[tuple(place)].set(smallest).at[tuple(neighbour)].set(top_value)


def block_scale(key, shape, split, least, largest):
    level = 1.0
    for dim, parts in split:
        draws = jax.random.uniform(jax.random.fold_in(jax.random.fold_in(key, 6), dim), (parts,), jnp.float32, least / len(split), largest / len(split))
        level = level * jnp.repeat(jnp.exp(draws), shape[dim] // parts).reshape((-1,) + (1,) * (len(shape) - 1 - dim))
    return level


def cumulative_ranks(number_of, slope):
    weights = [(1 << 20) // math.isqrt(grade ** slope) + 1 for grade in range(1, number_of + 1)]
    spread = 1 + sum(weights) // (1 << 30)
    return np.cumsum(np.array([max(1, weight // spread) for weight in weights]))


def skewed_ids(own_key, shape, number_of, lean):
    listing = cumulative_ranks(number_of, lean)
    ticket = jax.random.randint(jax.random.fold_in(own_key, 1), shape, 0, int(listing[number_of - 1]))
    standing = jnp.searchsorted(jnp.asarray(listing, jnp.int32), ticket, side="right")
    return jax.random.permutation(jax.random.fold_in(own_key, 2), number_of)[standing].astype(jnp.int32)


def split_up(amount, total, bound, lean):
    weights = [(1 << 20) // math.isqrt(rank ** lean) + 1 for rank in range(2, amount + 1)]
    rest, given = total - bound - (amount - 1), [1] * (amount - 1)
    while rest > 0:
        movable = [i for i in range(amount - 1) if given[i] < bound]
        mass, left = sum([weights[i] for i in movable]), rest
        for i in movable:
            extra = min(bound - given[i], max(1, left * weights[i] // mass), rest)
            given[i] = given[i] + extra
            rest = rest - extra
    return np.array([bound] + given)


def uneven(stream_key, count, total, most, lean):
    if count == 2:
        one = jax.random.randint(stream_key, (), max(1, total - most), min(most, total - 1) + 1)
        return jnp.stack([one, total - one])
    sizes = jnp.asarray(split_up(count, total, most, lean), jnp.int32)
    twos = (count - 1) // 2
    giver, sink = sizes[1:1 + 2 * twos:2], sizes[2:2 + 2 * twos:2]
    margin = jnp.minimum(giver - 1, most - sink)
    moved = jax.random.randint(jax.random.fold_in(stream_key, 1), (twos,), 0, 1 << 20) % (margin + 1)
    sizes = sizes.at[1:1 + 2 * twos:2].set(giver - moved).at[2:2 + 2 * twos:2].set(sink + moved)
    return sizes[jax.random.permutation(jax.random.fold_in(stream_key, 2), count)]


def scatter_about(stream_key, dims, spread, most, cuts=(), kind=jnp.bfloat16):
    level = block_scale(stream_key, dims, cuts, -0.22, 0.18) if cuts else 1.0
    values = jax.random.normal(stream_key, dims, jnp.float32) * spread * level
    return jnp.minimum(jnp.maximum(values, -most), most).astype(kind)


def setup_inputs(seed: int = 0) -> dict:
    keys = jax.random.split(jax.random.key(seed), 16)
    byte_ids = set_ends(skewed_ids(keys[0], (SEQS, SEQ_LEN), VOCAB, 2), jax.random.fold_in(keys[0], 3), 0, VOCAB - 1).astype(jnp.int32)
    segments = jax.vmap(lambda own: jnp.searchsorted(jnp.cumsum(uneven(own, DOCS, SEQ_LEN, MOST_DOC, 2)), jnp.arange(SEQ_LEN), side="right"))(jax.random.split(keys[1], SEQS)).reshape((SEQS, SEQ_LEN)).astype(jnp.int32)
    embed_table = scatter_about(keys[2], (VOCAB, D), 1.0, 6.0, ((0, 32),))
    conv_weight = scatter_about(keys[3], (D, KW), KW ** -0.5, 2.5, ((0, 32),))
    score_vector = scatter_about(keys[4], (D,), (D // 4) ** -0.5, 0.4375, ((0, 32),))
    first_gain = jnp.clip(1.0 + 0.15 * jax.random.normal(keys[5], (D,), jnp.float32), 0.25, 1.75).astype(jnp.bfloat16)
    w_query = scatter_about(keys[6], (D, D), D ** -0.5, 0.21875, ((0, 32),))
    w_key = scatter_about(keys[7], (D, D), D ** -0.5, 0.21875, ((0, 32),))
    w_value = scatter_about(keys[8], (D, D), D ** -0.5, 0.21875, ((0, 32),))
    w_output = scatter_about(keys[9], (D, D), (D // 48) ** -0.5, 1.5, ((0, 32),))
    second_gain = jnp.clip(1.0 + 0.15 * jax.random.normal(keys[10], (D,), jnp.float32), 0.25, 1.75).astype(jnp.bfloat16)
    w_gate = scatter_about(keys[11], (D, FF), D ** -0.5, 0.21875, ((0, 32),))
    w_up = scatter_about(keys[12], (D, FF), D ** -0.5, 0.21875, ((0, 32),))
    w_down = scatter_about(keys[13], (FF, D), FF ** -0.5, 0.125, ((0, 32),))
    out_grad = scatter_about(keys[14], (SEQS, TOK_SEQ, D), 1.0, 6.0, ((0, 8), (1, 4)))
    return {"byte_ids": byte_ids, "segments": segments, "embed_table": embed_table, "conv_weight": conv_weight, "score_vector": score_vector, "first_gain": first_gain, "w_query": w_query, "w_key": w_key, "w_value": w_value, "w_output": w_output, "second_gain": second_gain, "w_gate": w_gate, "w_up": w_up, "w_down": w_down, "out_grad": out_grad}


@jax.custom_vjp
def low(v):
    return lax.optimization_barrier(v.astype(jnp.bfloat16)).astype(jnp.float32)

@jax.custom_vjp
def low_back(v):
    return v

def low_keep(v):
    return (low(v), None)

def low_pass(kept, grad):
    return (grad,)

def back_keep(v):
    return (v, None)

def back_low(kept, grad):
    return (low(grad),)
low.defvjp(low_keep, low_pass)
low_back.defvjp(back_keep, back_low)

def product(left, right):
    return jnp.dot(left, right, precision=lax.Precision.HIGHEST)

def rms_scale(values, gain):
    return values * lax.rsqrt(lax.optimization_barrier(jnp.mean(values * values, axis=-1, keepdims=True)) + 1e-06) * gain

def gelu_tanh(values):
    return jax.nn.gelu(values, approximate=True)

def byte_mixer(embeds, marks, offset, conv_weight, score_vector):
    width_all = embeds.shape[1]
    reach = KW // 2
    inner = width_all - 2 * reach
    centre = lax.slice_in_dim(marks, reach, reach + inner, axis=1)
    conv = jnp.zeros((embeds.shape[0], inner, embeds.shape[2]), jnp.float32)
    for tap_index in range(KW):
        other_marks = lax.slice_in_dim(marks, tap_index, tap_index + inner, axis=1)
        same_doc = (other_marks == centre).astype(jnp.float32)[:, :, None]
        conv = conv + lax.slice_in_dim(embeds, tap_index, tap_index + inner, axis=1) * same_doc * conv_weight[:, tap_index]
    edge = MAXBLOCK - 1
    count = inner - 2 * edge
    here_marks = lax.slice_in_dim(centre, edge, edge + count, axis=1)
    places = offset + reach + edge + jnp.arange(count, dtype=jnp.int32)
    pooled_all = []
    score_all = []
    for block_size in range(1, MAXBLOCK + 1):
        summed = jnp.zeros((embeds.shape[0], count, embeds.shape[2]), jnp.float32)
        number = jnp.zeros((embeds.shape[0], count), jnp.float32)
        for shift_by in range(1 - block_size, block_size):
            other_marks = lax.slice_in_dim(centre, edge + shift_by, edge + shift_by + count, axis=1)
            in_block = jnp.floor_divide(places + shift_by, block_size) == jnp.floor_divide(places, block_size)
            weight_on = ((other_marks == here_marks) & in_block[None, :]).astype(jnp.float32)
            summed = summed + lax.slice_in_dim(conv, edge + shift_by, edge + shift_by + count, axis=1) * weight_on[:, :, None]
            number = number + weight_on
        pooled = summed / number[:, :, None]
        pooled_all.append(pooled)
        score_all.append(lax.optimization_barrier(jnp.sum(pooled * score_vector, axis=-1)))
    size_scores = jnp.stack(score_all, axis=-1)
    size_scores = size_scores - lax.optimization_barrier(jnp.max(size_scores, axis=-1, keepdims=True))
    size_expo = jnp.exp(size_scores)
    size_prob = size_expo / lax.optimization_barrier(jnp.sum(size_expo, axis=-1, keepdims=True))
    mixed = pooled_all[0] * size_prob[:, :, 0:1]
    for block_index in range(1, MAXBLOCK):
        mixed = mixed + pooled_all[block_index] * size_prob[:, :, block_index:block_index + 1]
    paired = mixed.reshape(mixed.shape[0], count // 2, 2, mixed.shape[2])
    return (paired[:, :, 0] + paired[:, :, 1]) * 0.5

def split_heads(rows):
    return rows.reshape(rows.shape[0], HEADS, HEAD_DIM)

def attend(queries, key_rows, value_rows, token_marks):
    scores = jnp.einsum('qhd,khd->hqk', split_heads(queries), split_heads(key_rows), precision=lax.Precision.HIGHEST) * HEAD_DIM ** (-0.5)
    scores = low_back(scores)
    same_doc = (token_marks[:, None] == token_marks[None, :])[None]
    scores = jnp.where(same_doc, scores, -1e+30)
    row_max = lax.optimization_barrier(jnp.max(scores, axis=-1, keepdims=True))
    expo_terms = jnp.exp(scores - row_max)
    soft_probs = expo_terms / lax.optimization_barrier(jnp.sum(expo_terms, axis=-1, keepdims=True))
    attended = jnp.einsum('hqk,khd->qhd', low(soft_probs), split_heads(value_rows), precision=lax.Precision.HIGHEST)
    return attended.reshape(queries.shape[0], -1)

def layer_forward(weights, byte_row, mark_row):
    byte_table, conv_taps, score_taps, gain_one, query_w, key_w, value_w, output_w, gain_two, gate_w, up_w, down_w = weights
    margin_width = KW // 2 + MAXBLOCK - 1
    embeds = jnp.pad(byte_table[byte_row], ((margin_width, margin_width), (0, 0)))[None]
    marks = jnp.pad(mark_row, margin_width)[None]
    stream = byte_mixer(embeds, marks, -margin_width, conv_taps, score_taps)[0]
    token_marks = mark_row[::2]
    normed_one = low(rms_scale(stream, gain_one))
    queries = low(low_back(product(normed_one, query_w)))
    key_rows = low(low_back(product(normed_one, key_w)))
    value_rows = low(low_back(product(normed_one, value_w)))
    attn_out = low(low_back(attend(queries, key_rows, value_rows, token_marks)))
    resid_one = stream + low_back(product(attn_out, output_w))
    normed_two = low(rms_scale(resid_one, gain_two))
    gate_pre = low_back(product(normed_two, gate_w))
    up_pre = low_back(product(normed_two, up_w))
    hidden = low(gelu_tanh(gate_pre) * up_pre)
    return resid_one + low_back(product(hidden, down_w))

def reference(byte_ids, segments, embed_table, conv_weight, score_vector, first_gain, w_query, w_key, w_value, w_output, second_gain, w_gate, w_up, w_down, out_grad):
    weights = (embed_table.astype(jnp.float32), conv_weight.astype(jnp.float32), score_vector.astype(jnp.float32), first_gain.astype(jnp.float32), w_query.astype(jnp.float32), w_key.astype(jnp.float32), w_value.astype(jnp.float32), w_output.astype(jnp.float32), second_gain.astype(jnp.float32), w_gate.astype(jnp.float32), w_up.astype(jnp.float32), w_down.astype(jnp.float32))

    def per_sequence(running, pieces):
        byte_row, mark_row, cotangent = pieces

        def forward(params):
            return layer_forward(params, byte_row, mark_row)
        result, pullback = jax.vjp(forward, weights)
        fresh = pullback(cotangent.astype(jnp.float32))[0]
        return (jax.tree.map(jnp.add, running, fresh), result.astype(jnp.bfloat16))
    initial = jax.tree.map(jnp.zeros_like, weights)
    totals, outputs = lax.scan(per_sequence, initial, (byte_ids, segments + 1, out_grad))
    return (outputs, totals[0], totals[1], totals[2], totals[3], totals[4], totals[5], totals[6], totals[7], totals[8], totals[9], totals[10], totals[11])
```

```python
import functools

import jax
import jax.numpy as jnp
from jax import lax
from jax.experimental import pallas as pl
from jax.experimental.pallas import tpu as pltpu
from jax.sharding import PartitionSpec as P

HEADS = 12
HEAD_DIM = 64
VOCAB = 256
MAXBLOCK = 4
KW = 5
ALL = ("dp", "seq")
EDGE = 4
PAD = 8

MESH = pl.DeviceIdType.MESH


def position():
    dp = lax.axis_index("dp")
    place = lax.axis_index("seq")
    lines = lax.axis_size("dp") // 4
    group = dp // 2
    return group // 2, group % 2, dp % 2, place, lines, lax.axis_size("seq")


def dp_of(y, x, core):
    return (y * 2 + x) * 2 + core


def meet(targets):
    barrier = pltpu.get_barrier_semaphore()
    for dp, place in targets:
        pl.semaphore_signal(barrier, inc=1, device_id=(dp, place), device_id_type=MESH)
    pl.semaphore_wait(barrier, len(targets))


def remote(src, dst, send_sem, recv_sem, dp, place):
    return pltpu.make_async_remote_copy(
        src_ref=src,
        dst_ref=dst,
        send_sem=send_sem,
        recv_sem=recv_sem,
        device_id=(dp, place),
        device_id_type=MESH,
    )


GATHER_ITEMS = (
    (7, 0, 0, 0),
    (8, 0, 0, 0),
    (0, 0, 0, 0),
    (2, 0, 0, 1),
    (1, 0, 0, 0),
    (3, 0, 0, 1),
    (4, 0, 0, 0),
    (5, 0, 0, 1),
    (6, 0, 1, 0),
    (6, 1, 1, 1),
)
GATHER_PHASES = ((0, 1), (2, 3, 4, 5), (6, 7), (8, 9))


def gather_kernel(arrays, *refs):
    ins = refs[:arrays]
    cells_in, cot_in = refs[arrays], refs[arrays + 1]
    outs = refs[arrays + 2 : 2 * arrays + 2]
    cells_out, cot_out = refs[2 * arrays + 2], refs[2 * arrays + 3]
    recv, recv_sib, send_z, send_x, send_y, send_sib, own_sem, cell_recv, cell_send, cot_recv, cot_send = refs[
        2 * arrays + 4 :
    ]
    y, x, core, place, lines, count = position()
    seqs = cells_in.shape[0]
    groups = lines * 2
    group = y * 2 + x
    dp = dp_of(y, x, core)
    twin = dp_of(y, x, 1 - core)
    side = dp_of(y, 1 - x, core)
    ahead = [(y + k) % lines for k in range(1, lines)]

    targets = [(twin, place), (side, place)]
    for k in range(1, count):
        targets += [(dp, (place + k) % count), (twin, (place + k) % count)]
    for other_y in ahead:
        targets.append((dp_of(other_y, x, core), place))
    meet(targets)

    def cell_copies(fn_remote, fn_local):
        for r in range(seqs):
            chip = seqs * core + r
            for c in range(2):
                home = (chip == place) & (core == c)

                @pl.when(home)
                def _():
                    fn_local(r, c)

                @pl.when(jnp.logical_not(home))
                def _():
                    fn_remote(r, c, chip)

    def cell_remote(r, c, chip):
        return remote(
            cells_in.at[r],
            cells_out.at[place],
            cell_send.at[r, c],
            cell_recv.at[place],
            dp_of(y, x, c),
            chip,
        )

    cell_copies(
        lambda r, c, chip: cell_remote(r, c, chip).start(),
        lambda r, c: pltpu.make_async_copy(
            cells_in.at[r], cells_out.at[place], cell_recv.at[place]
        ).start(),
    )

    def view(item):
        array, first, columns, _ = GATHER_ITEMS[item]
        in_ref, out_ref = ins[array], outs[array]
        if columns:
            cols = in_ref.shape[1] // 2
            lanes = pl.ds(first * cols, cols)
        else:
            lanes = pl.ds(0, in_ref.shape[1])
        return in_ref.at[:, lanes], out_ref, lanes

    def block(item, g, z):
        _, out_ref, lanes = view(item)
        return out_ref.at[(g * 2 + core) * count + z, :, lanes]

    def group_block(item, g, c):
        _, out_ref, lanes = view(item)
        return out_ref.at[pl.ds((g * 2 + c) * count, count), :, lanes]

    def many(item, blocks):
        _, out_ref, lanes = view(item)
        return out_ref.at[pl.ds(0, blocks), :, lanes]

    def arrived(item, g, z):
        dst = block(item, g, z)
        remote(dst, dst, send_x.at[item], recv.at[item, g * count + z], twin, place).wait_recv()

    def to_side(item, src, g, z):
        remote(src, block(item, g, z), send_x.at[item], recv.at[item, g * count + z], side, place).start()

    def to_lines(item, src, g, z):
        for other_y in ahead:
            remote(
                src,
                block(item, g, z),
                send_y.at[item],
                recv.at[item, g * count + z],
                dp_of(other_y, x, core),
                place,
            ).start()

    def to_z(item, src, z, step):
        return remote(
            src,
            block(item, group, z),
            send_z.at[item, z, step],
            recv.at[item, group * count + z],
            dp,
            place + 1 - 2 * step,
        )

    def to_twin(item, g):
        src = group_block(item, g, core)
        remote(src, src, send_sib.at[item], recv_sib.at[item, g], twin, place).start()

    def own_copy(item):
        return pltpu.make_async_copy(view(item)[0], block(item, group, place), own_sem.at[item])

    def first_own(items):
        for item in items:
            src = view(item)[0]

            @pl.when(place < count - 1)
            def _():
                to_z(item, src, place, 0).start()

            @pl.when(place > 0)
            def _():
                to_z(item, src, place, 1).start()

            own_copy(item).start()

    def first_sides(items):
        for item in items:
            src = view(item)[0]
            to_side(item, src, group, place)
            to_lines(item, src, group, place)

    def first_level(items):
        def step(s, carry):
            low = place - s
            high = place + s
            for item in items:

                @pl.when(low >= 0)
                def _():
                    arrived(item, group, low)
                    src = block(item, group, low)

                    @pl.when(place < count - 1)
                    def _():
                        to_z(item, src, low, 0).start()

                    to_side(item, src, group, low)
                    to_lines(item, src, group, low)

                @pl.when(high < count)
                def _():
                    arrived(item, group, high)
                    src = block(item, group, high)

                    @pl.when(place > 0)
                    def _():
                        to_z(item, src, high, 1).start()

                    to_side(item, src, group, high)
                    to_lines(item, src, group, high)

            return carry

        lax.fori_loop(1, count, step, 0)
        for item in items:
            own_copy(item).wait()
            to_twin(item, group)

    def second_level(items):
        def step(s, carry):
            z = (place + s) % count
            for item in items:
                if GATHER_ITEMS[item][3] == 0:
                    g = y * 2 + (1 - x)
                    arrived(item, g, z)
                    to_lines(item, block(item, g, z), g, z)
                else:
                    for other_y in ahead:
                        g = other_y * 2 + x
                        arrived(item, g, z)
                        to_side(item, block(item, g, z), g, z)
            return carry

        lax.fori_loop(0, count, step, 0)
        for item in items:
            if GATHER_ITEMS[item][3] == 0:
                to_twin(item, y * 2 + (1 - x))
            else:
                for other_y in ahead:
                    to_twin(item, other_y * 2 + x)

    def third_level(items):
        def rest(item):
            if GATHER_ITEMS[item][3] == 0:
                return [other_y * 2 + other_x for other_y in ahead for other_x in (x, 1 - x)]
            return [other_y * 2 + (1 - x) for other_y in [y] + ahead]

        def step(s, carry):
            z = (place + s) % count
            for item in items:
                for g in rest(item):
                    arrived(item, g, z)
            return carry

        lax.fori_loop(0, count, step, 0)
        for item in items:
            for g in rest(item):
                to_twin(item, g)

    def cot_copies(fn_remote, fn_local):
        for r in range(seqs):
            chip = seqs * core + r
            home = (chip == place) & (core == place // seqs)

            @pl.when(home)
            def _():
                fn_local(r)

            @pl.when(jnp.logical_not(home))
            def _():
                fn_remote(r, chip)

    def cot_remote(r, chip):
        return remote(
            cot_in.at[r],
            cot_out.at[place % seqs],
            cot_send.at[r],
            cot_recv.at[place % seqs],
            dp_of(y, x, place // seqs),
            chip,
        )

    phases = GATHER_PHASES
    for items in phases:
        first_own(items)
    first_sides(phases[0])
    first_level(phases[0])
    for k in range(1, len(phases)):
        first_sides(phases[k])
        first_level(phases[k])
        second_level(phases[k - 1])
        if k == 1:
            cot_copies(
                lambda r, chip: cot_remote(r, chip).start(),
                lambda r: pltpu.make_async_copy(
                    cot_in.at[r], cot_out.at[place % seqs], cot_recv.at[place % seqs]
                ).start(),
            )
        if k > 1:
            third_level(phases[k - 2])
    second_level(phases[-1])
    third_level(phases[-2])
    third_level(phases[-1])

    for item in range(len(GATHER_ITEMS)):
        for g in range(groups):
            dst = group_block(item, g, 1 - core)
            remote(dst, dst, send_sib.at[item], recv_sib.at[item, g], twin, place).wait_recv()
        tree = GATHER_ITEMS[item][3]

        def sent(blocks, sem):
            src = many(item, blocks)
            remote(src, src, sem, recv.at[item, 0], twin, place).wait_send()

        sent(count * (1 if tree == 0 else lines), send_x.at[item])
        sent(count * (lines - 1) * (2 if tree == 0 else 1), send_y.at[item])
        sent(count * groups, send_sib.at[item])

        def drain(z, carry):
            @pl.when((z <= place) & (place < count - 1))
            def _():
                to_z(item, block(item, group, z), z, 0).wait_send()

            @pl.when((z >= place) & (place > 0))
            def _():
                to_z(item, block(item, group, z), z, 1).wait_send()

            return carry

        lax.fori_loop(0, count, drain, 0)
    for q in range(count):
        dst = cells_out.at[q]
        remote(dst, dst, cell_send.at[0, 0], cell_recv.at[q], twin, place).wait_recv()
    for q in range(seqs):
        dst = cot_out.at[q]
        remote(dst, dst, cot_send.at[0], cot_recv.at[q], twin, place).wait_recv()
    cell_copies(lambda r, c, chip: cell_remote(r, c, chip).wait_send(), lambda r, c: None)
    cot_copies(lambda r, chip: cot_remote(r, chip).wait_send(), lambda r: None)


def gather_all(shards, cells, cot):
    count = lax.axis_size("seq")
    group_count = lax.axis_size(ALL)
    groups = group_count // (2 * count)
    items = len(GATHER_ITEMS)
    seqs = cells.shape[0]
    vmem = pl.BlockSpec(memory_space=pltpu.VMEM)
    hbm = pl.BlockSpec(memory_space=pltpu.HBM)
    shapes = [jax.ShapeDtypeStruct((group_count,) + s.shape, s.dtype) for s in shards]
    shapes.append(jax.ShapeDtypeStruct((count,) + cells.shape[1:], cells.dtype))
    shapes.append(jax.ShapeDtypeStruct(cot.shape, cot.dtype))
    dma = pltpu.SemaphoreType.DMA
    out = pl.pallas_call(
        functools.partial(gather_kernel, len(shards)),
        name="gather_all",
        out_shape=shapes,
        in_specs=[vmem] * (len(shards) + 2),
        out_specs=[hbm] * len(shapes),
        scratch_shapes=[
            dma((items, groups * count)),
            dma((items, groups)),
            dma((items, count, 2)),
            dma((items,)),
            dma((items,)),
            dma((items,)),
            dma((items,)),
            dma((count,)),
            dma((seqs, 2)),
            dma((seqs,)),
            dma((seqs,)),
        ],
        compiler_params=pltpu.CompilerParams(collective_id=0, has_side_effects=True),
    )(*shards, cells, cot)
    full = [o.reshape(-1, o.shape[2]) for o in out[: len(shards)]]
    return full + list(out[len(shards) :])


SCATTER_ITEMS = (
    (6, 0, 0),
    (6, 1, 1),
    (4, None, 0),
    (5, None, 1),
    (3, None, 1),
    (0, None, 0),
    (1, None, 0),
    (2, None, 1),
    (7, None, 0),
    (8, None, 0),
)


def scatter_kernel(arrays, *refs):
    ins = refs[:arrays]
    layer_in = refs[arrays]
    outs = refs[arrays + 1 : 2 * arrays + 1]
    layer_out = refs[2 * arrays + 1]
    items = len(SCATTER_ITEMS)
    at = 2 * arrays + 2
    own = refs[at : at + items]
    from_twin = refs[at + items : at + 2 * items]
    first_in = refs[at + 2 * items : at + 3 * items]
    second_in = refs[at + 3 * items : at + 4 * items]
    line_in = refs[at + 4 * items : at + 5 * items]
    (
        own_sem,
        twin_send,
        twin_recv,
        x_send,
        x_recv,
        y_send,
        y_recv,
        z_send,
        z_recv,
        layer_send,
        layer_recv,
    ) = refs[at + 5 * items :]
    y, x, core, place, lines, count = position()
    seqs = layer_in.shape[0]
    dp = dp_of(y, x, core)
    twin = dp_of(y, x, 1 - core)
    side = dp_of(y, 1 - x, core)
    ahead = [(y + k) % lines for k in range(1, lines)]
    back = [(y - k + lines) % lines for k in range(1, lines)]

    targets = [(twin, place), (side, place)]
    for k in range(1, count):
        targets += [(dp, (place + k) % count), (twin, (place + k) % count)]
    for other_y in ahead:
        targets.append((dp_of(other_y, x, core), place))
    meet(targets)

    def columns(item):
        array, part, _ = SCATTER_ITEMS[item]
        cols = ins[array].shape[-1]
        if part is None:
            return pl.ds(0, cols)
        return pl.ds(part * (cols // 2), cols // 2)

    def to_twin(item):
        src = ins[SCATTER_ITEMS[item][0]].at[:, :, 1 - core, :, :, columns(item)]
        return remote(src, from_twin[item], twin_send.at[item], twin_recv.at[item], twin, place)

    def own_in(item):
        src = ins[SCATTER_ITEMS[item][0]].at[:, :, core, :, :, columns(item)]
        return pltpu.make_async_copy(src, own[item], own_sem.at[item])

    def plus(left, right):
        total = left.astype(jnp.float32) + right.astype(jnp.float32)
        return total.astype(left.dtype)

    def x_copy(item):
        if SCATTER_ITEMS[item][2] == 0:
            return remote(
                own[item].at[y, 1 - x], second_in[item].at[0], x_send.at[item], x_recv.at[item], side, place
            )
        return remote(own[item].at[:, 1 - x], first_in[item], x_send.at[item], x_recv.at[item], side, place)

    def y_copy(item, k):
        other_y = ahead[k]
        if SCATTER_ITEMS[item][2] == 0:
            src, dst = own[item].at[other_y], first_in[item].at[k]
        else:
            src, dst = own[item].at[other_y, x], second_in[item].at[k]
        return remote(
            src, dst, y_send.at[item, k], y_recv.at[item, k], dp_of(other_y, x, core), place
        )

    def stage_core(item):
        own_in(item).wait()
        to_twin(item).wait_recv()

        def step(i, carry):
            a, b = i // 2, i % 2
            own[item][a, b] = plus(own[item][a, b], from_twin[item][a, b])
            return carry

        lax.fori_loop(0, 2 * lines, step, 0)
        if SCATTER_ITEMS[item][2] == 0:
            for k in range(lines - 1):
                y_copy(item, k).start()
        else:
            x_copy(item).start()

    def stage_first(item):
        if SCATTER_ITEMS[item][2] == 0:
            for k in range(lines - 1):
                y_copy(item, k).wait_recv()
            for b in range(2):
                total = own[item][y, b]
                for k in range(lines - 1):
                    total = plus(total, first_in[item][k, b])
                own[item][y, b] = total
            x_copy(item).start()
        else:
            x_copy(item).wait_recv()

            def step(a, carry):
                own[item][a, x] = plus(own[item][a, x], first_in[item][a])
                return carry

            lax.fori_loop(0, lines, step, 0)
            for k in range(lines - 1):
                y_copy(item, k).start()

    def mine(item, z):
        return own[item].at[y, x, z]

    def z_copy(item, z, way):
        return remote(
            mine(item, z),
            line_in[item].at[way, z],
            z_send.at[item, z],
            z_recv.at[item, way, z],
            dp,
            place + 1 - 2 * way,
        )

    def z_forward(item, way, first):
        def step(z, carry):
            beyond = (z > place) if way == 0 else (z < place)

            @pl.when(beyond)
            def _():
                if not first:
                    z_copy(item, z, way).wait_recv()
                    ref = mine(item, z)
                    ref[...] = plus(ref[...], line_in[item][way, z])
                z_copy(item, z, way).start()

            return carry

        lax.fori_loop(0, count, step, 0)

    def stage_second(item):
        if SCATTER_ITEMS[item][2] == 0:
            x_copy(item).wait_recv()
            total = plus(own[item][y, x], second_in[item][0])
        else:
            total = own[item][y, x]
            for k in range(lines - 1):
                y_copy(item, k).wait_recv()
                total = plus(total, second_in[item][k])
        own[item][y, x] = total

        @pl.when(place == 0)
        def _():
            z_forward(item, 0, True)

        @pl.when(place == count - 1)
        def _():
            z_forward(item, 1, True)

    def stage_hop(item, hop):
        @pl.when(place == hop)
        def _():
            z_forward(item, 0, False)

        @pl.when(count - 1 - place == hop)
        def _():
            z_forward(item, 1, False)

    def stage_last(item):
        array, part, _ = SCATTER_ITEMS[item]
        outs[array][:, columns(item)] = mine(item, place)[...].astype(jnp.float32)

        def add(way):
            z_copy(item, place, way).wait_recv()
            outs[array][:, columns(item)] += line_in[item][way, place].astype(jnp.float32)

        @pl.when(place > 0)
        def _():
            add(0)

        @pl.when(place < count - 1)
        def _():
            add(1)

    def layer_copies(fn_remote, fn_local):
        for k in range(seqs):
            chip = seqs * core + k
            home = (chip == place) & (core == place // seqs)

            @pl.when(home)
            def _():
                fn_local(k)

            @pl.when(jnp.logical_not(home))
            def _():
                fn_remote(k, chip)

    def layer_remote(k, chip):
        return remote(
            layer_in.at[k],
            layer_out.at[place % seqs],
            layer_send.at[k],
            layer_recv.at[place % seqs],
            dp_of(y, x, place // seqs),
            chip,
        )

    layer_copies(
        lambda k, chip: layer_remote(k, chip).start(),
        lambda k: pltpu.make_async_copy(
            layer_in.at[k], layer_out.at[place % seqs], layer_recv.at[place % seqs]
        ).start(),
    )
    for item in range(items):
        to_twin(item).start()
        own_in(item).start()
    stages = [stage_core, stage_first, stage_second]
    for hop in range(1, count - 1):
        stages.append(functools.partial(lambda hop, item: stage_hop(item, hop), hop))
    stages.append(stage_last)
    for t in range(items + len(stages) - 1):
        for lag, stage in enumerate(stages):
            if 0 <= t - lag < items:
                stage(t - lag)

    for item in range(items):
        to_twin(item).wait_send()
        x_copy(item).wait_send()
        for k in range(lines - 1):
            y_copy(item, k).wait_send()

        def drain(z, carry):
            @pl.when(z > place)
            def _():
                z_copy(item, z, 0).wait_send()

            @pl.when(z < place)
            def _():
                z_copy(item, z, 1).wait_send()

            return carry

        lax.fori_loop(0, count, drain, 0)
    for r in range(seqs):
        dst = layer_out.at[r]
        remote(dst, dst, layer_send.at[0], layer_recv.at[r], twin, place).wait_recv()
    layer_copies(lambda k, chip: layer_remote(k, chip).wait_send(), lambda k: None)


def scatter_all(grads, layer_rows):
    count = lax.axis_size("seq")
    lines = lax.axis_size("dp") // 4
    items = len(SCATTER_ITEMS)
    seqs = layer_rows.shape[0]
    vmem = pl.BlockSpec(memory_space=pltpu.VMEM)
    hbm = pl.BlockSpec(memory_space=pltpu.HBM)
    total = lines * 4 * count
    shapes = [jax.ShapeDtypeStruct((g.shape[0] // total, g.shape[1]), jnp.float32) for g in grads]
    shapes.append(jax.ShapeDtypeStruct(layer_rows.shape, layer_rows.dtype))
    own, first_in, second_in, line_in = [], [], [], []
    for array, part, order in SCATTER_ITEMS:
        grad = grads[array]
        cols = grad.shape[1] // (1 if part is None else 2)
        rows = grad.shape[0] // total
        kind = grad.dtype
        own.append(pltpu.VMEM((lines, 2, count, rows, cols), kind))
        if order == 0:
            first_in.append(pltpu.VMEM((lines - 1, 2, count, rows, cols), kind))
            second_in.append(pltpu.VMEM((1, count, rows, cols), kind))
        else:
            first_in.append(pltpu.VMEM((lines, count, rows, cols), kind))
            second_in.append(pltpu.VMEM((lines - 1, count, rows, cols), kind))
        line_in.append(pltpu.VMEM((2, count, rows, cols), kind))
    dma = pltpu.SemaphoreType.DMA
    sems = [
        dma((items,)),
        dma((items,)),
        dma((items,)),
        dma((items,)),
        dma((items,)),
        dma((items, lines - 1)),
        dma((items, lines - 1)),
        dma((items, count)),
        dma((items, 2, count)),
        dma((seqs,)),
        dma((seqs,)),
    ]
    views = [g.reshape(lines, 2, 2, count, g.shape[0] // total, g.shape[1]) for g in grads]
    return pl.pallas_call(
        functools.partial(scatter_kernel, len(grads)),
        name="scatter_all",
        out_shape=shapes,
        in_specs=[hbm] * len(grads) + [vmem],
        out_specs=[vmem] * len(grads) + [hbm],
        scratch_shapes=own + own + first_in + second_in + line_in + sems,
        compiler_params=pltpu.CompilerParams(
            collective_id=1, has_side_effects=True, vmem_limit_bytes=50 * 1024 * 1024
        ),
    )(*views, layer_rows)


def mm(left, right):
    return jnp.dot(left, right, preferred_element_type=jnp.float32)


def mm_nt(left, right):
    return lax.dot_general(left, right, (((1,), (1,)), ((), ())), preferred_element_type=jnp.float32)


def mm_tn(left, right):
    return lax.dot_general(left, right, (((0,), (0,)), ((), ())), preferred_element_type=jnp.float32)


def rms_scale(values, gain):
    return values * lax.rsqrt(jnp.mean(values * values, axis=-1, keepdims=True) + 1e-06) * gain


def gelu_tanh(values):
    return jax.nn.gelu(values, approximate=True)


def split_heads(rows):
    return rows.reshape(rows.shape[0], HEADS, HEAD_DIM)


def per_device(
    byte_ids,
    segments,
    embed_table,
    conv_weight,
    score_vector,
    first_gain,
    w_query,
    w_key,
    w_value,
    w_output,
    second_gain,
    w_gate,
    w_up,
    w_down,
    out_grad,
):
    seqs, part_bytes = byte_ids.shape
    count = lax.axis_size("seq")
    group_count = lax.axis_size(ALL)
    seq_len = part_bytes * count
    width = w_query.shape[1]
    wide = w_gate.shape[1]
    half_bytes = seq_len // 2
    half = half_bytes // 2
    core = lax.axis_index("dp") % 2
    place = lax.axis_index("seq")

    chan = conv_weight.shape[0]
    small = jnp.concatenate(
        [conv_weight.T, score_vector[None], first_gain[None], second_gain[None]], axis=0
    ).astype(jnp.float32)
    small = jnp.pad(small, ((0, 0), (0, 128 - chan)))
    cells = jnp.stack([byte_ids, segments + 1], axis=1).reshape(seqs, -1, 128)
    shards = (w_query, w_key, w_value, w_output, w_gate, w_up, w_down, embed_table, small)
    wq, wk, wv, wo, wg, wu, wd, table, small_full, cells, cot = gather_all(shards, cells, out_grad)
    cells = cells.reshape(count, 2, part_bytes).transpose(1, 0, 2).reshape(2, seq_len)
    ids_row, marks_row = cells[0], cells[1]
    cot = cot.reshape(half, width)
    table = table.astype(jnp.float32)
    small_full = small_full.reshape(group_count, 8, 128)[:, :, :chan].transpose(1, 0, 2).reshape(8, width)
    taps = small_full[:KW]
    score = small_full[KW]
    gain_one = small_full[KW + 1 : KW + 2]
    gain_two = small_full[KW + 2 : KW + 3]

    span = half_bytes + 2 * EDGE
    start = core * half_bytes
    ids_pad = jnp.pad(ids_row, (PAD, PAD), constant_values=-1)
    marks_pad = jnp.pad(marks_row, (PAD, PAD))

    def window(padded, lead, length):
        return lax.dynamic_slice_in_dim(padded, start + PAD - lead, length, axis=0)

    marks_win = window(marks_pad, EDGE, span)
    ids_of_tap = []
    for tap in range(KW):
        ids_t = window(ids_pad, EDGE + KW // 2 - tap, span)
        marks_t = window(marks_pad, EDGE + KW // 2 - tap, span)
        ids_of_tap.append(jnp.where((marks_t == marks_win) & (marks_win > 0), ids_t, -1))
    ids_of_tap = jnp.stack(ids_of_tap, axis=1)
    vocab = jnp.arange(VOCAB, dtype=jnp.int32)
    one_hot = (ids_of_tap[:, :, None] == vocab).astype(jnp.bfloat16).reshape(span, KW * VOCAB)
    tap_table32 = (taps[:, None, :] * table[None]).reshape(KW * VOCAB, width)
    tap_table = tap_table32.astype(jnp.bfloat16)
    scored = jnp.sum(tap_table32 * score, axis=-1)
    u_win = jnp.sum(one_hot.astype(jnp.float32) * scored[None], axis=-1)

    places = start + jnp.arange(half_bytes, dtype=jnp.int32)
    here = marks_win[EDGE : EDGE + half_bytes]
    member = []
    numbers = []
    scores = []
    for block in range(1, MAXBLOCK + 1):
        inside = {}
        number = jnp.zeros((half_bytes,), jnp.float32)
        summed = jnp.zeros((half_bytes,), jnp.float32)
        for shift in range(1 - block, block):
            same_block = (places + shift) // block == places // block
            same_doc = marks_win[EDGE + shift : EDGE + shift + half_bytes] == here
            on = (same_block & same_doc).astype(jnp.float32)
            inside[shift] = on
            number = number + on
            summed = summed + on * u_win[EDGE + shift : EDGE + shift + half_bytes]
        member.append(inside)
        numbers.append(1.0 / number)
        scores.append(summed / number)
    scores = jnp.stack(scores)
    expo = jnp.exp(scores - jnp.max(scores, axis=0, keepdims=True))
    prob = expo / jnp.sum(expo, axis=0, keepdims=True)

    def band(coefs):
        col = jnp.arange(span, dtype=jnp.int32)[None, :]
        centre = 2 * jnp.arange(half, dtype=jnp.int32)[:, None] + EDGE
        out = jnp.zeros((half, span), jnp.float32)
        for shift in range(1 - MAXBLOCK, MAXBLOCK):
            value = jnp.zeros((half_bytes,), jnp.float32)
            for b in range(MAXBLOCK):
                if shift in member[b]:
                    value = value + coefs[b] * numbers[b] * member[b][shift]
            value = value.reshape(half, 2)
            for e in range(2):
                out = out + jnp.where(col == centre + (e + shift), value[:, e : e + 1], 0.0)
        return out

    rows_of = band(0.5 * prob)
    coef = mm(rows_of.astype(jnp.bfloat16), one_hot).astype(jnp.bfloat16)
    stream = mm(coef, tap_table)

    normed_one, norm_pull_one = jax.vjp(rms_scale, stream, gain_one)
    normed_one = normed_one.astype(jnp.bfloat16)
    queries = mm(normed_one, wq).astype(jnp.bfloat16)
    keys = mm(normed_one, wk).astype(jnp.bfloat16)
    vals = mm(normed_one, wv).astype(jnp.bfloat16)

    twins = [(i, i ^ 1) for i in range(lax.axis_size("dp"))]
    other = lax.ppermute(jnp.stack([keys, vals]), "dp", twins)
    low = jnp.where(core == 0, jnp.stack([keys, vals]), other)
    high = jnp.where(core == 0, other, jnp.stack([keys, vals]))
    both_kv = jnp.concatenate([low, high], axis=1)
    all_keys, all_vals = both_kv[0], both_kv[1]
    key_marks = marks_row[::2]
    query_marks = lax.dynamic_slice_in_dim(key_marks, core * half, half, axis=0)
    same = (query_marks[:, None] == key_marks[None, :])[None]
    att = jnp.einsum(
        "qhd,khd->hqk", split_heads(queries), split_heads(all_keys), preferred_element_type=jnp.float32
    ) * HEAD_DIM ** (-0.5)
    att = jnp.where(same, att, -1e30)
    expo = jnp.exp(att - jnp.max(att, axis=-1, keepdims=True))
    soft = expo / jnp.sum(expo, axis=-1, keepdims=True)
    soft16 = soft.astype(jnp.bfloat16)
    attn_out = jnp.einsum(
        "hqk,khd->qhd", soft16, split_heads(all_vals), preferred_element_type=jnp.float32
    )
    attn_out = attn_out.reshape(half, width).astype(jnp.bfloat16)

    resid_one = stream + mm(attn_out, wo)
    normed_two, norm_pull_two = jax.vjp(rms_scale, resid_one, gain_two)
    normed_two = normed_two.astype(jnp.bfloat16)
    gate_pre = mm(normed_two, wg)
    up_pre = mm(normed_two, wu)
    gate_act, gelu_pull = jax.vjp(gelu_tanh, gate_pre)
    hidden = (gate_act * up_pre).astype(jnp.bfloat16)
    layer_rows = (resid_one + mm(hidden, wd)).astype(jnp.bfloat16)
    layer_rows = layer_rows.reshape(seqs, part_bytes // 2, width)

    hidden_grad = mm_nt(cot, wd)
    grad_down = mm_tn(hidden, cot)
    up_grad = (hidden_grad * gate_act).astype(jnp.bfloat16)
    gate_grad = gelu_pull(hidden_grad * up_pre)[0].astype(jnp.bfloat16)
    grad_gate = mm_tn(normed_two, gate_grad)
    grad_up = mm_tn(normed_two, up_grad)
    normed_two_grad = mm_nt(gate_grad, wg) + mm_nt(up_grad, wu)
    resid_part, gain_two_grad = norm_pull_two(normed_two_grad)
    resid_grad = cot.astype(jnp.float32) + resid_part
    proj_grad = resid_grad.astype(jnp.bfloat16)
    grad_output = mm_tn(attn_out, proj_grad)
    attn_grad = mm_nt(proj_grad, wo).astype(jnp.bfloat16)

    prob_grad = jnp.einsum(
        "qhd,khd->hqk", split_heads(attn_grad), split_heads(all_vals), preferred_element_type=jnp.float32
    )
    row_dot = jnp.sum(soft * prob_grad, axis=-1, keepdims=True)
    score_grad = (soft * (prob_grad - row_dot)).astype(jnp.bfloat16)
    scale = HEAD_DIM ** (-0.5)
    query_grad = (
        jnp.einsum("hqk,khd->qhd", score_grad, split_heads(all_keys), preferred_element_type=jnp.float32)
        * scale
    )
    key_grad = (
        jnp.einsum("hqk,qhd->khd", score_grad, split_heads(queries), preferred_element_type=jnp.float32)
        * scale
    )
    value_grad = jnp.einsum(
        "hqk,qhd->khd", soft16, split_heads(attn_grad), preferred_element_type=jnp.float32
    )
    kv_grad = jnp.stack([key_grad.reshape(2, half, width), value_grad.reshape(2, half, width)])
    away = lax.dynamic_index_in_dim(kv_grad, 1 - core, 1, keepdims=False).astype(jnp.bfloat16)
    own = lax.dynamic_index_in_dim(kv_grad, core, 1, keepdims=False)
    kv_sum = (own + lax.ppermute(away, "dp", twins).astype(jnp.float32)).astype(jnp.bfloat16)
    key_grad, value_grad = kv_sum[0], kv_sum[1]
    query_grad = query_grad.reshape(half, width).astype(jnp.bfloat16)
    grad_query = mm_tn(normed_one, query_grad)
    grad_key = mm_tn(normed_one, key_grad)
    grad_value = mm_tn(normed_one, value_grad)
    normed_one_grad = mm_nt(query_grad, wq) + mm_nt(key_grad, wk) + mm_nt(value_grad, wv)
    stream_part, gain_one_grad = norm_pull_one(normed_one_grad)
    stream_grad = resid_grad + stream_part

    stream_grad16 = stream_grad.astype(jnp.bfloat16)
    through = mm_nt(stream_grad16, tap_table).astype(jnp.bfloat16)
    near = mm_nt(through, one_hot)
    centre = 2 * jnp.arange(half, dtype=jnp.int32)[:, None] + EDGE
    col = jnp.arange(span, dtype=jnp.int32)[None, :]
    diag = {}
    for offset in range(1 - MAXBLOCK, MAXBLOCK + 1):
        diag[offset] = jnp.sum(jnp.where(col == centre + offset, near, 0.0), axis=-1)
    prob_grads = []
    for b in range(MAXBLOCK):
        total = jnp.zeros((half_bytes,), jnp.float32)
        for shift, on in member[b].items():
            both_bytes = jnp.stack([diag[shift], diag[shift + 1]], axis=1).reshape(half_bytes)
            total = total + on * both_bytes
        prob_grads.append(0.5 * total * numbers[b])
    prob_grads = jnp.stack(prob_grads)
    size_grad = prob * (prob_grads - jnp.sum(prob * prob_grads, axis=0, keepdims=True))
    u_grad = jnp.sum(band(size_grad), axis=0)
    picked = jnp.sum(one_hot.astype(jnp.float32) * u_grad[:, None], axis=0)
    tap_grad = mm_tn(coef, stream_grad16) + picked[:, None] * score[None]
    tap_grad = tap_grad.reshape(KW, VOCAB, width)
    grad_table = jnp.sum(tap_grad * taps[:, None, :], axis=0)
    conv_grad = jnp.sum(tap_grad * table[None], axis=1)
    score_grad_vec = jnp.sum(tap_table32 * picked[:, None], axis=0)

    small_grad = jnp.concatenate([conv_grad, score_grad_vec[None], gain_one_grad, gain_two_grad], axis=0)
    small_grad = small_grad.reshape(8, group_count, chan).transpose(1, 0, 2)
    small_grad = jnp.pad(small_grad, ((0, 0), (0, 0), (0, 128 - chan))).reshape(-1, 128)
    grads = [grad_query, grad_key, grad_value, grad_output, grad_gate, grad_up, grad_down, grad_table]
    grads = [g.astype(jnp.bfloat16) for g in grads] + [small_grad]
    out = scatter_all(grads, layer_rows)
    small_out = out[8][:, :chan]
    return (
        out[9],
        out[7],
        small_out[:KW].T,
        small_out[KW],
        small_out[KW + 1],
        out[0],
        out[1],
        out[2],
        out[3],
        small_out[KW + 2],
        out[4],
        out[5],
        out[6],
    )


def solution(mesh):
    flat = P(ALL)
    rows = P(ALL, None)
    in_specs = (
        P("dp", "seq"),
        P("dp", "seq"),
        rows,
        rows,
        flat,
        flat,
        rows,
        rows,
        rows,
        rows,
        flat,
        rows,
        rows,
        rows,
        P("dp", "seq", None),
    )
    out_specs = (
        P("dp", "seq", None),
        rows,
        rows,
        flat,
        flat,
        rows,
        rows,
        rows,
        rows,
        flat,
        rows,
        rows,
        rows,
    )
    return jax.shard_map(
        per_device, mesh=mesh, in_specs=in_specs, out_specs=out_specs, check_vma=False
    )
```

```python
import functools

import jax
import jax.numpy as jnp
from jax import lax
from jax.experimental import pallas as pl
from jax.experimental.pallas import tpu as pltpu
from jax.sharding import PartitionSpec as P

HEADS = 12
HEAD_DIM = 64
VOCAB = 256
MAXBLOCK = 4
KW = 5
ALL = ("dp", "seq")
VMEM_BYTES = 56 * 1024 * 1024


def mm(left, right):
    return jnp.dot(left, right, preferred_element_type=jnp.float32)


def mm_nt(left, right):
    return lax.dot_general(left, right, (((1,), (1,)), ((), ())), preferred_element_type=jnp.float32)


def mm_tn(left, right):
    return lax.dot_general(left, right, (((0,), (0,)), ((), ())), preferred_element_type=jnp.float32)


def mm_tt(left, right):
    return lax.dot_general(left, right, (((0,), (1,)), ((), ())), preferred_element_type=jnp.float32)


def rms_scale(values, gain):
    return values * lax.rsqrt(jnp.mean(values * values, axis=-1, keepdims=True) + 1e-06) * gain


def gelu_tanh(values):
    return jax.nn.gelu(values, approximate=True)


MESH = pl.DeviceIdType.MESH


def position():
    dp = lax.axis_index("dp")
    place = lax.axis_index("seq")
    lines = lax.axis_size("dp") // 4
    group = dp // 2
    return group // 2, group % 2, dp % 2, place, lines, lax.axis_size("seq")


def dp_of(y, x, core):
    return (y * 2 + x) * 2 + core


def meet(targets):
    barrier = pltpu.get_barrier_semaphore()
    for dp, place in targets:
        pl.semaphore_signal(barrier, inc=1, device_id=(dp, place), device_id_type=MESH)
    pl.semaphore_wait(barrier, len(targets))


def remote(src, dst, send_sem, recv_sem, dp, place):
    return pltpu.make_async_remote_copy(
        src_ref=src,
        dst_ref=dst,
        send_sem=send_sem,
        recv_sem=recv_sem,
        device_id=(dp, place),
        device_id_type=MESH,
    )


GATHER_ITEMS = (
    (7, 0, 0, 0),
    (8, 0, 0, 0),
    (0, 0, 0, 0),
    (2, 0, 0, 1),
    (1, 0, 0, 0),
    (3, 0, 0, 1),
    (4, 0, 0, 0),
    (5, 0, 0, 1),
    (6, 0, 1, 0),
    (6, 1, 1, 1),
)
GATHER_PHASES = ((0, 1), (2, 3, 4, 5), (6, 7), (8, 9))


def gather_kernel(arrays, *refs):
    ins = refs[:arrays]
    cells_in, cot_in = refs[arrays], refs[arrays + 1]
    outs = refs[arrays + 2 : 2 * arrays + 2]
    cells_out, cot_out = refs[2 * arrays + 2], refs[2 * arrays + 3]
    recv, recv_sib, send_z, send_x, send_y, send_sib, own_sem, cell_recv, cell_send, cot_recv, cot_send = refs[
        2 * arrays + 4 :
    ]
    y, x, core, place, lines, count = position()
    seqs = cells_in.shape[0]
    groups = lines * 2
    group = y * 2 + x
    dp = dp_of(y, x, core)
    twin = dp_of(y, x, 1 - core)
    side = dp_of(y, 1 - x, core)
    ahead = [(y + k) % lines for k in range(1, lines)]

    targets = [(twin, place), (side, place)]
    for k in range(1, count):
        targets += [(dp, (place + k) % count), (twin, (place + k) % count)]
    for other_y in ahead:
        targets.append((dp_of(other_y, x, core), place))
    meet(targets)

    def cell_copies(fn_remote, fn_local):
        for r in range(seqs):
            chip = seqs * core + r
            for c in range(2):
                home = (chip == place) & (core == c)

                @pl.when(home)
                def _():
                    fn_local(r, c)

                @pl.when(jnp.logical_not(home))
                def _():
                    fn_remote(r, c, chip)

    def cell_remote(r, c, chip):
        return remote(
            cells_in.at[r],
            cells_out.at[place],
            cell_send.at[r, c],
            cell_recv.at[place],
            dp_of(y, x, c),
            chip,
        )

    cell_copies(
        lambda r, c, chip: cell_remote(r, c, chip).start(),
        lambda r, c: pltpu.make_async_copy(
            cells_in.at[r], cells_out.at[place], cell_recv.at[place]
        ).start(),
    )

    def view(item):
        array, first, columns, _ = GATHER_ITEMS[item]
        in_ref, out_ref = ins[array], outs[array]
        if columns:
            cols = in_ref.shape[1] // 2
            lanes = pl.ds(first * cols, cols)
        else:
            lanes = pl.ds(0, in_ref.shape[1])
        return in_ref.at[:, lanes], out_ref, lanes

    def block(item, g, z):
        _, out_ref, lanes = view(item)
        return out_ref.at[(g * 2 + core) * count + z, :, lanes]

    def group_block(item, g, c):
        _, out_ref, lanes = view(item)
        return out_ref.at[pl.ds((g * 2 + c) * count, count), :, lanes]

    def many(item, blocks):
        _, out_ref, lanes = view(item)
        return out_ref.at[pl.ds(0, blocks), :, lanes]

    def arrived(item, g, z):
        dst = block(item, g, z)
        remote(dst, dst, send_x.at[item], recv.at[item, g * count + z], twin, place).wait_recv()

    def to_side(item, src, g, z):
        remote(src, block(item, g, z), send_x.at[item], recv.at[item, g * count + z], side, place).start()

    def to_lines(item, src, g, z):
        for other_y in ahead:
            remote(
                src,
                block(item, g, z),
                send_y.at[item],
                recv.at[item, g * count + z],
                dp_of(other_y, x, core),
                place,
            ).start()

    def to_z(item, src, z, step):
        return remote(
            src,
            block(item, group, z),
            send_z.at[item, z, step],
            recv.at[item, group * count + z],
            dp,
            place + 1 - 2 * step,
        )

    def to_twin(item, g):
        src = group_block(item, g, core)
        remote(src, src, send_sib.at[item], recv_sib.at[item, g], twin, place).start()

    def own_copy(item):
        return pltpu.make_async_copy(view(item)[0], block(item, group, place), own_sem.at[item])

    def first_own(items):
        for item in items:
            src = view(item)[0]

            @pl.when(place < count - 1)
            def _():
                to_z(item, src, place, 0).start()

            @pl.when(place > 0)
            def _():
                to_z(item, src, place, 1).start()

            own_copy(item).start()

    def first_sides(items):
        for item in items:
            src = view(item)[0]
            to_side(item, src, group, place)
            to_lines(item, src, group, place)

    def first_level(items):
        def step(s, carry):
            low = place - s
            high = place + s
            for item in items:

                @pl.when(low >= 0)
                def _():
                    arrived(item, group, low)
                    src = block(item, group, low)

                    @pl.when(place < count - 1)
                    def _():
                        to_z(item, src, low, 0).start()

                    to_side(item, src, group, low)
                    to_lines(item, src, group, low)

                @pl.when(high < count)
                def _():
                    arrived(item, group, high)
                    src = block(item, group, high)

                    @pl.when(place > 0)
                    def _():
                        to_z(item, src, high, 1).start()

                    to_side(item, src, group, high)
                    to_lines(item, src, group, high)

            return carry

        lax.fori_loop(1, count, step, 0)
        for item in items:
            own_copy(item).wait()
            to_twin(item, group)

    def second_level(items):
        def step(s, carry):
            z = (place + s) % count
            for item in items:
                if GATHER_ITEMS[item][3] == 0:
                    g = y * 2 + (1 - x)
                    arrived(item, g, z)
                    to_lines(item, block(item, g, z), g, z)
                else:
                    for other_y in ahead:
                        g = other_y * 2 + x
                        arrived(item, g, z)
                        to_side(item, block(item, g, z), g, z)
            return carry

        lax.fori_loop(0, count, step, 0)
        for item in items:
            if GATHER_ITEMS[item][3] == 0:
                to_twin(item, y * 2 + (1 - x))
            else:
                for other_y in ahead:
                    to_twin(item, other_y * 2 + x)

    def third_level(items):
        def rest(item):
            if GATHER_ITEMS[item][3] == 0:
                return [other_y * 2 + other_x for other_y in ahead for other_x in (x, 1 - x)]
            return [other_y * 2 + (1 - x) for other_y in [y] + ahead]

        def step(s, carry):
            z = (place + s) % count
            for item in items:
                for g in rest(item):
                    arrived(item, g, z)
            return carry

        lax.fori_loop(0, count, step, 0)
        for item in items:
            for g in rest(item):
                to_twin(item, g)

    def cot_copies(fn_remote, fn_local):
        for r in range(seqs):
            chip = seqs * core + r
            home = (chip == place) & (core == place // seqs)

            @pl.when(home)
            def _():
                fn_local(r)

            @pl.when(jnp.logical_not(home))
            def _():
                fn_remote(r, chip)

    def cot_remote(r, chip):
        return remote(
            cot_in.at[r],
            cot_out.at[place % seqs],
            cot_send.at[r],
            cot_recv.at[place % seqs],
            dp_of(y, x, place // seqs),
            chip,
        )

    phases = GATHER_PHASES
    for items in phases:
        first_own(items)
    first_sides(phases[0])
    first_level(phases[0])
    for k in range(1, len(phases)):
        first_sides(phases[k])
        first_level(phases[k])
        second_level(phases[k - 1])
        if k == 1:
            cot_copies(
                lambda r, chip: cot_remote(r, chip).start(),
                lambda r: pltpu.make_async_copy(
                    cot_in.at[r], cot_out.at[place % seqs], cot_recv.at[place % seqs]
                ).start(),
            )
        if k > 1:
            third_level(phases[k - 2])
    second_level(phases[-1])
    third_level(phases[-2])
    third_level(phases[-1])

    for item in range(len(GATHER_ITEMS)):
        for g in range(groups):
            dst = group_block(item, g, 1 - core)
            remote(dst, dst, send_sib.at[item], recv_sib.at[item, g], twin, place).wait_recv()
        tree = GATHER_ITEMS[item][3]

        def sent(blocks, sem):
            src = many(item, blocks)
            remote(src, src, sem, recv.at[item, 0], twin, place).wait_send()

        sent(count * (1 if tree == 0 else lines), send_x.at[item])
        sent(count * (lines - 1) * (2 if tree == 0 else 1), send_y.at[item])
        sent(count * groups, send_sib.at[item])

        def drain(z, carry):
            @pl.when((z <= place) & (place < count - 1))
            def _():
                to_z(item, block(item, group, z), z, 0).wait_send()

            @pl.when((z >= place) & (place > 0))
            def _():
                to_z(item, block(item, group, z), z, 1).wait_send()

            return carry

        lax.fori_loop(0, count, drain, 0)
    for q in range(count):
        dst = cells_out.at[q]
        remote(dst, dst, cell_send.at[0, 0], cell_recv.at[q], twin, place).wait_recv()
    for q in range(seqs):
        dst = cot_out.at[q]
        remote(dst, dst, cot_send.at[0], cot_recv.at[q], twin, place).wait_recv()
    cell_copies(lambda r, c, chip: cell_remote(r, c, chip).wait_send(), lambda r, c: None)
    cot_copies(lambda r, chip: cot_remote(r, chip).wait_send(), lambda r: None)


def gather_all(shards, cells, cot):
    count = lax.axis_size("seq")
    group_count = lax.axis_size(ALL)
    groups = group_count // (2 * count)
    items = len(GATHER_ITEMS)
    seqs = cells.shape[0]
    vmem = pl.BlockSpec(memory_space=pltpu.VMEM)
    hbm = pl.BlockSpec(memory_space=pltpu.HBM)
    shapes = [jax.ShapeDtypeStruct((group_count,) + s.shape, s.dtype) for s in shards]
    shapes.append(jax.ShapeDtypeStruct((count,) + cells.shape[1:], cells.dtype))
    shapes.append(jax.ShapeDtypeStruct(cot.shape, cot.dtype))
    dma = pltpu.SemaphoreType.DMA
    out = pl.pallas_call(
        functools.partial(gather_kernel, len(shards)),
        name="gather_all",
        out_shape=shapes,
        in_specs=[vmem] * (len(shards) + 2),
        out_specs=[hbm] * len(shapes),
        scratch_shapes=[
            dma((items, groups * count)),
            dma((items, groups)),
            dma((items, count, 2)),
            dma((items,)),
            dma((items,)),
            dma((items,)),
            dma((items,)),
            dma((count,)),
            dma((seqs, 2)),
            dma((seqs,)),
            dma((seqs,)),
        ],
        compiler_params=pltpu.CompilerParams(collective_id=0, has_side_effects=True),
    )(*shards, cells, cot)
    full = [o.reshape(-1, o.shape[2]) for o in out[: len(shards)]]
    return full + list(out[len(shards) :])


SCATTER_ITEMS = (
    (6, 0, 0),
    (6, 1, 1),
    (4, None, 0),
    (5, None, 1),
    (3, None, 1),
    (0, None, 0),
    (1, None, 0),
    (2, None, 1),
    (7, None, 0),
    (8, None, 0),
)


def scatter_kernel(arrays, *refs):
    ins = refs[:arrays]
    layer_in = refs[arrays]
    outs = refs[arrays + 1 : 2 * arrays + 1]
    layer_out = refs[2 * arrays + 1]
    items = len(SCATTER_ITEMS)
    at = 2 * arrays + 2
    own = refs[at : at + items]
    from_twin = refs[at + items : at + 2 * items]
    first_in = refs[at + 2 * items : at + 3 * items]
    second_in = refs[at + 3 * items : at + 4 * items]
    line_in = refs[at + 4 * items : at + 5 * items]
    (
        own_sem,
        twin_send,
        twin_recv,
        x_send,
        x_recv,
        y_send,
        y_recv,
        z_send,
        z_recv,
        layer_send,
        layer_recv,
    ) = refs[at + 5 * items :]
    y, x, core, place, lines, count = position()
    seqs = layer_in.shape[0]
    dp = dp_of(y, x, core)
    twin = dp_of(y, x, 1 - core)
    side = dp_of(y, 1 - x, core)
    ahead = [(y + k) % lines for k in range(1, lines)]
    back = [(y - k + lines) % lines for k in range(1, lines)]

    targets = [(twin, place), (side, place)]
    for k in range(1, count):
        targets += [(dp, (place + k) % count), (twin, (place + k) % count)]
    for other_y in ahead:
        targets.append((dp_of(other_y, x, core), place))
    meet(targets)

    def columns(item):
        array, part, _ = SCATTER_ITEMS[item]
        cols = ins[array].shape[-1]
        if part is None:
            return pl.ds(0, cols)
        return pl.ds(part * (cols // 2), cols // 2)

    def to_twin(item):
        src = ins[SCATTER_ITEMS[item][0]].at[:, :, 1 - core, :, :, columns(item)]
        return remote(src, from_twin[item], twin_send.at[item], twin_recv.at[item], twin, place)

    def own_in(item):
        src = ins[SCATTER_ITEMS[item][0]].at[:, :, core, :, :, columns(item)]
        return pltpu.make_async_copy(src, own[item], own_sem.at[item])

    def plus(left, right):
        total = left.astype(jnp.float32) + right.astype(jnp.float32)
        return total.astype(left.dtype)

    def x_copy(item):
        if SCATTER_ITEMS[item][2] == 0:
            return remote(
                own[item].at[y, 1 - x], second_in[item].at[0], x_send.at[item], x_recv.at[item], side, place
            )
        return remote(own[item].at[:, 1 - x], first_in[item], x_send.at[item], x_recv.at[item], side, place)

    def y_copy(item, k):
        other_y = ahead[k]
        if SCATTER_ITEMS[item][2] == 0:
            src, dst = own[item].at[other_y], first_in[item].at[k]
        else:
            src, dst = own[item].at[other_y, x], second_in[item].at[k]
        return remote(
            src, dst, y_send.at[item, k], y_recv.at[item, k], dp_of(other_y, x, core), place
        )

    def stage_core(item):
        own_in(item).wait()
        to_twin(item).wait_recv()

        def step(i, carry):
            a, b = i // 2, i % 2
            own[item][a, b] = plus(own[item][a, b], from_twin[item][a, b])
            return carry

        lax.fori_loop(0, 2 * lines, step, 0)
        if SCATTER_ITEMS[item][2] == 0:
            for k in range(lines - 1):
                y_copy(item, k).start()
        else:
            x_copy(item).start()

    def stage_first(item):
        if SCATTER_ITEMS[item][2] == 0:
            for k in range(lines - 1):
                y_copy(item, k).wait_recv()
            for b in range(2):
                total = own[item][y, b]
                for k in range(lines - 1):
                    total = plus(total, first_in[item][k, b])
                own[item][y, b] = total
            x_copy(item).start()
        else:
            x_copy(item).wait_recv()

            def step(a, carry):
                own[item][a, x] = plus(own[item][a, x], first_in[item][a])
                return carry

            lax.fori_loop(0, lines, step, 0)
            for k in range(lines - 1):
                y_copy(item, k).start()

    def mine(item, z):
        return own[item].at[y, x, z]

    def z_copy(item, z, way):
        return remote(
            mine(item, z),
            line_in[item].at[way, z],
            z_send.at[item, z],
            z_recv.at[item, way, z],
            dp,
            place + 1 - 2 * way,
        )

    def z_forward(item, way, first):
        def step(z, carry):
            beyond = (z > place) if way == 0 else (z < place)

            @pl.when(beyond)
            def _():
                if not first:
                    z_copy(item, z, way).wait_recv()
                    ref = mine(item, z)
                    ref[...] = plus(ref[...], line_in[item][way, z])
                z_copy(item, z, way).start()

            return carry

        lax.fori_loop(0, count, step, 0)

    def stage_second(item):
        if SCATTER_ITEMS[item][2] == 0:
            x_copy(item).wait_recv()
            total = plus(own[item][y, x], second_in[item][0])
        else:
            total = own[item][y, x]
            for k in range(lines - 1):
                y_copy(item, k).wait_recv()
                total = plus(total, second_in[item][k])
        own[item][y, x] = total

        @pl.when(place == 0)
        def _():
            z_forward(item, 0, True)

        @pl.when(place == count - 1)
        def _():
            z_forward(item, 1, True)

    def stage_hop(item, hop):
        @pl.when(place == hop)
        def _():
            z_forward(item, 0, False)

        @pl.when(count - 1 - place == hop)
        def _():
            z_forward(item, 1, False)

    def stage_last(item):
        array, part, _ = SCATTER_ITEMS[item]
        outs[array][:, columns(item)] = mine(item, place)[...].astype(jnp.float32)

        def add(way):
            z_copy(item, place, way).wait_recv()
            outs[array][:, columns(item)] += line_in[item][way, place].astype(jnp.float32)

        @pl.when(place > 0)
        def _():
            add(0)

        @pl.when(place < count - 1)
        def _():
            add(1)

    def layer_copies(fn_remote, fn_local):
        for k in range(seqs):
            chip = seqs * core + k
            home = (chip == place) & (core == place // seqs)

            @pl.when(home)
            def _():
                fn_local(k)

            @pl.when(jnp.logical_not(home))
            def _():
                fn_remote(k, chip)

    def layer_remote(k, chip):
        return remote(
            layer_in.at[k],
            layer_out.at[place % seqs],
            layer_send.at[k],
            layer_recv.at[place % seqs],
            dp_of(y, x, place // seqs),
            chip,
        )

    layer_copies(
        lambda k, chip: layer_remote(k, chip).start(),
        lambda k: pltpu.make_async_copy(
            layer_in.at[k], layer_out.at[place % seqs], layer_recv.at[place % seqs]
        ).start(),
    )
    for item in range(items):
        to_twin(item).start()
        own_in(item).start()
    stages = [stage_core, stage_first, stage_second]
    for hop in range(1, count - 1):
        stages.append(functools.partial(lambda hop, item: stage_hop(item, hop), hop))
    stages.append(stage_last)
    for t in range(items + len(stages) - 1):
        for lag, stage in enumerate(stages):
            if 0 <= t - lag < items:
                stage(t - lag)

    for item in range(items):
        to_twin(item).wait_send()
        x_copy(item).wait_send()
        for k in range(lines - 1):
            y_copy(item, k).wait_send()

        def drain(z, carry):
            @pl.when(z > place)
            def _():
                z_copy(item, z, 0).wait_send()

            @pl.when(z < place)
            def _():
                z_copy(item, z, 1).wait_send()

            return carry

        lax.fori_loop(0, count, drain, 0)
    for r in range(seqs):
        dst = layer_out.at[r]
        remote(dst, dst, layer_send.at[0], layer_recv.at[r], twin, place).wait_recv()
    layer_copies(lambda k, chip: layer_remote(k, chip).wait_send(), lambda k: None)


def scatter_all(grads, layer_rows):
    count = lax.axis_size("seq")
    lines = lax.axis_size("dp") // 4
    items = len(SCATTER_ITEMS)
    seqs = layer_rows.shape[0]
    vmem = pl.BlockSpec(memory_space=pltpu.VMEM)
    hbm = pl.BlockSpec(memory_space=pltpu.HBM)
    total = lines * 4 * count
    shapes = [jax.ShapeDtypeStruct((g.shape[0] // total, g.shape[1]), jnp.float32) for g in grads]
    shapes.append(jax.ShapeDtypeStruct(layer_rows.shape, layer_rows.dtype))
    own, first_in, second_in, line_in = [], [], [], []
    for array, part, order in SCATTER_ITEMS:
        grad = grads[array]
        cols = grad.shape[1] // (1 if part is None else 2)
        rows = grad.shape[0] // total
        kind = grad.dtype
        own.append(pltpu.VMEM((lines, 2, count, rows, cols), kind))
        if order == 0:
            first_in.append(pltpu.VMEM((lines - 1, 2, count, rows, cols), kind))
            second_in.append(pltpu.VMEM((1, count, rows, cols), kind))
        else:
            first_in.append(pltpu.VMEM((lines, count, rows, cols), kind))
            second_in.append(pltpu.VMEM((lines - 1, count, rows, cols), kind))
        line_in.append(pltpu.VMEM((2, count, rows, cols), kind))
    dma = pltpu.SemaphoreType.DMA
    sems = [
        dma((items,)),
        dma((items,)),
        dma((items,)),
        dma((items,)),
        dma((items,)),
        dma((items, lines - 1)),
        dma((items, lines - 1)),
        dma((items, count)),
        dma((items, 2, count)),
        dma((seqs,)),
        dma((seqs,)),
    ]
    views = [g.reshape(lines, 2, 2, count, g.shape[0] // total, g.shape[1]) for g in grads]
    return pl.pallas_call(
        functools.partial(scatter_kernel, len(grads)),
        name="scatter_all",
        out_shape=shapes,
        in_specs=[hbm] * len(grads) + [vmem],
        out_specs=[vmem] * len(grads) + [hbm],
        scratch_shapes=own + own + first_in + second_in + line_in + sems,
        compiler_params=pltpu.CompilerParams(
            collective_id=1, has_side_effects=True, vmem_limit_bytes=50 * 1024 * 1024
        ),
    )(*views, layer_rows)


LEFT = 128
BAND = 256


def split_two(values):
    high = values.astype(jnp.bfloat16)
    return high, (values - high.astype(jnp.float32)).astype(jnp.bfloat16)


def lane_shift(row, by):
    by = by % row.shape[1]
    return row if by == 0 else pltpu.roll(row, row.shape[1] - by, 1)


def pool_rows(marks, core, half_bytes):
    lanes = lax.broadcasted_iota(jnp.int32, marks[0].shape, 1)
    inside, inverse = {}, {}
    for e in range(2):
        place = core * half_bytes + 2 * (lanes - LEFT) + e + 768
        third = lax.shift_right_logical(place * 21846, 16)
        remains = {2: place & 1, 3: place - 3 * third, 4: place & 3}
        shifted = {}
        for s in range(1 - MAXBLOCK, MAXBLOCK):
            f = (e + s) % 2
            shifted[s] = lane_shift(marks[f], (e + s - f) // 2) == marks[e]
        for b in range(2, MAXBLOCK + 1):
            number = jnp.ones(marks[0].shape, jnp.float32)
            for s in range(1 - b, b):
                if s == 0:
                    continue
                at = remains[b] + s
                on = (shifted[s] & (at >= 0) & (at < b)).astype(jnp.float32)
                inside[b, e, s] = on
                number = number + on
            inverse[b, e] = 1.0 / number
    return inside, inverse


def band_coefs(per_byte, inside, inverse):
    coefs = {}
    for o in range(1 - MAXBLOCK, MAXBLOCK + 1):
        total = None
        for e in range(2):
            s = o - e
            if not 1 - MAXBLOCK <= s < MAXBLOCK:
                continue
            for b in range(1, MAXBLOCK + 1):
                if b == 1:
                    if s != 0:
                        continue
                    term = per_byte[b, e]
                elif s == 0:
                    term = per_byte[b, e] * inverse[b, e]
                elif (b, e, s) in inside:
                    term = per_byte[b, e] * inverse[b, e] * inside[b, e, s]
                else:
                    continue
                total = term if total is None else total + term
        coefs[o] = total
    return coefs


def band_matrix(coefs, block):
    shape = (3 * BAND, BAND)
    delta = lax.broadcasted_iota(jnp.int32, shape, 0) - LEFT - 2 * lax.broadcasted_iota(jnp.int32, shape, 1)
    out = jnp.zeros(shape, jnp.float32)
    for o, row in coefs.items():
        part = row[0:1, LEFT + BAND * block : LEFT + BAND * (block + 1)]
        out = jnp.where(delta == o, part, out)
    return out


def fill_one_hot(one_hot, idm_of_tap):
    span = one_hot.shape[1]
    vocab = lax.broadcasted_iota(jnp.int32, (VOCAB, span), 0)
    for tap in range(KW):
        hit = vocab == idm_of_tap(tap)
        one_hot[tap * VOCAB : (tap + 1) * VOCAB] = hit.astype(jnp.float32).astype(jnp.bfloat16)


def tok_forward_kernel(ids_ref, marks_ref, table_ref, small_ref, stream_ref, normed_ref, coef_ref, tap_ref, rows_ref, idm_ref, one_hot):
    core = lax.axis_index("dp") % 2
    tokens = stream_ref.shape[0]
    half_bytes = 2 * tokens
    span = one_hot.shape[1]
    wide = span + 2 * LEFT
    first = pl.ds(pl.multiple_of(core * half_bytes, 128), wide)
    ids = ids_ref[:, first]
    marks = marks_ref[:, first]
    for tap in range(KW):
        by = tap - KW // 2
        same = (lane_shift(marks, by) == marks) & (marks > 0)
        idm_ref[tap] = jnp.where(same, lane_shift(ids, by), -1)[:, LEFT : LEFT + span]
    fill_one_hot(one_hot, lambda tap: idm_ref[tap, 0:1])

    score = jnp.broadcast_to(small_ref[KW : KW + 1], (8, small_ref.shape[1])).astype(jnp.bfloat16)
    scored = []
    for tap in range(KW):
        product = table_ref[...].astype(jnp.float32) * small_ref[tap : tap + 1]
        high, low = split_two(product)
        tap_ref[tap * VOCAB : (tap + 1) * VOCAB] = high
        scored.append(mm_nt(score, high) + mm_nt(score, low))
    high, low = split_two(jnp.concatenate(scored, axis=1))
    u_row = mm(high, one_hot[...]) + mm(low, one_hot[...])

    high = u_row.astype(jnp.bfloat16).astype(jnp.float32)
    marks_here = marks[:, LEFT : LEFT + span].astype(jnp.float32)
    packed = jnp.concatenate([marks_here, high, u_row - high, jnp.zeros_like(high)], axis=0).astype(jnp.bfloat16)
    shape = (span, wide // 2)
    twice = 2 * lax.broadcasted_iota(jnp.int32, shape, 1) - lax.broadcasted_iota(jnp.int32, shape, 0) - LEFT
    marks_of, u_of = [], []
    for e in range(2):
        pick = (twice == -e).astype(jnp.float32).astype(jnp.bfloat16)
        apart = mm(packed, pick)
        marks_of.append(apart[0:8])
        u_of.append(apart[8:16] + apart[16:24])

    inside, inverse = pool_rows(marks_of, core, half_bytes)
    prob = {}
    for e in range(2):
        shifted = {}
        for s in range(1 - MAXBLOCK, MAXBLOCK):
            f = (e + s) % 2
            shifted[s] = lane_shift(u_of[f], (e + s - f) // 2)
        scores = [u_of[e]]
        for b in range(2, MAXBLOCK + 1):
            total = u_of[e]
            for s in range(1 - b, b):
                if s != 0:
                    total = total + inside[b, e, s] * shifted[s]
            scores.append(total * inverse[b, e])
        top = scores[0]
        for value in scores[1:]:
            top = jnp.maximum(top, value)
        expo = [jnp.exp(value - top) for value in scores]
        whole = expo[0] + expo[1] + expo[2] + expo[3]
        for b in range(1, MAXBLOCK + 1):
            prob[b, e] = expo[b - 1] / whole
            rows_ref[2 * b + e] = prob[b, e]
        rows_ref[e] = marks_of[e]
    coefs = band_coefs({key: 0.5 * value for key, value in prob.items()}, inside, inverse)
    gain = small_ref[KW + 1 : KW + 2]
    for i in range(tokens // BAND):
        matrix = band_matrix(coefs, i).astype(jnp.bfloat16)
        lanes = slice(i * BAND, (i + 1) * BAND)
        part = mm(one_hot[:, 2 * i * BAND : (2 * i + 3) * BAND], matrix).astype(jnp.bfloat16)
        coef_ref[:, lanes] = part
        stream = mm_tn(part, tap_ref[...])
        stream_ref[lanes] = stream
        scale = lax.rsqrt(jnp.mean(stream * stream, axis=-1, keepdims=True) + 1e-06)
        normed_ref[lanes] = (stream * scale * gain).astype(jnp.bfloat16)


def tok_forward(ids_row, marks_row, table, small, tokens):
    width = table.shape[1]
    span = 2 * tokens + 2 * LEFT
    wide = span + 2 * LEFT

    def padded(row, fill):
        row = jnp.pad(row, (2 * LEFT, 2 * LEFT), constant_values=fill)
        return jnp.broadcast_to(row[None], (8, row.shape[0]))

    return pl.pallas_call(
        tok_forward_kernel,
        name="tok_forward",
        out_shape=[
            jax.ShapeDtypeStruct((tokens, width), jnp.float32),
            jax.ShapeDtypeStruct((tokens, width), jnp.bfloat16),
            jax.ShapeDtypeStruct((KW * VOCAB, tokens), jnp.bfloat16),
            jax.ShapeDtypeStruct((KW * VOCAB, width), jnp.bfloat16),
            jax.ShapeDtypeStruct((10, 8, wide // 2), jnp.float32),
            jax.ShapeDtypeStruct((KW, 8, span), jnp.int32),
        ],
        scratch_shapes=[pltpu.VMEM((KW * VOCAB, span), jnp.bfloat16)],
        compiler_params=pltpu.CompilerParams(vmem_limit_bytes=VMEM_BYTES),
    )(padded(ids_row, -1), padded(marks_row, 0), table, small)


def tok_backward_kernel(grad_ref, coef_ref, tap_ref, rows_ref, idm_ref, table_ref, small_ref, table_grad_ref, small_grad_ref, one_hot):
    core = lax.axis_index("dp") % 2
    tokens = grad_ref.shape[0]
    fill_one_hot(one_hot, lambda tap: idm_ref[tap, 0:1])
    marks_of = [rows_ref[0], rows_ref[1]]
    inside, inverse = pool_rows(marks_of, core, 2 * tokens)
    shape = (3 * BAND, BAND)
    delta = lax.broadcasted_iota(jnp.int32, shape, 0) - LEFT - 2 * lax.broadcasted_iota(jnp.int32, shape, 1)
    grad16 = grad_ref[...].astype(jnp.bfloat16)
    through = mm_nt(tap_ref[...], grad16).astype(jnp.bfloat16)
    diag = {o: [] for o in range(1 - MAXBLOCK, MAXBLOCK + 1)}
    edge = jnp.zeros((8, LEFT), jnp.float32)
    for i in range(tokens // BAND):
        near = mm_tn(one_hot[:, 2 * i * BAND : (2 * i + 3) * BAND], through[:, i * BAND : (i + 1) * BAND])
        for o in diag:
            total = jnp.sum(jnp.where(delta == o, near, 0.0), axis=0, keepdims=True)
            diag[o].append(jnp.broadcast_to(total, (8, BAND)))
    diag = {o: jnp.concatenate([edge] + parts + [edge], axis=1) for o, parts in diag.items()}
    size_grad = {}
    for e in range(2):
        grads = [0.5 * diag[e]]
        for b in range(2, MAXBLOCK + 1):
            total = diag[e]
            for s in range(1 - b, b):
                if s != 0:
                    total = total + inside[b, e, s] * diag[s + e]
            grads.append(0.5 * total * inverse[b, e])
        probs = [rows_ref[2 * b + e] for b in range(1, MAXBLOCK + 1)]
        mean = probs[0] * grads[0]
        for p, g in zip(probs[1:], grads[1:]):
            mean = mean + p * g
        for b in range(1, MAXBLOCK + 1):
            size_grad[b, e] = probs[b - 1] * (grads[b - 1] - mean)
    coefs = band_coefs(size_grad, inside, inverse)
    picked = None
    for i in range(tokens // BAND):
        matrix = band_matrix(coefs, i).astype(jnp.bfloat16)
        part = mm(one_hot[:, 2 * i * BAND : (2 * i + 3) * BAND], matrix)
        part = jnp.sum(part, axis=1, keepdims=True)
        picked = part if picked is None else picked + part
    score = small_ref[KW : KW + 1]
    table = table_ref[...].astype(jnp.float32)
    table_grad = None
    score_grad = None
    for tap in range(KW):
        rows = slice(tap * VOCAB, (tap + 1) * VOCAB)
        here = picked[rows]
        part = mm(coef_ref[rows], grad16) + here * score
        taps = small_ref[tap : tap + 1]
        table_grad = part * taps if table_grad is None else table_grad + part * taps
        small_grad_ref[tap : tap + 1] = jnp.sum(part * table, axis=0, keepdims=True)
        summed = jnp.sum(table * here, axis=0, keepdims=True) * taps
        score_grad = summed if score_grad is None else score_grad + summed
    table_grad_ref[...] = table_grad.astype(jnp.bfloat16)
    small_grad_ref[KW : KW + 1] = score_grad


def tok_backward(grad, coef, tap_table, rows, idm, table, small):
    width = table.shape[1]
    return pl.pallas_call(
        tok_backward_kernel,
        name="tok_backward",
        out_shape=[
            jax.ShapeDtypeStruct(table.shape, jnp.bfloat16),
            jax.ShapeDtypeStruct((8, width), jnp.float32),
        ],
        scratch_shapes=[pltpu.VMEM((KW * VOCAB, idm.shape[2]), jnp.bfloat16)],
        compiler_params=pltpu.CompilerParams(vmem_limit_bytes=VMEM_BYTES),
    )(grad, coef, tap_table, rows, idm, table, small)


CHUNK = 256


def pair_rows(ref, h):
    values = ref[...]
    rows = lax.broadcasted_iota(jnp.int32, values.shape, 0)
    return jnp.where((rows // HEAD_DIM) == h, values, jnp.zeros_like(values))


def fill_bias(bias, key_marks, query_marks):
    bias[...] = jnp.where(key_marks[...] == query_marks[...], 0.0, -1e30)


def attend_forward_kernel(qt_ref, kt_ref, vt_ref, key_marks, query_marks, out_ref, lse_ref, bias, scores):
    @pl.when(pl.program_id(0) == 0)
    def _():
        fill_bias(bias, key_marks, query_marks)

    keys = kt_ref[...].T
    chunks = keys.shape[0] // CHUNK
    for h in range(2):
        query = pair_rows(qt_ref, h)
        top = None
        for c in range(chunks):
            rows = slice(c * CHUNK, (c + 1) * CHUNK)
            part = mm(keys[rows], query) + bias[rows]
            scores[h, rows] = part
            high = jnp.max(part, axis=0, keepdims=True)
            top = high if top is None else jnp.maximum(top, high)
        total = None
        out = None
        for c in range(chunks):
            rows = slice(c * CHUNK, (c + 1) * CHUNK)
            expo = jnp.exp(scores[h, rows] - top)
            part = jnp.sum(expo, axis=0, keepdims=True)
            total = part if total is None else total + part
            part = mm(vt_ref[h * HEAD_DIM : (h + 1) * HEAD_DIM, rows], expo.astype(jnp.bfloat16))
            out = part if out is None else out + part
        out_ref[h * HEAD_DIM : (h + 1) * HEAD_DIM] = (out / total).astype(jnp.bfloat16)
        lse_ref[0, h : h + 1] = top + jnp.log(total)


def attend_forward(qt, kt, vt, key_marks, query_marks):
    width, tokens = qt.shape
    keys = kt.shape[1]
    pairs = width // 128
    rows = lambda size: pl.BlockSpec((128, size), lambda i: (i, 0))
    whole = lambda shape: pl.BlockSpec(shape, lambda i: (0, 0))
    return pl.pallas_call(
        attend_forward_kernel,
        name="attend_forward",
        grid=(pairs,),
        in_specs=[rows(tokens), rows(keys), rows(keys), whole((keys, 1)), whole((1, tokens))],
        out_specs=[rows(tokens), pl.BlockSpec((1, 2, tokens), lambda i: (i, 0, 0))],
        out_shape=[
            jax.ShapeDtypeStruct((width, tokens), jnp.bfloat16),
            jax.ShapeDtypeStruct((pairs, 2, tokens), jnp.float32),
        ],
        scratch_shapes=[
            pltpu.VMEM((keys, tokens), jnp.float32),
            pltpu.VMEM((2, keys, tokens), jnp.float32),
        ],
        compiler_params=pltpu.CompilerParams(vmem_limit_bytes=VMEM_BYTES),
    )(qt, kt, vt, key_marks[:, None], query_marks[None])


def attend_backward_kernel(qt_ref, kt_ref, vt_ref, got_ref, out_ref, lse_ref, key_marks, query_marks, dq_ref, dk_ref, dv_ref, bias):
    @pl.when(pl.program_id(0) == 0)
    def _():
        fill_bias(bias, key_marks, query_marks)

    keys = kt_ref[...].T
    vals = vt_ref[...].T
    chunks = keys.shape[0] // CHUNK
    for h in range(2):
        own = slice(h * HEAD_DIM, (h + 1) * HEAD_DIM)
        query = pair_rows(qt_ref, h)
        got = pair_rows(got_ref, h)
        dots = jnp.sum(
            got_ref[own].astype(jnp.float32) * out_ref[own].astype(jnp.float32), axis=0, keepdims=True
        )
        lse = lse_ref[0, h : h + 1]
        query_grad = None
        for c in range(chunks):
            rows = slice(c * CHUNK, (c + 1) * CHUNK)
            soft = jnp.exp(mm(keys[rows], query) + (bias[rows] - lse))
            change = soft * (mm(vals[rows], got) - dots)
            soft16 = soft.astype(jnp.bfloat16)
            change16 = change.astype(jnp.bfloat16)
            dv_ref[own, rows] = mm_nt(got_ref[own], soft16).astype(jnp.bfloat16)
            dk_ref[own, rows] = mm_nt(qt_ref[own], change16).astype(jnp.bfloat16)
            part = mm(kt_ref[own, rows], change16)
            query_grad = part if query_grad is None else query_grad + part
        dq_ref[own] = (query_grad * HEAD_DIM ** (-0.5)).astype(jnp.bfloat16)


def attend_backward(qt, kt, vt, got, out, lse, key_marks, query_marks):
    width, tokens = qt.shape
    keys = kt.shape[1]
    pairs = width // 128
    rows = lambda size: pl.BlockSpec((128, size), lambda i: (i, 0))
    whole = lambda shape: pl.BlockSpec(shape, lambda i: (0, 0))
    return pl.pallas_call(
        attend_backward_kernel,
        name="attend_backward",
        grid=(pairs,),
        in_specs=[
            rows(tokens),
            rows(keys),
            rows(keys),
            rows(tokens),
            rows(tokens),
            pl.BlockSpec((1, 2, tokens), lambda i: (i, 0, 0)),
            whole((keys, 1)),
            whole((1, tokens)),
        ],
        out_specs=[rows(tokens), rows(keys), rows(keys)],
        out_shape=[
            jax.ShapeDtypeStruct((width, tokens), jnp.bfloat16),
            jax.ShapeDtypeStruct((width, keys), jnp.bfloat16),
            jax.ShapeDtypeStruct((width, keys), jnp.bfloat16),
        ],
        scratch_shapes=[pltpu.VMEM((keys, tokens), jnp.float32)],
        compiler_params=pltpu.CompilerParams(vmem_limit_bytes=VMEM_BYTES),
    )(qt, kt, vt, got, out, lse, key_marks[:, None], query_marks[None])


def per_device(
    byte_ids,
    segments,
    embed_table,
    conv_weight,
    score_vector,
    first_gain,
    w_query,
    w_key,
    w_value,
    w_output,
    second_gain,
    w_gate,
    w_up,
    w_down,
    out_grad,
):
    seqs, part_bytes = byte_ids.shape
    count = lax.axis_size("seq")
    group_count = lax.axis_size(ALL)
    seq_len = part_bytes * count
    width = w_query.shape[1]
    wide = w_gate.shape[1]
    half_bytes = seq_len // 2
    half = half_bytes // 2
    core = lax.axis_index("dp") % 2
    place = lax.axis_index("seq")

    chan = conv_weight.shape[0]
    small = jnp.concatenate(
        [conv_weight.T, score_vector[None], first_gain[None], second_gain[None]], axis=0
    ).astype(jnp.float32)
    small = jnp.pad(small, ((0, 0), (0, 128 - chan)))
    cells = jnp.stack([byte_ids, segments + 1], axis=1).reshape(seqs, -1, 128)
    shards = (w_query, w_key, w_value, w_output, w_gate, w_up, w_down, embed_table, small)
    wq, wk, wv, wo, wg, wu, wd, table, small_full, cells, cot = gather_all(shards, cells, out_grad)
    cells = cells.reshape(count, 2, part_bytes).transpose(1, 0, 2).reshape(2, seq_len)
    ids_row, marks_row = cells[0], cells[1]
    cot = cot.reshape(half, width)
    small_full = small_full.reshape(group_count, 8, 128)[:, :, :chan].transpose(1, 0, 2).reshape(8, width)
    gain_one = small_full[KW + 1 : KW + 2]
    gain_two = small_full[KW + 2 : KW + 3]

    stream, normed_one, coef, tap_table, rows, idm = tok_forward(ids_row, marks_row, table, small_full, half)

    twins = [(i, i ^ 1) for i in range(lax.axis_size("dp"))]
    normed_other = lax.ppermute(normed_one, "dp", twins)
    token_marks = marks_row[::2]
    query_marks = lax.dynamic_slice_in_dim(token_marks, core * half, half, axis=0)
    other_marks = lax.dynamic_slice_in_dim(token_marks, (1 - core) * half, half, axis=0)
    key_marks = jnp.concatenate([query_marks, other_marks])
    queries = (mm_tt(wq, normed_one).astype(jnp.bfloat16) * HEAD_DIM ** (-0.5)).astype(jnp.bfloat16)
    normed_keys = jnp.concatenate([normed_one, normed_other], axis=0)
    keys = mm_tt(wk, normed_keys).astype(jnp.bfloat16)
    vals = mm_tt(wv, normed_keys).astype(jnp.bfloat16)
    attn_out, lse = attend_forward(queries, keys, vals, key_marks, query_marks)

    resid_one = stream + mm_tn(attn_out, wo)
    normed_two, norm_pull_two = jax.vjp(rms_scale, resid_one, gain_two)
    normed_two = normed_two.astype(jnp.bfloat16)
    gate_pre = mm(normed_two, wg)
    up_pre = mm(normed_two, wu)
    gate_act, gelu_pull = jax.vjp(gelu_tanh, gate_pre)
    hidden = (gate_act * up_pre).astype(jnp.bfloat16)
    layer_rows = (resid_one + mm(hidden, wd)).astype(jnp.bfloat16)
    layer_rows = layer_rows.reshape(seqs, part_bytes // 2, width)

    hidden_grad = mm_nt(cot, wd)
    grad_down = mm_tn(hidden, cot)
    up_grad = (hidden_grad * gate_act).astype(jnp.bfloat16)
    gate_grad = gelu_pull(hidden_grad * up_pre)[0].astype(jnp.bfloat16)
    grad_gate = mm_tn(normed_two, gate_grad)
    grad_up = mm_tn(normed_two, up_grad)
    normed_two_grad = mm_nt(gate_grad, wg) + mm_nt(up_grad, wu)
    resid_part, gain_two_grad = norm_pull_two(normed_two_grad)
    resid_grad = cot.astype(jnp.float32) + resid_part
    proj_grad = resid_grad.astype(jnp.bfloat16)
    grad_output = mm(attn_out, proj_grad)
    attn_grad = mm_nt(wo, proj_grad).astype(jnp.bfloat16)

    query_grad, key_part, value_part = attend_backward(
        queries, keys, vals, attn_grad, attn_out, lse, key_marks, query_marks
    )
    away = jnp.concatenate([key_part[:, half:], value_part[:, half:]], axis=0)
    came = lax.ppermute(away, "dp", twins).astype(jnp.float32)
    key_grad = (key_part[:, :half].astype(jnp.float32) + came[:width]).astype(jnp.bfloat16)
    value_grad = (value_part[:, :half].astype(jnp.float32) + came[width:]).astype(jnp.bfloat16)
    grad_query = mm_tt(normed_one, query_grad)
    grad_key = mm_tt(normed_one, key_grad)
    grad_value = mm_tt(normed_one, value_grad)
    normed_one_grad = mm_tt(query_grad, wq) + mm_tt(key_grad, wk) + mm_tt(value_grad, wv)
    norm_pull_one = jax.vjp(rms_scale, stream, gain_one)[1]
    stream_part, gain_one_grad = norm_pull_one(normed_one_grad)
    stream_grad = resid_grad + stream_part

    grad_table, small_grad = tok_backward(stream_grad, coef, tap_table, rows, idm, table, small_full)
    small_grad = jnp.concatenate([small_grad[: KW + 1], gain_one_grad, gain_two_grad], axis=0)
    small_grad = small_grad.reshape(8, group_count, chan).transpose(1, 0, 2)
    small_grad = jnp.pad(small_grad, ((0, 0), (0, 0), (0, 128 - chan))).reshape(-1, 128)
    grads = [grad_query, grad_key, grad_value, grad_output, grad_gate, grad_up, grad_down, grad_table]
    grads = [g.astype(jnp.bfloat16) for g in grads] + [small_grad]
    out = scatter_all(grads, layer_rows)
    small_out = out[8][:, :chan]
    return (
        out[9],
        out[7],
        small_out[:KW].T,
        small_out[KW],
        small_out[KW + 1],
        out[0],
        out[1],
        out[2],
        out[3],
        small_out[KW + 2],
        out[4],
        out[5],
        out[6],
    )


def solution(mesh):
    flat = P(ALL)
    rows = P(ALL, None)
    in_specs = (
        P("dp", "seq"),
        P("dp", "seq"),
        rows,
        rows,
        flat,
        flat,
        rows,
        rows,
        rows,
        rows,
        flat,
        rows,
        rows,
        rows,
        P("dp", "seq", None),
    )
    out_specs = (
        P("dp", "seq", None),
        rows,
        rows,
        flat,
        flat,
        rows,
        rows,
        rows,
        rows,
        flat,
        rows,
        rows,
        rows,
    )
    return jax.shard_map(
        per_device, mesh=mesh, in_specs=in_specs, out_specs=out_specs, check_vma=False
    )
```

```python
import functools

import jax
import jax.numpy as jnp
from jax import lax
from jax.experimental import pallas as pl
from jax.experimental.pallas import tpu as pltpu
from jax.sharding import PartitionSpec as P

HEADS = 12
HEAD_DIM = 64
VOCAB = 256
MAXBLOCK = 4
KW = 5
DOCS = 8
ALL = ("dp", "seq")
VMEM_BYTES = 56 * 1024 * 1024


def mm(left, right):
    return jnp.dot(left, right, preferred_element_type=jnp.float32)


def mm_nt(left, right):
    return lax.dot_general(left, right, (((1,), (1,)), ((), ())), preferred_element_type=jnp.float32)


def mm_tn(left, right):
    return lax.dot_general(left, right, (((0,), (0,)), ((), ())), preferred_element_type=jnp.float32)


def mm_tt(left, right):
    return lax.dot_general(left, right, (((0,), (1,)), ((), ())), preferred_element_type=jnp.float32)


def rms_scale(values, gain):
    return values * lax.rsqrt(jnp.mean(values * values, axis=-1, keepdims=True) + 1e-06) * gain


def gelu_tanh(values):
    return jax.nn.gelu(values, approximate=True)


MESH = pl.DeviceIdType.MESH


def position():
    dp = lax.axis_index("dp")
    place = lax.axis_index("seq")
    lines = lax.axis_size("dp") // 4
    group = dp // 2
    return group // 2, group % 2, dp % 2, place, lines, lax.axis_size("seq")


def dp_of(y, x, core):
    return (y * 2 + x) * 2 + core


def meet(targets):
    barrier = pltpu.get_barrier_semaphore()
    for dp, place in targets:
        pl.semaphore_signal(barrier, inc=1, device_id=(dp, place), device_id_type=MESH)
    pl.semaphore_wait(barrier, len(targets))


def remote(src, dst, send_sem, recv_sem, dp, place):
    return pltpu.make_async_remote_copy(
        src_ref=src,
        dst_ref=dst,
        send_sem=send_sem,
        recv_sem=recv_sem,
        device_id=(dp, place),
        device_id_type=MESH,
    )


GATHER_ITEMS = (
    (7, 0, 0, 0),
    (8, 0, 0, 0),
    (0, 0, 0, 0),
    (2, 0, 0, 1),
    (1, 0, 0, 0),
    (3, 0, 0, 1),
    (4, 0, 0, 0),
    (5, 0, 0, 1),
    (6, 0, 1, 0),
    (6, 1, 1, 1),
)
GATHER_PHASES = ((0, 1), (2, 3, 4, 5), (6, 7), (8, 9))


def gather_kernel(arrays, *refs):
    ins = refs[:arrays]
    cells_in, cot_in = refs[arrays], refs[arrays + 1]
    outs = refs[arrays + 2 : 2 * arrays + 2]
    cells_out, cot_out = refs[2 * arrays + 2], refs[2 * arrays + 3]
    recv, recv_sib, send_z, send_x, send_y, send_sib, own_sem, cell_recv, cell_send, cot_recv, cot_send = refs[
        2 * arrays + 4 :
    ]
    y, x, core, place, lines, count = position()
    seqs = cells_in.shape[0]
    groups = lines * 2
    group = y * 2 + x
    dp = dp_of(y, x, core)
    twin = dp_of(y, x, 1 - core)
    side = dp_of(y, 1 - x, core)
    ahead = [(y + k) % lines for k in range(1, lines)]

    targets = [(twin, place), (side, place)]
    for k in range(1, count):
        targets += [(dp, (place + k) % count), (twin, (place + k) % count)]
    for other_y in ahead:
        targets.append((dp_of(other_y, x, core), place))
    meet(targets)

    def cell_copies(fn_remote, fn_local):
        for r in range(seqs):
            chip = seqs * core + r
            for c in range(2):
                home = (chip == place) & (core == c)

                @pl.when(home)
                def _():
                    fn_local(r, c)

                @pl.when(jnp.logical_not(home))
                def _():
                    fn_remote(r, c, chip)

    def cell_remote(r, c, chip):
        return remote(
            cells_in.at[r],
            cells_out.at[place],
            cell_send.at[r, c],
            cell_recv.at[place],
            dp_of(y, x, c),
            chip,
        )

    cell_copies(
        lambda r, c, chip: cell_remote(r, c, chip).start(),
        lambda r, c: pltpu.make_async_copy(
            cells_in.at[r], cells_out.at[place], cell_recv.at[place]
        ).start(),
    )

    def view(item):
        array, first, columns, _ = GATHER_ITEMS[item]
        in_ref, out_ref = ins[array], outs[array]
        if columns:
            cols = in_ref.shape[1] // 2
            lanes = pl.ds(first * cols, cols)
        else:
            lanes = pl.ds(0, in_ref.shape[1])
        return in_ref.at[:, lanes], out_ref, lanes

    def block(item, g, z):
        _, out_ref, lanes = view(item)
        return out_ref.at[(g * 2 + core) * count + z, :, lanes]

    def group_block(item, g, c):
        _, out_ref, lanes = view(item)
        return out_ref.at[pl.ds((g * 2 + c) * count, count), :, lanes]

    def many(item, blocks):
        _, out_ref, lanes = view(item)
        return out_ref.at[pl.ds(0, blocks), :, lanes]

    def arrived(item, g, z):
        dst = block(item, g, z)
        remote(dst, dst, send_x.at[item], recv.at[item, g * count + z], twin, place).wait_recv()

    def to_side(item, src, g, z):
        remote(src, block(item, g, z), send_x.at[item], recv.at[item, g * count + z], side, place).start()

    def to_lines(item, src, g, z):
        for other_y in ahead:
            remote(
                src,
                block(item, g, z),
                send_y.at[item],
                recv.at[item, g * count + z],
                dp_of(other_y, x, core),
                place,
            ).start()

    def to_z(item, src, z, step):
        return remote(
            src,
            block(item, group, z),
            send_z.at[item, z, step],
            recv.at[item, group * count + z],
            dp,
            place + 1 - 2 * step,
        )

    def to_twin(item, g):
        src = group_block(item, g, core)
        remote(src, src, send_sib.at[item], recv_sib.at[item, g], twin, place).start()

    def own_copy(item):
        return pltpu.make_async_copy(view(item)[0], block(item, group, place), own_sem.at[item])

    def first_own(items):
        for item in items:
            src = view(item)[0]

            @pl.when(place < count - 1)
            def _():
                to_z(item, src, place, 0).start()

            @pl.when(place > 0)
            def _():
                to_z(item, src, place, 1).start()

            own_copy(item).start()

    def first_sides(items):
        for item in items:
            src = view(item)[0]
            to_side(item, src, group, place)
            to_lines(item, src, group, place)

    def first_level(items):
        def step(s, carry):
            low = place - s
            high = place + s
            for item in items:

                @pl.when(low >= 0)
                def _():
                    arrived(item, group, low)
                    src = block(item, group, low)

                    @pl.when(place < count - 1)
                    def _():
                        to_z(item, src, low, 0).start()

                    to_side(item, src, group, low)
                    to_lines(item, src, group, low)

                @pl.when(high < count)
                def _():
                    arrived(item, group, high)
                    src = block(item, group, high)

                    @pl.when(place > 0)
                    def _():
                        to_z(item, src, high, 1).start()

                    to_side(item, src, group, high)
                    to_lines(item, src, group, high)

            return carry

        lax.fori_loop(1, count, step, 0)
        for item in items:
            own_copy(item).wait()
            to_twin(item, group)

    def second_level(items):
        def step(s, carry):
            z = (place + s) % count
            for item in items:
                if GATHER_ITEMS[item][3] == 0:
                    g = y * 2 + (1 - x)
                    arrived(item, g, z)
                    to_lines(item, block(item, g, z), g, z)
                else:
                    for other_y in ahead:
                        g = other_y * 2 + x
                        arrived(item, g, z)
                        to_side(item, block(item, g, z), g, z)
            return carry

        lax.fori_loop(0, count, step, 0)
        for item in items:
            if GATHER_ITEMS[item][3] == 0:
                to_twin(item, y * 2 + (1 - x))
            else:
                for other_y in ahead:
                    to_twin(item, other_y * 2 + x)

    def third_level(items):
        def rest(item):
            if GATHER_ITEMS[item][3] == 0:
                return [other_y * 2 + other_x for other_y in ahead for other_x in (x, 1 - x)]
            return [other_y * 2 + (1 - x) for other_y in [y] + ahead]

        def step(s, carry):
            z = (place + s) % count
            for item in items:
                for g in rest(item):
                    arrived(item, g, z)
            return carry

        lax.fori_loop(0, count, step, 0)
        for item in items:
            for g in rest(item):
                to_twin(item, g)

    def cot_copies(fn_remote, fn_local):
        for r in range(seqs):
            chip = seqs * core + r
            home = (chip == place) & (core == place // seqs)

            @pl.when(home)
            def _():
                fn_local(r)

            @pl.when(jnp.logical_not(home))
            def _():
                fn_remote(r, chip)

    def cot_remote(r, chip):
        return remote(
            cot_in.at[r],
            cot_out.at[place % seqs],
            cot_send.at[r],
            cot_recv.at[place % seqs],
            dp_of(y, x, place // seqs),
            chip,
        )

    phases = GATHER_PHASES
    for items in phases:
        first_own(items)
    first_sides(phases[0])
    first_level(phases[0])
    for k in range(1, len(phases)):
        first_sides(phases[k])
        first_level(phases[k])
        second_level(phases[k - 1])
        if k == 1:
            cot_copies(
                lambda r, chip: cot_remote(r, chip).start(),
                lambda r: pltpu.make_async_copy(
                    cot_in.at[r], cot_out.at[place % seqs], cot_recv.at[place % seqs]
                ).start(),
            )
        if k > 1:
            third_level(phases[k - 2])
    second_level(phases[-1])
    third_level(phases[-2])
    third_level(phases[-1])

    for item in range(len(GATHER_ITEMS)):
        for g in range(groups):
            dst = group_block(item, g, 1 - core)
            remote(dst, dst, send_sib.at[item], recv_sib.at[item, g], twin, place).wait_recv()
        tree = GATHER_ITEMS[item][3]

        def sent(blocks, sem):
            src = many(item, blocks)
            remote(src, src, sem, recv.at[item, 0], twin, place).wait_send()

        sent(count * (1 if tree == 0 else lines), send_x.at[item])
        sent(count * (lines - 1) * (2 if tree == 0 else 1), send_y.at[item])
        sent(count * groups, send_sib.at[item])

        def drain(z, carry):
            @pl.when((z <= place) & (place < count - 1))
            def _():
                to_z(item, block(item, group, z), z, 0).wait_send()

            @pl.when((z >= place) & (place > 0))
            def _():
                to_z(item, block(item, group, z), z, 1).wait_send()

            return carry

        lax.fori_loop(0, count, drain, 0)
    for q in range(count):
        dst = cells_out.at[q]
        remote(dst, dst, cell_send.at[0, 0], cell_recv.at[q], twin, place).wait_recv()
    for q in range(seqs):
        dst = cot_out.at[q]
        remote(dst, dst, cot_send.at[0], cot_recv.at[q], twin, place).wait_recv()
    cell_copies(lambda r, c, chip: cell_remote(r, c, chip).wait_send(), lambda r, c: None)
    cot_copies(lambda r, chip: cot_remote(r, chip).wait_send(), lambda r: None)


def gather_all(shards, cells, cot):
    count = lax.axis_size("seq")
    group_count = lax.axis_size(ALL)
    groups = group_count // (2 * count)
    items = len(GATHER_ITEMS)
    seqs = cells.shape[0]
    vmem = pl.BlockSpec(memory_space=pltpu.VMEM)
    hbm = pl.BlockSpec(memory_space=pltpu.HBM)
    shapes = [jax.ShapeDtypeStruct((group_count,) + s.shape, s.dtype) for s in shards]
    shapes.append(jax.ShapeDtypeStruct((count,) + cells.shape[1:], cells.dtype))
    shapes.append(jax.ShapeDtypeStruct(cot.shape, cot.dtype))
    dma = pltpu.SemaphoreType.DMA
    out = pl.pallas_call(
        functools.partial(gather_kernel, len(shards)),
        name="gather_all",
        out_shape=shapes,
        in_specs=[vmem] * (len(shards) + 2),
        out_specs=[hbm] * len(shapes),
        scratch_shapes=[
            dma((items, groups * count)),
            dma((items, groups)),
            dma((items, count, 2)),
            dma((items,)),
            dma((items,)),
            dma((items,)),
            dma((items,)),
            dma((count,)),
            dma((seqs, 2)),
            dma((seqs,)),
            dma((seqs,)),
        ],
        compiler_params=pltpu.CompilerParams(collective_id=0, has_side_effects=True),
    )(*shards, cells, cot)
    full = [o.reshape(-1, o.shape[2]) for o in out[: len(shards)]]
    return full + list(out[len(shards) :])


LEFT = 128
BAND = 256


def split_two(values):
    high = values.astype(jnp.bfloat16)
    return high, (values - high.astype(jnp.float32)).astype(jnp.bfloat16)


def lane_shift(row, by):
    by = by % row.shape[1]
    return row if by == 0 else pltpu.roll(row, row.shape[1] - by, 1)


def pool_rows(marks, core, half_bytes):
    lanes = lax.broadcasted_iota(jnp.int32, marks[0].shape, 1)
    inside, inverse = {}, {}
    for e in range(2):
        place = core * half_bytes + 2 * (lanes - LEFT) + e + 768
        third = lax.shift_right_logical(place * 21846, 16)
        remains = {2: place & 1, 3: place - 3 * third, 4: place & 3}
        shifted = {}
        for s in range(1 - MAXBLOCK, MAXBLOCK):
            f = (e + s) % 2
            shifted[s] = lane_shift(marks[f], (e + s - f) // 2) == marks[e]
        for b in range(2, MAXBLOCK + 1):
            number = jnp.ones(marks[0].shape, jnp.float32)
            for s in range(1 - b, b):
                if s == 0:
                    continue
                at = remains[b] + s
                on = (shifted[s] & (at >= 0) & (at < b)).astype(jnp.float32)
                inside[b, e, s] = on
                number = number + on
            inverse[b, e] = 1.0 / number
    return inside, inverse


def band_coefs(per_byte, inside, inverse):
    coefs = {}
    for o in range(1 - MAXBLOCK, MAXBLOCK + 1):
        total = None
        for e in range(2):
            s = o - e
            if not 1 - MAXBLOCK <= s < MAXBLOCK:
                continue
            for b in range(1, MAXBLOCK + 1):
                if b == 1:
                    if s != 0:
                        continue
                    term = per_byte[b, e]
                elif s == 0:
                    term = per_byte[b, e] * inverse[b, e]
                elif (b, e, s) in inside:
                    term = per_byte[b, e] * inverse[b, e] * inside[b, e, s]
                else:
                    continue
                total = term if total is None else total + term
        coefs[o] = total
    return coefs


def band_matrix(coefs, block):
    shape = (3 * BAND, BAND)
    delta = lax.broadcasted_iota(jnp.int32, shape, 0) - LEFT - 2 * lax.broadcasted_iota(jnp.int32, shape, 1)
    out = jnp.zeros(shape, jnp.float32)
    for o, row in coefs.items():
        part = row[0:1, LEFT + BAND * block : LEFT + BAND * (block + 1)]
        out = jnp.where(delta == o, part, out)
    return out


def fill_one_hot(one_hot, idm_of_tap):
    span = one_hot.shape[1]
    vocab = lax.broadcasted_iota(jnp.int32, (VOCAB, span), 0)
    for tap in range(KW):
        hit = vocab == idm_of_tap(tap)
        one_hot[tap * VOCAB : (tap + 1) * VOCAB] = hit.astype(jnp.float32).astype(jnp.bfloat16)


def tok_forward_kernel(ids_ref, marks_ref, table_ref, small_ref, stream_ref, normed_ref, coef_ref, tap_ref, rows_ref, idm_ref, one_hot):
    core = lax.axis_index("dp") % 2
    tokens = stream_ref.shape[0]
    half_bytes = 2 * tokens
    span = one_hot.shape[1]
    wide = span + 2 * LEFT
    first = pl.ds(pl.multiple_of(core * half_bytes, 128), wide)
    ids = ids_ref[:, first]
    marks = marks_ref[:, first]
    for tap in range(KW):
        by = tap - KW // 2
        same = (lane_shift(marks, by) == marks) & (marks > 0)
        idm_ref[tap : tap + 1] = jnp.where(same, lane_shift(ids, by), -1)[0:1, LEFT : LEFT + span]
    fill_one_hot(one_hot, lambda tap: idm_ref[tap : tap + 1])

    score = jnp.broadcast_to(small_ref[KW : KW + 1], (8, small_ref.shape[1])).astype(jnp.bfloat16)
    scored = []
    for tap in range(KW):
        product = table_ref[...].astype(jnp.float32) * small_ref[tap : tap + 1]
        high, low = split_two(product)
        tap_ref[tap * VOCAB : (tap + 1) * VOCAB] = high
        scored.append(mm_nt(score, high) + mm_nt(score, low))
    high, low = split_two(jnp.concatenate(scored, axis=1))
    u_row = mm(high, one_hot[...]) + mm(low, one_hot[...])

    high = u_row.astype(jnp.bfloat16).astype(jnp.float32)
    marks_here = marks[:, LEFT : LEFT + span].astype(jnp.float32)
    packed = jnp.concatenate([marks_here, high, u_row - high, jnp.zeros_like(high)], axis=0).astype(jnp.bfloat16)
    shape = (span, wide // 2)
    twice = 2 * lax.broadcasted_iota(jnp.int32, shape, 1) - lax.broadcasted_iota(jnp.int32, shape, 0) - LEFT
    marks_of, u_of = [], []
    for e in range(2):
        pick = (twice == -e).astype(jnp.float32).astype(jnp.bfloat16)
        apart = mm(packed, pick)
        marks_of.append(apart[0:8])
        u_of.append(apart[8:16] + apart[16:24])

    inside, inverse = pool_rows(marks_of, core, half_bytes)
    prob = {}
    for e in range(2):
        shifted = {}
        for s in range(1 - MAXBLOCK, MAXBLOCK):
            f = (e + s) % 2
            shifted[s] = lane_shift(u_of[f], (e + s - f) // 2)
        scores = [u_of[e]]
        for b in range(2, MAXBLOCK + 1):
            total = u_of[e]
            for s in range(1 - b, b):
                if s != 0:
                    total = total + inside[b, e, s] * shifted[s]
            scores.append(total * inverse[b, e])
        top = scores[0]
        for value in scores[1:]:
            top = jnp.maximum(top, value)
        expo = [jnp.exp(value - top) for value in scores]
        whole = expo[0] + expo[1] + expo[2] + expo[3]
        for b in range(1, MAXBLOCK + 1):
            prob[b, e] = expo[b - 1] / whole
            rows_ref[2 * b + e : 2 * b + e + 1] = prob[b, e][0:1]
        rows_ref[e : e + 1] = marks_of[e][0:1]
    coefs = band_coefs({key: 0.5 * value for key, value in prob.items()}, inside, inverse)
    gain = small_ref[KW + 1 : KW + 2]
    for i in range(tokens // BAND):
        matrix = band_matrix(coefs, i).astype(jnp.bfloat16)
        lanes = slice(i * BAND, (i + 1) * BAND)
        part = mm(one_hot[:, 2 * i * BAND : (2 * i + 3) * BAND], matrix).astype(jnp.bfloat16)
        coef_ref[:, lanes] = part
        stream = mm_tn(part, tap_ref[...])
        stream_ref[lanes] = stream
        scale = lax.rsqrt(jnp.mean(stream * stream, axis=-1, keepdims=True) + 1e-06)
        normed_ref[lanes] = (stream * scale * gain).astype(jnp.bfloat16)


def tok_forward(ids_row, marks_row, table, small, tokens):
    width = table.shape[1]
    span = 2 * tokens + 2 * LEFT
    wide = span + 2 * LEFT

    def padded(row, fill):
        row = jnp.pad(row, (2 * LEFT, 2 * LEFT), constant_values=fill)
        return jnp.broadcast_to(row[None], (8, row.shape[0]))

    return pl.pallas_call(
        tok_forward_kernel,
        name="tok_forward",
        out_shape=[
            jax.ShapeDtypeStruct((tokens, width), jnp.float32),
            jax.ShapeDtypeStruct((tokens, width), jnp.bfloat16),
            jax.ShapeDtypeStruct((KW * VOCAB, tokens), jnp.bfloat16),
            jax.ShapeDtypeStruct((KW * VOCAB, width), jnp.bfloat16),
            jax.ShapeDtypeStruct((16, wide // 2), jnp.float32),
            jax.ShapeDtypeStruct((8, span), jnp.int32),
        ],
        scratch_shapes=[pltpu.VMEM((KW * VOCAB, span), jnp.bfloat16)],
        compiler_params=pltpu.CompilerParams(vmem_limit_bytes=VMEM_BYTES),
    )(padded(ids_row, -1), padded(marks_row, 0), table, small)


def tok_backward_body(grad16, coef_ref, tap_ref, rows_ref, idm_ref, table_ref, small_ref, one_hot, tick):
    core = lax.axis_index("dp") % 2
    tokens = grad16.shape[0]
    fill_one_hot(one_hot, lambda tap: idm_ref[tap : tap + 1])
    tick()

    def whole_row(k):
        return jnp.broadcast_to(rows_ref[k : k + 1], (8, rows_ref.shape[1]))

    marks_of = [whole_row(0), whole_row(1)]
    inside, inverse = pool_rows(marks_of, core, 2 * tokens)
    shape = (3 * BAND, BAND)
    delta = lax.broadcasted_iota(jnp.int32, shape, 0) - LEFT - 2 * lax.broadcasted_iota(jnp.int32, shape, 1)
    through = mm_nt(tap_ref[...], grad16).astype(jnp.bfloat16)
    tick()
    diag = {o: [] for o in range(1 - MAXBLOCK, MAXBLOCK + 1)}
    edge = jnp.zeros((8, LEFT), jnp.float32)
    for i in range(tokens // BAND):
        near = mm_tn(one_hot[:, 2 * i * BAND : (2 * i + 3) * BAND], through[:, i * BAND : (i + 1) * BAND])
        for o in diag:
            total = jnp.sum(jnp.where(delta == o, near, 0.0), axis=0, keepdims=True)
            diag[o].append(jnp.broadcast_to(total, (8, BAND)))
        tick()
    diag = {o: jnp.concatenate([edge] + parts + [edge], axis=1) for o, parts in diag.items()}
    size_grad = {}
    for e in range(2):
        grads = [0.5 * diag[e]]
        for b in range(2, MAXBLOCK + 1):
            total = diag[e]
            for s in range(1 - b, b):
                if s != 0:
                    total = total + inside[b, e, s] * diag[s + e]
            grads.append(0.5 * total * inverse[b, e])
        probs = [whole_row(2 * b + e) for b in range(1, MAXBLOCK + 1)]
        mean = probs[0] * grads[0]
        for p, g in zip(probs[1:], grads[1:]):
            mean = mean + p * g
        for b in range(1, MAXBLOCK + 1):
            size_grad[b, e] = probs[b - 1] * (grads[b - 1] - mean)
    coefs = band_coefs(size_grad, inside, inverse)
    picked = None
    for i in range(tokens // BAND):
        matrix = band_matrix(coefs, i).astype(jnp.bfloat16)
        part = mm(one_hot[:, 2 * i * BAND : (2 * i + 3) * BAND], matrix)
        part = jnp.sum(part, axis=1, keepdims=True)
        picked = part if picked is None else picked + part
        tick()
    score = small_ref[KW : KW + 1]
    table = table_ref[...].astype(jnp.float32)
    table_grad = None
    score_grad = None
    small_rows = []
    for tap in range(KW):
        rows = slice(tap * VOCAB, (tap + 1) * VOCAB)
        here = picked[rows]
        part = mm(coef_ref[rows], grad16) + here * score
        taps = small_ref[tap : tap + 1]
        table_grad = part * taps if table_grad is None else table_grad + part * taps
        small_rows.append(jnp.sum(part * table, axis=0, keepdims=True))
        summed = jnp.sum(table * here, axis=0, keepdims=True) * taps
        score_grad = summed if score_grad is None else score_grad + summed
        if tap < KW - 1:
            tick()
    return table_grad, small_rows + [score_grad]


CHUNK = 256


def pair_rows(ref, h):
    values = ref[...]
    rows = lax.broadcasted_iota(jnp.int32, values.shape, 0)
    return jnp.where((rows // HEAD_DIM) == h, values, jnp.zeros_like(values))


def fill_bias(bias, key_marks, query_marks):
    def apart(marks):
        rows = lax.broadcasted_iota(jnp.int32, (2 * DOCS, marks.shape[1]), 0)
        return (rows == marks[...]).astype(jnp.float32).astype(jnp.bfloat16)

    queries = apart(query_marks)
    for c in range(key_marks.shape[1] // CHUNK):
        keys = slice(c * CHUNK, (c + 1) * CHUNK)
        same = mm_tn(apart(key_marks.at[:, keys]), queries)
        bias[keys] = jnp.where(same > 0.5, 0.0, -1e30).astype(bias.dtype)


def attend_forward_kernel(qt_ref, kt_ref, vt_ref, key_marks, query_marks, out_ref, lse_ref, bias, scores):
    @pl.when(pl.program_id(0) == 0)
    def _():
        fill_bias(bias, key_marks, query_marks)

    keys = kt_ref[...].T
    chunks = keys.shape[0] // CHUNK
    for h in range(2):
        query = pair_rows(qt_ref, h)
        top = None
        for c in range(chunks):
            rows = slice(c * CHUNK, (c + 1) * CHUNK)
            part = mm(keys[rows], query) + bias[rows]
            scores[h, rows] = part
            high = jnp.max(part, axis=0, keepdims=True)
            top = high if top is None else jnp.maximum(top, high)
        total = None
        out = None
        for c in range(chunks):
            rows = slice(c * CHUNK, (c + 1) * CHUNK)
            expo = jnp.exp(scores[h, rows] - top)
            part = jnp.sum(expo, axis=0, keepdims=True)
            total = part if total is None else total + part
            part = mm(vt_ref[h * HEAD_DIM : (h + 1) * HEAD_DIM, rows], expo.astype(jnp.bfloat16))
            out = part if out is None else out + part
        out_ref[h * HEAD_DIM : (h + 1) * HEAD_DIM] = (out / total).astype(jnp.bfloat16)
        lse_ref[0, h : h + 1] = top + jnp.log(total)


def attend_forward(qt, kt, vt, key_marks, query_marks):
    width, tokens = qt.shape
    keys = kt.shape[1]
    pairs = width // 128
    rows = lambda size: pl.BlockSpec((128, size), lambda i: (i, 0))
    whole = lambda shape: pl.BlockSpec(shape, lambda i: (0, 0))
    return pl.pallas_call(
        attend_forward_kernel,
        name="attend_forward",
        grid=(pairs,),
        in_specs=[rows(tokens), rows(keys), rows(keys), whole((1, keys)), whole((1, tokens))],
        out_specs=[rows(tokens), pl.BlockSpec((1, 2, tokens), lambda i: (i, 0, 0))],
        out_shape=[
            jax.ShapeDtypeStruct((width, tokens), jnp.bfloat16),
            jax.ShapeDtypeStruct((pairs, 2, tokens), jnp.float32),
        ],
        scratch_shapes=[
            pltpu.VMEM((keys, tokens), jnp.float32),
            pltpu.VMEM((2, keys, tokens), jnp.float32),
        ],
        compiler_params=pltpu.CompilerParams(vmem_limit_bytes=VMEM_BYTES),
    )(qt, kt, vt, key_marks[None], query_marks[None])


def attend_backward_pair(qt, kt, vt, got_ref, out, lse_ref, bias, dq, dk_own, dv_own, dk_away, dv_away):
    keys = kt[...].T
    vals = vt[...].T
    chunks = keys.shape[0] // CHUNK
    for h in range(2):
        own = slice(h * HEAD_DIM, (h + 1) * HEAD_DIM)
        query = pair_rows(qt, h)
        got = pair_rows(got_ref, h)
        dots = jnp.sum(
            got_ref[own].astype(jnp.float32) * out[own].astype(jnp.float32), axis=0, keepdims=True
        )
        lse = lse_ref[h : h + 1]
        query_grad = None
        for c in range(chunks):
            rows = slice(c * CHUNK, (c + 1) * CHUNK)
            soft = jnp.exp(mm(keys[rows], query) + (bias[rows].astype(jnp.float32) - lse))
            change = soft * (mm(vals[rows], got) - dots)
            soft16 = soft.astype(jnp.bfloat16)
            change16 = change.astype(jnp.bfloat16)
            first = c < chunks // 2
            to = slice((c % (chunks // 2)) * CHUNK, (c % (chunks // 2) + 1) * CHUNK)
            (dv_own if first else dv_away)[own, to] = mm_nt(got_ref[own], soft16).astype(jnp.bfloat16)
            (dk_own if first else dk_away)[own, to] = mm_nt(qt[own], change16).astype(jnp.bfloat16)
            part = mm(kt[own, rows], change16)
            query_grad = part if query_grad is None else query_grad + part
        dq[own] = (query_grad * HEAD_DIM ** (-0.5)).astype(jnp.bfloat16)


SCATTER_ITEMS = (
    (4, 0, 1, 0),
    (6, 0, 2, 1),
    (5, 1, 2, 1),
    (3, 0, 1, 1),
    (5, 0, 2, 1),
    (6, 1, 2, 0),
    (0, 0, 1, 0),
    (1, 0, 1, 1),
    (2, 0, 1, 0),
    (7, 0, 1, 0),
    (8, 0, 1, 1),
)
FIRST_ITEMS = 6
SCHEDULE = (
    (),
    ((0, 0), (0, 1), (0, 2), (0, 3), (0, 4), (0, 5)),
    (),
    ((1, 1),),
    (),
    ((1, 0), (1, 2)),
    (),
    ((1, 3), (1, 5)),
    ((0, 6), (2, 1)),
    ((0, 7),),
    ((2, 2), (3, 1), (1, 4), (0, 8)),
    ((4, 1), (3, 2), (2, 3)),
    (),
    ((2, 0), (5, 1)),
    ((4, 2), (3, 3), (1, 6)),
    ((2, 5),),
    ((5, 2), (4, 3), (2, 4)),
    (),
    ((3, 0), (5, 3)),
    (),
    ((1, 7),),
    ((3, 5),),
    (
        (1, 8), (2, 6), (0, 9), (0, 10), (3, 4), (4, 0), (2, 7), (4, 5),
        (3, 6), (2, 8), (1, 9), (5, 0), (1, 10), (4, 4), (3, 7), (5, 5),
        (4, 6), (2, 10), (2, 9), (5, 4), (3, 8), (4, 7), (3, 10), (5, 6),
        (3, 9), (5, 7), (4, 8), (4, 10), (4, 9), (5, 8), (5, 10), (5, 9),
    ),
)


class Scatter:
    def __init__(self, sources, outs, layer_in, layer_out, buffers, sems):
        items = len(SCATTER_ITEMS)
        self.sources, self.outs = sources, outs
        self.layer_in, self.layer_out = layer_in, layer_out
        self.sems = sems
        self.y, self.x, self.core, self.place, self.lines, self.count = position()
        y, x, core = self.y, self.x, self.core
        self.own = list(buffers[:FIRST_ITEMS])
        for array, _, _, _ in SCATTER_ITEMS[FIRST_ITEMS:]:
            self.own.append(sources[array].at[:, :, core])
        buffers = buffers[FIRST_ITEMS:]
        self.from_twin, self.first_in, self.second_in, self.line_in = [
            buffers[k * items : (k + 1) * items] for k in range(4)
        ]
        self.dp = dp_of(y, x, core)
        self.twin = dp_of(y, x, 1 - core)
        self.side = dp_of(y, 1 - x, core)
        self.ahead = [(y + k) % self.lines for k in range(1, self.lines)]

    def meet(self):
        targets = [(self.twin, self.place), (self.side, self.place)]
        for k in range(1, self.count):
            other = (self.place + k) % self.count
            targets += [(self.dp, other), (self.twin, other)]
        for other_y in self.ahead:
            targets.append((dp_of(other_y, self.x, self.core), self.place))
        meet(targets)

    def order(self, item):
        return SCATTER_ITEMS[item][3]

    def columns(self, item):
        array, part, parts, _ = SCATTER_ITEMS[item]
        cols = self.sources[array].shape[-1] // parts
        return pl.ds(part * cols, cols)

    def to_twin(self, item):
        src = self.sources[SCATTER_ITEMS[item][0]].at[:, :, 1 - self.core, :, :, self.columns(item)]
        sems = self.sems
        return remote(
            src, self.from_twin[item], sems["twin_send"].at[item], sems["twin_recv"].at[item], self.twin, self.place
        )

    def own_in(self, item):
        src = self.sources[SCATTER_ITEMS[item][0]].at[:, :, self.core, :, :, self.columns(item)]
        return pltpu.make_async_copy(src, self.own[item], self.sems["own"].at[item])

    def x_copy(self, item):
        own = self.own[item]
        if self.order(item) == 0:
            src, dst = own.at[self.y, 1 - self.x], self.second_in[item].at[0]
        else:
            src, dst = own.at[:, 1 - self.x], self.first_in[item]
        return remote(
            src, dst, self.sems["x_send"].at[item], self.sems["x_recv"].at[item], self.side, self.place
        )

    def y_copy(self, item, k):
        other_y = self.ahead[k]
        own = self.own[item]
        if self.order(item) == 0:
            src, dst = own.at[other_y], self.first_in[item].at[k]
        else:
            src, dst = own.at[other_y, self.x], self.second_in[item].at[k]
        return remote(
            src,
            dst,
            self.sems["y_send"].at[item, k],
            self.sems["y_recv"].at[item, k],
            dp_of(other_y, self.x, self.core),
            self.place,
        )

    def stage_begin(self, item):
        self.to_twin(item).start()
        if item < FIRST_ITEMS:
            self.own_in(item).start()

    def stage_core(self, item):
        if item < FIRST_ITEMS:
            self.own_in(item).wait()
        self.to_twin(item).wait_recv()
        own, came = self.own[item], self.from_twin[item]

        def step(i, carry):
            a, b = i // 2, i % 2
            own[a, b] = plus(own[a, b], came[a, b])
            return carry

        lax.fori_loop(0, 2 * self.lines, step, 0)
        if self.order(item) == 0:
            for k in range(self.lines - 1):
                self.y_copy(item, k).start()
        else:
            self.x_copy(item).start()

    def stage_first(self, item):
        own, came = self.own[item], self.first_in[item]
        y, x, lines = self.y, self.x, self.lines
        if self.order(item) == 0:
            for k in range(lines - 1):
                self.y_copy(item, k).wait_recv()

            def step(b, carry):
                total = own[y, b]
                for k in range(lines - 1):
                    total = plus(total, came[k, b])
                own[y, b] = total
                return carry

            lax.fori_loop(0, 2, step, 0)
            self.x_copy(item).start()
        else:
            self.x_copy(item).wait_recv()

            def step(a, carry):
                own[a, x] = plus(own[a, x], came[a])
                return carry

            lax.fori_loop(0, lines, step, 0)
            for k in range(lines - 1):
                self.y_copy(item, k).start()

    def mine(self, item, z):
        return self.own[item].at[self.y, self.x, z]

    def z_copy(self, item, z, way):
        return remote(
            self.mine(item, z),
            self.line_in[item].at[way, z],
            self.sems["z_send"].at[item, z],
            self.sems["z_recv"].at[item, way, z],
            self.dp,
            self.place + 1 - 2 * way,
        )

    def z_forward(self, item, way, first):
        def step(z, carry):
            beyond = (z > self.place) if way == 0 else (z < self.place)

            @pl.when(beyond)
            def _():
                if not first:
                    self.z_copy(item, z, way).wait_recv()
                    ref = self.mine(item, z)
                    ref[...] = plus(ref[...], self.line_in[item][way, z])
                self.z_copy(item, z, way).start()

            return carry

        lax.fori_loop(0, self.count, step, 0)

    def stage_second(self, item):
        own, came = self.own[item], self.second_in[item]
        y, x = self.y, self.x
        if self.order(item) == 0:
            self.x_copy(item).wait_recv()
            own[y, x] = plus(own[y, x], came[0])
        else:
            total = own[y, x]
            for k in range(self.lines - 1):
                self.y_copy(item, k).wait_recv()
                total = plus(total, came[k])
            own[y, x] = total

        @pl.when(self.place == 0)
        def _():
            self.z_forward(item, 0, True)

        @pl.when(self.place == self.count - 1)
        def _():
            self.z_forward(item, 1, True)

    def stage_hop(self, hop, item):
        @pl.when(self.place == hop)
        def _():
            self.z_forward(item, 0, False)

        @pl.when(self.count - 1 - self.place == hop)
        def _():
            self.z_forward(item, 1, False)

    def stage_last(self, item):
        out = self.outs[SCATTER_ITEMS[item][0]]
        columns = self.columns(item)
        place = self.place
        out[:, columns] = self.mine(item, place)[...].astype(jnp.float32)

        def add(way):
            self.z_copy(item, place, way).wait_recv()
            out[:, columns] += self.line_in[item][way, place].astype(jnp.float32)

        @pl.when(place > 0)
        def _():
            add(0)

        @pl.when(place < self.count - 1)
        def _():
            add(1)

    def layer_copies(self, fn_remote, fn_local):
        seqs = self.layer_in.shape[0]
        for k in range(seqs):
            chip = seqs * self.core + k
            home = (chip == self.place) & (self.core == self.place // seqs)

            @pl.when(home)
            def _():
                fn_local(k)

            @pl.when(jnp.logical_not(home))
            def _():
                fn_remote(k, chip)

    def layer_remote(self, k, chip):
        seqs = self.layer_in.shape[0]
        row = self.place % seqs
        return remote(
            self.layer_in.at[k],
            self.layer_out.at[row],
            self.sems["layer_send"].at[k],
            self.sems["layer_recv"].at[row],
            dp_of(self.y, self.x, self.place // seqs),
            chip,
        )

    def layer_start(self):
        row = self.place % self.layer_in.shape[0]
        self.layer_copies(
            lambda k, chip: self.layer_remote(k, chip).start(),
            lambda k: pltpu.make_async_copy(
                self.layer_in.at[k], self.layer_out.at[row], self.sems["layer_recv"].at[row]
            ).start(),
        )

    def stage_hop_one(self, item):
        self.stage_hop(1, item)

    def stage_hops(self, item):
        for hop in range(2, self.count - 1):
            self.stage_hop(hop, item)

    def stages(self):
        return (
            self.stage_core,
            self.stage_first,
            self.stage_second,
            self.stage_hop_one,
            self.stage_hops,
            self.stage_last,
        )

    def finish(self):
        for item in range(len(SCATTER_ITEMS)):
            self.to_twin(item).wait_send()
            self.x_copy(item).wait_send()
            for k in range(self.lines - 1):
                self.y_copy(item, k).wait_send()

            def drain(z, carry):
                @pl.when(z > self.place)
                def _():
                    self.z_copy(item, z, 0).wait_send()

                @pl.when(z < self.place)
                def _():
                    self.z_copy(item, z, 1).wait_send()

                return carry

            lax.fori_loop(0, self.count, drain, 0)
        for r in range(self.layer_in.shape[0]):
            dst = self.layer_out.at[r]
            remote(
                dst, dst, self.sems["layer_send"].at[0], self.sems["layer_recv"].at[r], self.twin, self.place
            ).wait_recv()
        self.layer_copies(lambda k, chip: self.layer_remote(k, chip).wait_send(), lambda k: None)


SCATTER_SEMS = (
    "own",
    "twin_send",
    "twin_recv",
    "x_send",
    "x_recv",
    "y_send",
    "y_recv",
    "z_send",
    "z_recv",
    "layer_send",
    "layer_recv",
)


def plus(left, right):
    total = left.astype(jnp.float32) + right.astype(jnp.float32)
    return total.astype(left.dtype)


def scatter_scratch(shapes, lines, count, seqs):
    items = len(SCATTER_ITEMS)
    own, first_in, second_in, line_in = [], [], [], []
    for array, _, parts, order in SCATTER_ITEMS:
        rows, cols, kind = shapes[array]
        cols = cols // parts
        own.append(pltpu.VMEM((lines, 2, count, rows, cols), kind))
        if order == 0:
            first_in.append(pltpu.VMEM((lines - 1, 2, count, rows, cols), kind))
            second_in.append(pltpu.VMEM((1, count, rows, cols), kind))
        else:
            first_in.append(pltpu.VMEM((lines, count, rows, cols), kind))
            second_in.append(pltpu.VMEM((lines - 1, count, rows, cols), kind))
        line_in.append(pltpu.VMEM((2, count, rows, cols), kind))
    dma = pltpu.SemaphoreType.DMA
    sems = [dma((FIRST_ITEMS,))] + [dma((items,))] * 4
    sems += [dma((items, lines - 1))] * 2 + [dma((items, count)), dma((items, 2, count))]
    sems += [dma((seqs,))] * 2
    return own[:FIRST_ITEMS] + own + first_in + second_in + line_in, sems


BACK_INPUTS = (
    "gate",
    "up",
    "down",
    "output",
    "coef",
    "resid",
    "qt",
    "kt",
    "vt",
    "got",
    "out",
    "lse",
    "key_marks",
    "query_marks",
    "normed",
    "stream",
    "wq",
    "wk",
    "wv",
    "small",
    "gain_two",
    "table",
    "tap",
    "rows",
    "idm",
    "layer",
)


def backward_kernel(*refs):
    ref = dict(zip(BACK_INPUTS, refs))
    rest = refs[len(BACK_INPUTS) :]
    outs, layer_out = rest[:9], rest[9]
    rest = rest[10:]
    held = FIRST_ITEMS + 4 * len(SCATTER_ITEMS)
    buffers, rest = rest[:held], rest[held:]
    sems = dict(zip(SCATTER_SEMS, rest[: len(SCATTER_SEMS)]))
    names = ("dq", "dkv", "away", "came", "wide", "one_hot", "src_q", "src_k", "src_v", "src_table", "src_small", "swap_send", "swap_recv", "coef_sem", "resid_sem")
    own = dict(zip(names, rest[len(SCATTER_SEMS) :]))
    sources = (
        own["src_q"],
        own["src_k"],
        own["src_v"],
        ref["output"],
        ref["gate"],
        ref["up"],
        ref["down"],
        own["src_table"],
        own["src_small"],
    )
    scatter = Scatter(sources, outs, ref["layer"], layer_out, buffers, sems)
    stages = scatter.stages()
    width, tokens = ref["qt"].shape
    pairs = width // 128
    bias = own["one_hot"].at[0 : ref["kt"].shape[1], 0:tokens]
    scatter.meet()
    for item in range(FIRST_ITEMS):
        scatter.stage_begin(item)

    queue = [[functools.partial(stages[stage], item) for stage, item in group] for group in SCHEDULE]

    def tick():
        for task in queue.pop(0):
            task()

    scatter.layer_start()
    tick()
    fill_bias(bias, ref["key_marks"], ref["query_marks"])

    def swap(i, which):
        rows = pl.ds(pl.multiple_of(which * width + 128 * i, 128), 128)
        return remote(
            own["away"].at[rows],
            own["came"].at[rows],
            own["swap_send"].at[which, i],
            own["swap_recv"].at[which, i],
            scatter.twin,
            scatter.place,
        )

    ticks = [queue.pop(0) for _ in range(pairs)]

    def pair_step(i, carry):
        at = pl.ds(pl.multiple_of(128 * i, 128), 128)
        attend_backward_pair(
            ref["qt"].at[at],
            ref["kt"].at[at],
            ref["vt"].at[at],
            ref["got"].at[at],
            ref["out"].at[at],
            ref["lse"].at[i],
            bias,
            own["dq"].at[at],
            own["dkv"].at[at],
            own["dkv"].at[pl.ds(pl.multiple_of(width + 128 * i, 128), 128)],
            own["away"].at[at],
            own["away"].at[pl.ds(pl.multiple_of(width + 128 * i, 128), 128)],
        )
        swap(i, 0).start()
        swap(i, 1).start()
        for k, group in enumerate(ticks):
            if group:

                @pl.when(i == k)
                def _():
                    for task in group:
                        task()

        return carry

    lax.fori_loop(0, pairs, pair_step, 0)

    normed_t = ref["normed"][...].T
    wide = own["wide"]

    def hand_out(source, item):
        lines, _, _, count, size, _ = source.shape
        total = lines * 4 * count

        for o in range(total):
            where = (o // (4 * count), o // (2 * count) % 2, o // count % 2, o % count)
            source[where] = wide[size * o : size * (o + 1)].astype(source.dtype)
        scatter.stage_begin(item)

    wide[...] = mm_nt(normed_t, own["dq"][...])
    hand_out(own["src_q"], 6)
    tick()
    for which in range(2):

        def add_half(i, carry):
            swap(i, which).wait_recv()
            rows = pl.ds(pl.multiple_of(which * width + 128 * i, 128), 128)
            own["dkv"][rows] = plus(own["dkv"][rows], own["came"][rows])
            return carry

        lax.fori_loop(0, pairs, add_half, 0)
    coef = own["came"].at[0 : KW * VOCAB]
    coef_copy = pltpu.make_async_copy(ref["coef"], coef, own["coef_sem"])
    coef_copy.start()
    wide[...] = mm_nt(normed_t, own["dkv"][0:width])
    hand_out(own["src_k"], 7)
    tick()
    wide[...] = mm_nt(normed_t, own["dkv"][width:])
    hand_out(own["src_v"], 8)
    tick()

    wide[:, 0:tokens] = mm(ref["wq"][...], own["dq"][...])
    wide[:, 0:tokens] += mm(ref["wk"][...], own["dkv"][0:width])
    tick()
    wide[:, 0:tokens] += mm(ref["wv"][...], own["dkv"][width:])
    normed_grad = wide[:, 0:tokens].T
    resid_copy = pltpu.make_async_copy(ref["resid"], wide.at[0:tokens], own["resid_sem"])
    resid_copy.start()
    stream = ref["stream"][...]
    gain = ref["small"][KW + 1 : KW + 2]
    scale = lax.rsqrt(jnp.mean(stream * stream, axis=-1, keepdims=True) + 1e-06)
    gain_grad = jnp.sum(normed_grad * stream * scale, axis=0, keepdims=True)
    scaled = normed_grad * gain
    inner = jnp.mean(scaled * stream, axis=-1, keepdims=True)
    resid_copy.wait()
    grad16 = (wide[0:tokens] + scale * scaled - stream * (scale * scale * scale * inner)).astype(jnp.bfloat16)
    tick()
    coef_copy.wait()
    table_grad, rows = tok_backward_body(
        grad16, coef, ref["tap"], ref["rows"], ref["idm"], ref["table"], ref["small"], own["one_hot"], tick
    )
    wide[0:VOCAB] = table_grad
    hand_out(own["src_table"], 9)
    rows = jnp.concatenate(rows + [gain_grad, ref["gain_two"][...]], axis=0)
    source = own["src_small"]
    lines, _, _, count, _, _ = source.shape
    total = lines * 4 * count
    for o in range(total):
        where = (o // (4 * count), o // (2 * count) % 2, o // count % 2, o % count)
        source[where] = lane_shift(rows, o * (width // total))[:, 0:128]
    scatter.stage_begin(10)
    while queue:
        tick()
    scatter.finish()

    def drain(i, carry):
        swap(i, 0).wait_send()
        swap(i, 1).wait_send()
        return carry

    lax.fori_loop(0, pairs, drain, 0)


def backward_all(arrays, shapes):
    count = lax.axis_size("seq")
    lines = lax.axis_size("dp") // 4
    total = lines * 4 * count
    vmem = pl.BlockSpec(memory_space=pltpu.VMEM)
    hbm = pl.BlockSpec(memory_space=pltpu.HBM)
    layer = arrays["layer"]
    width, tokens = arrays["qt"].shape
    out_shape = [jax.ShapeDtypeStruct(shape[:2], jnp.float32) for shape in shapes]
    out_shape.append(jax.ShapeDtypeStruct(layer.shape, layer.dtype))
    buffers, sems = scatter_scratch(shapes, lines, count, layer.shape[0])
    views = dict(arrays)
    for name in ("gate", "up", "down", "output"):
        grad = arrays[name]
        views[name] = grad.reshape(lines, 2, 2, count, grad.shape[0] // total, grad.shape[1])

    def source(index):
        rows, cols, kind = shapes[index]
        return pltpu.VMEM((lines, 2, 2, count, rows, cols), kind)

    half = jnp.bfloat16
    own = [
        pltpu.VMEM((width, tokens), half),
        pltpu.VMEM((2 * width, tokens), half),
        pltpu.VMEM((2 * width, tokens), half),
        pltpu.VMEM((2 * width, tokens), half),
        pltpu.VMEM((width, width), jnp.float32),
        pltpu.VMEM((KW * VOCAB, arrays["idm"].shape[1]), half),
        source(0),
        source(1),
        source(2),
        source(7),
        source(8),
        pltpu.SemaphoreType.DMA((2, width // 128)),
        pltpu.SemaphoreType.DMA((2, width // 128)),
        pltpu.SemaphoreType.DMA,
        pltpu.SemaphoreType.DMA,
    ]
    return pl.pallas_call(
        backward_kernel,
        name="backward_all",
        out_shape=out_shape,
        in_specs=[hbm] * 6 + [vmem] * (len(BACK_INPUTS) - 6),
        out_specs=[vmem] * 9 + [hbm],
        scratch_shapes=buffers + sems + own,
        compiler_params=pltpu.CompilerParams(
            collective_id=1, has_side_effects=True, vmem_limit_bytes=63 * 1024 * 1024
        ),
    )(*[views[name] for name in BACK_INPUTS])


def per_device(
    byte_ids,
    segments,
    embed_table,
    conv_weight,
    score_vector,
    first_gain,
    w_query,
    w_key,
    w_value,
    w_output,
    second_gain,
    w_gate,
    w_up,
    w_down,
    out_grad,
):
    seqs, part_bytes = byte_ids.shape
    count = lax.axis_size("seq")
    group_count = lax.axis_size(ALL)
    seq_len = part_bytes * count
    width = w_query.shape[1]
    wide = w_gate.shape[1]
    half_bytes = seq_len // 2
    half = half_bytes // 2
    core = lax.axis_index("dp") % 2
    place = lax.axis_index("seq")

    chan = conv_weight.shape[0]
    small = jnp.concatenate(
        [conv_weight.T, score_vector[None], first_gain[None], second_gain[None]], axis=0
    ).astype(jnp.float32)
    small = jnp.pad(small, ((0, 0), (0, 128 - chan)))
    cells = jnp.stack([byte_ids, segments + 1], axis=1).reshape(seqs, -1, 128)
    shards = (w_query, w_key, w_value, w_output, w_gate, w_up, w_down, embed_table, small)
    wq, wk, wv, wo, wg, wu, wd, table, small_full, cells, cot = gather_all(shards, cells, out_grad)
    cells = cells.reshape(count, 2, part_bytes).transpose(1, 0, 2).reshape(2, seq_len)
    ids_row, marks_row = cells[0], cells[1]
    cot = cot.reshape(half, width)
    small_full = small_full.reshape(group_count, 8, 128)[:, :, :chan].transpose(1, 0, 2).reshape(8, width)
    gain_one = small_full[KW + 1 : KW + 2]
    gain_two = small_full[KW + 2 : KW + 3]

    stream, normed_one, coef, tap_table, rows, idm = tok_forward(ids_row, marks_row, table, small_full, half)

    twins = [(i, i ^ 1) for i in range(lax.axis_size("dp"))]
    normed_other = lax.ppermute(normed_one, "dp", twins)
    token_marks = marks_row[::2]
    query_marks = lax.dynamic_slice_in_dim(token_marks, core * half, half, axis=0)
    other_marks = lax.dynamic_slice_in_dim(token_marks, (1 - core) * half, half, axis=0)
    key_marks = jnp.concatenate([query_marks, other_marks])
    queries = (mm_tt(wq, normed_one).astype(jnp.bfloat16) * HEAD_DIM ** (-0.5)).astype(jnp.bfloat16)
    normed_keys = jnp.concatenate([normed_one, normed_other], axis=0)
    keys = mm_tt(wk, normed_keys).astype(jnp.bfloat16)
    vals = mm_tt(wv, normed_keys).astype(jnp.bfloat16)
    attn_out, lse = attend_forward(queries, keys, vals, key_marks, query_marks)

    resid_one = stream + mm_tn(attn_out, wo)
    normed_two, norm_pull_two = jax.vjp(rms_scale, resid_one, gain_two)
    normed_two = normed_two.astype(jnp.bfloat16)
    gate_pre = mm(normed_two, wg)
    up_pre = mm(normed_two, wu)
    gate_act, gelu_pull = jax.vjp(gelu_tanh, gate_pre)
    hidden = (gate_act * up_pre).astype(jnp.bfloat16)
    layer_rows = (resid_one + mm(hidden, wd)).astype(jnp.bfloat16)
    layer_rows = layer_rows.reshape(seqs, part_bytes // 2, width)

    hidden_grad = mm_nt(cot, wd)
    grad_down = mm_tn(hidden, cot)
    up_grad = (hidden_grad * gate_act).astype(jnp.bfloat16)
    gate_grad = gelu_pull(hidden_grad * up_pre)[0].astype(jnp.bfloat16)
    grad_gate = mm_tn(normed_two, gate_grad)
    grad_up = mm_tn(normed_two, up_grad)
    normed_two_grad = mm_nt(gate_grad, wg) + mm_nt(up_grad, wu)
    resid_part, gain_two_grad = norm_pull_two(normed_two_grad)
    resid_grad = cot.astype(jnp.float32) + resid_part
    proj_grad = resid_grad.astype(jnp.bfloat16)
    grad_output = mm(attn_out, proj_grad)
    attn_grad = mm_nt(wo, proj_grad).astype(jnp.bfloat16)

    shapes = [(w.shape[0], w.shape[1], jnp.bfloat16) for w in shards[:8]] + [small.shape + (jnp.float32,)]
    out = backward_all(
        {
            "gate": grad_gate.astype(jnp.bfloat16),
            "up": grad_up.astype(jnp.bfloat16),
            "down": grad_down.astype(jnp.bfloat16),
            "output": grad_output.astype(jnp.bfloat16),
            "qt": queries,
            "kt": keys,
            "vt": vals,
            "got": attn_grad,
            "out": attn_out,
            "lse": lse,
            "key_marks": key_marks[None],
            "query_marks": query_marks[None],
            "normed": normed_one,
            "stream": stream,
            "resid": resid_grad,
            "wq": wq,
            "wk": wk,
            "wv": wv,
            "small": small_full,
            "gain_two": gain_two_grad,
            "table": table,
            "coef": coef,
            "tap": tap_table,
            "rows": rows,
            "idm": idm,
            "layer": layer_rows,
        },
        shapes,
    )
    small_out = out[8][:, :chan]
    return (
        out[9],
        out[7],
        small_out[:KW].T,
        small_out[KW],
        small_out[KW + 1],
        out[0],
        out[1],
        out[2],
        out[3],
        small_out[KW + 2],
        out[4],
        out[5],
        out[6],
    )


def solution(mesh):
    flat = P(ALL)
    rows = P(ALL, None)
    in_specs = (
        P("dp", "seq"),
        P("dp", "seq"),
        rows,
        rows,
        flat,
        flat,
        rows,
        rows,
        rows,
        rows,
        flat,
        rows,
        rows,
        rows,
        P("dp", "seq", None),
    )
    out_specs = (
        P("dp", "seq", None),
        rows,
        rows,
        flat,
        flat,
        rows,
        rows,
        rows,
        rows,
        flat,
        rows,
        rows,
        rows,
    )
    return jax.shard_map(
        per_device, mesh=mesh, in_specs=in_specs, out_specs=out_specs, check_vma=False
    )
```

```python
import functools

import jax
import jax.numpy as jnp
from jax import lax
from jax.experimental import pallas as pl
from jax.experimental.pallas import tpu as pltpu
from jax.sharding import PartitionSpec as P

HEADS = 12
HEAD_DIM = 64
VOCAB = 256
MAXBLOCK = 4
KW = 5
DOCS = 8
ALL = ("dp", "seq")
VMEM_BYTES = 56 * 1024 * 1024


def mm(left, right):
    return jnp.dot(left, right, preferred_element_type=jnp.float32)


def mm_nt(left, right):
    return lax.dot_general(left, right, (((1,), (1,)), ((), ())), preferred_element_type=jnp.float32)


def mm_tn(left, right):
    return lax.dot_general(left, right, (((0,), (0,)), ((), ())), preferred_element_type=jnp.float32)


def mm_tt(left, right):
    return lax.dot_general(left, right, (((0,), (1,)), ((), ())), preferred_element_type=jnp.float32)


def rms_scale(values, gain):
    return values * lax.rsqrt(jnp.mean(values * values, axis=-1, keepdims=True) + 1e-06) * gain


def gelu_tanh(values):
    return jax.nn.gelu(values, approximate=True)


MESH = pl.DeviceIdType.MESH


def position():
    dp = lax.axis_index("dp")
    place = lax.axis_index("seq")
    lines = lax.axis_size("dp") // 4
    group = dp // 2
    return group // 2, group % 2, dp % 2, place, lines, lax.axis_size("seq")


def dp_of(y, x, core):
    return (y * 2 + x) * 2 + core


def meet(targets):
    barrier = pltpu.get_barrier_semaphore()
    for dp, place in targets:
        pl.semaphore_signal(barrier, inc=1, device_id=(dp, place), device_id_type=MESH)
    pl.semaphore_wait(barrier, len(targets))


def remote(src, dst, send_sem, recv_sem, dp, place):
    return pltpu.make_async_remote_copy(
        src_ref=src,
        dst_ref=dst,
        send_sem=send_sem,
        recv_sem=recv_sem,
        device_id=(dp, place),
        device_id_type=MESH,
    )


GATHER_ITEMS = (
    (7, 0, 0, 0),
    (8, 0, 0, 0),
    (0, 0, 0, 0),
    (2, 0, 0, 1),
    (1, 0, 0, 0),
    (3, 0, 0, 1),
    (4, 0, 0, 0),
    (5, 0, 0, 1),
    (6, 0, 1, 0),
    (6, 1, 1, 1),
)
GATHER_PHASES = ((0, 1), (2, 3, 4, 5), (6, 7), (8, 9))


def gather_kernel(arrays, *refs):
    ins = refs[:arrays]
    cells_in, cot_in = refs[arrays], refs[arrays + 1]
    outs = refs[arrays + 2 : 2 * arrays + 2]
    cells_out, cot_out = refs[2 * arrays + 2], refs[2 * arrays + 3]
    recv, recv_sib, send_z, send_x, send_y, send_sib, own_sem, cell_recv, cell_send, cot_recv, cot_send = refs[
        2 * arrays + 4 :
    ]
    y, x, core, place, lines, count = position()
    seqs = cells_in.shape[0]
    groups = lines * 2
    group = y * 2 + x
    dp = dp_of(y, x, core)
    twin = dp_of(y, x, 1 - core)
    side = dp_of(y, 1 - x, core)
    ahead = [(y + k) % lines for k in range(1, lines)]

    targets = [(twin, place), (side, place)]
    for k in range(1, count):
        targets += [(dp, (place + k) % count), (twin, (place + k) % count)]
    for other_y in ahead:
        targets.append((dp_of(other_y, x, core), place))
    meet(targets)

    def cell_copies(fn_remote, fn_local):
        for r in range(seqs):
            chip = seqs * core + r
            for c in range(2):
                home = (chip == place) & (core == c)

                @pl.when(home)
                def _():
                    fn_local(r, c)

                @pl.when(jnp.logical_not(home))
                def _():
                    fn_remote(r, c, chip)

    def cell_remote(r, c, chip):
        return remote(
            cells_in.at[r],
            cells_out.at[place],
            cell_send.at[r, c],
            cell_recv.at[place],
            dp_of(y, x, c),
            chip,
        )

    cell_copies(
        lambda r, c, chip: cell_remote(r, c, chip).start(),
        lambda r, c: pltpu.make_async_copy(
            cells_in.at[r], cells_out.at[place], cell_recv.at[place]
        ).start(),
    )

    def view(item):
        array, first, columns, _ = GATHER_ITEMS[item]
        in_ref, out_ref = ins[array], outs[array]
        if columns:
            cols = in_ref.shape[1] // 2
            lanes = pl.ds(first * cols, cols)
        else:
            lanes = pl.ds(0, in_ref.shape[1])
        return in_ref.at[:, lanes], out_ref, lanes

    def block(item, g, z):
        _, out_ref, lanes = view(item)
        return out_ref.at[(g * 2 + core) * count + z, :, lanes]

    def group_block(item, g, c):
        _, out_ref, lanes = view(item)
        return out_ref.at[pl.ds((g * 2 + c) * count, count), :, lanes]

    def many(item, blocks):
        _, out_ref, lanes = view(item)
        return out_ref.at[pl.ds(0, blocks), :, lanes]

    def arrived(item, g, z):
        dst = block(item, g, z)
        remote(dst, dst, send_x.at[item], recv.at[item, g * count + z], twin, place).wait_recv()

    def to_side(item, src, g, z):
        remote(src, block(item, g, z), send_x.at[item], recv.at[item, g * count + z], side, place).start()

    def to_lines(item, src, g, z):
        for other_y in ahead:
            remote(
                src,
                block(item, g, z),
                send_y.at[item],
                recv.at[item, g * count + z],
                dp_of(other_y, x, core),
                place,
            ).start()

    def to_z(item, src, z, step):
        return remote(
            src,
            block(item, group, z),
            send_z.at[item, z, step],
            recv.at[item, group * count + z],
            dp,
            place + 1 - 2 * step,
        )

    def to_twin(item, g):
        src = group_block(item, g, core)
        remote(src, src, send_sib.at[item], recv_sib.at[item, g], twin, place).start()

    def own_copy(item):
        return pltpu.make_async_copy(view(item)[0], block(item, group, place), own_sem.at[item])

    def first_own(items):
        for item in items:
            src = view(item)[0]

            @pl.when(place < count - 1)
            def _():
                to_z(item, src, place, 0).start()

            @pl.when(place > 0)
            def _():
                to_z(item, src, place, 1).start()

            own_copy(item).start()

    def first_sides(items):
        for item in items:
            src = view(item)[0]
            to_side(item, src, group, place)
            to_lines(item, src, group, place)

    def first_level(items):
        def step(s, carry):
            low = place - s
            high = place + s
            for item in items:

                @pl.when(low >= 0)
                def _():
                    arrived(item, group, low)
                    src = block(item, group, low)

                    @pl.when(place < count - 1)
                    def _():
                        to_z(item, src, low, 0).start()

                    to_side(item, src, group, low)
                    to_lines(item, src, group, low)

                @pl.when(high < count)
                def _():
                    arrived(item, group, high)
                    src = block(item, group, high)

                    @pl.when(place > 0)
                    def _():
                        to_z(item, src, high, 1).start()

                    to_side(item, src, group, high)
                    to_lines(item, src, group, high)

            return carry

        lax.fori_loop(1, count, step, 0)
        for item in items:
            own_copy(item).wait()
            to_twin(item, group)

    def second_level(items):
        def step(s, carry):
            z = (place + s) % count
            for item in items:
                if GATHER_ITEMS[item][3] == 0:
                    g = y * 2 + (1 - x)
                    arrived(item, g, z)
                    to_lines(item, block(item, g, z), g, z)
                else:
                    for other_y in ahead:
                        g = other_y * 2 + x
                        arrived(item, g, z)
                        to_side(item, block(item, g, z), g, z)
            return carry

        lax.fori_loop(0, count, step, 0)
        for item in items:
            if GATHER_ITEMS[item][3] == 0:
                to_twin(item, y * 2 + (1 - x))
            else:
                for other_y in ahead:
                    to_twin(item, other_y * 2 + x)

    def third_level(items):
        def rest(item):
            if GATHER_ITEMS[item][3] == 0:
                return [other_y * 2 + other_x for other_y in ahead for other_x in (x, 1 - x)]
            return [other_y * 2 + (1 - x) for other_y in [y] + ahead]

        def step(s, carry):
            z = (place + s) % count
            for item in items:
                for g in rest(item):
                    arrived(item, g, z)
            return carry

        lax.fori_loop(0, count, step, 0)
        for item in items:
            for g in rest(item):
                to_twin(item, g)

    def cot_copies(fn_remote, fn_local):
        for r in range(seqs):
            chip = seqs * core + r
            home = (chip == place) & (core == place // seqs)

            @pl.when(home)
            def _():
                fn_local(r)

            @pl.when(jnp.logical_not(home))
            def _():
                fn_remote(r, chip)

    def cot_remote(r, chip):
        return remote(
            cot_in.at[r],
            cot_out.at[place % seqs],
            cot_send.at[r],
            cot_recv.at[place % seqs],
            dp_of(y, x, place // seqs),
            chip,
        )

    phases = GATHER_PHASES
    for items in phases:
        first_own(items)
    first_sides(phases[0])
    first_level(phases[0])
    for k in range(1, len(phases)):
        first_sides(phases[k])
        first_level(phases[k])
        second_level(phases[k - 1])
        if k == 1:
            cot_copies(
                lambda r, chip: cot_remote(r, chip).start(),
                lambda r: pltpu.make_async_copy(
                    cot_in.at[r], cot_out.at[place % seqs], cot_recv.at[place % seqs]
                ).start(),
            )
        if k > 1:
            third_level(phases[k - 2])
    second_level(phases[-1])
    third_level(phases[-2])
    third_level(phases[-1])

    for item in range(len(GATHER_ITEMS)):
        for g in range(groups):
            dst = group_block(item, g, 1 - core)
            remote(dst, dst, send_sib.at[item], recv_sib.at[item, g], twin, place).wait_recv()
        tree = GATHER_ITEMS[item][3]

        def sent(blocks, sem):
            src = many(item, blocks)
            remote(src, src, sem, recv.at[item, 0], twin, place).wait_send()

        sent(count * (1 if tree == 0 else lines), send_x.at[item])
        sent(count * (lines - 1) * (2 if tree == 0 else 1), send_y.at[item])
        sent(count * groups, send_sib.at[item])

        def drain(z, carry):
            @pl.when((z <= place) & (place < count - 1))
            def _():
                to_z(item, block(item, group, z), z, 0).wait_send()

            @pl.when((z >= place) & (place > 0))
            def _():
                to_z(item, block(item, group, z), z, 1).wait_send()

            return carry

        lax.fori_loop(0, count, drain, 0)
    for q in range(count):
        dst = cells_out.at[q]
        remote(dst, dst, cell_send.at[0, 0], cell_recv.at[q], twin, place).wait_recv()
    for q in range(seqs):
        dst = cot_out.at[q]
        remote(dst, dst, cot_send.at[0], cot_recv.at[q], twin, place).wait_recv()
    cell_copies(lambda r, c, chip: cell_remote(r, c, chip).wait_send(), lambda r, c: None)
    cot_copies(lambda r, chip: cot_remote(r, chip).wait_send(), lambda r: None)


def gather_all(shards, cells, cot):
    count = lax.axis_size("seq")
    group_count = lax.axis_size(ALL)
    groups = group_count // (2 * count)
    items = len(GATHER_ITEMS)
    seqs = cells.shape[0]
    vmem = pl.BlockSpec(memory_space=pltpu.VMEM)
    hbm = pl.BlockSpec(memory_space=pltpu.HBM)
    shapes = [jax.ShapeDtypeStruct((group_count,) + s.shape, s.dtype) for s in shards]
    shapes.append(jax.ShapeDtypeStruct((count,) + cells.shape[1:], cells.dtype))
    shapes.append(jax.ShapeDtypeStruct(cot.shape, cot.dtype))
    dma = pltpu.SemaphoreType.DMA
    out = pl.pallas_call(
        functools.partial(gather_kernel, len(shards)),
        name="gather_all",
        out_shape=shapes,
        in_specs=[vmem] * (len(shards) + 2),
        out_specs=[hbm] * len(shapes),
        scratch_shapes=[
            dma((items, groups * count)),
            dma((items, groups)),
            dma((items, count, 2)),
            dma((items,)),
            dma((items,)),
            dma((items,)),
            dma((items,)),
            dma((count,)),
            dma((seqs, 2)),
            dma((seqs,)),
            dma((seqs,)),
        ],
        compiler_params=pltpu.CompilerParams(collective_id=0, has_side_effects=True),
    )(*shards, cells, cot)
    full = [o.reshape(-1, o.shape[2]) for o in out[: len(shards)]]
    return full + list(out[len(shards) :])


LEFT = 128
BAND = 256


def split_two(values):
    high = values.astype(jnp.bfloat16)
    return high, (values - high.astype(jnp.float32)).astype(jnp.bfloat16)


def lane_shift(row, by):
    by = by % row.shape[1]
    return row if by == 0 else pltpu.roll(row, row.shape[1] - by, 1)


def pool_rows(marks, core, half_bytes):
    lanes = lax.broadcasted_iota(jnp.int32, marks[0].shape, 1)
    inside, inverse = {}, {}
    for e in range(2):
        place = core * half_bytes + 2 * (lanes - LEFT) + e + 768
        third = lax.shift_right_logical(place * 21846, 16)
        remains = {2: place & 1, 3: place - 3 * third, 4: place & 3}
        shifted = {}
        for s in range(1 - MAXBLOCK, MAXBLOCK):
            f = (e + s) % 2
            shifted[s] = lane_shift(marks[f], (e + s - f) // 2) == marks[e]
        for b in range(2, MAXBLOCK + 1):
            number = jnp.ones(marks[0].shape, jnp.float32)
            for s in range(1 - b, b):
                if s == 0:
                    continue
                at = remains[b] + s
                on = (shifted[s] & (at >= 0) & (at < b)).astype(jnp.float32)
                inside[b, e, s] = on
                number = number + on
            inverse[b, e] = 1.0 / number
    return inside, inverse


def band_coefs(per_byte, inside, inverse):
    coefs = {}
    for o in range(1 - MAXBLOCK, MAXBLOCK + 1):
        total = None
        for e in range(2):
            s = o - e
            if not 1 - MAXBLOCK <= s < MAXBLOCK:
                continue
            for b in range(1, MAXBLOCK + 1):
                if b == 1:
                    if s != 0:
                        continue
                    term = per_byte[b, e]
                elif s == 0:
                    term = per_byte[b, e] * inverse[b, e]
                elif (b, e, s) in inside:
                    term = per_byte[b, e] * inverse[b, e] * inside[b, e, s]
                else:
                    continue
                total = term if total is None else total + term
        coefs[o] = total
    return coefs


def band_matrix(coefs, block):
    shape = (3 * BAND, BAND)
    delta = lax.broadcasted_iota(jnp.int32, shape, 0) - LEFT - 2 * lax.broadcasted_iota(jnp.int32, shape, 1)
    out = jnp.zeros(shape, jnp.float32)
    for o, row in coefs.items():
        part = row[0:1, LEFT + BAND * block : LEFT + BAND * (block + 1)]
        out = jnp.where(delta == o, part, out)
    return out


def fill_one_hot(one_hot, idm_of_tap):
    span = one_hot.shape[1]
    vocab = lax.broadcasted_iota(jnp.int32, (VOCAB, span), 0)
    for tap in range(KW):
        hit = vocab == idm_of_tap(tap)
        one_hot[tap * VOCAB : (tap + 1) * VOCAB] = hit.astype(jnp.float32).astype(jnp.bfloat16)


def tok_forward_kernel(ids_ref, marks_ref, table_ref, small_ref, stream_ref, normed_ref, coef_ref, tap_ref, rows_ref, idm_ref, one_hot):
    core = lax.axis_index("dp") % 2
    tokens = stream_ref.shape[0]
    half_bytes = 2 * tokens
    span = one_hot.shape[1]
    wide = span + 2 * LEFT
    first = pl.ds(pl.multiple_of(core * half_bytes, 128), wide)
    ids = ids_ref[:, first]
    marks = marks_ref[:, first]
    for tap in range(KW):
        by = tap - KW // 2
        same = (lane_shift(marks, by) == marks) & (marks > 0)
        idm_ref[tap : tap + 1] = jnp.where(same, lane_shift(ids, by), -1)[0:1, LEFT : LEFT + span]
    fill_one_hot(one_hot, lambda tap: idm_ref[tap : tap + 1])

    score = jnp.broadcast_to(small_ref[KW : KW + 1], (8, small_ref.shape[1])).astype(jnp.bfloat16)
    scored = []
    for tap in range(KW):
        product = table_ref[...].astype(jnp.float32) * small_ref[tap : tap + 1]
        high, low = split_two(product)
        tap_ref[tap * VOCAB : (tap + 1) * VOCAB] = high
        scored.append(mm_nt(score, high) + mm_nt(score, low))
    high, low = split_two(jnp.concatenate(scored, axis=1))
    u_row = mm(high, one_hot[...]) + mm(low, one_hot[...])

    high = u_row.astype(jnp.bfloat16).astype(jnp.float32)
    marks_here = marks[:, LEFT : LEFT + span].astype(jnp.float32)
    packed = jnp.concatenate([marks_here, high, u_row - high, jnp.zeros_like(high)], axis=0).astype(jnp.bfloat16)
    shape = (span, wide // 2)
    twice = 2 * lax.broadcasted_iota(jnp.int32, shape, 1) - lax.broadcasted_iota(jnp.int32, shape, 0) - LEFT
    marks_of, u_of = [], []
    for e in range(2):
        pick = (twice == -e).astype(jnp.float32).astype(jnp.bfloat16)
        apart = mm(packed, pick)
        marks_of.append(apart[0:8])
        u_of.append(apart[8:16] + apart[16:24])

    inside, inverse = pool_rows(marks_of, core, half_bytes)
    prob = {}
    for e in range(2):
        shifted = {}
        for s in range(1 - MAXBLOCK, MAXBLOCK):
            f = (e + s) % 2
            shifted[s] = lane_shift(u_of[f], (e + s - f) // 2)
        scores = [u_of[e]]
        for b in range(2, MAXBLOCK + 1):
            total = u_of[e]
            for s in range(1 - b, b):
                if s != 0:
                    total = total + inside[b, e, s] * shifted[s]
            scores.append(total * inverse[b, e])
        top = scores[0]
        for value in scores[1:]:
            top = jnp.maximum(top, value)
        expo = [jnp.exp(value - top) for value in scores]
        whole = expo[0] + expo[1] + expo[2] + expo[3]
        for b in range(1, MAXBLOCK + 1):
            prob[b, e] = expo[b - 1] / whole
            rows_ref[2 * b + e : 2 * b + e + 1] = prob[b, e][0:1]
        rows_ref[e : e + 1] = marks_of[e][0:1]
    coefs = band_coefs({key: 0.5 * value for key, value in prob.items()}, inside, inverse)
    gain = small_ref[KW + 1 : KW + 2]
    for i in range(tokens // BAND):
        matrix = band_matrix(coefs, i).astype(jnp.bfloat16)
        lanes = slice(i * BAND, (i + 1) * BAND)
        part = mm(one_hot[:, 2 * i * BAND : (2 * i + 3) * BAND], matrix).astype(jnp.bfloat16)
        coef_ref[:, lanes] = part
        stream = mm_tn(part, tap_ref[...])
        stream_ref[lanes] = stream
        scale = lax.rsqrt(jnp.mean(stream * stream, axis=-1, keepdims=True) + 1e-06)
        normed_ref[lanes] = (stream * scale * gain).astype(jnp.bfloat16)


def tok_forward(ids_row, marks_row, table, small, tokens):
    width = table.shape[1]
    span = 2 * tokens + 2 * LEFT
    wide = span + 2 * LEFT

    def padded(row, fill):
        row = jnp.pad(row, (2 * LEFT, 2 * LEFT), constant_values=fill)
        return jnp.broadcast_to(row[None], (8, row.shape[0]))

    return pl.pallas_call(
        tok_forward_kernel,
        name="tok_forward",
        out_shape=[
            jax.ShapeDtypeStruct((tokens, width), jnp.float32),
            jax.ShapeDtypeStruct((tokens, width), jnp.bfloat16),
            jax.ShapeDtypeStruct((KW * VOCAB, tokens), jnp.bfloat16),
            jax.ShapeDtypeStruct((KW * VOCAB, width), jnp.bfloat16),
            jax.ShapeDtypeStruct((16, wide // 2), jnp.float32),
            jax.ShapeDtypeStruct((8, span), jnp.int32),
        ],
        scratch_shapes=[pltpu.VMEM((KW * VOCAB, span), jnp.bfloat16)],
        compiler_params=pltpu.CompilerParams(vmem_limit_bytes=VMEM_BYTES),
    )(padded(ids_row, -1), padded(marks_row, 0), table, small)


def tok_backward_body(grad16, coef_ref, tap_ref, rows_ref, idm_ref, table_ref, small_ref, one_hot, tick):
    core = lax.axis_index("dp") % 2
    tokens = grad16.shape[0]
    fill_one_hot(one_hot, lambda tap: idm_ref[tap : tap + 1])
    tick()

    def whole_row(k):
        return jnp.broadcast_to(rows_ref[k : k + 1], (8, rows_ref.shape[1]))

    marks_of = [whole_row(0), whole_row(1)]
    inside, inverse = pool_rows(marks_of, core, 2 * tokens)
    shape = (3 * BAND, BAND)
    delta = lax.broadcasted_iota(jnp.int32, shape, 0) - LEFT - 2 * lax.broadcasted_iota(jnp.int32, shape, 1)
    through = mm_nt(tap_ref[...], grad16).astype(jnp.bfloat16)
    tick()
    diag = {o: [] for o in range(1 - MAXBLOCK, MAXBLOCK + 1)}
    edge = jnp.zeros((8, LEFT), jnp.float32)
    for i in range(tokens // BAND):
        near = mm_tn(one_hot[:, 2 * i * BAND : (2 * i + 3) * BAND], through[:, i * BAND : (i + 1) * BAND])
        for o in diag:
            total = jnp.sum(jnp.where(delta == o, near, 0.0), axis=0, keepdims=True)
            diag[o].append(jnp.broadcast_to(total, (8, BAND)))
        tick()
    diag = {o: jnp.concatenate([edge] + parts + [edge], axis=1) for o, parts in diag.items()}
    size_grad = {}
    for e in range(2):
        grads = [0.5 * diag[e]]
        for b in range(2, MAXBLOCK + 1):
            total = diag[e]
            for s in range(1 - b, b):
                if s != 0:
                    total = total + inside[b, e, s] * diag[s + e]
            grads.append(0.5 * total * inverse[b, e])
        probs = [whole_row(2 * b + e) for b in range(1, MAXBLOCK + 1)]
        mean = probs[0] * grads[0]
        for p, g in zip(probs[1:], grads[1:]):
            mean = mean + p * g
        for b in range(1, MAXBLOCK + 1):
            size_grad[b, e] = probs[b - 1] * (grads[b - 1] - mean)
    coefs = band_coefs(size_grad, inside, inverse)
    picked = None
    for i in range(tokens // BAND):
        matrix = band_matrix(coefs, i).astype(jnp.bfloat16)
        part = mm(one_hot[:, 2 * i * BAND : (2 * i + 3) * BAND], matrix)
        part = jnp.sum(part, axis=1, keepdims=True)
        picked = part if picked is None else picked + part
        tick()
    score = small_ref[KW : KW + 1]
    table = table_ref[...].astype(jnp.float32)
    table_grad = None
    score_grad = None
    small_rows = []
    for tap in range(KW):
        rows = slice(tap * VOCAB, (tap + 1) * VOCAB)
        here = picked[rows]
        part = mm(coef_ref[rows], grad16) + here * score
        taps = small_ref[tap : tap + 1]
        table_grad = part * taps if table_grad is None else table_grad + part * taps
        small_rows.append(jnp.sum(part * table, axis=0, keepdims=True))
        summed = jnp.sum(table * here, axis=0, keepdims=True) * taps
        score_grad = summed if score_grad is None else score_grad + summed
        if tap < KW - 1:
            tick()
    return table_grad, small_rows + [score_grad]


CHUNK = 256


def pair_rows(ref, h):
    values = ref[...]
    rows = lax.broadcasted_iota(jnp.int32, values.shape, 0)
    return jnp.where((rows // HEAD_DIM) == h, values, jnp.zeros_like(values))


def fill_bias(bias, key_marks, query_marks):
    def apart(marks):
        rows = lax.broadcasted_iota(jnp.int32, (2 * DOCS, marks.shape[1]), 0)
        return (rows == marks[...]).astype(jnp.float32).astype(jnp.bfloat16)

    queries = apart(query_marks)
    for c in range(key_marks.shape[1] // CHUNK):
        keys = slice(c * CHUNK, (c + 1) * CHUNK)
        same = mm_tn(apart(key_marks.at[:, keys]), queries)
        bias[keys] = jnp.where(same > 0.5, 0.0, -1e30).astype(bias.dtype)


def attend_forward_kernel(qt_ref, kt_ref, vt_ref, key_marks, query_marks, out_ref, lse_ref, bias, scores):
    @pl.when(pl.program_id(0) == 0)
    def _():
        fill_bias(bias, key_marks, query_marks)

    keys = kt_ref[...].T
    chunks = keys.shape[0] // CHUNK
    for h in range(2):
        query = pair_rows(qt_ref, h)
        top = None
        for c in range(chunks):
            rows = slice(c * CHUNK, (c + 1) * CHUNK)
            part = mm(keys[rows], query) + bias[rows]
            scores[h, rows] = part
            high = jnp.max(part, axis=0, keepdims=True)
            top = high if top is None else jnp.maximum(top, high)
        total = None
        out = None
        for c in range(chunks):
            rows = slice(c * CHUNK, (c + 1) * CHUNK)
            expo = jnp.exp(scores[h, rows] - top)
            part = jnp.sum(expo, axis=0, keepdims=True)
            total = part if total is None else total + part
            part = mm(vt_ref[h * HEAD_DIM : (h + 1) * HEAD_DIM, rows], expo.astype(jnp.bfloat16))
            out = part if out is None else out + part
        out_ref[h * HEAD_DIM : (h + 1) * HEAD_DIM] = (out / total).astype(jnp.bfloat16)
        lse_ref[0, h : h + 1] = top + jnp.log(total)


def attend_forward(qt, kt, vt, key_marks, query_marks):
    width, tokens = qt.shape
    keys = kt.shape[1]
    pairs = width // 128
    rows = lambda size: pl.BlockSpec((128, size), lambda i: (i, 0))
    whole = lambda shape: pl.BlockSpec(shape, lambda i: (0, 0))
    return pl.pallas_call(
        attend_forward_kernel,
        name="attend_forward",
        grid=(pairs,),
        in_specs=[rows(tokens), rows(keys), rows(keys), whole((1, keys)), whole((1, tokens))],
        out_specs=[rows(tokens), pl.BlockSpec((1, 2, tokens), lambda i: (i, 0, 0))],
        out_shape=[
            jax.ShapeDtypeStruct((width, tokens), jnp.bfloat16),
            jax.ShapeDtypeStruct((pairs, 2, tokens), jnp.float32),
        ],
        scratch_shapes=[
            pltpu.VMEM((keys, tokens), jnp.float32),
            pltpu.VMEM((2, keys, tokens), jnp.float32),
        ],
        compiler_params=pltpu.CompilerParams(vmem_limit_bytes=VMEM_BYTES),
    )(qt, kt, vt, key_marks[None], query_marks[None])


def attend_backward_pair(qt, kt, vt, got_ref, out, lse_ref, bias, dq, dk_own, dv_own, dk_away, dv_away):
    keys = kt[...].T
    vals = vt[...].T
    chunks = keys.shape[0] // CHUNK
    for h in range(2):
        own = slice(h * HEAD_DIM, (h + 1) * HEAD_DIM)
        query = pair_rows(qt, h)
        got = pair_rows(got_ref, h)
        dots = jnp.sum(
            got_ref[own].astype(jnp.float32) * out[own].astype(jnp.float32), axis=0, keepdims=True
        )
        lse = lse_ref[h : h + 1]
        query_grad = None
        for c in range(chunks):
            rows = slice(c * CHUNK, (c + 1) * CHUNK)
            soft = jnp.exp(mm(keys[rows], query) + (bias[rows].astype(jnp.float32) - lse))
            change = soft * (mm(vals[rows], got) - dots)
            soft16 = soft.astype(jnp.bfloat16)
            change16 = change.astype(jnp.bfloat16)
            first = c < chunks // 2
            to = slice((c % (chunks // 2)) * CHUNK, (c % (chunks // 2) + 1) * CHUNK)
            (dv_own if first else dv_away)[own, to] = mm_nt(got_ref[own], soft16).astype(jnp.bfloat16)
            (dk_own if first else dk_away)[own, to] = mm_nt(qt[own], change16).astype(jnp.bfloat16)
            part = mm(kt[own, rows], change16)
            query_grad = part if query_grad is None else query_grad + part
        dq[own] = (query_grad * HEAD_DIM ** (-0.5)).astype(jnp.bfloat16)


SCATTER_ITEMS = (
    (4, 0, 1, 0),
    (6, 0, 2, 1),
    (5, 1, 2, 1),
    (3, 0, 1, 1),
    (5, 0, 2, 1),
    (6, 1, 2, 0),
    (0, 0, 1, 0),
    (1, 0, 1, 1),
    (2, 0, 1, 0),
    (7, 0, 1, 0),
    (8, 0, 1, 1),
)
FIRST_ITEMS = 6
SCHEDULE = (
    (),
    ((0, 0), (0, 1), (0, 2), (0, 3), (0, 4), (0, 5)),
    (),
    ((1, 1),),
    (),
    ((1, 0), (1, 2)),
    (),
    ((1, 3), (1, 5)),
    ((0, 6), (2, 1)),
    ((0, 7),),
    ((2, 2), (3, 1), (1, 4), (0, 8)),
    ((4, 1), (3, 2), (2, 3)),
    (),
    ((2, 0), (5, 1)),
    ((4, 2), (3, 3), (1, 6)),
    ((2, 5),),
    ((5, 2), (4, 3), (2, 4)),
    (),
    ((3, 0), (5, 3)),
    (),
    ((1, 7),),
    ((3, 5),),
    (
        (1, 8), (2, 6), (0, 9), (0, 10), (3, 4), (4, 0), (2, 7), (4, 5),
        (3, 6), (2, 8), (1, 9), (5, 0), (1, 10), (4, 4), (3, 7), (5, 5),
        (4, 6), (2, 10), (2, 9), (5, 4), (3, 8), (4, 7), (3, 10), (5, 6),
        (3, 9), (5, 7), (4, 8), (4, 10), (4, 9), (5, 8), (5, 10), (5, 9),
    ),
)


class Scatter:
    def __init__(self, sources, outs, layer_in, layer_out, buffers, sems):
        items = len(SCATTER_ITEMS)
        self.sources, self.outs = sources, outs
        self.layer_in, self.layer_out = layer_in, layer_out
        self.sems = sems
        self.y, self.x, self.core, self.place, self.lines, self.count = position()
        y, x, core = self.y, self.x, self.core
        self.own = list(buffers[:FIRST_ITEMS])
        for array, _, _, _ in SCATTER_ITEMS[FIRST_ITEMS:]:
            self.own.append(sources[array].at[:, :, core])
        buffers = buffers[FIRST_ITEMS:]
        self.from_twin, self.first_in, self.second_in, self.line_in = [
            buffers[k * items : (k + 1) * items] for k in range(4)
        ]
        self.dp = dp_of(y, x, core)
        self.twin = dp_of(y, x, 1 - core)
        self.side = dp_of(y, 1 - x, core)
        self.ahead = [(y + k) % self.lines for k in range(1, self.lines)]

    def meet(self):
        targets = [(self.twin, self.place), (self.side, self.place)]
        for k in range(1, self.count):
            other = (self.place + k) % self.count
            targets += [(self.dp, other), (self.twin, other)]
        for other_y in self.ahead:
            targets.append((dp_of(other_y, self.x, self.core), self.place))
        meet(targets)

    def order(self, item):
        return SCATTER_ITEMS[item][3]

    def columns(self, item):
        array, part, parts, _ = SCATTER_ITEMS[item]
        cols = self.sources[array].shape[-1] // parts
        return pl.ds(part * cols, cols)

    def to_twin(self, item):
        src = self.sources[SCATTER_ITEMS[item][0]].at[:, :, 1 - self.core, :, :, self.columns(item)]
        sems = self.sems
        return remote(
            src, self.from_twin[item], sems["twin_send"].at[item], sems["twin_recv"].at[item], self.twin, self.place
        )

    def own_in(self, item):
        src = self.sources[SCATTER_ITEMS[item][0]].at[:, :, self.core, :, :, self.columns(item)]
        return pltpu.make_async_copy(src, self.own[item], self.sems["own"].at[item])

    def x_copy(self, item):
        own = self.own[item]
        if self.order(item) == 0:
            src, dst = own.at[self.y, 1 - self.x], self.second_in[item].at[0]
        else:
            src, dst = own.at[:, 1 - self.x], self.first_in[item]
        return remote(
            src, dst, self.sems["x_send"].at[item], self.sems["x_recv"].at[item], self.side, self.place
        )

    def y_copy(self, item, k):
        other_y = self.ahead[k]
        own = self.own[item]
        if self.order(item) == 0:
            src, dst = own.at[other_y], self.first_in[item].at[k]
        else:
            src, dst = own.at[other_y, self.x], self.second_in[item].at[k]
        return remote(
            src,
            dst,
            self.sems["y_send"].at[item, k],
            self.sems["y_recv"].at[item, k],
            dp_of(other_y, self.x, self.core),
            self.place,
        )

    def stage_begin(self, item):
        self.to_twin(item).start()
        if item < FIRST_ITEMS:
            self.own_in(item).start()

    def stage_core(self, item):
        if item < FIRST_ITEMS:
            self.own_in(item).wait()
        self.to_twin(item).wait_recv()
        own, came = self.own[item], self.from_twin[item]

        def step(i, carry):
            a, b = i // 2, i % 2
            own[a, b] = plus(own[a, b], came[a, b])
            return carry

        lax.fori_loop(0, 2 * self.lines, step, 0)
        if self.order(item) == 0:
            for k in range(self.lines - 1):
                self.y_copy(item, k).start()
        else:
            self.x_copy(item).start()

    def stage_first(self, item):
        own, came = self.own[item], self.first_in[item]
        y, x, lines = self.y, self.x, self.lines
        if self.order(item) == 0:
            for k in range(lines - 1):
                self.y_copy(item, k).wait_recv()

            def step(b, carry):
                total = own[y, b]
                for k in range(lines - 1):
                    total = plus(total, came[k, b])
                own[y, b] = total
                return carry

            lax.fori_loop(0, 2, step, 0)
            self.x_copy(item).start()
        else:
            self.x_copy(item).wait_recv()

            def step(a, carry):
                own[a, x] = plus(own[a, x], came[a])
                return carry

            lax.fori_loop(0, lines, step, 0)
            for k in range(lines - 1):
                self.y_copy(item, k).start()

    def mine(self, item, z):
        return self.own[item].at[self.y, self.x, z]

    def z_copy(self, item, z, way):
        return remote(
            self.mine(item, z),
            self.line_in[item].at[way, z],
            self.sems["z_send"].at[item, z],
            self.sems["z_recv"].at[item, way, z],
            self.dp,
            self.place + 1 - 2 * way,
        )

    def z_forward(self, item, way, first):
        def step(z, carry):
            beyond = (z > self.place) if way == 0 else (z < self.place)

            @pl.when(beyond)
            def _():
                if not first:
                    self.z_copy(item, z, way).wait_recv()
                    ref = self.mine(item, z)
                    ref[...] = plus(ref[...], self.line_in[item][way, z])
                self.z_copy(item, z, way).start()

            return carry

        lax.fori_loop(0, self.count, step, 0)

    def stage_second(self, item):
        own, came = self.own[item], self.second_in[item]
        y, x = self.y, self.x
        if self.order(item) == 0:
            self.x_copy(item).wait_recv()
            own[y, x] = plus(own[y, x], came[0])
        else:
            total = own[y, x]
            for k in range(self.lines - 1):
                self.y_copy(item, k).wait_recv()
                total = plus(total, came[k])
            own[y, x] = total

        @pl.when(self.place == 0)
        def _():
            self.z_forward(item, 0, True)

        @pl.when(self.place == self.count - 1)
        def _():
            self.z_forward(item, 1, True)

    def stage_hop(self, hop, item):
        @pl.when(self.place == hop)
        def _():
            self.z_forward(item, 0, False)

        @pl.when(self.count - 1 - self.place == hop)
        def _():
            self.z_forward(item, 1, False)

    def stage_last(self, item):
        out = self.outs[SCATTER_ITEMS[item][0]]
        columns = self.columns(item)
        place = self.place
        out[:, columns] = self.mine(item, place)[...].astype(jnp.float32)

        def add(way):
            self.z_copy(item, place, way).wait_recv()
            out[:, columns] += self.line_in[item][way, place].astype(jnp.float32)

        @pl.when(place > 0)
        def _():
            add(0)

        @pl.when(place < self.count - 1)
        def _():
            add(1)

    def layer_copies(self, fn_remote, fn_local):
        seqs = self.layer_in.shape[0]
        for k in range(seqs):
            chip = seqs * self.core + k
            home = (chip == self.place) & (self.core == self.place // seqs)

            @pl.when(home)
            def _():
                fn_local(k)

            @pl.when(jnp.logical_not(home))
            def _():
                fn_remote(k, chip)

    def layer_remote(self, k, chip):
        seqs = self.layer_in.shape[0]
        row = self.place % seqs
        return remote(
            self.layer_in.at[k],
            self.layer_out.at[row],
            self.sems["layer_send"].at[k],
            self.sems["layer_recv"].at[row],
            dp_of(self.y, self.x, self.place // seqs),
            chip,
        )

    def layer_start(self):
        row = self.place % self.layer_in.shape[0]
        self.layer_copies(
            lambda k, chip: self.layer_remote(k, chip).start(),
            lambda k: pltpu.make_async_copy(
                self.layer_in.at[k], self.layer_out.at[row], self.sems["layer_recv"].at[row]
            ).start(),
        )

    def stage_hop_one(self, item):
        self.stage_hop(1, item)

    def stage_hops(self, item):
        for hop in range(2, self.count - 1):
            self.stage_hop(hop, item)

    def stages(self):
        return (
            self.stage_core,
            self.stage_first,
            self.stage_second,
            self.stage_hop_one,
            self.stage_hops,
            self.stage_last,
        )

    def finish(self):
        for item in range(len(SCATTER_ITEMS)):
            self.to_twin(item).wait_send()
            self.x_copy(item).wait_send()
            for k in range(self.lines - 1):
                self.y_copy(item, k).wait_send()

            def drain(z, carry):
                @pl.when(z > self.place)
                def _():
                    self.z_copy(item, z, 0).wait_send()

                @pl.when(z < self.place)
                def _():
                    self.z_copy(item, z, 1).wait_send()

                return carry

            lax.fori_loop(0, self.count, drain, 0)
        for r in range(self.layer_in.shape[0]):
            dst = self.layer_out.at[r]
            remote(
                dst, dst, self.sems["layer_send"].at[0], self.sems["layer_recv"].at[r], self.twin, self.place
            ).wait_recv()
        self.layer_copies(lambda k, chip: self.layer_remote(k, chip).wait_send(), lambda k: None)


SCATTER_SEMS = (
    "own",
    "twin_send",
    "twin_recv",
    "x_send",
    "x_recv",
    "y_send",
    "y_recv",
    "z_send",
    "z_recv",
    "layer_send",
    "layer_recv",
)


def plus(left, right):
    total = left.astype(jnp.float32) + right.astype(jnp.float32)
    return total.astype(left.dtype)


def scatter_scratch(shapes, lines, count, seqs):
    items = len(SCATTER_ITEMS)
    own, first_in, second_in, line_in = [], [], [], []
    for array, _, parts, order in SCATTER_ITEMS:
        rows, cols, kind = shapes[array]
        cols = cols // parts
        own.append(pltpu.VMEM((lines, 2, count, rows, cols), kind))
        if order == 0:
            first_in.append(pltpu.VMEM((lines - 1, 2, count, rows, cols), kind))
            second_in.append(pltpu.VMEM((1, count, rows, cols), kind))
        else:
            first_in.append(pltpu.VMEM((lines, count, rows, cols), kind))
            second_in.append(pltpu.VMEM((lines - 1, count, rows, cols), kind))
        line_in.append(pltpu.VMEM((2, count, rows, cols), kind))
    dma = pltpu.SemaphoreType.DMA
    sems = [dma((FIRST_ITEMS,))] + [dma((items,))] * 4
    sems += [dma((items, lines - 1))] * 2 + [dma((items, count)), dma((items, 2, count))]
    sems += [dma((seqs,))] * 2
    return own[:FIRST_ITEMS] + own + first_in + second_in + line_in, sems


BACK_INPUTS = (
    "gate",
    "up",
    "down",
    "output",
    "coef",
    "resid",
    "qt",
    "kt",
    "vt",
    "got",
    "out",
    "lse",
    "key_marks",
    "query_marks",
    "normed",
    "stream",
    "wq",
    "wk",
    "wv",
    "small",
    "gain_two",
    "table",
    "tap",
    "rows",
    "idm",
    "layer",
)


def backward_kernel(*refs):
    ref = dict(zip(BACK_INPUTS, refs))
    rest = refs[len(BACK_INPUTS) :]
    outs, layer_out = rest[:9], rest[9]
    rest = rest[10:]
    held = FIRST_ITEMS + 4 * len(SCATTER_ITEMS)
    buffers, rest = rest[:held], rest[held:]
    sems = dict(zip(SCATTER_SEMS, rest[: len(SCATTER_SEMS)]))
    names = ("dq", "dkv", "away", "came", "wide", "one_hot", "src_q", "src_k", "src_v", "src_table", "src_small", "swap_send", "swap_recv", "coef_sem", "resid_sem")
    own = dict(zip(names, rest[len(SCATTER_SEMS) :]))
    sources = (
        own["src_q"],
        own["src_k"],
        own["src_v"],
        ref["output"],
        ref["gate"],
        ref["up"],
        ref["down"],
        own["src_table"],
        own["src_small"],
    )
    scatter = Scatter(sources, outs, ref["layer"], layer_out, buffers, sems)
    stages = scatter.stages()
    width, tokens = ref["qt"].shape
    pairs = width // 128
    bias = own["one_hot"].at[0 : ref["kt"].shape[1], 0:tokens]
    scatter.meet()
    for item in range(FIRST_ITEMS):
        scatter.stage_begin(item)

    queue = [[functools.partial(stages[stage], item) for stage, item in group] for group in SCHEDULE]

    def tick():
        for task in queue.pop(0):
            task()

    scatter.layer_start()
    tick()
    fill_bias(bias, ref["key_marks"], ref["query_marks"])

    def swap(i, which):
        rows = pl.ds(pl.multiple_of(which * width + 128 * i, 128), 128)
        return remote(
            own["away"].at[rows],
            own["came"].at[rows],
            own["swap_send"].at[which, i],
            own["swap_recv"].at[which, i],
            scatter.twin,
            scatter.place,
        )

    ticks = [queue.pop(0) for _ in range(pairs)]

    def pair_step(i, carry):
        at = pl.ds(pl.multiple_of(128 * i, 128), 128)
        attend_backward_pair(
            ref["qt"].at[at],
            ref["kt"].at[at],
            ref["vt"].at[at],
            ref["got"].at[at],
            ref["out"].at[at],
            ref["lse"].at[i],
            bias,
            own["dq"].at[at],
            own["dkv"].at[at],
            own["dkv"].at[pl.ds(pl.multiple_of(width + 128 * i, 128), 128)],
            own["away"].at[at],
            own["away"].at[pl.ds(pl.multiple_of(width + 128 * i, 128), 128)],
        )
        swap(i, 0).start()
        swap(i, 1).start()
        for k, group in enumerate(ticks):
            if group:

                @pl.when(i == k)
                def _():
                    for task in group:
                        task()

        return carry

    lax.fori_loop(0, pairs, pair_step, 0)

    normed_t = ref["normed"][...].T
    wide = own["wide"]

    def hand_out(source, item):
        lines, _, _, count, size, _ = source.shape
        total = lines * 4 * count

        for o in range(total):
            where = (o // (4 * count), o // (2 * count) % 2, o // count % 2, o % count)
            source[where] = wide[size * o : size * (o + 1)].astype(source.dtype)
        scatter.stage_begin(item)

    wide[...] = mm_nt(normed_t, own["dq"][...])
    hand_out(own["src_q"], 6)
    tick()
    for which in range(2):

        def add_half(i, carry):
            swap(i, which).wait_recv()
            rows = pl.ds(pl.multiple_of(which * width + 128 * i, 128), 128)
            own["dkv"][rows] = plus(own["dkv"][rows], own["came"][rows])
            return carry

        lax.fori_loop(0, pairs, add_half, 0)
    coef = own["came"].at[0 : KW * VOCAB]
    coef_copy = pltpu.make_async_copy(ref["coef"], coef, own["coef_sem"])
    coef_copy.start()
    wide[...] = mm_nt(normed_t, own["dkv"][0:width])
    hand_out(own["src_k"], 7)
    tick()
    wide[...] = mm_nt(normed_t, own["dkv"][width:])
    hand_out(own["src_v"], 8)
    tick()

    wide[:, 0:tokens] = mm(ref["wq"][...], own["dq"][...])
    wide[:, 0:tokens] += mm(ref["wk"][...], own["dkv"][0:width])
    tick()
    wide[:, 0:tokens] += mm(ref["wv"][...], own["dkv"][width:])
    normed_grad = wide[:, 0:tokens].T
    resid_copy = pltpu.make_async_copy(ref["resid"], wide.at[0:tokens], own["resid_sem"])
    resid_copy.start()
    stream = ref["stream"][...]
    gain = ref["small"][KW + 1 : KW + 2]
    scale = lax.rsqrt(jnp.mean(stream * stream, axis=-1, keepdims=True) + 1e-06)
    gain_grad = jnp.sum(normed_grad * stream * scale, axis=0, keepdims=True)
    scaled = normed_grad * gain
    inner = jnp.mean(scaled * stream, axis=-1, keepdims=True)
    resid_copy.wait()
    grad16 = (wide[0:tokens] + scale * scaled - stream * (scale * scale * scale * inner)).astype(jnp.bfloat16)
    tick()
    coef_copy.wait()
    table_grad, rows = tok_backward_body(
        grad16, coef, ref["tap"], ref["rows"], ref["idm"], ref["table"], ref["small"], own["one_hot"], tick
    )
    wide[0:VOCAB] = table_grad
    hand_out(own["src_table"], 9)
    rows = jnp.concatenate(rows + [gain_grad, ref["gain_two"][...]], axis=0)
    source = own["src_small"]
    lines, _, _, count, _, _ = source.shape
    total = lines * 4 * count
    for o in range(total):
        where = (o // (4 * count), o // (2 * count) % 2, o // count % 2, o % count)
        source[where] = lane_shift(rows, o * (width // total))[:, 0:128]
    scatter.stage_begin(10)
    while queue:
        tick()
    scatter.finish()

    def drain(i, carry):
        swap(i, 0).wait_send()
        swap(i, 1).wait_send()
        return carry

    lax.fori_loop(0, pairs, drain, 0)


def backward_all(arrays, shapes):
    count = lax.axis_size("seq")
    lines = lax.axis_size("dp") // 4
    total = lines * 4 * count
    vmem = pl.BlockSpec(memory_space=pltpu.VMEM)
    hbm = pl.BlockSpec(memory_space=pltpu.HBM)
    layer = arrays["layer"]
    width, tokens = arrays["qt"].shape
    out_shape = [jax.ShapeDtypeStruct(shape[:2], jnp.float32) for shape in shapes]
    out_shape.append(jax.ShapeDtypeStruct(layer.shape, layer.dtype))
    buffers, sems = scatter_scratch(shapes, lines, count, layer.shape[0])
    views = dict(arrays)
    for name in ("gate", "up", "down", "output"):
        grad = arrays[name]
        views[name] = grad.reshape(lines, 2, 2, count, grad.shape[0] // total, grad.shape[1])

    def source(index):
        rows, cols, kind = shapes[index]
        return pltpu.VMEM((lines, 2, 2, count, rows, cols), kind)

    half = jnp.bfloat16
    own = [
        pltpu.VMEM((width, tokens), half),
        pltpu.VMEM((2 * width, tokens), half),
        pltpu.VMEM((2 * width, tokens), half),
        pltpu.VMEM((2 * width, tokens), half),
        pltpu.VMEM((width, width), jnp.float32),
        pltpu.VMEM((KW * VOCAB, arrays["idm"].shape[1]), half),
        source(0),
        source(1),
        source(2),
        source(7),
        source(8),
        pltpu.SemaphoreType.DMA((2, width // 128)),
        pltpu.SemaphoreType.DMA((2, width // 128)),
        pltpu.SemaphoreType.DMA,
        pltpu.SemaphoreType.DMA,
    ]
    return pl.pallas_call(
        backward_kernel,
        name="backward_all",
        out_shape=out_shape,
        in_specs=[hbm] * 6 + [vmem] * (len(BACK_INPUTS) - 6),
        out_specs=[vmem] * 9 + [hbm],
        scratch_shapes=buffers + sems + own,
        compiler_params=pltpu.CompilerParams(
            collective_id=1, has_side_effects=True, vmem_limit_bytes=63 * 1024 * 1024
        ),
    )(*[views[name] for name in BACK_INPUTS])


def tok_forward_body(own, core, tokens, tick):
    ids_ref, marks_ref, table_ref, small_ref = own["ids_pad"], own["marks_pad"], own["table"], own["small"]
    stream_ref, normed_ref, coef_ref, tap_ref = own["stream"], own["normed"], own["coef"], own["tap"]
    rows_ref, idm_ref, one_hot = own["rows"], own["idm"], own["one_hot"]
    half_bytes = 2 * tokens
    span = one_hot.shape[1]
    wide = span + 2 * LEFT
    first = pl.ds(pl.multiple_of(core * half_bytes, 128), wide)
    ids = ids_ref[:, first]
    marks = marks_ref[:, first]
    for tap in range(KW):
        by = tap - KW // 2
        same = (lane_shift(marks, by) == marks) & (marks > 0)
        idm_ref[tap : tap + 1] = jnp.where(same, lane_shift(ids, by), -1)[0:1, LEFT : LEFT + span]
    tick()
    fill_one_hot(one_hot, lambda tap: idm_ref[tap : tap + 1])

    tick()
    score = jnp.broadcast_to(small_ref[KW : KW + 1], (8, small_ref.shape[1])).astype(jnp.bfloat16)
    scored = []
    for tap in range(KW):
        product = table_ref[...].astype(jnp.float32) * small_ref[tap : tap + 1]
        high, low = split_two(product)
        tap_ref[tap * VOCAB : (tap + 1) * VOCAB] = high
        scored.append(mm_nt(score, high) + mm_nt(score, low))
    tick()
    high, low = split_two(jnp.concatenate(scored, axis=1))
    u_row = mm(high, one_hot[...]) + mm(low, one_hot[...])

    tick()
    high = u_row.astype(jnp.bfloat16).astype(jnp.float32)
    marks_here = marks[:, LEFT : LEFT + span].astype(jnp.float32)
    away = marks_ref[:, pl.ds(pl.multiple_of((1 - core) * half_bytes, 128), wide)][:, LEFT : LEFT + span]
    away = away.astype(jnp.float32)
    packed = jnp.concatenate([marks_here, high, u_row - high, away], axis=0).astype(jnp.bfloat16)
    shape = (span, wide // 2)
    twice = 2 * lax.broadcasted_iota(jnp.int32, shape, 1) - lax.broadcasted_iota(jnp.int32, shape, 0) - LEFT
    marks_of, u_of = [], []
    for e in range(2):
        pick = (twice == -e).astype(jnp.float32).astype(jnp.bfloat16)
        apart = mm(packed, pick)
        marks_of.append(apart[0:8])
        u_of.append(apart[8:16] + apart[16:24])
        if e == 0:
            kept = slice(LEFT, LEFT + tokens)
            both = jnp.concatenate([apart[0:1, kept], apart[24:25, kept]], axis=1)
            own["marks"][...] = both.astype(jnp.int32)

    tick()
    inside, inverse = pool_rows(marks_of, core, half_bytes)
    prob = {}
    for e in range(2):
        shifted = {}
        for s in range(1 - MAXBLOCK, MAXBLOCK):
            f = (e + s) % 2
            shifted[s] = lane_shift(u_of[f], (e + s - f) // 2)
        scores = [u_of[e]]
        for b in range(2, MAXBLOCK + 1):
            total = u_of[e]
            for s in range(1 - b, b):
                if s != 0:
                    total = total + inside[b, e, s] * shifted[s]
            scores.append(total * inverse[b, e])
        top = scores[0]
        for value in scores[1:]:
            top = jnp.maximum(top, value)
        expo = [jnp.exp(value - top) for value in scores]
        whole = expo[0] + expo[1] + expo[2] + expo[3]
        for b in range(1, MAXBLOCK + 1):
            prob[b, e] = expo[b - 1] / whole
            rows_ref[2 * b + e : 2 * b + e + 1] = prob[b, e][0:1]
        rows_ref[e : e + 1] = marks_of[e][0:1]
    coefs = band_coefs({key: 0.5 * value for key, value in prob.items()}, inside, inverse)
    gain = small_ref[KW + 1 : KW + 2]
    tick()
    for i in range(tokens // BAND):
        matrix = band_matrix(coefs, i).astype(jnp.bfloat16)
        lanes = slice(i * BAND, (i + 1) * BAND)
        part = mm(one_hot[:, 2 * i * BAND : (2 * i + 3) * BAND], matrix).astype(jnp.bfloat16)
        coef_ref[:, lanes] = part
        stream = mm_tn(part, tap_ref[...])
        stream_ref[lanes] = stream
        scale = lax.rsqrt(jnp.mean(stream * stream, axis=-1, keepdims=True) + 1e-06)
        normed_ref[lanes] = (stream * scale * gain).astype(jnp.bfloat16)
        if i < tokens // BAND - 1:
            tick()


FUSED_ITEMS = (
    (7, 0, 1, 0, 0),
    (8, 0, 1, 0, 0),
    (0, 0, 1, 1, 1),
    (1, 0, 1, 0, 1),
    (2, 0, 1, 1, 1),
    (3, 0, 1, 0, 1),
    (6, 0, 2, 0, 2),
    (4, 1, 2, 0, 2),
    (6, 1, 2, 1, 3),
    (5, 0, 2, 1, 3),
    (4, 0, 2, 1, 4),
    (5, 1, 2, 0, 4),
)
FUSED_SCHEDULE = (
    (
        (0, 0, 0), (1, 0, 0), (0, 1, 0), (1, 1, 0), (2, 0, 1), (3, 0, 0),
        (3, 1, 0), (2, 0, 2), (4, 0, 0), (3, 0, 1), (2, 0, 3), (2, 1, 1),
        (0, 2, 0), (3, 0, 2), (4, 1, 0), (3, 0, 3), (2, 1, 2), (4, 0, 1),
        (3, 1, 1), (4, 0, 2), (4, 0, 3), (2, 1, 3), (1, 2, 0), (2, 2, 1),
        (0, 3, 0),
    ),
    (),
    (),
    (
        (2, 2, 2), (3, 1, 2),
    ),
    ((4, 1, 1),),
    ((3, 1, 3),),
    (),
    (
        (2, 2, 3), (1, 3, 0), (2, 3, 1), (0, 4, 0), (3, 2, 0),
    ),
    (
        (3, 2, 1), (3, 2, 2), (2, 3, 2), (4, 1, 2), (4, 1, 3),
    ),
    (
        (2, 3, 3), (1, 4, 0), (2, 4, 1), (3, 2, 3),
    ),
    (),
    (
        (2, 4, 2), (3, 3, 0),
    ),
    (
        (3, 3, 1), (4, 2, 0),
    ),
    (
        (2, 4, 3), (5, 0, 0),
    ),
    (),
    ((4, 2, 1),),
    (
        (3, 3, 2), (3, 3, 3), (4, 2, 2), (4, 3, 0),
    ),
    ((3, 4, 0),),
    (
        (3, 4, 1), (4, 2, 3), (4, 3, 1), (4, 3, 2),
    ),
    (
        (3, 4, 2), (3, 4, 3), (4, 3, 3), (4, 4, 0),
    ),
    (
        (4, 4, 1), (4, 4, 2), (4, 4, 3),
    ),
)


class Gather:
    def __init__(self, ins, outs, cells_in, cells_out, cot_in, cot_out, sems):
        self.ins, self.outs, self.sems = ins, outs, sems
        self.cells_in, self.cells_out, self.cot_in, self.cot_out = cells_in, cells_out, cot_in, cot_out
        self.y, self.x, self.core, self.place, self.lines, self.count = position()
        y, x, core = self.y, self.x, self.core
        self.group = y * 2 + x
        self.dp = dp_of(y, x, core)
        self.twin = dp_of(y, x, 1 - core)
        self.side = dp_of(y, 1 - x, core)
        self.ahead = [(y + k) % self.lines for k in range(1, self.lines)]
        self.phases = {}
        for item, entry in enumerate(FUSED_ITEMS):
            self.phases.setdefault(entry[4], []).append(item)

    def meet(self):
        targets = [(self.twin, self.place), (self.side, self.place)]
        for k in range(1, self.count):
            other = (self.place + k) % self.count
            targets += [(self.dp, other), (self.twin, other)]
        for other_y in self.ahead:
            targets.append((dp_of(other_y, self.x, self.core), self.place))
        meet(targets)

    def lanes(self, item):
        array, part, parts, _, _ = FUSED_ITEMS[item]
        cols = self.ins[array].shape[1] // parts
        return pl.ds(part * cols, cols)

    def shard(self, item):
        return self.ins[FUSED_ITEMS[item][0]].at[:, self.lanes(item)]

    def rows(self, item, first, blocks):
        array = FUSED_ITEMS[item][0]
        size = self.ins[array].shape[0]
        start = pl.multiple_of(first * size, 8)
        return self.outs[array].at[pl.ds(start, blocks * size), self.lanes(item)]

    def block(self, item, g, z):
        return self.rows(item, (g * 2 + self.core) * self.count + z, 1)

    def group_block(self, item, g, core):
        return self.rows(item, (g * 2 + core) * self.count, self.count)

    def came(self, item, g, z):
        return self.sems["recv"].at[item, g * self.count + z]

    def arrived(self, item, g, z):
        dst = self.block(item, g, z)
        remote(dst, dst, self.sems["x"].at[item], self.came(item, g, z), self.twin, self.place).wait_recv()

    def to_side(self, item, src, g, z):
        remote(
            src, self.block(item, g, z), self.sems["x"].at[item], self.came(item, g, z), self.side, self.place
        ).start()

    def to_lines(self, item, src, g, z):
        for other_y in self.ahead:
            remote(
                src,
                self.block(item, g, z),
                self.sems["y"].at[item],
                self.came(item, g, z),
                dp_of(other_y, self.x, self.core),
                self.place,
            ).start()

    def to_z(self, item, src, z, way):
        return remote(
            src,
            self.block(item, self.group, z),
            self.sems["z"].at[item, z, way],
            self.came(item, self.group, z),
            self.dp,
            self.place + 1 - 2 * way,
        )

    def to_twin(self, item, g):
        src = self.group_block(item, g, self.core)
        remote(
            src, src, self.sems["twin"].at[item], self.sems["twin_recv"].at[item, g], self.twin, self.place
        ).start()

    def own_copy(self, item):
        return pltpu.make_async_copy(
            self.shard(item), self.block(item, self.group, self.place), self.sems["own"].at[item]
        )

    def task_own(self, phase):
        for item in self.phases[phase]:
            src = self.shard(item)

            @pl.when(self.place < self.count - 1)
            def _():
                self.to_z(item, src, self.place, 0).start()

            @pl.when(self.place > 0)
            def _():
                self.to_z(item, src, self.place, 1).start()

            self.own_copy(item).start()

    def task_sides(self, phase):
        for item in self.phases[phase]:
            src = self.shard(item)
            self.to_side(item, src, self.group, self.place)
            self.to_lines(item, src, self.group, self.place)

    def both_ways(self, step, body):
        low, high = self.place - step, self.place + step

        @pl.when(low >= 0)
        def _():
            body(low, 0)

        @pl.when(high < self.count)
        def _():
            body(high, 1)

    def steps(self, step, body):
        if step < 3:
            body(step)
            return

        def loop(s, carry):
            body(s)
            return carry

        lax.fori_loop(3, self.count, loop, 0)

    def task_first(self, phase, step):
        items = self.phases[phase]

        def receive(z, way):
            for item in items:
                self.arrived(item, self.group, z)
                src = self.block(item, self.group, z)
                onward = self.place < self.count - 1 if way == 0 else self.place > 0

                @pl.when(onward)
                def _():
                    self.to_z(item, src, z, way).start()

                self.to_side(item, src, self.group, z)
                self.to_lines(item, src, self.group, z)

        self.steps(step, lambda s: self.both_ways(s, receive))
        if step == 3:
            for item in items:
                self.own_copy(item).wait()
                self.to_twin(item, self.group)

    def at_distance(self, step, body):
        if step == 0:
            body(self.place, 0)
        else:
            self.steps(step, lambda s: self.both_ways(s, body))

    def task_second(self, phase, step):
        items = self.phases[phase]

        def receive(z, way):
            for item in items:
                if FUSED_ITEMS[item][3] == 0:
                    g = self.y * 2 + (1 - self.x)
                    self.arrived(item, g, z)
                    self.to_lines(item, self.block(item, g, z), g, z)
                else:
                    for other_y in self.ahead:
                        g = other_y * 2 + self.x
                        self.arrived(item, g, z)
                        self.to_side(item, self.block(item, g, z), g, z)

        self.at_distance(step, receive)
        if step == 3:
            for item in items:
                if FUSED_ITEMS[item][3] == 0:
                    self.to_twin(item, self.y * 2 + (1 - self.x))
                else:
                    for other_y in self.ahead:
                        self.to_twin(item, other_y * 2 + self.x)

    def task_third(self, phase, step):
        items = self.phases[phase]

        def rest(item):
            if FUSED_ITEMS[item][3] == 0:
                return [other_y * 2 + x for other_y in self.ahead for x in (self.x, 1 - self.x)]
            return [other_y * 2 + (1 - self.x) for other_y in [self.y] + self.ahead]

        def receive(z, way):
            for item in items:
                for g in rest(item):
                    self.arrived(item, g, z)

        self.at_distance(step, receive)
        if step == 3:
            for item in items:
                for g in rest(item):
                    self.to_twin(item, g)

    def full(self, item):
        for g in range(self.lines * 2):
            dst = self.group_block(item, g, 1 - self.core)
            remote(
                dst, dst, self.sems["twin"].at[item], self.sems["twin_recv"].at[item, g], self.twin, self.place
            ).wait_recv()

    def cell_copies(self, fn_remote, fn_local):
        seqs = self.cells_in.shape[0]
        for r in range(seqs):
            chip = seqs * self.core + r
            for c in range(2):
                home = (chip == self.place) & (self.core == c)

                @pl.when(home)
                def _():
                    fn_local(r)

                @pl.when(jnp.logical_not(home))
                def _():
                    fn_remote(r, c, chip)

    def cell_remote(self, r, c, chip):
        return remote(
            self.cells_in.at[r],
            self.cells_out.at[self.place],
            self.sems["cell_send"].at[r, c],
            self.sems["cell_recv"].at[self.place],
            dp_of(self.y, self.x, c),
            chip,
        )

    def cells_start(self):
        self.cell_copies(
            lambda r, c, chip: self.cell_remote(r, c, chip).start(),
            lambda r: pltpu.make_async_copy(
                self.cells_in.at[r], self.cells_out.at[self.place], self.sems["cell_recv"].at[self.place]
            ).start(),
        )

    def cells_wait(self):
        for q in range(self.count):
            dst = self.cells_out.at[q]
            remote(
                dst, dst, self.sems["cell_send"].at[0, 0], self.sems["cell_recv"].at[q], self.twin, self.place
            ).wait_recv()

    def cot_copies(self, fn_remote, fn_local):
        seqs = self.cot_in.shape[0]
        for r in range(seqs):
            chip = seqs * self.core + r
            home = (chip == self.place) & (self.core == self.place // seqs)

            @pl.when(home)
            def _():
                fn_local(r)

            @pl.when(jnp.logical_not(home))
            def _():
                fn_remote(r, chip)

    def cot_remote(self, r, chip):
        seqs = self.cot_in.shape[0]
        slot = self.place % seqs
        return remote(
            self.cot_in.at[r],
            self.cot_out.at[slot],
            self.sems["cot_send"].at[r],
            self.sems["cot_recv"].at[slot],
            dp_of(self.y, self.x, self.place // seqs),
            chip,
        )

    def task_cot(self):
        slot = self.place % self.cot_in.shape[0]
        self.cot_copies(
            lambda r, chip: self.cot_remote(r, chip).start(),
            lambda r: pltpu.make_async_copy(
                self.cot_in.at[r], self.cot_out.at[slot], self.sems["cot_recv"].at[slot]
            ).start(),
        )

    def task(self, kind, phase, step):
        if kind == 0:
            self.task_own(phase)
        elif kind == 1:
            self.task_sides(phase)
        elif kind == 2:
            self.task_first(phase, step)
        elif kind == 3:
            self.task_second(phase, step)
        elif kind == 4:
            self.task_third(phase, step)
        else:
            self.task_cot()

    def finish(self, waited):
        count, groups = self.count, self.lines * 2
        for item in range(len(FUSED_ITEMS)):
            if item not in waited:
                self.full(item)
            tree = FUSED_ITEMS[item][3]

            def sent(blocks, sem):
                src = self.rows(item, 0, blocks)
                remote(src, src, sem, self.came(item, 0, 0), self.twin, self.place).wait_send()

            sent(count * (1 if tree == 0 else self.lines), self.sems["x"].at[item])
            sent(count * (self.lines - 1) * (2 if tree == 0 else 1), self.sems["y"].at[item])
            sent(count * groups, self.sems["twin"].at[item])

            def drain(z, carry):
                @pl.when((z <= self.place) & (self.place < count - 1))
                def _():
                    self.to_z(item, self.block(item, self.group, z), z, 0).wait_send()

                @pl.when((z >= self.place) & (self.place > 0))
                def _():
                    self.to_z(item, self.block(item, self.group, z), z, 1).wait_send()

                return carry

            lax.fori_loop(0, count, drain, 0)
        for q in range(self.cot_in.shape[0]):
            dst = self.cot_out.at[q]
            remote(
                dst, dst, self.sems["cot_send"].at[0], self.sems["cot_recv"].at[q], self.twin, self.place
            ).wait_recv()
        self.cell_copies(lambda r, c, chip: self.cell_remote(r, c, chip).wait_send(), lambda r: None)
        self.cot_copies(lambda r, chip: self.cot_remote(r, chip).wait_send(), lambda r: None)


GATHER_SEMS = (
    "recv",
    "twin_recv",
    "z",
    "x",
    "y",
    "twin",
    "own",
    "cell_recv",
    "cell_send",
    "cot_recv",
    "cot_send",
)
FRONT_OUTS = (
    "cot",
    "stream",
    "normed",
    "coef",
    "tap",
    "rows",
    "idm",
    "qt",
    "kt",
    "vt",
    "out",
    "lse",
    "marks",
    "small",
    "resid",
    "normed_two",
)


def attend_forward_pair(qt, kt, vt, bias, scores, out, lse):
    keys = kt[...].T
    chunks = keys.shape[0] // CHUNK
    for h in range(2):
        query = pair_rows(qt, h)
        own = slice(h * HEAD_DIM, (h + 1) * HEAD_DIM)
        top = None
        for c in range(chunks):
            rows = slice(c * CHUNK, (c + 1) * CHUNK)
            part = mm(keys[rows], query) + bias[rows]
            scores[h, rows] = part
            high = jnp.max(part, axis=0, keepdims=True)
            top = high if top is None else jnp.maximum(top, high)
        total = None
        summed = None
        for c in range(chunks):
            rows = slice(c * CHUNK, (c + 1) * CHUNK)
            expo = jnp.exp(scores[h, rows] - top)
            part = jnp.sum(expo, axis=0, keepdims=True)
            total = part if total is None else total + part
            part = mm(vt[own, rows], expo.astype(jnp.bfloat16))
            summed = part if summed is None else summed + part
        out[own] = (summed / total).astype(jnp.bfloat16)
        lse[h : h + 1] = top + jnp.log(total)


def forward_kernel(*refs):
    arrays = 9
    ins, cells_in, cot_in = refs[:arrays], refs[arrays], refs[arrays + 1]
    rest = refs[arrays + 2 :]
    full, cells_out = rest[:arrays], rest[arrays]
    to = dict(zip(FRONT_OUTS, rest[arrays + 1 :]))
    rest = rest[arrays + 1 + len(FRONT_OUTS) :]
    sems = dict(zip(GATHER_SEMS, rest))
    rest = rest[len(GATHER_SEMS) :]
    held = FRONT_OUTS[1:]
    own = dict(zip(held, rest))
    rest = rest[len(held) :]
    names = ("cells", "ids_pad", "marks_pad", "table", "blocks", "wq", "wk", "wv", "wo", "other", "one_hot", "bias", "scores", "out_sem", "load_sem", "swap_send", "swap_recv")
    own.update(zip(names, rest))
    gather = Gather(ins, full, cells_in, cells_out, cot_in, to["cot"], sems)
    which = {}
    for item, entry in enumerate(FUSED_ITEMS):
        which[entry[0]] = item
    queue = [list(group) for group in FUSED_SCHEDULE]

    def tick():
        for entry in queue.pop(0):
            gather.task(*entry)

    def save(name):
        return pltpu.make_async_copy(own[name], to[name], own["out_sem"].at[held.index(name)])

    loads = {}

    def load(array, name):
        gather.full(which[array])
        loads[name] = pltpu.make_async_copy(full[array], own[name], own["load_sem"].at[len(loads)])
        loads[name].start()

    gather.meet()
    gather.cells_start()
    tick()

    core, place = gather.core, gather.place
    tokens, width = own["stream"].shape
    half_bytes = 2 * tokens
    span = own["one_hot"].shape[1]
    wide = span + 2 * LEFT
    gather.cells_wait()
    cell_copy = pltpu.make_async_copy(cells_out, own["cells"], own["load_sem"].at[6])
    cell_copy.start()
    load(7, "table")
    load(8, "blocks")
    cell_copy.wait()
    ids_pad, marks_pad = own["ids_pad"], own["marks_pad"]
    ids_pad[:, 0 : 2 * LEFT] = jnp.full((8, 2 * LEFT), -1, jnp.int32)
    marks_pad[:, 0 : 2 * LEFT] = jnp.zeros((8, 2 * LEFT), jnp.int32)
    end = 2 * LEFT + 2 * half_bytes
    ids_pad[:, end : end + 2 * LEFT] = jnp.full((8, 2 * LEFT), -1, jnp.int32)
    marks_pad[:, end : end + 2 * LEFT] = jnp.zeros((8, 2 * LEFT), jnp.int32)
    parts, per_part = own["cells"].shape[0], own["cells"].shape[1] // 2
    for q in range(parts):
        for r in range(per_part):
            at = slice(2 * LEFT + (q * per_part + r) * 128, 2 * LEFT + (q * per_part + r + 1) * 128)
            ids_pad[:, at] = jnp.broadcast_to(own["cells"][q, r : r + 1], (8, 128))
            marks_pad[:, at] = jnp.broadcast_to(own["cells"][q, per_part + r : per_part + r + 1], (8, 128))
    loads["blocks"].wait()
    total = gather.lines * 4 * gather.count
    chan = width // total
    lane = lax.broadcasted_iota(jnp.int32, (8, 128), 1)
    columns = [jnp.zeros((8, 128), jnp.float32) for _ in range(width // 128)]
    for o in range(total):
        piece = jnp.where(lane < chan, own["blocks"][8 * o : 8 * o + 8], 0.0)
        at, by = divmod(o * chan, 128)
        turned = piece if by == 0 else pltpu.roll(piece, by, 1)
        columns[at] = columns[at] + jnp.where(lane >= by, turned, 0.0)
        if by + chan > 128:
            columns[at + 1] = columns[at + 1] + jnp.where(lane < by, turned, 0.0)
    own["small"][...] = jnp.concatenate(columns, axis=1)
    save("small").start()
    loads["table"].wait()
    tok_forward_body(own, core, tokens, tick)
    for name in ("stream", "normed", "coef", "tap", "rows", "idm", "marks"):
        save(name).start()

    swap = remote(own["normed"], own["other"], own["swap_send"], own["swap_recv"], gather.twin, place)
    swap.start()
    tick()
    load(0, "wq")
    load(1, "wk")
    load(2, "wv")

    def project(rows, weight):
        return mm(rows[...], weight[...]).astype(jnp.bfloat16)

    loads["wq"].wait()
    own["qt"][...] = (project(own["normed"], own["wq"]) * HEAD_DIM ** (-0.5)).astype(jnp.bfloat16).T
    save("qt").start()
    tick()
    loads["wk"].wait()
    own["kt"][:, 0:tokens] = project(own["normed"], own["wk"]).T
    tick()
    loads["wv"].wait()
    own["vt"][:, 0:tokens] = project(own["normed"], own["wv"]).T
    tick()
    swap.wait_recv()
    own["kt"][:, tokens:] = project(own["other"], own["wk"]).T
    tick()
    own["vt"][:, tokens:] = project(own["other"], own["wv"]).T
    save("kt").start()
    save("vt").start()
    tick()
    load(3, "wo")
    fill_bias(own["bias"], own["marks"], own["marks"].at[:, 0:tokens])
    pairs = width // 128
    ticks = [queue.pop(0) for _ in range(pairs)]

    def pair_step(i, carry):
        at = pl.ds(pl.multiple_of(128 * i, 128), 128)
        attend_forward_pair(
            own["qt"].at[at],
            own["kt"].at[at],
            own["vt"].at[at],
            own["bias"],
            own["scores"],
            own["out"].at[at],
            own["lse"].at[i],
        )
        for k, group in enumerate(ticks):
            if group:

                @pl.when(i == k)
                def _():
                    for entry in group:
                        gather.task(*entry)

        return carry

    lax.fori_loop(0, pairs, pair_step, 0)
    save("out").start()
    save("lse").start()
    loads["wo"].wait()
    resid = own["stream"][...] + mm(own["out"][...].T, own["wo"][...])
    own["resid"][...] = resid
    save("resid").start()
    scale = lax.rsqrt(jnp.mean(resid * resid, axis=-1, keepdims=True) + 1e-06)
    own["normed_two"][...] = (resid * scale * own["small"][KW + 2 : KW + 3]).astype(jnp.bfloat16)
    save("normed_two").start()
    while queue:
        tick()
    gather.finish([which[a] for a in (0, 1, 2, 3, 7, 8)])
    for name in held:
        save(name).wait()
    swap.wait_send()


def forward_all(shards, cells, cot, tokens):
    count = lax.axis_size("seq")
    group_count = lax.axis_size(ALL)
    groups = group_count // (2 * count)
    items = len(FUSED_ITEMS)
    seqs = cells.shape[0]
    width = shards[0].shape[1]
    span = 2 * tokens + 2 * LEFT
    half, single = jnp.bfloat16, jnp.float32
    vmem = pl.BlockSpec(memory_space=pltpu.VMEM)
    hbm = pl.BlockSpec(memory_space=pltpu.HBM)
    pairs = width // 128
    held = {
        "stream": ((tokens, width), single),
        "normed": ((tokens, width), half),
        "coef": ((KW * VOCAB, tokens), half),
        "tap": ((KW * VOCAB, width), half),
        "rows": ((16, (span + 2 * LEFT) // 2), single),
        "idm": ((8, span), jnp.int32),
        "qt": ((width, tokens), half),
        "kt": ((width, 2 * tokens), half),
        "vt": ((width, 2 * tokens), half),
        "out": ((width, tokens), half),
        "lse": ((pairs, 2, tokens), single),
        "marks": ((1, 2 * tokens), jnp.int32),
        "small": ((8, width), single),
        "resid": ((tokens, width), single),
        "normed_two": ((tokens, width), half),
    }
    shapes = [jax.ShapeDtypeStruct((s.shape[0] * group_count, s.shape[1]), s.dtype) for s in shards]
    shapes.append(jax.ShapeDtypeStruct((count,) + cells.shape[1:], cells.dtype))
    shapes.append(jax.ShapeDtypeStruct(cot.shape, cot.dtype))
    shapes += [jax.ShapeDtypeStruct(*held[name]) for name in FRONT_OUTS[1:]]
    dma = pltpu.SemaphoreType.DMA
    scratch = [
        dma((items, groups * count)),
        dma((items, groups)),
        dma((items, count, 2)),
        dma((items,)),
        dma((items,)),
        dma((items,)),
        dma((items,)),
        dma((count,)),
        dma((seqs, 2)),
        dma((seqs,)),
        dma((seqs,)),
    ]
    scratch += [pltpu.VMEM(*held[name]) for name in FRONT_OUTS[1:]]
    scratch += [
        pltpu.VMEM((count,) + cells.shape[1:], cells.dtype),
        pltpu.VMEM((8, 4 * tokens + 4 * LEFT), jnp.int32),
        pltpu.VMEM((8, 4 * tokens + 4 * LEFT), jnp.int32),
        pltpu.VMEM((VOCAB, width), half),
        pltpu.VMEM((8 * group_count, 128), single),
        pltpu.VMEM((width, width), half),
        pltpu.VMEM((width, width), half),
        pltpu.VMEM((width, width), half),
        pltpu.VMEM((width, width), half),
        pltpu.VMEM((tokens, width), half),
        pltpu.VMEM((KW * VOCAB, span), half),
        pltpu.VMEM((2 * tokens, tokens), single),
        pltpu.VMEM((2, 2 * tokens, tokens), single),
        dma((len(FRONT_OUTS) - 1,)),
        dma((8,)),
        dma,
        dma,
    ]
    out = pl.pallas_call(
        forward_kernel,
        name="forward_all",
        out_shape=shapes,
        in_specs=[vmem] * (len(shards) + 2),
        out_specs=[hbm] * len(shapes),
        scratch_shapes=scratch,
        compiler_params=pltpu.CompilerParams(
            collective_id=0, has_side_effects=True, vmem_limit_bytes=60 * 1024 * 1024
        ),
    )(*shards, cells, cot)
    return list(out[:9]), dict(zip(FRONT_OUTS, out[10:]))


def per_device(
    byte_ids,
    segments,
    embed_table,
    conv_weight,
    score_vector,
    first_gain,
    w_query,
    w_key,
    w_value,
    w_output,
    second_gain,
    w_gate,
    w_up,
    w_down,
    out_grad,
):
    seqs, part_bytes = byte_ids.shape
    count = lax.axis_size("seq")
    seq_len = part_bytes * count
    width = w_query.shape[1]
    wide = w_gate.shape[1]
    half_bytes = seq_len // 2
    half = half_bytes // 2
    core = lax.axis_index("dp") % 2
    place = lax.axis_index("seq")

    chan = conv_weight.shape[0]
    small = jnp.concatenate(
        [conv_weight.T, score_vector[None], first_gain[None], second_gain[None]], axis=0
    ).astype(jnp.float32)
    small = jnp.pad(small, ((0, 0), (0, 128 - chan)))
    cells = jnp.stack([byte_ids, segments + 1], axis=1).reshape(seqs, -1, 128)
    shards = (w_query, w_key, w_value, w_output, w_gate, w_up, w_down, embed_table, small)
    if all(shard.shape[0] % 8 == 0 for shard in shards):
        full, held = forward_all(shards, cells, out_grad, half)
        wq, wk, wv, wo, wg, wu, wd, table, _ = full
        cot = held["cot"].reshape(half, width)
        small_full, stream, normed_one, resid_one = held["small"], held["stream"], held["normed"], held["resid"]
        coef, tap_table, rows, idm = held["coef"], held["tap"], held["rows"], held["idm"]
        queries, keys, vals, attn_out, lse = held["qt"], held["kt"], held["vt"], held["out"], held["lse"]
        key_marks = held["marks"][0]
        query_marks = key_marks[:half]
        gain_two = small_full[KW + 2 : KW + 3]
        normed_two = held["normed_two"]
    else:
        wq, wk, wv, wo, wg, wu, wd, table, small_full, cells, cot = gather_all(shards, cells, out_grad)
        cells = cells.reshape(count, 2, part_bytes).transpose(1, 0, 2).reshape(2, seq_len)
        ids_row, marks_row = cells[0], cells[1]
        cot = cot.reshape(half, width)
        small_full = small_full.reshape(lax.axis_size(ALL), 8, 128)[:, :, :chan].transpose(1, 0, 2).reshape(8, width)
        gain_two = small_full[KW + 2 : KW + 3]

        stream, normed_one, coef, tap_table, rows, idm = tok_forward(ids_row, marks_row, table, small_full, half)

        twins = [(i, i ^ 1) for i in range(lax.axis_size("dp"))]
        normed_other = lax.ppermute(normed_one, "dp", twins)
        token_marks = marks_row[::2]
        query_marks = lax.dynamic_slice_in_dim(token_marks, core * half, half, axis=0)
        other_marks = lax.dynamic_slice_in_dim(token_marks, (1 - core) * half, half, axis=0)
        key_marks = jnp.concatenate([query_marks, other_marks])
        queries = (mm_tt(wq, normed_one).astype(jnp.bfloat16) * HEAD_DIM ** (-0.5)).astype(jnp.bfloat16)
        normed_keys = jnp.concatenate([normed_one, normed_other], axis=0)
        keys = mm_tt(wk, normed_keys).astype(jnp.bfloat16)
        vals = mm_tt(wv, normed_keys).astype(jnp.bfloat16)
        attn_out, lse = attend_forward(queries, keys, vals, key_marks, query_marks)

        resid_one = stream + mm_tn(attn_out, wo)
        normed_two = rms_scale(resid_one, gain_two).astype(jnp.bfloat16)
    norm_pull_two = jax.vjp(rms_scale, resid_one, gain_two)[1]
    gate_pre = mm(normed_two, wg)
    up_pre = mm(normed_two, wu)
    gate_act, gelu_pull = jax.vjp(gelu_tanh, gate_pre)
    hidden = (gate_act * up_pre).astype(jnp.bfloat16)
    layer_rows = (resid_one + mm(hidden, wd)).astype(jnp.bfloat16)
    layer_rows = layer_rows.reshape(seqs, part_bytes // 2, width)

    hidden_grad = mm_nt(cot, wd)
    grad_down = mm_tn(hidden, cot)
    up_grad = (hidden_grad * gate_act).astype(jnp.bfloat16)
    gate_grad = gelu_pull(hidden_grad * up_pre)[0].astype(jnp.bfloat16)
    grad_gate = mm_tn(normed_two, gate_grad)
    grad_up = mm_tn(normed_two, up_grad)
    normed_two_grad = mm_nt(gate_grad, wg) + mm_nt(up_grad, wu)
    resid_part, gain_two_grad = norm_pull_two(normed_two_grad)
    resid_grad = cot.astype(jnp.float32) + resid_part
    proj_grad = resid_grad.astype(jnp.bfloat16)
    grad_output = mm(attn_out, proj_grad)
    attn_grad = mm_nt(wo, proj_grad).astype(jnp.bfloat16)

    shapes = [(w.shape[0], w.shape[1], jnp.bfloat16) for w in shards[:8]] + [small.shape + (jnp.float32,)]
    out = backward_all(
        {
            "gate": grad_gate.astype(jnp.bfloat16),
            "up": grad_up.astype(jnp.bfloat16),
            "down": grad_down.astype(jnp.bfloat16),
            "output": grad_output.astype(jnp.bfloat16),
            "qt": queries,
            "kt": keys,
            "vt": vals,
            "got": attn_grad,
            "out": attn_out,
            "lse": lse,
            "key_marks": key_marks[None],
            "query_marks": query_marks[None],
            "normed": normed_one,
            "stream": stream,
            "resid": resid_grad,
            "wq": wq,
            "wk": wk,
            "wv": wv,
            "small": small_full,
            "gain_two": gain_two_grad,
            "table": table,
            "coef": coef,
            "tap": tap_table,
            "rows": rows,
            "idm": idm,
            "layer": layer_rows,
        },
        shapes,
    )
    small_out = out[8][:, :chan]
    return (
        out[9],
        out[7],
        small_out[:KW].T,
        small_out[KW],
        small_out[KW + 1],
        out[0],
        out[1],
        out[2],
        out[3],
        small_out[KW + 2],
        out[4],
        out[5],
        out[6],
    )


def solution(mesh):
    flat = P(ALL)
    rows = P(ALL, None)
    in_specs = (
        P("dp", "seq"),
        P("dp", "seq"),
        rows,
        rows,
        flat,
        flat,
        rows,
        rows,
        rows,
        rows,
        flat,
        rows,
        rows,
        rows,
        P("dp", "seq", None),
    )
    out_specs = (
        P("dp", "seq", None),
        rows,
        rows,
        flat,
        flat,
        rows,
        rows,
        rows,
        rows,
        flat,
        rows,
        rows,
        rows,
    )
    return jax.shard_map(
        per_device, mesh=mesh, in_specs=in_specs, out_specs=out_specs, check_vma=False
    )
```

```python
import functools
from typing import NamedTuple

import jax
import jax.numpy as jnp
from jax import lax
from jax.experimental import pallas as pl
from jax.experimental.pallas import tpu as pltpu
from jax.sharding import PartitionSpec as P

HEADS = 12
HEAD_DIM = 64
VOCAB = 256
MAXBLOCK = 4
KW = 5
DOCS = 8
ALL = ("dp", "seq")
VMEM_BYTES = 56 * 1024 * 1024


def mm(left, right):
    return jnp.dot(left, right, preferred_element_type=jnp.float32)


def mm_nt(left, right):
    return lax.dot_general(left, right, (((1,), (1,)), ((), ())), preferred_element_type=jnp.float32)


def mm_tn(left, right):
    return lax.dot_general(left, right, (((0,), (0,)), ((), ())), preferred_element_type=jnp.float32)


def mm_tt(left, right):
    return lax.dot_general(left, right, (((0,), (1,)), ((), ())), preferred_element_type=jnp.float32)


def rms_scale(values, gain):
    return values * lax.rsqrt(jnp.mean(values * values, axis=-1, keepdims=True) + 1e-06) * gain


def gelu_tanh(values):
    return jax.nn.gelu(values, approximate=True)


MESH = pl.DeviceIdType.MESH


def position():
    dp = lax.axis_index("dp")
    place = lax.axis_index("seq")
    lines = lax.axis_size("dp") // 4
    group = dp // 2
    return group // 2, group % 2, dp % 2, place, lines, lax.axis_size("seq")


def dp_of(y, x, core):
    return (y * 2 + x) * 2 + core


def meet(targets):
    barrier = pltpu.get_barrier_semaphore()
    for dp, place in targets:
        pl.semaphore_signal(barrier, inc=1, device_id=(dp, place), device_id_type=MESH)
    pl.semaphore_wait(barrier, len(targets))


def remote(src, dst, send_sem, recv_sem, dp, place):
    return pltpu.make_async_remote_copy(
        src_ref=src,
        dst_ref=dst,
        send_sem=send_sem,
        recv_sem=recv_sem,
        device_id=(dp, place),
        device_id_type=MESH,
    )


GATHER_ITEMS = (
    (7, 0, 0, 0),
    (8, 0, 0, 0),
    (0, 0, 0, 0),
    (2, 0, 0, 1),
    (1, 0, 0, 0),
    (3, 0, 0, 1),
    (4, 0, 0, 0),
    (5, 0, 0, 1),
    (6, 0, 1, 0),
    (6, 1, 1, 1),
)
GATHER_PHASES = ((0, 1), (2, 3, 4, 5), (6, 7), (8, 9))


def gather_kernel(arrays, *refs):
    ins = refs[:arrays]
    cells_in, cot_in = refs[arrays], refs[arrays + 1]
    outs = refs[arrays + 2 : 2 * arrays + 2]
    cells_out, cot_out = refs[2 * arrays + 2], refs[2 * arrays + 3]
    recv, recv_sib, send_z, send_x, send_y, send_sib, own_sem, cell_recv, cell_send, cot_recv, cot_send = refs[
        2 * arrays + 4 :
    ]
    y, x, core, place, lines, count = position()
    seqs = cells_in.shape[0]
    groups = lines * 2
    group = y * 2 + x
    dp = dp_of(y, x, core)
    twin = dp_of(y, x, 1 - core)
    side = dp_of(y, 1 - x, core)
    ahead = [(y + k) % lines for k in range(1, lines)]

    targets = [(twin, place), (side, place)]
    for k in range(1, count):
        targets += [(dp, (place + k) % count), (twin, (place + k) % count)]
    for other_y in ahead:
        targets.append((dp_of(other_y, x, core), place))
    meet(targets)

    def cell_copies(fn_remote, fn_local):
        for r in range(seqs):
            chip = seqs * core + r
            for c in range(2):
                home = (chip == place) & (core == c)

                @pl.when(home)
                def _():
                    fn_local(r, c)

                @pl.when(jnp.logical_not(home))
                def _():
                    fn_remote(r, c, chip)

    def cell_remote(r, c, chip):
        return remote(
            cells_in.at[r],
            cells_out.at[place],
            cell_send.at[r, c],
            cell_recv.at[place],
            dp_of(y, x, c),
            chip,
        )

    cell_copies(
        lambda r, c, chip: cell_remote(r, c, chip).start(),
        lambda r, c: pltpu.make_async_copy(
            cells_in.at[r], cells_out.at[place], cell_recv.at[place]
        ).start(),
    )

    def view(item):
        array, first, columns, _ = GATHER_ITEMS[item]
        in_ref, out_ref = ins[array], outs[array]
        if columns:
            cols = in_ref.shape[1] // 2
            lanes = pl.ds(first * cols, cols)
        else:
            lanes = pl.ds(0, in_ref.shape[1])
        return in_ref.at[:, lanes], out_ref, lanes

    def block(item, g, z):
        _, out_ref, lanes = view(item)
        return out_ref.at[(g * 2 + core) * count + z, :, lanes]

    def group_block(item, g, c):
        _, out_ref, lanes = view(item)
        return out_ref.at[pl.ds((g * 2 + c) * count, count), :, lanes]

    def many(item, blocks):
        _, out_ref, lanes = view(item)
        return out_ref.at[pl.ds(0, blocks), :, lanes]

    def arrived(item, g, z):
        dst = block(item, g, z)
        remote(dst, dst, send_x.at[item], recv.at[item, g * count + z], twin, place).wait_recv()

    def to_side(item, src, g, z):
        remote(src, block(item, g, z), send_x.at[item], recv.at[item, g * count + z], side, place).start()

    def to_lines(item, src, g, z):
        for other_y in ahead:
            remote(
                src,
                block(item, g, z),
                send_y.at[item],
                recv.at[item, g * count + z],
                dp_of(other_y, x, core),
                place,
            ).start()

    def to_z(item, src, z, step):
        return remote(
            src,
            block(item, group, z),
            send_z.at[item, z, step],
            recv.at[item, group * count + z],
            dp,
            place + 1 - 2 * step,
        )

    def to_twin(item, g):
        src = group_block(item, g, core)
        remote(src, src, send_sib.at[item], recv_sib.at[item, g], twin, place).start()

    def own_copy(item):
        return pltpu.make_async_copy(view(item)[0], block(item, group, place), own_sem.at[item])

    def first_own(items):
        for item in items:
            src = view(item)[0]

            @pl.when(place < count - 1)
            def _():
                to_z(item, src, place, 0).start()

            @pl.when(place > 0)
            def _():
                to_z(item, src, place, 1).start()

            own_copy(item).start()

    def first_sides(items):
        for item in items:
            src = view(item)[0]
            to_side(item, src, group, place)
            to_lines(item, src, group, place)

    def first_level(items):
        def step(s, carry):
            low = place - s
            high = place + s
            for item in items:

                @pl.when(low >= 0)
                def _():
                    arrived(item, group, low)
                    src = block(item, group, low)

                    @pl.when(place < count - 1)
                    def _():
                        to_z(item, src, low, 0).start()

                    to_side(item, src, group, low)
                    to_lines(item, src, group, low)

                @pl.when(high < count)
                def _():
                    arrived(item, group, high)
                    src = block(item, group, high)

                    @pl.when(place > 0)
                    def _():
                        to_z(item, src, high, 1).start()

                    to_side(item, src, group, high)
                    to_lines(item, src, group, high)

            return carry

        lax.fori_loop(1, count, step, 0)
        for item in items:
            own_copy(item).wait()
            to_twin(item, group)

    def second_level(items):
        def step(s, carry):
            z = (place + s) % count
            for item in items:
                if GATHER_ITEMS[item][3] == 0:
                    g = y * 2 + (1 - x)
                    arrived(item, g, z)
                    to_lines(item, block(item, g, z), g, z)
                else:
                    for other_y in ahead:
                        g = other_y * 2 + x
                        arrived(item, g, z)
                        to_side(item, block(item, g, z), g, z)
            return carry

        lax.fori_loop(0, count, step, 0)
        for item in items:
            if GATHER_ITEMS[item][3] == 0:
                to_twin(item, y * 2 + (1 - x))
            else:
                for other_y in ahead:
                    to_twin(item, other_y * 2 + x)

    def third_level(items):
        def rest(item):
            if GATHER_ITEMS[item][3] == 0:
                return [other_y * 2 + other_x for other_y in ahead for other_x in (x, 1 - x)]
            return [other_y * 2 + (1 - x) for other_y in [y] + ahead]

        def step(s, carry):
            z = (place + s) % count
            for item in items:
                for g in rest(item):
                    arrived(item, g, z)
            return carry

        lax.fori_loop(0, count, step, 0)
        for item in items:
            for g in rest(item):
                to_twin(item, g)

    def cot_copies(fn_remote, fn_local):
        for r in range(seqs):
            chip = seqs * core + r
            home = (chip == place) & (core == place // seqs)

            @pl.when(home)
            def _():
                fn_local(r)

            @pl.when(jnp.logical_not(home))
            def _():
                fn_remote(r, chip)

    def cot_remote(r, chip):
        return remote(
            cot_in.at[r],
            cot_out.at[place % seqs],
            cot_send.at[r],
            cot_recv.at[place % seqs],
            dp_of(y, x, place // seqs),
            chip,
        )

    phases = GATHER_PHASES
    for items in phases:
        first_own(items)
    first_sides(phases[0])
    first_level(phases[0])
    for k in range(1, len(phases)):
        first_sides(phases[k])
        first_level(phases[k])
        second_level(phases[k - 1])
        if k == 1:
            cot_copies(
                lambda r, chip: cot_remote(r, chip).start(),
                lambda r: pltpu.make_async_copy(
                    cot_in.at[r], cot_out.at[place % seqs], cot_recv.at[place % seqs]
                ).start(),
            )
        if k > 1:
            third_level(phases[k - 2])
    second_level(phases[-1])
    third_level(phases[-2])
    third_level(phases[-1])

    for item in range(len(GATHER_ITEMS)):
        for g in range(groups):
            dst = group_block(item, g, 1 - core)
            remote(dst, dst, send_sib.at[item], recv_sib.at[item, g], twin, place).wait_recv()
        tree = GATHER_ITEMS[item][3]

        def sent(blocks, sem):
            src = many(item, blocks)
            remote(src, src, sem, recv.at[item, 0], twin, place).wait_send()

        sent(count * (1 if tree == 0 else lines), send_x.at[item])
        sent(count * (lines - 1) * (2 if tree == 0 else 1), send_y.at[item])
        sent(count * groups, send_sib.at[item])

        def drain(z, carry):
            @pl.when((z <= place) & (place < count - 1))
            def _():
                to_z(item, block(item, group, z), z, 0).wait_send()

            @pl.when((z >= place) & (place > 0))
            def _():
                to_z(item, block(item, group, z), z, 1).wait_send()

            return carry

        lax.fori_loop(0, count, drain, 0)
    for q in range(count):
        dst = cells_out.at[q]
        remote(dst, dst, cell_send.at[0, 0], cell_recv.at[q], twin, place).wait_recv()
    for q in range(seqs):
        dst = cot_out.at[q]
        remote(dst, dst, cot_send.at[0], cot_recv.at[q], twin, place).wait_recv()
    cell_copies(lambda r, c, chip: cell_remote(r, c, chip).wait_send(), lambda r, c: None)
    cot_copies(lambda r, chip: cot_remote(r, chip).wait_send(), lambda r: None)


def gather_all(shards, cells, cot):
    count = lax.axis_size("seq")
    group_count = lax.axis_size(ALL)
    groups = group_count // (2 * count)
    items = len(GATHER_ITEMS)
    seqs = cells.shape[0]
    vmem = pl.BlockSpec(memory_space=pltpu.VMEM)
    hbm = pl.BlockSpec(memory_space=pltpu.HBM)
    shapes = [jax.ShapeDtypeStruct((group_count,) + s.shape, s.dtype) for s in shards]
    shapes.append(jax.ShapeDtypeStruct((count,) + cells.shape[1:], cells.dtype))
    shapes.append(jax.ShapeDtypeStruct(cot.shape, cot.dtype))
    dma = pltpu.SemaphoreType.DMA
    out = pl.pallas_call(
        functools.partial(gather_kernel, len(shards)),
        name="gather_all",
        out_shape=shapes,
        in_specs=[vmem] * (len(shards) + 2),
        out_specs=[hbm] * len(shapes),
        scratch_shapes=[
            dma((items, groups * count)),
            dma((items, groups)),
            dma((items, count, 2)),
            dma((items,)),
            dma((items,)),
            dma((items,)),
            dma((items,)),
            dma((count,)),
            dma((seqs, 2)),
            dma((seqs,)),
            dma((seqs,)),
        ],
        compiler_params=pltpu.CompilerParams(collective_id=0, has_side_effects=True),
    )(*shards, cells, cot)
    full = [o.reshape(-1, o.shape[2]) for o in out[: len(shards)]]
    return full + list(out[len(shards) :])


LEFT = 128
BAND = 256


def split_two(values):
    high = values.astype(jnp.bfloat16)
    return high, (values - high.astype(jnp.float32)).astype(jnp.bfloat16)


def lane_shift(row, by):
    by = by % row.shape[1]
    return row if by == 0 else pltpu.roll(row, row.shape[1] - by, 1)


def pool_rows(marks, core, half_bytes):
    lanes = lax.broadcasted_iota(jnp.int32, marks[0].shape, 1)
    inside, inverse = {}, {}
    for e in range(2):
        place = core * half_bytes + 2 * (lanes - LEFT) + e + 768
        third = lax.shift_right_logical(place * 21846, 16)
        remains = {2: place & 1, 3: place - 3 * third, 4: place & 3}
        shifted = {}
        for s in range(1 - MAXBLOCK, MAXBLOCK):
            f = (e + s) % 2
            shifted[s] = lane_shift(marks[f], (e + s - f) // 2) == marks[e]
        for b in range(2, MAXBLOCK + 1):
            number = jnp.ones(marks[0].shape, jnp.float32)
            for s in range(1 - b, b):
                if s == 0:
                    continue
                at = remains[b] + s
                on = (shifted[s] & (at >= 0) & (at < b)).astype(jnp.float32)
                inside[b, e, s] = on
                number = number + on
            inverse[b, e] = 1.0 / number
    return inside, inverse


def band_coefs(per_byte, inside, inverse):
    coefs = {}
    for o in range(1 - MAXBLOCK, MAXBLOCK + 1):
        total = None
        for e in range(2):
            s = o - e
            if not 1 - MAXBLOCK <= s < MAXBLOCK:
                continue
            for b in range(1, MAXBLOCK + 1):
                if b == 1:
                    if s != 0:
                        continue
                    term = per_byte[b, e]
                elif s == 0:
                    term = per_byte[b, e] * inverse[b, e]
                elif (b, e, s) in inside:
                    term = per_byte[b, e] * inverse[b, e] * inside[b, e, s]
                else:
                    continue
                total = term if total is None else total + term
        coefs[o] = total
    return coefs


def band_matrix(coefs, block):
    shape = (3 * BAND, BAND)
    delta = lax.broadcasted_iota(jnp.int32, shape, 0) - LEFT - 2 * lax.broadcasted_iota(jnp.int32, shape, 1)
    out = jnp.zeros(shape, jnp.float32)
    for o, row in coefs.items():
        part = row[0:1, LEFT + BAND * block : LEFT + BAND * (block + 1)]
        out = jnp.where(delta == o, part, out)
    return out


def fill_one_hot(one_hot, idm_of_tap):
    span = one_hot.shape[1]
    vocab = lax.broadcasted_iota(jnp.int32, (VOCAB, span), 0)
    for tap in range(KW):
        hit = vocab == idm_of_tap(tap)
        one_hot[tap * VOCAB : (tap + 1) * VOCAB] = hit.astype(jnp.float32).astype(jnp.bfloat16)


def tok_forward_kernel(ids_ref, marks_ref, table_ref, small_ref, stream_ref, normed_ref, coef_ref, tap_ref, rows_ref, idm_ref, one_hot):
    core = lax.axis_index("dp") % 2
    tokens = stream_ref.shape[0]
    half_bytes = 2 * tokens
    span = one_hot.shape[1]
    wide = span + 2 * LEFT
    first = pl.ds(pl.multiple_of(core * half_bytes, 128), wide)
    ids = ids_ref[:, first]
    marks = marks_ref[:, first]
    for tap in range(KW):
        by = tap - KW // 2
        same = (lane_shift(marks, by) == marks) & (marks > 0)
        idm_ref[tap : tap + 1] = jnp.where(same, lane_shift(ids, by), -1)[0:1, LEFT : LEFT + span]
    fill_one_hot(one_hot, lambda tap: idm_ref[tap : tap + 1])

    score = jnp.broadcast_to(small_ref[KW : KW + 1], (8, small_ref.shape[1])).astype(jnp.bfloat16)
    scored = []
    for tap in range(KW):
        product = table_ref[...].astype(jnp.float32) * small_ref[tap : tap + 1]
        high, low = split_two(product)
        tap_ref[tap * VOCAB : (tap + 1) * VOCAB] = high
        scored.append(mm_nt(score, high) + mm_nt(score, low))
    high, low = split_two(jnp.concatenate(scored, axis=1))
    u_row = mm(high, one_hot[...]) + mm(low, one_hot[...])

    high = u_row.astype(jnp.bfloat16).astype(jnp.float32)
    marks_here = marks[:, LEFT : LEFT + span].astype(jnp.float32)
    packed = jnp.concatenate([marks_here, high, u_row - high, jnp.zeros_like(high)], axis=0).astype(jnp.bfloat16)
    shape = (span, wide // 2)
    twice = 2 * lax.broadcasted_iota(jnp.int32, shape, 1) - lax.broadcasted_iota(jnp.int32, shape, 0) - LEFT
    marks_of, u_of = [], []
    for e in range(2):
        pick = (twice == -e).astype(jnp.float32).astype(jnp.bfloat16)
        apart = mm(packed, pick)
        marks_of.append(apart[0:8])
        u_of.append(apart[8:16] + apart[16:24])

    inside, inverse = pool_rows(marks_of, core, half_bytes)
    prob = {}
    for e in range(2):
        shifted = {}
        for s in range(1 - MAXBLOCK, MAXBLOCK):
            f = (e + s) % 2
            shifted[s] = lane_shift(u_of[f], (e + s - f) // 2)
        scores = [u_of[e]]
        for b in range(2, MAXBLOCK + 1):
            total = u_of[e]
            for s in range(1 - b, b):
                if s != 0:
                    total = total + inside[b, e, s] * shifted[s]
            scores.append(total * inverse[b, e])
        top = scores[0]
        for value in scores[1:]:
            top = jnp.maximum(top, value)
        expo = [jnp.exp(value - top) for value in scores]
        whole = expo[0] + expo[1] + expo[2] + expo[3]
        for b in range(1, MAXBLOCK + 1):
            prob[b, e] = expo[b - 1] / whole
            rows_ref[2 * b + e : 2 * b + e + 1] = prob[b, e][0:1]
        rows_ref[e : e + 1] = marks_of[e][0:1]
    coefs = band_coefs({key: 0.5 * value for key, value in prob.items()}, inside, inverse)
    gain = small_ref[KW + 1 : KW + 2]
    for i in range(tokens // BAND):
        matrix = band_matrix(coefs, i).astype(jnp.bfloat16)
        lanes = slice(i * BAND, (i + 1) * BAND)
        part = mm(one_hot[:, 2 * i * BAND : (2 * i + 3) * BAND], matrix).astype(jnp.bfloat16)
        coef_ref[:, lanes] = part
        stream = mm_tn(part, tap_ref[...])
        stream_ref[lanes] = stream
        scale = lax.rsqrt(jnp.mean(stream * stream, axis=-1, keepdims=True) + 1e-06)
        normed_ref[lanes] = (stream * scale * gain).astype(jnp.bfloat16)


def tok_forward(ids_row, marks_row, table, small, tokens):
    width = table.shape[1]
    span = 2 * tokens + 2 * LEFT
    wide = span + 2 * LEFT

    def padded(row, fill):
        row = jnp.pad(row, (2 * LEFT, 2 * LEFT), constant_values=fill)
        return jnp.broadcast_to(row[None], (8, row.shape[0]))

    return pl.pallas_call(
        tok_forward_kernel,
        name="tok_forward",
        out_shape=[
            jax.ShapeDtypeStruct((tokens, width), jnp.float32),
            jax.ShapeDtypeStruct((tokens, width), jnp.bfloat16),
            jax.ShapeDtypeStruct((KW * VOCAB, tokens), jnp.bfloat16),
            jax.ShapeDtypeStruct((KW * VOCAB, width), jnp.bfloat16),
            jax.ShapeDtypeStruct((16, wide // 2), jnp.float32),
            jax.ShapeDtypeStruct((8, span), jnp.int32),
        ],
        scratch_shapes=[pltpu.VMEM((KW * VOCAB, span), jnp.bfloat16)],
        compiler_params=pltpu.CompilerParams(vmem_limit_bytes=VMEM_BYTES),
    )(padded(ids_row, -1), padded(marks_row, 0), table, small)


def tok_backward_body(grad16, coef_ref, tap_ref, rows_ref, idm_ref, table_ref, small_ref, one_hot, tick):
    core = lax.axis_index("dp") % 2
    tokens = grad16.shape[0]
    fill_one_hot(one_hot, lambda tap: idm_ref[tap : tap + 1])
    tick()

    def whole_row(k):
        return jnp.broadcast_to(rows_ref[k : k + 1], (8, rows_ref.shape[1]))

    marks_of = [whole_row(0), whole_row(1)]
    inside, inverse = pool_rows(marks_of, core, 2 * tokens)
    shape = (3 * BAND, BAND)
    delta = lax.broadcasted_iota(jnp.int32, shape, 0) - LEFT - 2 * lax.broadcasted_iota(jnp.int32, shape, 1)
    through = mm_nt(tap_ref[...], grad16).astype(jnp.bfloat16)
    tick()
    diag = {o: [] for o in range(1 - MAXBLOCK, MAXBLOCK + 1)}
    edge = jnp.zeros((8, LEFT), jnp.float32)
    for i in range(tokens // BAND):
        near = mm_tn(one_hot[:, 2 * i * BAND : (2 * i + 3) * BAND], through[:, i * BAND : (i + 1) * BAND])
        for o in diag:
            total = jnp.sum(jnp.where(delta == o, near, 0.0), axis=0, keepdims=True)
            diag[o].append(jnp.broadcast_to(total, (8, BAND)))
        tick()
    diag = {o: jnp.concatenate([edge] + parts + [edge], axis=1) for o, parts in diag.items()}
    size_grad = {}
    for e in range(2):
        grads = [0.5 * diag[e]]
        for b in range(2, MAXBLOCK + 1):
            total = diag[e]
            for s in range(1 - b, b):
                if s != 0:
                    total = total + inside[b, e, s] * diag[s + e]
            grads.append(0.5 * total * inverse[b, e])
        probs = [whole_row(2 * b + e) for b in range(1, MAXBLOCK + 1)]
        mean = probs[0] * grads[0]
        for p, g in zip(probs[1:], grads[1:]):
            mean = mean + p * g
        for b in range(1, MAXBLOCK + 1):
            size_grad[b, e] = probs[b - 1] * (grads[b - 1] - mean)
    coefs = band_coefs(size_grad, inside, inverse)
    picked = None
    for i in range(tokens // BAND):
        matrix = band_matrix(coefs, i).astype(jnp.bfloat16)
        part = mm(one_hot[:, 2 * i * BAND : (2 * i + 3) * BAND], matrix)
        part = jnp.sum(part, axis=1, keepdims=True)
        picked = part if picked is None else picked + part
        tick()
    score = small_ref[KW : KW + 1]
    table = table_ref[...].astype(jnp.float32)
    table_grad = None
    score_grad = None
    small_rows = []
    for tap in range(KW):
        rows = slice(tap * VOCAB, (tap + 1) * VOCAB)
        here = picked[rows]
        part = mm(coef_ref[rows], grad16) + here * score
        taps = small_ref[tap : tap + 1]
        table_grad = part * taps if table_grad is None else table_grad + part * taps
        small_rows.append(jnp.sum(part * table, axis=0, keepdims=True))
        summed = jnp.sum(table * here, axis=0, keepdims=True) * taps
        score_grad = summed if score_grad is None else score_grad + summed
        if tap < KW - 1:
            tick()
    return table_grad, small_rows + [score_grad]


CHUNK = 256


def pair_rows(ref, h):
    values = ref[...]
    rows = lax.broadcasted_iota(jnp.int32, values.shape, 0)
    return jnp.where((rows // HEAD_DIM) == h, values, jnp.zeros_like(values))


def fill_bias(bias, key_marks, query_marks):
    def apart(marks):
        rows = lax.broadcasted_iota(jnp.int32, (2 * DOCS, marks.shape[1]), 0)
        return (rows == marks[...]).astype(jnp.float32).astype(jnp.bfloat16)

    queries = apart(query_marks)
    for c in range(key_marks.shape[1] // CHUNK):
        keys = slice(c * CHUNK, (c + 1) * CHUNK)
        same = mm_tn(apart(key_marks.at[:, keys]), queries)
        bias[keys] = jnp.where(same > 0.5, 0.0, -1e30).astype(bias.dtype)


def attend_forward_kernel(qt_ref, kt_ref, vt_ref, key_marks, query_marks, out_ref, lse_ref, bias, scores):
    @pl.when(pl.program_id(0) == 0)
    def _():
        fill_bias(bias, key_marks, query_marks)

    keys = kt_ref[...].T
    chunks = keys.shape[0] // CHUNK
    for h in range(2):
        query = pair_rows(qt_ref, h)
        top = None
        for c in range(chunks):
            rows = slice(c * CHUNK, (c + 1) * CHUNK)
            part = mm(keys[rows], query) + bias[rows]
            scores[h, rows] = part
            high = jnp.max(part, axis=0, keepdims=True)
            top = high if top is None else jnp.maximum(top, high)
        total = None
        out = None
        for c in range(chunks):
            rows = slice(c * CHUNK, (c + 1) * CHUNK)
            expo = jnp.exp(scores[h, rows] - top)
            part = jnp.sum(expo, axis=0, keepdims=True)
            total = part if total is None else total + part
            part = mm(vt_ref[h * HEAD_DIM : (h + 1) * HEAD_DIM, rows], expo.astype(jnp.bfloat16))
            out = part if out is None else out + part
        out_ref[h * HEAD_DIM : (h + 1) * HEAD_DIM] = (out / total).astype(jnp.bfloat16)
        lse_ref[0, h : h + 1] = top + jnp.log(total)


def attend_forward(qt, kt, vt, key_marks, query_marks):
    width, tokens = qt.shape
    keys = kt.shape[1]
    pairs = width // 128
    rows = lambda size: pl.BlockSpec((128, size), lambda i: (i, 0))
    whole = lambda shape: pl.BlockSpec(shape, lambda i: (0, 0))
    return pl.pallas_call(
        attend_forward_kernel,
        name="attend_forward",
        grid=(pairs,),
        in_specs=[rows(tokens), rows(keys), rows(keys), whole((1, keys)), whole((1, tokens))],
        out_specs=[rows(tokens), pl.BlockSpec((1, 2, tokens), lambda i: (i, 0, 0))],
        out_shape=[
            jax.ShapeDtypeStruct((width, tokens), jnp.bfloat16),
            jax.ShapeDtypeStruct((pairs, 2, tokens), jnp.float32),
        ],
        scratch_shapes=[
            pltpu.VMEM((keys, tokens), jnp.float32),
            pltpu.VMEM((2, keys, tokens), jnp.float32),
        ],
        compiler_params=pltpu.CompilerParams(vmem_limit_bytes=VMEM_BYTES),
    )(qt, kt, vt, key_marks[None], query_marks[None])


def attend_backward_pair(qt, kt, vt, got_ref, out, lse_ref, bias, dq, dk_own, dv_own, dk_away, dv_away):
    keys = kt[...].T
    vals = vt[...].T
    chunks = keys.shape[0] // CHUNK
    for h in range(2):
        own = slice(h * HEAD_DIM, (h + 1) * HEAD_DIM)
        query = pair_rows(qt, h)
        got = pair_rows(got_ref, h)
        dots = jnp.sum(
            got_ref[own].astype(jnp.float32) * out[own].astype(jnp.float32), axis=0, keepdims=True
        )
        lse = lse_ref[h : h + 1]
        query_grad = None
        for c in range(chunks):
            rows = slice(c * CHUNK, (c + 1) * CHUNK)
            soft = jnp.exp(mm(keys[rows], query) + (bias[rows].astype(jnp.float32) - lse))
            change = soft * (mm(vals[rows], got) - dots)
            soft16 = soft.astype(jnp.bfloat16)
            change16 = change.astype(jnp.bfloat16)
            first = c < chunks // 2
            to = slice((c % (chunks // 2)) * CHUNK, (c % (chunks // 2) + 1) * CHUNK)
            (dv_own if first else dv_away)[own, to] = mm_nt(got_ref[own], soft16).astype(jnp.bfloat16)
            (dk_own if first else dk_away)[own, to] = mm_nt(qt[own], change16).astype(jnp.bfloat16)
            part = mm(kt[own, rows], change16)
            query_grad = part if query_grad is None else query_grad + part
        dq[own] = (query_grad * HEAD_DIM ** (-0.5)).astype(jnp.bfloat16)


SCATTER_ITEMS = (
    (4, 0, 1, 0),
    (6, 0, 2, 1),
    (5, 1, 2, 1),
    (3, 0, 1, 1),
    (5, 0, 2, 1),
    (6, 1, 2, 0),
    (0, 0, 1, 0),
    (1, 0, 1, 1),
    (2, 0, 1, 0),
    (7, 0, 1, 0),
    (8, 0, 1, 1),
)
FIRST_ITEMS = 6
SCHEDULE = (
    (),
    ((0, 0), (0, 1), (0, 2), (0, 3), (0, 4), (0, 5)),
    (),
    ((1, 1),),
    (),
    ((1, 0), (1, 2)),
    (),
    ((1, 3), (1, 5)),
    ((0, 6), (2, 1)),
    ((0, 7),),
    ((2, 2), (3, 1), (1, 4), (0, 8)),
    ((4, 1), (3, 2), (2, 3)),
    (),
    ((2, 0), (5, 1)),
    ((4, 2), (3, 3), (1, 6)),
    ((2, 5),),
    ((5, 2), (4, 3), (2, 4)),
    (),
    ((3, 0), (5, 3)),
    (),
    ((1, 7),),
    ((3, 5),),
    (
        (1, 8), (2, 6), (0, 9), (0, 10), (3, 4), (4, 0), (2, 7), (4, 5),
        (3, 6), (2, 8), (1, 9), (5, 0), (1, 10), (4, 4), (3, 7), (5, 5),
        (4, 6), (2, 10), (2, 9), (5, 4), (3, 8), (4, 7), (3, 10), (5, 6),
        (3, 9), (5, 7), (4, 8), (4, 10), (4, 9), (5, 8), (5, 10), (5, 9),
    ),
)


class Scatter:
    def __init__(self, sources, outs, layer_in, layer_out, buffers, sems):
        items = len(SCATTER_ITEMS)
        self.sources, self.outs = sources, outs
        self.layer_in, self.layer_out = layer_in, layer_out
        self.sems = sems
        self.y, self.x, self.core, self.place, self.lines, self.count = position()
        y, x, core = self.y, self.x, self.core
        self.own = list(buffers[:FIRST_ITEMS])
        for array, _, _, _ in SCATTER_ITEMS[FIRST_ITEMS:]:
            self.own.append(sources[array].at[:, :, core])
        buffers = buffers[FIRST_ITEMS:]
        self.from_twin, self.first_in, self.second_in, self.line_in = [
            buffers[k * items : (k + 1) * items] for k in range(4)
        ]
        self.dp = dp_of(y, x, core)
        self.twin = dp_of(y, x, 1 - core)
        self.side = dp_of(y, 1 - x, core)
        self.ahead = [(y + k) % self.lines for k in range(1, self.lines)]

    def meet(self):
        targets = [(self.twin, self.place), (self.side, self.place)]
        for k in range(1, self.count):
            other = (self.place + k) % self.count
            targets += [(self.dp, other), (self.twin, other)]
        for other_y in self.ahead:
            targets.append((dp_of(other_y, self.x, self.core), self.place))
        meet(targets)

    def order(self, item):
        return SCATTER_ITEMS[item][3]

    def columns(self, item):
        array, part, parts, _ = SCATTER_ITEMS[item]
        cols = self.sources[array].shape[-1] // parts
        return pl.ds(part * cols, cols)

    def to_twin(self, item):
        src = self.sources[SCATTER_ITEMS[item][0]].at[:, :, 1 - self.core, :, :, self.columns(item)]
        sems = self.sems
        return remote(
            src, self.from_twin[item], sems.twin_send.at[item], sems.twin_recv.at[item], self.twin, self.place
        )

    def own_in(self, item):
        src = self.sources[SCATTER_ITEMS[item][0]].at[:, :, self.core, :, :, self.columns(item)]
        return pltpu.make_async_copy(src, self.own[item], self.sems.own.at[item])

    def x_copy(self, item):
        own = self.own[item]
        if self.order(item) == 0:
            src, dst = own.at[self.y, 1 - self.x], self.second_in[item].at[0]
        else:
            src, dst = own.at[:, 1 - self.x], self.first_in[item]
        return remote(
            src, dst, self.sems.x_send.at[item], self.sems.x_recv.at[item], self.side, self.place
        )

    def y_copy(self, item, k):
        other_y = self.ahead[k]
        own = self.own[item]
        if self.order(item) == 0:
            src, dst = own.at[other_y], self.first_in[item].at[k]
        else:
            src, dst = own.at[other_y, self.x], self.second_in[item].at[k]
        return remote(
            src,
            dst,
            self.sems.y_send.at[item, k],
            self.sems.y_recv.at[item, k],
            dp_of(other_y, self.x, self.core),
            self.place,
        )

    def stage_begin(self, item):
        self.to_twin(item).start()
        if item < FIRST_ITEMS:
            self.own_in(item).start()

    def stage_core(self, item):
        if item < FIRST_ITEMS:
            self.own_in(item).wait()
        self.to_twin(item).wait_recv()
        own, came = self.own[item], self.from_twin[item]

        def step(i, carry):
            a, b = i // 2, i % 2
            own[a, b] = plus(own[a, b], came[a, b])
            return carry

        lax.fori_loop(0, 2 * self.lines, step, 0)
        if self.order(item) == 0:
            for k in range(self.lines - 1):
                self.y_copy(item, k).start()
        else:
            self.x_copy(item).start()

    def stage_first(self, item):
        own, came = self.own[item], self.first_in[item]
        y, x, lines = self.y, self.x, self.lines
        if self.order(item) == 0:
            for k in range(lines - 1):
                self.y_copy(item, k).wait_recv()

            def step(b, carry):
                total = own[y, b]
                for k in range(lines - 1):
                    total = plus(total, came[k, b])
                own[y, b] = total
                return carry

            lax.fori_loop(0, 2, step, 0)
            self.x_copy(item).start()
        else:
            self.x_copy(item).wait_recv()

            def step(a, carry):
                own[a, x] = plus(own[a, x], came[a])
                return carry

            lax.fori_loop(0, lines, step, 0)
            for k in range(lines - 1):
                self.y_copy(item, k).start()

    def mine(self, item, z):
        return self.own[item].at[self.y, self.x, z]

    def z_copy(self, item, z, way):
        return remote(
            self.mine(item, z),
            self.line_in[item].at[way, z],
            self.sems.z_send.at[item, z],
            self.sems.z_recv.at[item, way, z],
            self.dp,
            self.place + 1 - 2 * way,
        )

    def z_forward(self, item, way, first):
        def step(z, carry):
            beyond = (z > self.place) if way == 0 else (z < self.place)

            @pl.when(beyond)
            def _():
                if not first:
                    self.z_copy(item, z, way).wait_recv()
                    ref = self.mine(item, z)
                    ref[...] = plus(ref[...], self.line_in[item][way, z])
                self.z_copy(item, z, way).start()

            return carry

        lax.fori_loop(0, self.count, step, 0)

    def stage_second(self, item):
        own, came = self.own[item], self.second_in[item]
        y, x = self.y, self.x
        if self.order(item) == 0:
            self.x_copy(item).wait_recv()
            own[y, x] = plus(own[y, x], came[0])
        else:
            total = own[y, x]
            for k in range(self.lines - 1):
                self.y_copy(item, k).wait_recv()
                total = plus(total, came[k])
            own[y, x] = total

        @pl.when(self.place == 0)
        def _():
            self.z_forward(item, 0, True)

        @pl.when(self.place == self.count - 1)
        def _():
            self.z_forward(item, 1, True)

    def stage_hop(self, hop, item):
        @pl.when(self.place == hop)
        def _():
            self.z_forward(item, 0, False)

        @pl.when(self.count - 1 - self.place == hop)
        def _():
            self.z_forward(item, 1, False)

    def stage_last(self, item):
        out = self.outs[SCATTER_ITEMS[item][0]]
        columns = self.columns(item)
        place = self.place
        out[:, columns] = self.mine(item, place)[...].astype(jnp.float32)

        def add(way):
            self.z_copy(item, place, way).wait_recv()
            out[:, columns] += self.line_in[item][way, place].astype(jnp.float32)

        @pl.when(place > 0)
        def _():
            add(0)

        @pl.when(place < self.count - 1)
        def _():
            add(1)

    def layer_copies(self, fn_remote, fn_local):
        seqs = self.layer_in.shape[0]
        for k in range(seqs):
            chip = seqs * self.core + k
            home = (chip == self.place) & (self.core == self.place // seqs)

            @pl.when(home)
            def _():
                fn_local(k)

            @pl.when(jnp.logical_not(home))
            def _():
                fn_remote(k, chip)

    def layer_remote(self, k, chip):
        seqs = self.layer_in.shape[0]
        row = self.place % seqs
        return remote(
            self.layer_in.at[k],
            self.layer_out.at[row],
            self.sems.layer_send.at[k],
            self.sems.layer_recv.at[row],
            dp_of(self.y, self.x, self.place // seqs),
            chip,
        )

    def layer_start(self):
        row = self.place % self.layer_in.shape[0]
        self.layer_copies(
            lambda k, chip: self.layer_remote(k, chip).start(),
            lambda k: pltpu.make_async_copy(
                self.layer_in.at[k], self.layer_out.at[row], self.sems.layer_recv.at[row]
            ).start(),
        )

    def stage_hop_one(self, item):
        self.stage_hop(1, item)

    def stage_hops(self, item):
        for hop in range(2, self.count - 1):
            self.stage_hop(hop, item)

    def stages(self):
        return (
            self.stage_core,
            self.stage_first,
            self.stage_second,
            self.stage_hop_one,
            self.stage_hops,
            self.stage_last,
        )

    def finish(self):
        for item in range(len(SCATTER_ITEMS)):
            self.to_twin(item).wait_send()
            self.x_copy(item).wait_send()
            for k in range(self.lines - 1):
                self.y_copy(item, k).wait_send()

            def drain(z, carry):
                @pl.when(z > self.place)
                def _():
                    self.z_copy(item, z, 0).wait_send()

                @pl.when(z < self.place)
                def _():
                    self.z_copy(item, z, 1).wait_send()

                return carry

            lax.fori_loop(0, self.count, drain, 0)
        for r in range(self.layer_in.shape[0]):
            dst = self.layer_out.at[r]
            remote(
                dst, dst, self.sems.layer_send.at[0], self.sems.layer_recv.at[r], self.twin, self.place
            ).wait_recv()
        self.layer_copies(lambda k, chip: self.layer_remote(k, chip).wait_send(), lambda k: None)


class ScatterSems(NamedTuple):
    own: object
    twin_send: object
    twin_recv: object
    x_send: object
    x_recv: object
    y_send: object
    y_recv: object
    z_send: object
    z_recv: object
    layer_send: object
    layer_recv: object


def plus(left, right):
    total = left.astype(jnp.float32) + right.astype(jnp.float32)
    return total.astype(left.dtype)


def scatter_scratch(shapes, lines, count, seqs):
    items = len(SCATTER_ITEMS)
    own, first_in, second_in, line_in = [], [], [], []
    for array, _, parts, order in SCATTER_ITEMS:
        rows, cols, kind = shapes[array]
        cols = cols // parts
        own.append(pltpu.VMEM((lines, 2, count, rows, cols), kind))
        if order == 0:
            first_in.append(pltpu.VMEM((lines - 1, 2, count, rows, cols), kind))
            second_in.append(pltpu.VMEM((1, count, rows, cols), kind))
        else:
            first_in.append(pltpu.VMEM((lines, count, rows, cols), kind))
            second_in.append(pltpu.VMEM((lines - 1, count, rows, cols), kind))
        line_in.append(pltpu.VMEM((2, count, rows, cols), kind))
    dma = pltpu.SemaphoreType.DMA
    sems = [dma((FIRST_ITEMS,))] + [dma((items,))] * 4
    sems += [dma((items, lines - 1))] * 2 + [dma((items, count)), dma((items, 2, count))]
    sems += [dma((seqs,))] * 2
    return own[:FIRST_ITEMS] + own + first_in + second_in + line_in, sems


class BackInputs(NamedTuple):
    gate: object
    up: object
    down: object
    output: object
    coef: object
    resid: object
    qt: object
    kt: object
    vt: object
    got: object
    out: object
    lse: object
    key_marks: object
    query_marks: object
    normed: object
    stream: object
    wq: object
    wk: object
    wv: object
    small: object
    gain_two: object
    table: object
    tap: object
    rows: object
    idm: object
    layer: object


class BackWork(NamedTuple):
    dq: object
    dkv: object
    away: object
    came: object
    wide: object
    one_hot: object
    src_q: object
    src_k: object
    src_v: object
    src_table: object
    src_small: object
    swap_send: object
    swap_recv: object
    coef_sem: object
    resid_sem: object


def backward_kernel(*refs):
    ref = BackInputs(*refs[: len(BackInputs._fields)])
    rest = refs[len(BackInputs._fields) :]
    outs, layer_out = rest[:9], rest[9]
    rest = rest[10:]
    held = FIRST_ITEMS + 4 * len(SCATTER_ITEMS)
    buffers, rest = rest[:held], rest[held:]
    sems = ScatterSems(*rest[: len(ScatterSems._fields)])
    own = BackWork(*rest[len(ScatterSems._fields) :])
    sources = (
        own.src_q,
        own.src_k,
        own.src_v,
        ref.output,
        ref.gate,
        ref.up,
        ref.down,
        own.src_table,
        own.src_small,
    )
    scatter = Scatter(sources, outs, ref.layer, layer_out, buffers, sems)
    stages = scatter.stages()
    width, tokens = ref.qt.shape
    pairs = width // 128
    bias = own.one_hot.at[0 : ref.kt.shape[1], 0:tokens]
    scatter.meet()
    for item in range(FIRST_ITEMS):
        scatter.stage_begin(item)

    queue = [[functools.partial(stages[stage], item) for stage, item in group] for group in SCHEDULE]

    def tick():
        for task in queue.pop(0):
            task()

    scatter.layer_start()
    tick()
    fill_bias(bias, ref.key_marks, ref.query_marks)

    def swap(i, which):
        rows = pl.ds(pl.multiple_of(which * width + 128 * i, 128), 128)
        return remote(
            own.away.at[rows],
            own.came.at[rows],
            own.swap_send.at[which, i],
            own.swap_recv.at[which, i],
            scatter.twin,
            scatter.place,
        )

    ticks = [queue.pop(0) for _ in range(pairs)]

    def pair_step(i, carry):
        at = pl.ds(pl.multiple_of(128 * i, 128), 128)
        attend_backward_pair(
            ref.qt.at[at],
            ref.kt.at[at],
            ref.vt.at[at],
            ref.got.at[at],
            ref.out.at[at],
            ref.lse.at[i],
            bias,
            own.dq.at[at],
            own.dkv.at[at],
            own.dkv.at[pl.ds(pl.multiple_of(width + 128 * i, 128), 128)],
            own.away.at[at],
            own.away.at[pl.ds(pl.multiple_of(width + 128 * i, 128), 128)],
        )
        swap(i, 0).start()
        swap(i, 1).start()
        for k, group in enumerate(ticks):
            if group:

                @pl.when(i == k)
                def _():
                    for task in group:
                        task()

        return carry

    lax.fori_loop(0, pairs, pair_step, 0)

    normed_t = ref.normed[...].T
    wide = own.wide

    def hand_out(source, item):
        lines, _, _, count, size, _ = source.shape
        total = lines * 4 * count

        for o in range(total):
            where = (o // (4 * count), o // (2 * count) % 2, o // count % 2, o % count)
            source[where] = wide[size * o : size * (o + 1)].astype(source.dtype)
        scatter.stage_begin(item)

    wide[...] = mm_nt(normed_t, own.dq[...])
    hand_out(own.src_q, 6)
    tick()
    for which in range(2):

        def add_half(i, carry):
            swap(i, which).wait_recv()
            rows = pl.ds(pl.multiple_of(which * width + 128 * i, 128), 128)
            own.dkv[rows] = plus(own.dkv[rows], own.came[rows])
            return carry

        lax.fori_loop(0, pairs, add_half, 0)
    coef = own.came.at[0 : KW * VOCAB]
    coef_copy = pltpu.make_async_copy(ref.coef, coef, own.coef_sem)
    coef_copy.start()
    wide[...] = mm_nt(normed_t, own.dkv[0:width])
    hand_out(own.src_k, 7)
    tick()
    wide[...] = mm_nt(normed_t, own.dkv[width:])
    hand_out(own.src_v, 8)
    tick()

    wide[:, 0:tokens] = mm(ref.wq[...], own.dq[...])
    wide[:, 0:tokens] += mm(ref.wk[...], own.dkv[0:width])
    tick()
    wide[:, 0:tokens] += mm(ref.wv[...], own.dkv[width:])
    normed_grad = wide[:, 0:tokens].T
    resid_copy = pltpu.make_async_copy(ref.resid, wide.at[0:tokens], own.resid_sem)
    resid_copy.start()
    stream = ref.stream[...]
    gain = ref.small[KW + 1 : KW + 2]
    scale = lax.rsqrt(jnp.mean(stream * stream, axis=-1, keepdims=True) + 1e-06)
    gain_grad = jnp.sum(normed_grad * stream * scale, axis=0, keepdims=True)
    scaled = normed_grad * gain
    inner = jnp.mean(scaled * stream, axis=-1, keepdims=True)
    resid_copy.wait()
    grad16 = (wide[0:tokens] + scale * scaled - stream * (scale * scale * scale * inner)).astype(jnp.bfloat16)
    tick()
    coef_copy.wait()
    table_grad, rows = tok_backward_body(
        grad16, coef, ref.tap, ref.rows, ref.idm, ref.table, ref.small, own.one_hot, tick
    )
    wide[0:VOCAB] = table_grad
    hand_out(own.src_table, 9)
    rows = jnp.concatenate(rows + [gain_grad, ref.gain_two[...]], axis=0)
    source = own.src_small
    lines, _, _, count, _, _ = source.shape
    total = lines * 4 * count
    for o in range(total):
        where = (o // (4 * count), o // (2 * count) % 2, o // count % 2, o % count)
        source[where] = lane_shift(rows, o * (width // total))[:, 0:128]
    scatter.stage_begin(10)
    while queue:
        tick()
    scatter.finish()

    def drain(i, carry):
        swap(i, 0).wait_send()
        swap(i, 1).wait_send()
        return carry

    lax.fori_loop(0, pairs, drain, 0)


def backward_all(arrays, shapes):
    count = lax.axis_size("seq")
    lines = lax.axis_size("dp") // 4
    total = lines * 4 * count
    vmem = pl.BlockSpec(memory_space=pltpu.VMEM)
    hbm = pl.BlockSpec(memory_space=pltpu.HBM)
    layer = arrays.layer
    width, tokens = arrays.qt.shape
    out_shape = [jax.ShapeDtypeStruct(shape[:2], jnp.float32) for shape in shapes]
    out_shape.append(jax.ShapeDtypeStruct(layer.shape, layer.dtype))
    buffers, sems = scatter_scratch(shapes, lines, count, layer.shape[0])
    views = list(arrays)
    for k in range(4):
        grad = arrays[k]
        views[k] = grad.reshape(lines, 2, 2, count, grad.shape[0] // total, grad.shape[1])

    def source(index):
        rows, cols, kind = shapes[index]
        return pltpu.VMEM((lines, 2, 2, count, rows, cols), kind)

    half = jnp.bfloat16
    own = [
        pltpu.VMEM((width, tokens), half),
        pltpu.VMEM((2 * width, tokens), half),
        pltpu.VMEM((2 * width, tokens), half),
        pltpu.VMEM((2 * width, tokens), half),
        pltpu.VMEM((width, width), jnp.float32),
        pltpu.VMEM((KW * VOCAB, arrays.idm.shape[1]), half),
        source(0),
        source(1),
        source(2),
        source(7),
        source(8),
        pltpu.SemaphoreType.DMA((2, width // 128)),
        pltpu.SemaphoreType.DMA((2, width // 128)),
        pltpu.SemaphoreType.DMA,
        pltpu.SemaphoreType.DMA,
    ]
    return pl.pallas_call(
        backward_kernel,
        name="backward_all",
        out_shape=out_shape,
        in_specs=[hbm] * 6 + [vmem] * (len(views) - 6),
        out_specs=[vmem] * 9 + [hbm],
        scratch_shapes=buffers + sems + own,
        compiler_params=pltpu.CompilerParams(
            collective_id=1, has_side_effects=True, vmem_limit_bytes=63 * 1024 * 1024
        ),
    )(*views)


def tok_forward_body(own, core, tokens, tick):
    ids_ref, marks_ref, table_ref, small_ref = own.ids_pad, own.marks_pad, own.table, own.small
    stream_ref, normed_ref, coef_ref, tap_ref = own.stream, own.normed, own.coef, own.tap
    rows_ref, idm_ref, one_hot = own.rows, own.idm, own.one_hot
    half_bytes = 2 * tokens
    span = one_hot.shape[1]
    wide = span + 2 * LEFT
    first = pl.ds(pl.multiple_of(core * half_bytes, 128), wide)
    ids = ids_ref[:, first]
    marks = marks_ref[:, first]
    for tap in range(KW):
        by = tap - KW // 2
        same = (lane_shift(marks, by) == marks) & (marks > 0)
        idm_ref[tap : tap + 1] = jnp.where(same, lane_shift(ids, by), -1)[0:1, LEFT : LEFT + span]
    tick()
    fill_one_hot(one_hot, lambda tap: idm_ref[tap : tap + 1])

    tick()
    score = jnp.broadcast_to(small_ref[KW : KW + 1], (8, small_ref.shape[1])).astype(jnp.bfloat16)
    scored = []
    for tap in range(KW):
        product = table_ref[...].astype(jnp.float32) * small_ref[tap : tap + 1]
        high, low = split_two(product)
        tap_ref[tap * VOCAB : (tap + 1) * VOCAB] = high
        scored.append(mm_nt(score, high) + mm_nt(score, low))
    tick()
    high, low = split_two(jnp.concatenate(scored, axis=1))
    u_row = mm(high, one_hot[...]) + mm(low, one_hot[...])

    tick()
    high = u_row.astype(jnp.bfloat16).astype(jnp.float32)
    marks_here = marks[:, LEFT : LEFT + span].astype(jnp.float32)
    away = marks_ref[:, pl.ds(pl.multiple_of((1 - core) * half_bytes, 128), wide)][:, LEFT : LEFT + span]
    away = away.astype(jnp.float32)
    packed = jnp.concatenate([marks_here, high, u_row - high, away], axis=0).astype(jnp.bfloat16)
    shape = (span, wide // 2)
    twice = 2 * lax.broadcasted_iota(jnp.int32, shape, 1) - lax.broadcasted_iota(jnp.int32, shape, 0) - LEFT
    marks_of, u_of = [], []
    for e in range(2):
        pick = (twice == -e).astype(jnp.float32).astype(jnp.bfloat16)
        apart = mm(packed, pick)
        marks_of.append(apart[0:8])
        u_of.append(apart[8:16] + apart[16:24])
        if e == 0:
            kept = slice(LEFT, LEFT + tokens)
            both = jnp.concatenate([apart[0:1, kept], apart[24:25, kept]], axis=1)
            own.marks[...] = both.astype(jnp.int32)

    tick()
    inside, inverse = pool_rows(marks_of, core, half_bytes)
    prob = {}
    for e in range(2):
        shifted = {}
        for s in range(1 - MAXBLOCK, MAXBLOCK):
            f = (e + s) % 2
            shifted[s] = lane_shift(u_of[f], (e + s - f) // 2)
        scores = [u_of[e]]
        for b in range(2, MAXBLOCK + 1):
            total = u_of[e]
            for s in range(1 - b, b):
                if s != 0:
                    total = total + inside[b, e, s] * shifted[s]
            scores.append(total * inverse[b, e])
        top = scores[0]
        for value in scores[1:]:
            top = jnp.maximum(top, value)
        expo = [jnp.exp(value - top) for value in scores]
        whole = expo[0] + expo[1] + expo[2] + expo[3]
        for b in range(1, MAXBLOCK + 1):
            prob[b, e] = expo[b - 1] / whole
            rows_ref[2 * b + e : 2 * b + e + 1] = prob[b, e][0:1]
        rows_ref[e : e + 1] = marks_of[e][0:1]
    coefs = band_coefs({key: 0.5 * value for key, value in prob.items()}, inside, inverse)
    gain = small_ref[KW + 1 : KW + 2]
    tick()
    for i in range(tokens // BAND):
        matrix = band_matrix(coefs, i).astype(jnp.bfloat16)
        lanes = slice(i * BAND, (i + 1) * BAND)
        part = mm(one_hot[:, 2 * i * BAND : (2 * i + 3) * BAND], matrix).astype(jnp.bfloat16)
        coef_ref[:, lanes] = part
        stream = mm_tn(part, tap_ref[...])
        stream_ref[lanes] = stream
        scale = lax.rsqrt(jnp.mean(stream * stream, axis=-1, keepdims=True) + 1e-06)
        normed_ref[lanes] = (stream * scale * gain).astype(jnp.bfloat16)
        if i < tokens // BAND - 1:
            tick()


FUSED_ITEMS = (
    (7, 0, 1, 0, 0),
    (8, 0, 1, 0, 0),
    (0, 0, 1, 1, 1),
    (1, 0, 1, 0, 1),
    (2, 0, 1, 1, 1),
    (3, 0, 1, 0, 1),
    (6, 0, 2, 0, 2),
    (4, 1, 2, 0, 2),
    (6, 1, 2, 1, 3),
    (5, 0, 2, 1, 3),
    (4, 0, 2, 1, 4),
    (5, 1, 2, 0, 4),
)
FUSED_SCHEDULE = (
    (
        (0, 0, 0), (1, 0, 0), (0, 1, 0), (1, 1, 0), (2, 0, 1), (3, 0, 0),
        (3, 1, 0), (2, 0, 2), (4, 0, 0), (3, 0, 1), (2, 0, 3), (2, 1, 1),
        (0, 2, 0), (3, 0, 2), (4, 1, 0), (3, 0, 3), (2, 1, 2), (4, 0, 1),
        (3, 1, 1), (4, 0, 2), (4, 0, 3), (2, 1, 3), (1, 2, 0), (2, 2, 1),
        (0, 3, 0),
    ),
    (),
    (),
    (
        (2, 2, 2), (3, 1, 2),
    ),
    ((4, 1, 1),),
    ((3, 1, 3),),
    (),
    (
        (2, 2, 3), (1, 3, 0), (2, 3, 1), (0, 4, 0), (3, 2, 0),
    ),
    (
        (3, 2, 1), (3, 2, 2), (2, 3, 2), (4, 1, 2), (4, 1, 3),
    ),
    (
        (2, 3, 3), (1, 4, 0), (2, 4, 1), (3, 2, 3),
    ),
    (),
    (
        (2, 4, 2), (3, 3, 0),
    ),
    (
        (3, 3, 1), (4, 2, 0),
    ),
    (
        (2, 4, 3), (5, 0, 0),
    ),
    (),
    ((4, 2, 1),),
    (
        (3, 3, 2), (3, 3, 3), (4, 2, 2), (4, 3, 0),
    ),
    ((3, 4, 0),),
    (
        (3, 4, 1), (4, 2, 3), (4, 3, 1), (4, 3, 2),
    ),
    (
        (3, 4, 2), (3, 4, 3), (4, 3, 3), (4, 4, 0),
    ),
    (
        (4, 4, 1), (4, 4, 2), (4, 4, 3),
    ),
)


class Gather:
    def __init__(self, ins, outs, cells_in, cells_out, cot_in, cot_out, sems):
        self.ins, self.outs, self.sems = ins, outs, sems
        self.cells_in, self.cells_out, self.cot_in, self.cot_out = cells_in, cells_out, cot_in, cot_out
        self.y, self.x, self.core, self.place, self.lines, self.count = position()
        y, x, core = self.y, self.x, self.core
        self.group = y * 2 + x
        self.dp = dp_of(y, x, core)
        self.twin = dp_of(y, x, 1 - core)
        self.side = dp_of(y, 1 - x, core)
        self.ahead = [(y + k) % self.lines for k in range(1, self.lines)]
        self.phases = {}
        for item, entry in enumerate(FUSED_ITEMS):
            self.phases.setdefault(entry[4], []).append(item)

    def meet(self):
        targets = [(self.twin, self.place), (self.side, self.place)]
        for k in range(1, self.count):
            other = (self.place + k) % self.count
            targets += [(self.dp, other), (self.twin, other)]
        for other_y in self.ahead:
            targets.append((dp_of(other_y, self.x, self.core), self.place))
        meet(targets)

    def lanes(self, item):
        array, part, parts, _, _ = FUSED_ITEMS[item]
        cols = self.ins[array].shape[1] // parts
        return pl.ds(part * cols, cols)

    def shard(self, item):
        return self.ins[FUSED_ITEMS[item][0]].at[:, self.lanes(item)]

    def rows(self, item, first, blocks):
        array = FUSED_ITEMS[item][0]
        size = self.ins[array].shape[0]
        start = pl.multiple_of(first * size, 8)
        return self.outs[array].at[pl.ds(start, blocks * size), self.lanes(item)]

    def block(self, item, g, z):
        return self.rows(item, (g * 2 + self.core) * self.count + z, 1)

    def group_block(self, item, g, core):
        return self.rows(item, (g * 2 + core) * self.count, self.count)

    def came(self, item, g, z):
        return self.sems.recv.at[item, g * self.count + z]

    def arrived(self, item, g, z):
        dst = self.block(item, g, z)
        remote(dst, dst, self.sems.x.at[item], self.came(item, g, z), self.twin, self.place).wait_recv()

    def to_side(self, item, src, g, z):
        remote(
            src, self.block(item, g, z), self.sems.x.at[item], self.came(item, g, z), self.side, self.place
        ).start()

    def to_lines(self, item, src, g, z):
        for other_y in self.ahead:
            remote(
                src,
                self.block(item, g, z),
                self.sems.y.at[item],
                self.came(item, g, z),
                dp_of(other_y, self.x, self.core),
                self.place,
            ).start()

    def to_z(self, item, src, z, way):
        return remote(
            src,
            self.block(item, self.group, z),
            self.sems.z.at[item, z, way],
            self.came(item, self.group, z),
            self.dp,
            self.place + 1 - 2 * way,
        )

    def to_twin(self, item, g):
        src = self.group_block(item, g, self.core)
        remote(
            src, src, self.sems.twin.at[item], self.sems.twin_recv.at[item, g], self.twin, self.place
        ).start()

    def own_copy(self, item):
        return pltpu.make_async_copy(
            self.shard(item), self.block(item, self.group, self.place), self.sems.own.at[item]
        )

    def task_own(self, phase):
        for item in self.phases[phase]:
            src = self.shard(item)

            @pl.when(self.place < self.count - 1)
            def _():
                self.to_z(item, src, self.place, 0).start()

            @pl.when(self.place > 0)
            def _():
                self.to_z(item, src, self.place, 1).start()

            self.own_copy(item).start()

    def task_sides(self, phase):
        for item in self.phases[phase]:
            src = self.shard(item)
            self.to_side(item, src, self.group, self.place)
            self.to_lines(item, src, self.group, self.place)

    def both_ways(self, step, body):
        low, high = self.place - step, self.place + step

        @pl.when(low >= 0)
        def _():
            body(low, 0)

        @pl.when(high < self.count)
        def _():
            body(high, 1)

    def steps(self, step, body):
        if step < 3:
            body(step)
            return

        def loop(s, carry):
            body(s)
            return carry

        lax.fori_loop(3, self.count, loop, 0)

    def task_first(self, phase, step):
        items = self.phases[phase]

        def receive(z, way):
            for item in items:
                self.arrived(item, self.group, z)
                src = self.block(item, self.group, z)
                onward = self.place < self.count - 1 if way == 0 else self.place > 0

                @pl.when(onward)
                def _():
                    self.to_z(item, src, z, way).start()

                self.to_side(item, src, self.group, z)
                self.to_lines(item, src, self.group, z)

        self.steps(step, lambda s: self.both_ways(s, receive))
        if step == 3:
            for item in items:
                self.own_copy(item).wait()
                self.to_twin(item, self.group)

    def at_distance(self, step, body):
        if step == 0:
            body(self.place, 0)
        else:
            self.steps(step, lambda s: self.both_ways(s, body))

    def task_second(self, phase, step):
        items = self.phases[phase]

        def receive(z, way):
            for item in items:
                if FUSED_ITEMS[item][3] == 0:
                    g = self.y * 2 + (1 - self.x)
                    self.arrived(item, g, z)
                    self.to_lines(item, self.block(item, g, z), g, z)
                else:
                    for other_y in self.ahead:
                        g = other_y * 2 + self.x
                        self.arrived(item, g, z)
                        self.to_side(item, self.block(item, g, z), g, z)

        self.at_distance(step, receive)
        if step == 3:
            for item in items:
                if FUSED_ITEMS[item][3] == 0:
                    self.to_twin(item, self.y * 2 + (1 - self.x))
                else:
                    for other_y in self.ahead:
                        self.to_twin(item, other_y * 2 + self.x)

    def task_third(self, phase, step):
        items = self.phases[phase]

        def rest(item):
            if FUSED_ITEMS[item][3] == 0:
                return [other_y * 2 + x for other_y in self.ahead for x in (self.x, 1 - self.x)]
            return [other_y * 2 + (1 - self.x) for other_y in [self.y] + self.ahead]

        def receive(z, way):
            for item in items:
                for g in rest(item):
                    self.arrived(item, g, z)

        self.at_distance(step, receive)
        if step == 3:
            for item in items:
                for g in rest(item):
                    self.to_twin(item, g)

    def full(self, item):
        for g in range(self.lines * 2):
            dst = self.group_block(item, g, 1 - self.core)
            remote(
                dst, dst, self.sems.twin.at[item], self.sems.twin_recv.at[item, g], self.twin, self.place
            ).wait_recv()

    def cell_copies(self, fn_remote, fn_local):
        seqs = self.cells_in.shape[0]
        for r in range(seqs):
            chip = seqs * self.core + r
            for c in range(2):
                home = (chip == self.place) & (self.core == c)

                @pl.when(home)
                def _():
                    fn_local(r)

                @pl.when(jnp.logical_not(home))
                def _():
                    fn_remote(r, c, chip)

    def cell_remote(self, r, c, chip):
        return remote(
            self.cells_in.at[r],
            self.cells_out.at[self.place],
            self.sems.cell_send.at[r, c],
            self.sems.cell_recv.at[self.place],
            dp_of(self.y, self.x, c),
            chip,
        )

    def cells_start(self):
        self.cell_copies(
            lambda r, c, chip: self.cell_remote(r, c, chip).start(),
            lambda r: pltpu.make_async_copy(
                self.cells_in.at[r], self.cells_out.at[self.place], self.sems.cell_recv.at[self.place]
            ).start(),
        )

    def cells_wait(self):
        for q in range(self.count):
            dst = self.cells_out.at[q]
            remote(
                dst, dst, self.sems.cell_send.at[0, 0], self.sems.cell_recv.at[q], self.twin, self.place
            ).wait_recv()

    def cot_copies(self, fn_remote, fn_local):
        seqs = self.cot_in.shape[0]
        for r in range(seqs):
            chip = seqs * self.core + r
            home = (chip == self.place) & (self.core == self.place // seqs)

            @pl.when(home)
            def _():
                fn_local(r)

            @pl.when(jnp.logical_not(home))
            def _():
                fn_remote(r, chip)

    def cot_remote(self, r, chip):
        seqs = self.cot_in.shape[0]
        slot = self.place % seqs
        return remote(
            self.cot_in.at[r],
            self.cot_out.at[slot],
            self.sems.cot_send.at[r],
            self.sems.cot_recv.at[slot],
            dp_of(self.y, self.x, self.place // seqs),
            chip,
        )

    def task_cot(self):
        slot = self.place % self.cot_in.shape[0]
        self.cot_copies(
            lambda r, chip: self.cot_remote(r, chip).start(),
            lambda r: pltpu.make_async_copy(
                self.cot_in.at[r], self.cot_out.at[slot], self.sems.cot_recv.at[slot]
            ).start(),
        )

    def task(self, kind, phase, step):
        if kind == 0:
            self.task_own(phase)
        elif kind == 1:
            self.task_sides(phase)
        elif kind == 2:
            self.task_first(phase, step)
        elif kind == 3:
            self.task_second(phase, step)
        elif kind == 4:
            self.task_third(phase, step)
        else:
            self.task_cot()

    def finish(self, waited):
        count, groups = self.count, self.lines * 2
        for item in range(len(FUSED_ITEMS)):
            if item not in waited:
                self.full(item)
            tree = FUSED_ITEMS[item][3]

            def sent(blocks, sem):
                src = self.rows(item, 0, blocks)
                remote(src, src, sem, self.came(item, 0, 0), self.twin, self.place).wait_send()

            sent(count * (1 if tree == 0 else self.lines), self.sems.x.at[item])
            sent(count * (self.lines - 1) * (2 if tree == 0 else 1), self.sems.y.at[item])
            sent(count * groups, self.sems.twin.at[item])

            def drain(z, carry):
                @pl.when((z <= self.place) & (self.place < count - 1))
                def _():
                    self.to_z(item, self.block(item, self.group, z), z, 0).wait_send()

                @pl.when((z >= self.place) & (self.place > 0))
                def _():
                    self.to_z(item, self.block(item, self.group, z), z, 1).wait_send()

                return carry

            lax.fori_loop(0, count, drain, 0)
        for q in range(self.cot_in.shape[0]):
            dst = self.cot_out.at[q]
            remote(
                dst, dst, self.sems.cot_send.at[0], self.sems.cot_recv.at[q], self.twin, self.place
            ).wait_recv()
        self.cell_copies(lambda r, c, chip: self.cell_remote(r, c, chip).wait_send(), lambda r: None)
        self.cot_copies(lambda r, chip: self.cot_remote(r, chip).wait_send(), lambda r: None)


class GatherSems(NamedTuple):
    recv: object
    twin_recv: object
    z: object
    x: object
    y: object
    twin: object
    own: object
    cell_recv: object
    cell_send: object
    cot_recv: object
    cot_send: object
class FrontOuts(NamedTuple):
    cot: object
    stream: object
    normed: object
    coef: object
    tap: object
    rows: object
    idm: object
    qt: object
    kt: object
    vt: object
    out: object
    lse: object
    marks: object
    small: object
    resid: object
    normed_two: object


class FrontWork(NamedTuple):
    stream: object
    normed: object
    coef: object
    tap: object
    rows: object
    idm: object
    qt: object
    kt: object
    vt: object
    out: object
    lse: object
    marks: object
    small: object
    resid: object
    normed_two: object
    cells: object
    ids_pad: object
    marks_pad: object
    table: object
    blocks: object
    wq: object
    wk: object
    wv: object
    wo: object
    other: object
    one_hot: object
    bias: object
    scores: object
    out_sem: object
    load_sem: object
    swap_send: object
    swap_recv: object


def attend_forward_pair(qt, kt, vt, bias, scores, out, lse):
    keys = kt[...].T
    chunks = keys.shape[0] // CHUNK
    for h in range(2):
        query = pair_rows(qt, h)
        own = slice(h * HEAD_DIM, (h + 1) * HEAD_DIM)
        top = None
        for c in range(chunks):
            rows = slice(c * CHUNK, (c + 1) * CHUNK)
            part = mm(keys[rows], query) + bias[rows]
            scores[h, rows] = part
            high = jnp.max(part, axis=0, keepdims=True)
            top = high if top is None else jnp.maximum(top, high)
        total = None
        summed = None
        for c in range(chunks):
            rows = slice(c * CHUNK, (c + 1) * CHUNK)
            expo = jnp.exp(scores[h, rows] - top)
            part = jnp.sum(expo, axis=0, keepdims=True)
            total = part if total is None else total + part
            part = mm(vt[own, rows], expo.astype(jnp.bfloat16))
            summed = part if summed is None else summed + part
        out[own] = (summed / total).astype(jnp.bfloat16)
        lse[h : h + 1] = top + jnp.log(total)


def forward_kernel(*refs):
    arrays = 9
    ins, cells_in, cot_in = refs[:arrays], refs[arrays], refs[arrays + 1]
    rest = refs[arrays + 2 :]
    full, cells_out = rest[:arrays], rest[arrays]
    kept = len(FrontOuts._fields)
    to = FrontOuts(*rest[arrays + 1 : arrays + 1 + kept])
    rest = rest[arrays + 1 + kept :]
    sems = GatherSems(*rest[: len(GatherSems._fields)])
    own = FrontWork(*rest[len(GatherSems._fields) :])
    gather = Gather(ins, full, cells_in, cells_out, cot_in, to.cot, sems)
    which = {}
    for item, entry in enumerate(FUSED_ITEMS):
        which[entry[0]] = item
    queue = [list(group) for group in FUSED_SCHEDULE]

    def tick():
        for entry in queue.pop(0):
            gather.task(*entry)

    saved = []

    def save(src, dst):
        copy = pltpu.make_async_copy(src, dst, own.out_sem.at[len(saved)])
        copy.start()
        saved.append(copy)

    def load(array, dst):
        gather.full(which[array])
        copy = pltpu.make_async_copy(full[array], dst, own.load_sem.at[array])
        copy.start()
        return copy

    gather.meet()
    gather.cells_start()
    tick()

    core, place = gather.core, gather.place
    tokens, width = own.stream.shape
    half_bytes = 2 * tokens
    span = own.one_hot.shape[1]
    wide = span + 2 * LEFT
    gather.cells_wait()
    cell_copy = pltpu.make_async_copy(cells_out, own.cells, own.load_sem.at[4])
    cell_copy.start()
    load_table = load(7, own.table)
    load_blocks = load(8, own.blocks)
    cell_copy.wait()
    ids_pad, marks_pad = own.ids_pad, own.marks_pad
    ids_pad[:, 0 : 2 * LEFT] = jnp.full((8, 2 * LEFT), -1, jnp.int32)
    marks_pad[:, 0 : 2 * LEFT] = jnp.zeros((8, 2 * LEFT), jnp.int32)
    end = 2 * LEFT + 2 * half_bytes
    ids_pad[:, end : end + 2 * LEFT] = jnp.full((8, 2 * LEFT), -1, jnp.int32)
    marks_pad[:, end : end + 2 * LEFT] = jnp.zeros((8, 2 * LEFT), jnp.int32)
    parts, per_part = own.cells.shape[0], own.cells.shape[1] // 2
    for q in range(parts):
        for r in range(per_part):
            at = slice(2 * LEFT + (q * per_part + r) * 128, 2 * LEFT + (q * per_part + r + 1) * 128)
            ids_pad[:, at] = jnp.broadcast_to(own.cells[q, r : r + 1], (8, 128))
            marks_pad[:, at] = jnp.broadcast_to(own.cells[q, per_part + r : per_part + r + 1], (8, 128))
    load_blocks.wait()
    total = gather.lines * 4 * gather.count
    chan = width // total
    lane = lax.broadcasted_iota(jnp.int32, (8, 128), 1)
    columns = [jnp.zeros((8, 128), jnp.float32) for _ in range(width // 128)]
    for o in range(total):
        piece = jnp.where(lane < chan, own.blocks[8 * o : 8 * o + 8], 0.0)
        at, by = divmod(o * chan, 128)
        turned = piece if by == 0 else pltpu.roll(piece, by, 1)
        columns[at] = columns[at] + jnp.where(lane >= by, turned, 0.0)
        if by + chan > 128:
            columns[at + 1] = columns[at + 1] + jnp.where(lane < by, turned, 0.0)
    own.small[...] = jnp.concatenate(columns, axis=1)
    save(own.small, to.small)
    load_table.wait()
    tok_forward_body(own, core, tokens, tick)
    save(own.stream, to.stream)
    save(own.normed, to.normed)
    save(own.coef, to.coef)
    save(own.tap, to.tap)
    save(own.rows, to.rows)
    save(own.idm, to.idm)
    save(own.marks, to.marks)

    swap = remote(own.normed, own.other, own.swap_send, own.swap_recv, gather.twin, place)
    swap.start()
    tick()
    load_wq = load(0, own.wq)
    load_wk = load(1, own.wk)
    load_wv = load(2, own.wv)

    def project(rows, weight):
        return mm(rows[...], weight[...]).astype(jnp.bfloat16)

    load_wq.wait()
    own.qt[...] = (project(own.normed, own.wq) * HEAD_DIM ** (-0.5)).astype(jnp.bfloat16).T
    save(own.qt, to.qt)
    tick()
    load_wk.wait()
    own.kt[:, 0:tokens] = project(own.normed, own.wk).T
    tick()
    load_wv.wait()
    own.vt[:, 0:tokens] = project(own.normed, own.wv).T
    tick()
    swap.wait_recv()
    own.kt[:, tokens:] = project(own.other, own.wk).T
    tick()
    own.vt[:, tokens:] = project(own.other, own.wv).T
    save(own.kt, to.kt)
    save(own.vt, to.vt)
    tick()
    load_wo = load(3, own.wo)
    fill_bias(own.bias, own.marks, own.marks.at[:, 0:tokens])
    pairs = width // 128
    ticks = [queue.pop(0) for _ in range(pairs)]

    def pair_step(i, carry):
        at = pl.ds(pl.multiple_of(128 * i, 128), 128)
        attend_forward_pair(
            own.qt.at[at],
            own.kt.at[at],
            own.vt.at[at],
            own.bias,
            own.scores,
            own.out.at[at],
            own.lse.at[i],
        )
        for k, group in enumerate(ticks):
            if group:

                @pl.when(i == k)
                def _():
                    for entry in group:
                        gather.task(*entry)

        return carry

    lax.fori_loop(0, pairs, pair_step, 0)
    save(own.out, to.out)
    save(own.lse, to.lse)
    load_wo.wait()
    resid = own.stream[...] + mm(own.out[...].T, own.wo[...])
    own.resid[...] = resid
    save(own.resid, to.resid)
    scale = lax.rsqrt(jnp.mean(resid * resid, axis=-1, keepdims=True) + 1e-06)
    own.normed_two[...] = (resid * scale * own.small[KW + 2 : KW + 3]).astype(jnp.bfloat16)
    save(own.normed_two, to.normed_two)
    while queue:
        tick()
    gather.finish([which[a] for a in (0, 1, 2, 3, 7, 8)])
    for copy in saved:
        copy.wait()
    swap.wait_send()


def forward_all(shards, cells, cot, tokens):
    count = lax.axis_size("seq")
    group_count = lax.axis_size(ALL)
    groups = group_count // (2 * count)
    items = len(FUSED_ITEMS)
    seqs = cells.shape[0]
    width = shards[0].shape[1]
    span = 2 * tokens + 2 * LEFT
    half, single = jnp.bfloat16, jnp.float32
    vmem = pl.BlockSpec(memory_space=pltpu.VMEM)
    hbm = pl.BlockSpec(memory_space=pltpu.HBM)
    pairs = width // 128
    held = (
        ((tokens, width), single),
        ((tokens, width), half),
        ((KW * VOCAB, tokens), half),
        ((KW * VOCAB, width), half),
        ((16, (span + 2 * LEFT) // 2), single),
        ((8, span), jnp.int32),
        ((width, tokens), half),
        ((width, 2 * tokens), half),
        ((width, 2 * tokens), half),
        ((width, tokens), half),
        ((pairs, 2, tokens), single),
        ((1, 2 * tokens), jnp.int32),
        ((8, width), single),
        ((tokens, width), single),
        ((tokens, width), half),
    )
    shapes = [jax.ShapeDtypeStruct((s.shape[0] * group_count, s.shape[1]), s.dtype) for s in shards]
    shapes.append(jax.ShapeDtypeStruct((count,) + cells.shape[1:], cells.dtype))
    shapes.append(jax.ShapeDtypeStruct(cot.shape, cot.dtype))
    shapes += [jax.ShapeDtypeStruct(*entry) for entry in held]
    dma = pltpu.SemaphoreType.DMA
    scratch = [
        dma((items, groups * count)),
        dma((items, groups)),
        dma((items, count, 2)),
        dma((items,)),
        dma((items,)),
        dma((items,)),
        dma((items,)),
        dma((count,)),
        dma((seqs, 2)),
        dma((seqs,)),
        dma((seqs,)),
    ]
    scratch += [pltpu.VMEM(*entry) for entry in held]
    scratch += [
        pltpu.VMEM((count,) + cells.shape[1:], cells.dtype),
        pltpu.VMEM((8, 4 * tokens + 4 * LEFT), jnp.int32),
        pltpu.VMEM((8, 4 * tokens + 4 * LEFT), jnp.int32),
        pltpu.VMEM((VOCAB, width), half),
        pltpu.VMEM((8 * group_count, 128), single),
        pltpu.VMEM((width, width), half),
        pltpu.VMEM((width, width), half),
        pltpu.VMEM((width, width), half),
        pltpu.VMEM((width, width), half),
        pltpu.VMEM((tokens, width), half),
        pltpu.VMEM((KW * VOCAB, span), half),
        pltpu.VMEM((2 * tokens, tokens), single),
        pltpu.VMEM((2, 2 * tokens, tokens), single),
        dma((len(held),)),
        dma((9,)),
        dma,
        dma,
    ]
    out = pl.pallas_call(
        forward_kernel,
        name="forward_all",
        out_shape=shapes,
        in_specs=[vmem] * (len(shards) + 2),
        out_specs=[hbm] * len(shapes),
        scratch_shapes=scratch,
        compiler_params=pltpu.CompilerParams(
            collective_id=0, has_side_effects=True, vmem_limit_bytes=60 * 1024 * 1024
        ),
    )(*shards, cells, cot)
    return list(out[:9]), FrontOuts(*out[10:])

FF_BLOCK = 512


def feed_kernel(
    normed,
    cot,
    resid,
    small,
    out_t,
    w_gate,
    w_up,
    w_down,
    w_output,
    gate_grad,
    up_grad,
    down_grad,
    layer,
    output_grad,
    got,
    resid_grad,
    gain_grad,
    normed_t,
    total,
    normed_grad,
):
    step = pl.program_id(0)

    @pl.when(step == 0)
    def _():
        normed_t[...] = normed[...].T
        total[...] = jnp.zeros_like(total)
        normed_grad[...] = jnp.zeros_like(normed_grad)

    gate = mm(normed[...], w_gate[...])
    up = mm(normed[...], w_up[...])
    root = 0.7978845608028654
    square = gate * gate
    bent = jnp.tanh(root * gate * (1.0 + 0.044715 * square))
    half = 0.5 * (1.0 + bent)
    act = gate * half
    slope = half + 0.5 * gate * (1.0 - bent * bent) * (root * (1.0 + 3 * 0.044715 * square))
    hidden = (act * up).astype(jnp.bfloat16)
    total[...] += mm(hidden, w_down[...])
    hidden_grad = mm_nt(cot[...], w_down[...])
    up_part = (hidden_grad * act).astype(jnp.bfloat16)
    gate_part = (hidden_grad * up * slope).astype(jnp.bfloat16)
    down_grad[...] = mm(hidden.T, cot[...]).astype(jnp.bfloat16)
    gate_grad[...] = mm(normed_t[...], gate_part).astype(jnp.bfloat16)
    up_grad[...] = mm(normed_t[...], up_part).astype(jnp.bfloat16)
    normed_grad[...] += mm_nt(gate_part, w_gate[...]) + mm_nt(up_part, w_up[...])

    @pl.when(step == pl.num_programs(0) - 1)
    def _():
        stream = resid[...]
        layer[...] = (stream + total[...]).astype(jnp.bfloat16)
        scale = lax.rsqrt(jnp.mean(stream * stream, axis=-1, keepdims=True) + 1e-06)
        grad = normed_grad[...]
        gain_grad[...] = jnp.sum(grad * stream * scale, axis=0, keepdims=True)
        scaled = grad * small[KW + 2 : KW + 3]
        inner = jnp.mean(scaled * stream, axis=-1, keepdims=True)
        whole = cot[...].astype(jnp.float32) + scale * scaled - stream * (scale * scale * scale * inner)
        resid_grad[...] = whole
        proj = whole.astype(jnp.bfloat16)
        output_grad[...] = mm(out_t[...], proj).astype(jnp.bfloat16)
        got[...] = mm_nt(w_output[...], proj).astype(jnp.bfloat16)


def feed_forward(normed, cot, resid, small, out_t, w_gate, w_up, w_down, w_output):
    tokens, width = normed.shape
    wide = w_gate.shape[1]
    whole = lambda shape: pl.BlockSpec(shape, lambda f: (0, 0))
    columns = pl.BlockSpec((width, FF_BLOCK), lambda f: (0, f))
    rows = pl.BlockSpec((FF_BLOCK, width), lambda f: (f, 0))
    half, single = jnp.bfloat16, jnp.float32
    return pl.pallas_call(
        feed_kernel,
        name="feed_forward",
        grid=(wide // FF_BLOCK,),
        in_specs=[
            whole((tokens, width)),
            whole((tokens, width)),
            whole((tokens, width)),
            whole(small.shape),
            whole((width, tokens)),
            columns,
            columns,
            rows,
            whole((width, width)),
        ],
        out_specs=[
            columns,
            columns,
            rows,
            whole((tokens, width)),
            whole((width, width)),
            whole((width, tokens)),
            whole((tokens, width)),
            whole((1, width)),
        ],
        out_shape=[
            jax.ShapeDtypeStruct((width, wide), half),
            jax.ShapeDtypeStruct((width, wide), half),
            jax.ShapeDtypeStruct((wide, width), half),
            jax.ShapeDtypeStruct((tokens, width), half),
            jax.ShapeDtypeStruct((width, width), half),
            jax.ShapeDtypeStruct((width, tokens), half),
            jax.ShapeDtypeStruct((tokens, width), single),
            jax.ShapeDtypeStruct((1, width), single),
        ],
        scratch_shapes=[
            pltpu.VMEM((width, tokens), half),
            pltpu.VMEM((tokens, width), single),
            pltpu.VMEM((tokens, width), single),
        ],
        compiler_params=pltpu.CompilerParams(vmem_limit_bytes=VMEM_BYTES),
    )(normed, cot, resid, small, out_t, w_gate, w_up, w_down, w_output)


def result_kernel(count, chan, *refs):
    ins, outs, sem = refs[:count], refs[count:-1], refs[-1]
    small = ins[-1]
    copies = [pltpu.make_async_copy(ins[k], outs[k], sem.at[k]) for k in range(count - 1)]
    for copy in copies:
        copy.start()
    outs[count - 1][...] = small[0:KW, 0:chan]
    for k in range(3):
        outs[count + k][...] = small[KW + k : KW + k + 1, 0:chan]
    for copy in copies:
        copy.wait()


def results(arrays, small, chan):
    vmem = pl.BlockSpec(memory_space=pltpu.VMEM)
    hbm = pl.BlockSpec(memory_space=pltpu.HBM)
    count = len(arrays) + 1
    shapes = [jax.ShapeDtypeStruct(a.shape, a.dtype) for a in arrays]
    shapes.append(jax.ShapeDtypeStruct((KW, chan), jnp.float32))
    shapes += [jax.ShapeDtypeStruct((1, chan), jnp.float32)] * 3
    return pl.pallas_call(
        functools.partial(result_kernel, count, chan),
        name="results",
        out_shape=shapes,
        in_specs=[vmem] * count,
        out_specs=[hbm] * len(arrays) + [vmem] * 4,
        scratch_shapes=[pltpu.SemaphoreType.DMA((count,))],
    )(*arrays, small)


def per_device(
    byte_ids,
    segments,
    embed_table,
    conv_weight,
    score_vector,
    first_gain,
    w_query,
    w_key,
    w_value,
    w_output,
    second_gain,
    w_gate,
    w_up,
    w_down,
    out_grad,
):
    seqs, part_bytes = byte_ids.shape
    count = lax.axis_size("seq")
    seq_len = part_bytes * count
    width = w_query.shape[1]
    wide = w_gate.shape[1]
    half_bytes = seq_len // 2
    half = half_bytes // 2
    core = lax.axis_index("dp") % 2
    place = lax.axis_index("seq")

    chan = conv_weight.shape[0]
    small = jnp.concatenate(
        [conv_weight.T, score_vector[None], first_gain[None], second_gain[None]], axis=0
    ).astype(jnp.float32)
    small = jnp.pad(small, ((0, 0), (0, 128 - chan)))
    cells = jnp.stack([byte_ids, segments + 1], axis=1).reshape(seqs, -1, 128)
    shards = (w_query, w_key, w_value, w_output, w_gate, w_up, w_down, embed_table, small)
    if all(shard.shape[0] % 8 == 0 for shard in shards):
        full, held = forward_all(shards, cells, out_grad, half)
        wq, wk, wv, wo, wg, wu, wd, table, _ = full
        cot = held.cot.reshape(half, width)
        small_full, stream, normed_one, resid_one = held.small, held.stream, held.normed, held.resid
        coef, tap_table, rows, idm = held.coef, held.tap, held.rows, held.idm
        queries, keys, vals, attn_out, lse = held.qt, held.kt, held.vt, held.out, held.lse
        key_marks = held.marks[0]
        query_marks = key_marks[:half]
        normed_two = held.normed_two
    else:
        wq, wk, wv, wo, wg, wu, wd, table, small_full, cells, cot = gather_all(shards, cells, out_grad)
        cells = cells.reshape(count, 2, part_bytes).transpose(1, 0, 2).reshape(2, seq_len)
        ids_row, marks_row = cells[0], cells[1]
        cot = cot.reshape(half, width)
        small_full = small_full.reshape(lax.axis_size(ALL), 8, 128)[:, :, :chan].transpose(1, 0, 2).reshape(8, width)
        gain_two = small_full[KW + 2 : KW + 3]

        stream, normed_one, coef, tap_table, rows, idm = tok_forward(ids_row, marks_row, table, small_full, half)

        twins = [(i, i ^ 1) for i in range(lax.axis_size("dp"))]
        normed_other = lax.ppermute(normed_one, "dp", twins)
        token_marks = marks_row[::2]
        query_marks = lax.dynamic_slice_in_dim(token_marks, core * half, half, axis=0)
        other_marks = lax.dynamic_slice_in_dim(token_marks, (1 - core) * half, half, axis=0)
        key_marks = jnp.concatenate([query_marks, other_marks])
        queries = (mm_tt(wq, normed_one).astype(jnp.bfloat16) * HEAD_DIM ** (-0.5)).astype(jnp.bfloat16)
        normed_keys = jnp.concatenate([normed_one, normed_other], axis=0)
        keys = mm_tt(wk, normed_keys).astype(jnp.bfloat16)
        vals = mm_tt(wv, normed_keys).astype(jnp.bfloat16)
        attn_out, lse = attend_forward(queries, keys, vals, key_marks, query_marks)

        resid_one = stream + mm_tn(attn_out, wo)
        normed_two = rms_scale(resid_one, gain_two).astype(jnp.bfloat16)
    grad_gate, grad_up, grad_down, layer_rows, grad_output, attn_grad, resid_grad, gain_two_grad = feed_forward(
        normed_two, cot, resid_one, small_full, attn_out, wg, wu, wd, wo
    )
    layer_rows = layer_rows.reshape(seqs, part_bytes // 2, width)
    shapes = [(w.shape[0], w.shape[1], jnp.bfloat16) for w in shards[:8]] + [small.shape + (jnp.float32,)]
    out = backward_all(
        BackInputs(
            gate=grad_gate,
            up=grad_up,
            down=grad_down,
            output=grad_output,
            coef=coef,
            resid=resid_grad,
            qt=queries,
            kt=keys,
            vt=vals,
            got=attn_grad,
            out=attn_out,
            lse=lse,
            key_marks=key_marks[None],
            query_marks=query_marks[None],
            normed=normed_one,
            stream=stream,
            wq=wq,
            wk=wk,
            wv=wv,
            small=small_full,
            gain_two=gain_two_grad,
            table=table,
            tap=tap_table,
            rows=rows,
            idm=idm,
            layer=layer_rows,
        ),
        shapes,
    )
    done = results([out[9]] + list(out[:8]), out[8], chan)
    return (
        done[0],
        done[8],
        done[9].T,
        done[10][0],
        done[11][0],
        done[1],
        done[2],
        done[3],
        done[4],
        done[12][0],
        done[5],
        done[6],
        done[7],
    )


def solution(mesh):
    flat = P(ALL)
    rows = P(ALL, None)
    in_specs = (
        P("dp", "seq"),
        P("dp", "seq"),
        rows,
        rows,
        flat,
        flat,
        rows,
        rows,
        rows,
        rows,
        flat,
        rows,
        rows,
        rows,
        P("dp", "seq", None),
    )
    out_specs = (
        P("dp", "seq", None),
        rows,
        rows,
        flat,
        flat,
        rows,
        rows,
        rows,
        rows,
        flat,
        rows,
        rows,
        rows,
    )
    return jax.shard_map(
        per_device, mesh=mesh, in_specs=in_specs, out_specs=out_specs, check_vma=False
    )
```

```python
import functools
from typing import NamedTuple

import jax
import jax.numpy as jnp
from jax import lax
from jax.experimental import pallas as pl
from jax.experimental.pallas import tpu as pltpu
from jax.sharding import PartitionSpec as P

HEADS = 12
HEAD_DIM = 64
VOCAB = 256
MAXBLOCK = 4
KW = 5
DOCS = 8
ALL = ("dp", "seq")
VMEM_BYTES = 56 * 1024 * 1024


def mm(left, right):
    return jnp.dot(left, right, preferred_element_type=jnp.float32)


def mm_nt(left, right):
    return lax.dot_general(left, right, (((1,), (1,)), ((), ())), preferred_element_type=jnp.float32)


def mm_tn(left, right):
    return lax.dot_general(left, right, (((0,), (0,)), ((), ())), preferred_element_type=jnp.float32)


def mm_tt(left, right):
    return lax.dot_general(left, right, (((0,), (1,)), ((), ())), preferred_element_type=jnp.float32)


def rms_scale(values, gain):
    return values * lax.rsqrt(jnp.mean(values * values, axis=-1, keepdims=True) + 1e-06) * gain


def gelu_tanh(values):
    return jax.nn.gelu(values, approximate=True)


MESH = pl.DeviceIdType.MESH


def position():
    dp = lax.axis_index("dp")
    place = lax.axis_index("seq")
    lines = lax.axis_size("dp") // 4
    group = dp // 2
    return group // 2, group % 2, dp % 2, place, lines, lax.axis_size("seq")


def dp_of(y, x, core):
    return (y * 2 + x) * 2 + core


def meet(targets):
    barrier = pltpu.get_barrier_semaphore()
    for dp, place in targets:
        pl.semaphore_signal(barrier, inc=1, device_id=(dp, place), device_id_type=MESH)
    pl.semaphore_wait(barrier, len(targets))


def remote(src, dst, send_sem, recv_sem, dp, place):
    return pltpu.make_async_remote_copy(
        src_ref=src,
        dst_ref=dst,
        send_sem=send_sem,
        recv_sem=recv_sem,
        device_id=(dp, place),
        device_id_type=MESH,
    )


GATHER_ITEMS = (
    (7, 0, 0, 0),
    (8, 0, 0, 0),
    (0, 0, 0, 0),
    (2, 0, 0, 1),
    (1, 0, 0, 0),
    (3, 0, 0, 1),
    (4, 0, 0, 0),
    (5, 0, 0, 1),
    (6, 0, 1, 0),
    (6, 1, 1, 1),
)
GATHER_PHASES = ((0, 1), (2, 3, 4, 5), (6, 7), (8, 9))


def gather_kernel(arrays, *refs):
    ins = refs[:arrays]
    cells_in, cot_in = refs[arrays], refs[arrays + 1]
    outs = refs[arrays + 2 : 2 * arrays + 2]
    cells_out, cot_out = refs[2 * arrays + 2], refs[2 * arrays + 3]
    recv, recv_sib, send_z, send_x, send_y, send_sib, own_sem, cell_recv, cell_send, cot_recv, cot_send = refs[
        2 * arrays + 4 :
    ]
    y, x, core, place, lines, count = position()
    seqs = cells_in.shape[0]
    groups = lines * 2
    group = y * 2 + x
    dp = dp_of(y, x, core)
    twin = dp_of(y, x, 1 - core)
    side = dp_of(y, 1 - x, core)
    ahead = [(y + k) % lines for k in range(1, lines)]

    targets = [(twin, place), (side, place)]
    for k in range(1, count):
        targets += [(dp, (place + k) % count), (twin, (place + k) % count)]
    for other_y in ahead:
        targets.append((dp_of(other_y, x, core), place))
    meet(targets)

    def cell_copies(fn_remote, fn_local):
        for r in range(seqs):
            chip = seqs * core + r
            for c in range(2):
                home = (chip == place) & (core == c)

                @pl.when(home)
                def _():
                    fn_local(r, c)

                @pl.when(jnp.logical_not(home))
                def _():
                    fn_remote(r, c, chip)

    def cell_remote(r, c, chip):
        return remote(
            cells_in.at[r],
            cells_out.at[place],
            cell_send.at[r, c],
            cell_recv.at[place],
            dp_of(y, x, c),
            chip,
        )

    cell_copies(
        lambda r, c, chip: cell_remote(r, c, chip).start(),
        lambda r, c: pltpu.make_async_copy(
            cells_in.at[r], cells_out.at[place], cell_recv.at[place]
        ).start(),
    )

    def view(item):
        array, first, columns, _ = GATHER_ITEMS[item]
        in_ref, out_ref = ins[array], outs[array]
        if columns:
            cols = in_ref.shape[1] // 2
            lanes = pl.ds(first * cols, cols)
        else:
            lanes = pl.ds(0, in_ref.shape[1])
        return in_ref.at[:, lanes], out_ref, lanes

    def block(item, g, z):
        _, out_ref, lanes = view(item)
        return out_ref.at[(g * 2 + core) * count + z, :, lanes]

    def group_block(item, g, c):
        _, out_ref, lanes = view(item)
        return out_ref.at[pl.ds((g * 2 + c) * count, count), :, lanes]

    def many(item, blocks):
        _, out_ref, lanes = view(item)
        return out_ref.at[pl.ds(0, blocks), :, lanes]

    def arrived(item, g, z):
        dst = block(item, g, z)
        remote(dst, dst, send_x.at[item], recv.at[item, g * count + z], twin, place).wait_recv()

    def to_side(item, src, g, z):
        remote(src, block(item, g, z), send_x.at[item], recv.at[item, g * count + z], side, place).start()

    def to_lines(item, src, g, z):
        for other_y in ahead:
            remote(
                src,
                block(item, g, z),
                send_y.at[item],
                recv.at[item, g * count + z],
                dp_of(other_y, x, core),
                place,
            ).start()

    def to_z(item, src, z, step):
        return remote(
            src,
            block(item, group, z),
            send_z.at[item, z, step],
            recv.at[item, group * count + z],
            dp,
            place + 1 - 2 * step,
        )

    def to_twin(item, g):
        src = group_block(item, g, core)
        remote(src, src, send_sib.at[item], recv_sib.at[item, g], twin, place).start()

    def own_copy(item):
        return pltpu.make_async_copy(view(item)[0], block(item, group, place), own_sem.at[item])

    def first_own(items):
        for item in items:
            src = view(item)[0]

            @pl.when(place < count - 1)
            def _():
                to_z(item, src, place, 0).start()

            @pl.when(place > 0)
            def _():
                to_z(item, src, place, 1).start()

            own_copy(item).start()

    def first_sides(items):
        for item in items:
            src = view(item)[0]
            to_side(item, src, group, place)
            to_lines(item, src, group, place)

    def first_level(items):
        def step(s, carry):
            low = place - s
            high = place + s
            for item in items:

                @pl.when(low >= 0)
                def _():
                    arrived(item, group, low)
                    src = block(item, group, low)

                    @pl.when(place < count - 1)
                    def _():
                        to_z(item, src, low, 0).start()

                    to_side(item, src, group, low)
                    to_lines(item, src, group, low)

                @pl.when(high < count)
                def _():
                    arrived(item, group, high)
                    src = block(item, group, high)

                    @pl.when(place > 0)
                    def _():
                        to_z(item, src, high, 1).start()

                    to_side(item, src, group, high)
                    to_lines(item, src, group, high)

            return carry

        lax.fori_loop(1, count, step, 0)
        for item in items:
            own_copy(item).wait()
            to_twin(item, group)

    def second_level(items):
        def step(s, carry):
            z = (place + s) % count
            for item in items:
                if GATHER_ITEMS[item][3] == 0:
                    g = y * 2 + (1 - x)
                    arrived(item, g, z)
                    to_lines(item, block(item, g, z), g, z)
                else:
                    for other_y in ahead:
                        g = other_y * 2 + x
                        arrived(item, g, z)
                        to_side(item, block(item, g, z), g, z)
            return carry

        lax.fori_loop(0, count, step, 0)
        for item in items:
            if GATHER_ITEMS[item][3] == 0:
                to_twin(item, y * 2 + (1 - x))
            else:
                for other_y in ahead:
                    to_twin(item, other_y * 2 + x)

    def third_level(items):
        def rest(item):
            if GATHER_ITEMS[item][3] == 0:
                return [other_y * 2 + other_x for other_y in ahead for other_x in (x, 1 - x)]
            return [other_y * 2 + (1 - x) for other_y in [y] + ahead]

        def step(s, carry):
            z = (place + s) % count
            for item in items:
                for g in rest(item):
                    arrived(item, g, z)
            return carry

        lax.fori_loop(0, count, step, 0)
        for item in items:
            for g in rest(item):
                to_twin(item, g)

    def cot_copies(fn_remote, fn_local):
        for r in range(seqs):
            chip = seqs * core + r
            home = (chip == place) & (core == place // seqs)

            @pl.when(home)
            def _():
                fn_local(r)

            @pl.when(jnp.logical_not(home))
            def _():
                fn_remote(r, chip)

    def cot_remote(r, chip):
        return remote(
            cot_in.at[r],
            cot_out.at[place % seqs],
            cot_send.at[r],
            cot_recv.at[place % seqs],
            dp_of(y, x, place // seqs),
            chip,
        )

    phases = GATHER_PHASES
    for items in phases:
        first_own(items)
    first_sides(phases[0])
    first_level(phases[0])
    for k in range(1, len(phases)):
        first_sides(phases[k])
        first_level(phases[k])
        second_level(phases[k - 1])
        if k == 1:
            cot_copies(
                lambda r, chip: cot_remote(r, chip).start(),
                lambda r: pltpu.make_async_copy(
                    cot_in.at[r], cot_out.at[place % seqs], cot_recv.at[place % seqs]
                ).start(),
            )
        if k > 1:
            third_level(phases[k - 2])
    second_level(phases[-1])
    third_level(phases[-2])
    third_level(phases[-1])

    for item in range(len(GATHER_ITEMS)):
        for g in range(groups):
            dst = group_block(item, g, 1 - core)
            remote(dst, dst, send_sib.at[item], recv_sib.at[item, g], twin, place).wait_recv()
        tree = GATHER_ITEMS[item][3]

        def sent(blocks, sem):
            src = many(item, blocks)
            remote(src, src, sem, recv.at[item, 0], twin, place).wait_send()

        sent(count * (1 if tree == 0 else lines), send_x.at[item])
        sent(count * (lines - 1) * (2 if tree == 0 else 1), send_y.at[item])
        sent(count * groups, send_sib.at[item])

        def drain(z, carry):
            @pl.when((z <= place) & (place < count - 1))
            def _():
                to_z(item, block(item, group, z), z, 0).wait_send()

            @pl.when((z >= place) & (place > 0))
            def _():
                to_z(item, block(item, group, z), z, 1).wait_send()

            return carry

        lax.fori_loop(0, count, drain, 0)
    for q in range(count):
        dst = cells_out.at[q]
        remote(dst, dst, cell_send.at[0, 0], cell_recv.at[q], twin, place).wait_recv()
    for q in range(seqs):
        dst = cot_out.at[q]
        remote(dst, dst, cot_send.at[0], cot_recv.at[q], twin, place).wait_recv()
    cell_copies(lambda r, c, chip: cell_remote(r, c, chip).wait_send(), lambda r, c: None)
    cot_copies(lambda r, chip: cot_remote(r, chip).wait_send(), lambda r: None)


def gather_all(shards, cells, cot):
    count = lax.axis_size("seq")
    group_count = lax.axis_size(ALL)
    groups = group_count // (2 * count)
    items = len(GATHER_ITEMS)
    seqs = cells.shape[0]
    vmem = pl.BlockSpec(memory_space=pltpu.VMEM)
    hbm = pl.BlockSpec(memory_space=pltpu.HBM)
    shapes = [jax.ShapeDtypeStruct((group_count,) + s.shape, s.dtype) for s in shards]
    shapes.append(jax.ShapeDtypeStruct((count,) + cells.shape[1:], cells.dtype))
    shapes.append(jax.ShapeDtypeStruct(cot.shape, cot.dtype))
    dma = pltpu.SemaphoreType.DMA
    out = pl.pallas_call(
        functools.partial(gather_kernel, len(shards)),
        name="gather_all",
        out_shape=shapes,
        in_specs=[vmem] * (len(shards) + 2),
        out_specs=[hbm] * len(shapes),
        scratch_shapes=[
            dma((items, groups * count)),
            dma((items, groups)),
            dma((items, count, 2)),
            dma((items,)),
            dma((items,)),
            dma((items,)),
            dma((items,)),
            dma((count,)),
            dma((seqs, 2)),
            dma((seqs,)),
            dma((seqs,)),
        ],
        compiler_params=pltpu.CompilerParams(collective_id=0, has_side_effects=True),
    )(*shards, cells, cot)
    full = [o.reshape(-1, o.shape[2]) for o in out[: len(shards)]]
    return full + list(out[len(shards) :])


LEFT = 128
BAND = 256


def split_two(values):
    high = values.astype(jnp.bfloat16)
    return high, (values - high.astype(jnp.float32)).astype(jnp.bfloat16)


def lane_shift(row, by):
    by = by % row.shape[1]
    return row if by == 0 else pltpu.roll(row, row.shape[1] - by, 1)


def pool_rows(marks, core, half_bytes):
    lanes = lax.broadcasted_iota(jnp.int32, marks[0].shape, 1)
    inside, inverse = {}, {}
    for e in range(2):
        place = core * half_bytes + 2 * (lanes - LEFT) + e + 768
        third = lax.shift_right_logical(place * 21846, 16)
        remains = {2: place & 1, 3: place - 3 * third, 4: place & 3}
        shifted = {}
        for s in range(1 - MAXBLOCK, MAXBLOCK):
            f = (e + s) % 2
            shifted[s] = lane_shift(marks[f], (e + s - f) // 2) == marks[e]
        for b in range(2, MAXBLOCK + 1):
            number = jnp.ones(marks[0].shape, jnp.float32)
            for s in range(1 - b, b):
                if s == 0:
                    continue
                at = remains[b] + s
                on = (shifted[s] & (at >= 0) & (at < b)).astype(jnp.float32)
                inside[b, e, s] = on
                number = number + on
            inverse[b, e] = 1.0 / number
    return inside, inverse


def band_coefs(per_byte, inside, inverse):
    coefs = {}
    for o in range(1 - MAXBLOCK, MAXBLOCK + 1):
        total = None
        for e in range(2):
            s = o - e
            if not 1 - MAXBLOCK <= s < MAXBLOCK:
                continue
            for b in range(1, MAXBLOCK + 1):
                if b == 1:
                    if s != 0:
                        continue
                    term = per_byte[b, e]
                elif s == 0:
                    term = per_byte[b, e] * inverse[b, e]
                elif (b, e, s) in inside:
                    term = per_byte[b, e] * inverse[b, e] * inside[b, e, s]
                else:
                    continue
                total = term if total is None else total + term
        coefs[o] = total
    return coefs


def band_matrix(coefs, block):
    shape = (3 * BAND, BAND)
    delta = lax.broadcasted_iota(jnp.int32, shape, 0) - LEFT - 2 * lax.broadcasted_iota(jnp.int32, shape, 1)
    out = jnp.zeros(shape, jnp.float32)
    for o, row in coefs.items():
        part = row[0:1, LEFT + BAND * block : LEFT + BAND * (block + 1)]
        out = jnp.where(delta == o, part, out)
    return out


def tap_rows(tap):
    return pl.ds(pl.multiple_of(tap * VOCAB, VOCAB), VOCAB)


def fill_one_hot(one_hot, idm_ref):
    vocab = lax.broadcasted_iota(jnp.int32, (VOCAB, one_hot.shape[1]), 0)

    def step(tap, carry):
        hit = vocab == idm_ref[pl.ds(tap, 1)]
        one_hot[tap_rows(tap)] = hit.astype(jnp.float32).astype(jnp.bfloat16)
        return carry

    lax.fori_loop(0, KW, step, 0)


def tok_forward_kernel(ids_ref, marks_ref, table_ref, small_ref, stream_ref, normed_ref, coef_ref, tap_ref, rows_ref, idm_ref, one_hot):
    core = lax.axis_index("dp") % 2
    tokens = stream_ref.shape[0]
    half_bytes = 2 * tokens
    span = one_hot.shape[1]
    wide = span + 2 * LEFT
    first = pl.ds(pl.multiple_of(core * half_bytes, 128), wide)
    ids = ids_ref[:, first]
    marks = marks_ref[:, first]
    for tap in range(KW):
        by = tap - KW // 2
        same = (lane_shift(marks, by) == marks) & (marks > 0)
        idm_ref[tap : tap + 1] = jnp.where(same, lane_shift(ids, by), -1)[0:1, LEFT : LEFT + span]
    fill_one_hot(one_hot, idm_ref)

    score = jnp.broadcast_to(small_ref[KW : KW + 1], (8, small_ref.shape[1])).astype(jnp.bfloat16)
    scored = []
    for tap in range(KW):
        product = table_ref[...].astype(jnp.float32) * small_ref[tap : tap + 1]
        high, low = split_two(product)
        tap_ref[tap * VOCAB : (tap + 1) * VOCAB] = high
        scored.append(mm_nt(score, high) + mm_nt(score, low))
    high, low = split_two(jnp.concatenate(scored, axis=1))
    u_row = mm(high, one_hot[...]) + mm(low, one_hot[...])

    high = u_row.astype(jnp.bfloat16).astype(jnp.float32)
    marks_here = marks[:, LEFT : LEFT + span].astype(jnp.float32)
    packed = jnp.concatenate([marks_here, high, u_row - high, jnp.zeros_like(high)], axis=0).astype(jnp.bfloat16)
    shape = (span, wide // 2)
    twice = 2 * lax.broadcasted_iota(jnp.int32, shape, 1) - lax.broadcasted_iota(jnp.int32, shape, 0) - LEFT
    marks_of, u_of = [], []
    for e in range(2):
        pick = (twice == -e).astype(jnp.float32).astype(jnp.bfloat16)
        apart = mm(packed, pick)
        marks_of.append(apart[0:8])
        u_of.append(apart[8:16] + apart[16:24])

    inside, inverse = pool_rows(marks_of, core, half_bytes)
    prob = {}
    for e in range(2):
        shifted = {}
        for s in range(1 - MAXBLOCK, MAXBLOCK):
            f = (e + s) % 2
            shifted[s] = lane_shift(u_of[f], (e + s - f) // 2)
        scores = [u_of[e]]
        for b in range(2, MAXBLOCK + 1):
            total = u_of[e]
            for s in range(1 - b, b):
                if s != 0:
                    total = total + inside[b, e, s] * shifted[s]
            scores.append(total * inverse[b, e])
        top = scores[0]
        for value in scores[1:]:
            top = jnp.maximum(top, value)
        expo = [jnp.exp(value - top) for value in scores]
        whole = expo[0] + expo[1] + expo[2] + expo[3]
        for b in range(1, MAXBLOCK + 1):
            prob[b, e] = expo[b - 1] / whole
            rows_ref[2 * b + e : 2 * b + e + 1] = prob[b, e][0:1]
        rows_ref[e : e + 1] = marks_of[e][0:1]
    coefs = band_coefs({key: 0.5 * value for key, value in prob.items()}, inside, inverse)
    gain = small_ref[KW + 1 : KW + 2]
    for i in range(tokens // BAND):
        matrix = band_matrix(coefs, i).astype(jnp.bfloat16)
        lanes = slice(i * BAND, (i + 1) * BAND)
        part = mm(one_hot[:, 2 * i * BAND : (2 * i + 3) * BAND], matrix).astype(jnp.bfloat16)
        coef_ref[:, lanes] = part
        stream = mm_tn(part, tap_ref[...])
        stream_ref[lanes] = stream
        scale = lax.rsqrt(jnp.mean(stream * stream, axis=-1, keepdims=True) + 1e-06)
        normed_ref[lanes] = (stream * scale * gain).astype(jnp.bfloat16)


def tok_forward(ids_row, marks_row, table, small, tokens):
    width = table.shape[1]
    span = 2 * tokens + 2 * LEFT
    wide = span + 2 * LEFT

    def padded(row, fill):
        row = jnp.pad(row, (2 * LEFT, 2 * LEFT), constant_values=fill)
        return jnp.broadcast_to(row[None], (8, row.shape[0]))

    return pl.pallas_call(
        tok_forward_kernel,
        name="tok_forward",
        out_shape=[
            jax.ShapeDtypeStruct((tokens, width), jnp.float32),
            jax.ShapeDtypeStruct((tokens, width), jnp.bfloat16),
            jax.ShapeDtypeStruct((KW * VOCAB, tokens), jnp.bfloat16),
            jax.ShapeDtypeStruct((KW * VOCAB, width), jnp.bfloat16),
            jax.ShapeDtypeStruct((16, wide // 2), jnp.float32),
            jax.ShapeDtypeStruct((8, span), jnp.int32),
        ],
        scratch_shapes=[pltpu.VMEM((KW * VOCAB, span), jnp.bfloat16)],
        compiler_params=pltpu.CompilerParams(vmem_limit_bytes=VMEM_BYTES),
    )(padded(ids_row, -1), padded(marks_row, 0), table, small)


def tok_backward_body(grad16, coef_ref, ref, own, tick, take):
    tap_ref, rows_ref, idm_ref, table_ref, small_ref = ref.tap, ref.rows, ref.idm, ref.table, ref.small
    one_hot = own.one_hot
    core = lax.axis_index("dp") % 2
    tokens = grad16.shape[0]
    fill_one_hot(one_hot, idm_ref)
    tick()

    def whole_row(k):
        return jnp.broadcast_to(rows_ref[k : k + 1], (8, rows_ref.shape[1]))

    marks_of = [whole_row(0), whole_row(1)]
    inside, inverse = pool_rows(marks_of, core, 2 * tokens)
    shape = (3 * BAND, BAND)
    delta = lax.broadcasted_iota(jnp.int32, shape, 0) - LEFT - 2 * lax.broadcasted_iota(jnp.int32, shape, 1)
    through = mm_nt(tap_ref[...], grad16).astype(jnp.bfloat16)
    tick()
    diag = {o: [] for o in range(1 - MAXBLOCK, MAXBLOCK + 1)}
    edge = jnp.zeros((8, LEFT), jnp.float32)
    for i in range(tokens // BAND):
        near = mm_tn(one_hot[:, 2 * i * BAND : (2 * i + 3) * BAND], through[:, i * BAND : (i + 1) * BAND])
        for o in diag:
            total = jnp.sum(jnp.where(delta == o, near, 0.0), axis=0, keepdims=True)
            diag[o].append(jnp.broadcast_to(total, (8, BAND)))
        tick()
    diag = {o: jnp.concatenate([edge] + parts + [edge], axis=1) for o, parts in diag.items()}
    size_grad = {}
    for e in range(2):
        grads = [0.5 * diag[e]]
        for b in range(2, MAXBLOCK + 1):
            total = diag[e]
            for s in range(1 - b, b):
                if s != 0:
                    total = total + inside[b, e, s] * diag[s + e]
            grads.append(0.5 * total * inverse[b, e])
        probs = [whole_row(2 * b + e) for b in range(1, MAXBLOCK + 1)]
        mean = probs[0] * grads[0]
        for p, g in zip(probs[1:], grads[1:]):
            mean = mean + p * g
        for b in range(1, MAXBLOCK + 1):
            size_grad[b, e] = probs[b - 1] * (grads[b - 1] - mean)
    coefs = band_coefs(size_grad, inside, inverse)
    picked = None
    for i in range(tokens // BAND):
        matrix = band_matrix(coefs, i).astype(jnp.bfloat16)
        part = mm(one_hot[:, 2 * i * BAND : (2 * i + 3) * BAND], matrix)
        part = jnp.sum(part, axis=1, keepdims=True)
        picked = part if picked is None else picked + part
        tick()
    own.picked[...] = picked
    score = small_ref[KW : KW + 1]
    table_grad = own.wide.at[0:VOCAB]
    table_grad[...] = jnp.zeros(table_grad.shape, jnp.float32)
    own.rows[...] = jnp.zeros_like(own.rows)
    tap_tasks = take(KW - 1)

    def step(tap, carry):
        here = own.picked[tap_rows(tap)]
        table = table_ref[...].astype(jnp.float32)
        part = mm(coef_ref[tap_rows(tap)], grad16) + here * score
        taps = small_ref[pl.ds(tap, 1)]
        table_grad[...] += part * taps
        own.rows[pl.ds(tap, 1)] = jnp.sum(part * table, axis=0, keepdims=True)
        own.rows[KW : KW + 1] += jnp.sum(table * here, axis=0, keepdims=True) * taps
        tap_tasks(tap)
        return carry

    lax.fori_loop(0, KW, step, 0)


CHUNK = 256


def pair_rows(ref, h):
    values = ref[...]
    rows = lax.broadcasted_iota(jnp.int32, values.shape, 0)
    return jnp.where((rows // HEAD_DIM) == h, values, jnp.zeros_like(values))


def fill_bias(bias, key_marks, query_marks):
    def apart(marks):
        rows = lax.broadcasted_iota(jnp.int32, (2 * DOCS, marks.shape[1]), 0)
        return (rows == marks[...]).astype(jnp.float32).astype(jnp.bfloat16)

    queries = apart(query_marks)
    for c in range(key_marks.shape[1] // CHUNK):
        keys = slice(c * CHUNK, (c + 1) * CHUNK)
        same = mm_tn(apart(key_marks.at[:, keys]), queries)
        bias[keys] = jnp.where(same > 0.5, 0.0, -1e30).astype(bias.dtype)


def attend_forward_kernel(qt_ref, kt_ref, vt_ref, key_marks, query_marks, out_ref, lse_ref, bias, scores):
    @pl.when(pl.program_id(0) == 0)
    def _():
        fill_bias(bias, key_marks, query_marks)

    keys = kt_ref[...].T
    chunks = keys.shape[0] // CHUNK
    for h in range(2):
        query = pair_rows(qt_ref, h)
        top = None
        for c in range(chunks):
            rows = slice(c * CHUNK, (c + 1) * CHUNK)
            part = mm(keys[rows], query) + bias[rows]
            scores[h, rows] = part
            high = jnp.max(part, axis=0, keepdims=True)
            top = high if top is None else jnp.maximum(top, high)
        total = None
        out = None
        for c in range(chunks):
            rows = slice(c * CHUNK, (c + 1) * CHUNK)
            expo = jnp.exp(scores[h, rows] - top)
            part = jnp.sum(expo, axis=0, keepdims=True)
            total = part if total is None else total + part
            part = mm(vt_ref[h * HEAD_DIM : (h + 1) * HEAD_DIM, rows], expo.astype(jnp.bfloat16))
            out = part if out is None else out + part
        out_ref[h * HEAD_DIM : (h + 1) * HEAD_DIM] = (out / total).astype(jnp.bfloat16)
        lse_ref[0, h : h + 1] = top + jnp.log(total)


def attend_forward(qt, kt, vt, key_marks, query_marks):
    width, tokens = qt.shape
    keys = kt.shape[1]
    pairs = width // 128
    rows = lambda size: pl.BlockSpec((128, size), lambda i: (i, 0))
    whole = lambda shape: pl.BlockSpec(shape, lambda i: (0, 0))
    return pl.pallas_call(
        attend_forward_kernel,
        name="attend_forward",
        grid=(pairs,),
        in_specs=[rows(tokens), rows(keys), rows(keys), whole((1, keys)), whole((1, tokens))],
        out_specs=[rows(tokens), pl.BlockSpec((1, 2, tokens), lambda i: (i, 0, 0))],
        out_shape=[
            jax.ShapeDtypeStruct((width, tokens), jnp.bfloat16),
            jax.ShapeDtypeStruct((pairs, 2, tokens), jnp.float32),
        ],
        scratch_shapes=[
            pltpu.VMEM((keys, tokens), jnp.float32),
            pltpu.VMEM((2, keys, tokens), jnp.float32),
        ],
        compiler_params=pltpu.CompilerParams(vmem_limit_bytes=VMEM_BYTES),
    )(qt, kt, vt, key_marks[None], query_marks[None])


def attend_backward_pair(qt, kt, vt, got_ref, out, lse_ref, bias, dq, dk_own, dv_own, dk_away, dv_away):
    keys = kt[...].T
    vals = vt[...].T
    chunks = keys.shape[0] // CHUNK
    for h in range(2):
        own = slice(h * HEAD_DIM, (h + 1) * HEAD_DIM)
        query = pair_rows(qt, h)
        got = pair_rows(got_ref, h)
        dots = jnp.sum(
            got_ref[own].astype(jnp.float32) * out[own].astype(jnp.float32), axis=0, keepdims=True
        )
        lse = lse_ref[h : h + 1]
        query_grad = None
        for c in range(chunks):
            rows = slice(c * CHUNK, (c + 1) * CHUNK)
            soft = jnp.exp(mm(keys[rows], query) + (bias[rows].astype(jnp.float32) - lse))
            change = soft * (mm(vals[rows], got) - dots)
            soft16 = soft.astype(jnp.bfloat16)
            change16 = change.astype(jnp.bfloat16)
            first = c < chunks // 2
            to = slice((c % (chunks // 2)) * CHUNK, (c % (chunks // 2) + 1) * CHUNK)
            (dv_own if first else dv_away)[own, to] = mm_nt(got_ref[own], soft16).astype(jnp.bfloat16)
            (dk_own if first else dk_away)[own, to] = mm_nt(qt[own], change16).astype(jnp.bfloat16)
            part = mm(kt[own, rows], change16)
            query_grad = part if query_grad is None else query_grad + part
        dq[own] = (query_grad * HEAD_DIM ** (-0.5)).astype(jnp.bfloat16)


SCATTER_ITEMS = (
    (5, 1, 2, 1),
    (3, 0, 1, 0),
    (6, 0, 1, 0),
    (5, 0, 2, 1),
    (4, 1, 2, 1),
    (4, 0, 2, 0),
    (0, 0, 1, 1),
    (1, 0, 1, 1),
    (2, 0, 1, 0),
    (7, 0, 1, 1),
    (8, 0, 1, 1),
)
FIRST_ITEMS = 6
SCHEDULE = (
    (
        (0, 0), (0, 1),
    ),
    (
        (0, 2), (0, 3), (0, 4),
    ),
    (
        (1, 0), (1, 1), (0, 5),
    ),
    (),
    (),
    ((1, 3),),
    ((1, 2),),
    ((1, 4),),
    (
        (2, 0), (2, 1), (0, 6),
    ),
    ((0, 7),),
    ((0, 8),),
    (
        (3, 0), (3, 1), (2, 2), (1, 5),
    ),
    (),
    (),
    (
        (4, 0), (2, 3), (4, 1),
    ),
    ((1, 6),),
    (
        (5, 0), (5, 1), (3, 2), (2, 4),
    ),
    (),
    ((3, 3),),
    (),
    ((1, 7),),
    (),
    (
        (4, 2), (3, 4), (1, 8), (0, 9), (0, 10), (4, 3),
        (2, 5), (2, 6), (5, 2), (4, 4), (5, 3), (2, 8),
        (5, 4), (2, 7), (3, 5), (1, 9), (1, 10), (3, 6),
        (4, 5), (2, 9), (2, 10), (3, 8), (4, 6), (5, 5),
        (3, 7), (5, 6), (4, 8), (3, 9), (3, 10), (4, 7),
        (5, 8), (4, 9), (4, 10), (5, 7), (5, 9), (5, 10),
    ),
)


class Scatter:
    def __init__(self, sources, outs, layer_in, layer_out, buffers, sems):
        items = len(SCATTER_ITEMS)
        self.sources, self.outs = sources, outs
        self.layer_in, self.layer_out = layer_in, layer_out
        self.sems = sems
        self.y, self.x, self.core, self.place, self.lines, self.count = position()
        y, x, core = self.y, self.x, self.core
        self.own = list(buffers[:FIRST_ITEMS])
        for array, _, _, _ in SCATTER_ITEMS[FIRST_ITEMS:]:
            self.own.append(sources[array].at[:, :, core])
        buffers = buffers[FIRST_ITEMS:]
        self.from_twin, self.first_in, self.second_in, self.line_in = [
            buffers[k * items : (k + 1) * items] for k in range(4)
        ]
        self.dp = dp_of(y, x, core)
        self.twin = dp_of(y, x, 1 - core)
        self.side = dp_of(y, 1 - x, core)
        self.ahead = [(y + k) % self.lines for k in range(1, self.lines)]

    def meet(self):
        targets = [(self.twin, self.place), (self.side, self.place)]
        for k in range(1, self.count):
            other = (self.place + k) % self.count
            targets += [(self.dp, other), (self.twin, other)]
        for other_y in self.ahead:
            targets.append((dp_of(other_y, self.x, self.core), self.place))
        meet(targets)

    def order(self, item):
        return SCATTER_ITEMS[item][3]

    def columns(self, item):
        array, part, parts, _ = SCATTER_ITEMS[item]
        cols = self.sources[array].shape[-1] // parts
        return pl.ds(part * cols, cols)

    def to_twin(self, item):
        src = self.sources[SCATTER_ITEMS[item][0]].at[:, :, 1 - self.core, :, :, self.columns(item)]
        sems = self.sems
        return remote(
            src, self.from_twin[item], sems.twin_send.at[item], sems.twin_recv.at[item], self.twin, self.place
        )

    def own_in(self, item):
        src = self.sources[SCATTER_ITEMS[item][0]].at[:, :, self.core, :, :, self.columns(item)]
        return pltpu.make_async_copy(src, self.own[item], self.sems.own.at[item])

    def x_copy(self, item):
        own = self.own[item]
        if self.order(item) == 0:
            src, dst = own.at[self.y, 1 - self.x], self.second_in[item].at[0]
        else:
            src, dst = own.at[:, 1 - self.x], self.first_in[item]
        return remote(
            src, dst, self.sems.x_send.at[item], self.sems.x_recv.at[item], self.side, self.place
        )

    def y_copy(self, item, k):
        other_y = self.ahead[k]
        own = self.own[item]
        if self.order(item) == 0:
            src, dst = own.at[other_y], self.first_in[item].at[k]
        else:
            src, dst = own.at[other_y, self.x], self.second_in[item].at[k]
        return remote(
            src,
            dst,
            self.sems.y_send.at[item, k],
            self.sems.y_recv.at[item, k],
            dp_of(other_y, self.x, self.core),
            self.place,
        )

    def stage_begin(self, item):
        self.to_twin(item).start()
        if item < FIRST_ITEMS:
            self.own_in(item).start()

    def stage_core(self, item):
        if item < FIRST_ITEMS:
            self.own_in(item).wait()
        self.to_twin(item).wait_recv()
        own, came = self.own[item], self.from_twin[item]

        def step(i, carry):
            a, b, z = i // (2 * self.count), i // self.count % 2, i % self.count
            own[a, b, z] = plus(own[a, b, z], came[a, b, z])
            return carry

        lax.fori_loop(0, 2 * self.lines * self.count, step, 0)
        if self.order(item) == 0:
            for k in range(self.lines - 1):
                self.y_copy(item, k).start()
        else:
            self.x_copy(item).start()

    def stage_first(self, item):
        own, came = self.own[item], self.first_in[item]
        y, x, lines = self.y, self.x, self.lines
        if self.order(item) == 0:
            for k in range(lines - 1):
                self.y_copy(item, k).wait_recv()

            def step(i, carry):
                b, z = i // self.count, i % self.count
                total = own[y, b, z]
                for k in range(lines - 1):
                    total = plus(total, came[k, b, z])
                own[y, b, z] = total
                return carry

            lax.fori_loop(0, 2 * self.count, step, 0)
            self.x_copy(item).start()
        else:
            self.x_copy(item).wait_recv()

            def step(i, carry):
                a, z = i // self.count, i % self.count
                own[a, x, z] = plus(own[a, x, z], came[a, z])
                return carry

            lax.fori_loop(0, lines * self.count, step, 0)
            for k in range(lines - 1):
                self.y_copy(item, k).start()

    def mine(self, item, z):
        return self.own[item].at[self.y, self.x, z]

    def z_copy(self, item, z, way):
        return remote(
            self.mine(item, z),
            self.line_in[item].at[way, z],
            self.sems.z_send.at[item, z],
            self.sems.z_recv.at[item, way, z],
            self.dp,
            self.place + 1 - 2 * way,
        )

    def z_forward(self, item, way, first):
        def step(z, carry):
            @pl.when((z - self.place) * (1 - 2 * way) > 0)
            def _():
                if not first:
                    self.z_copy(item, z, way).wait_recv()
                    ref = self.mine(item, z)
                    ref[...] = plus(ref[...], self.line_in[item][way, z])
                self.z_copy(item, z, way).start()

            return carry

        lax.fori_loop(0, self.count, step, 0)

    def stage_second(self, item):
        own, came = self.own[item], self.second_in[item]
        y, x = self.y, self.x
        if self.order(item) == 0:
            self.x_copy(item).wait_recv()
        else:
            for k in range(self.lines - 1):
                self.y_copy(item, k).wait_recv()

        def step(z, carry):
            total = own[y, x, z]
            for k in range(came.shape[0]):
                total = plus(total, came[k, z])
            own[y, x, z] = total
            return carry

        lax.fori_loop(0, self.count, step, 0)

        self.each_way(lambda way, depth: pl.when(depth == 0)(lambda: self.z_forward(item, way, True)))

    def each_way(self, body):
        def step(way, carry):
            body(way, self.place + way * (self.count - 1 - 2 * self.place))
            return carry

        lax.fori_loop(0, 2, step, 0)

    def stage_hop(self, hop, item):
        self.each_way(lambda way, depth: pl.when(depth == hop)(lambda: self.z_forward(item, way, False)))

    def stage_last(self, item):
        out = self.outs[SCATTER_ITEMS[item][0]]
        columns = self.columns(item)
        place = self.place
        out[:, columns] = self.mine(item, place)[...].astype(jnp.float32)

        def add(way):
            self.z_copy(item, place, way).wait_recv()
            out[:, columns] += self.line_in[item][way, place].astype(jnp.float32)

        self.each_way(lambda way, depth: pl.when(depth > 0)(lambda: add(way)))

    def layer_copies(self, fn_remote, fn_local):
        seqs = self.layer_in.shape[0]
        for k in range(seqs):
            chip = seqs * self.core + k
            home = (chip == self.place) & (self.core == self.place // seqs)

            @pl.when(home)
            def _():
                fn_local(k)

            @pl.when(jnp.logical_not(home))
            def _():
                fn_remote(k, chip)

    def layer_remote(self, k, chip):
        seqs = self.layer_in.shape[0]
        row = self.place % seqs
        return remote(
            self.layer_in.at[k],
            self.layer_out.at[row],
            self.sems.layer_send.at[k],
            self.sems.layer_recv.at[row],
            dp_of(self.y, self.x, self.place // seqs),
            chip,
        )

    def layer_start(self):
        row = self.place % self.layer_in.shape[0]
        self.layer_copies(
            lambda k, chip: self.layer_remote(k, chip).start(),
            lambda k: pltpu.make_async_copy(
                self.layer_in.at[k], self.layer_out.at[row], self.sems.layer_recv.at[row]
            ).start(),
        )

    def stage_hop_one(self, item):
        self.stage_hop(1, item)

    def stage_hops(self, item):
        for hop in range(2, self.count - 1):
            self.stage_hop(hop, item)

    def stages(self):
        return (
            self.stage_core,
            self.stage_first,
            self.stage_second,
            self.stage_hop_one,
            self.stage_hops,
            self.stage_last,
        )

    def finish(self):
        for item in range(len(SCATTER_ITEMS)):
            self.to_twin(item).wait_send()
            self.x_copy(item).wait_send()
            for k in range(self.lines - 1):
                self.y_copy(item, k).wait_send()

            def drain(z, carry):
                @pl.when(z > self.place)
                def _():
                    self.z_copy(item, z, 0).wait_send()

                @pl.when(z < self.place)
                def _():
                    self.z_copy(item, z, 1).wait_send()

                return carry

            lax.fori_loop(0, self.count, drain, 0)
        for r in range(self.layer_in.shape[0]):
            dst = self.layer_out.at[r]
            remote(
                dst, dst, self.sems.layer_send.at[0], self.sems.layer_recv.at[r], self.twin, self.place
            ).wait_recv()
        self.layer_copies(lambda k, chip: self.layer_remote(k, chip).wait_send(), lambda k: None)


class ScatterSems(NamedTuple):
    own: object
    twin_send: object
    twin_recv: object
    x_send: object
    x_recv: object
    y_send: object
    y_recv: object
    z_send: object
    z_recv: object
    layer_send: object
    layer_recv: object


def plus(left, right):
    return left + right


def scatter_scratch(shapes, lines, count, seqs):
    items = len(SCATTER_ITEMS)
    own, first_in, second_in, line_in = [], [], [], []
    for array, _, parts, order in SCATTER_ITEMS:
        rows, cols, kind = shapes[array]
        cols = cols // parts
        own.append(pltpu.VMEM((lines, 2, count, rows, cols), kind))
        if order == 0:
            first_in.append(pltpu.VMEM((lines - 1, 2, count, rows, cols), kind))
            second_in.append(pltpu.VMEM((1, count, rows, cols), kind))
        else:
            first_in.append(pltpu.VMEM((lines, count, rows, cols), kind))
            second_in.append(pltpu.VMEM((lines - 1, count, rows, cols), kind))
        line_in.append(pltpu.VMEM((2, count, rows, cols), kind))
    dma = pltpu.SemaphoreType.DMA
    sems = [dma((FIRST_ITEMS,))] + [dma((items,))] * 4
    sems += [dma((items, lines - 1))] * 2 + [dma((items, count)), dma((items, 2, count))]
    sems += [dma((seqs,))] * 2
    return own[:FIRST_ITEMS] + own + first_in + second_in + line_in, sems


class BackInputs(NamedTuple):
    gate: object
    up: object
    down: object
    output: object
    coef: object
    resid: object
    layer: object
    qt: object
    kt: object
    vt: object
    got: object
    out: object
    normed: object
    stream: object
    tap: object
    wq: object
    wk: object
    wv: object
    lse: object
    key_marks: object
    small: object
    gain_two: object
    table: object
    rows: object
    idm: object


class BackWork(NamedTuple):
    grads: object
    away: object
    came: object
    wide: object
    one_hot: object
    src_qkv: object
    src_table: object
    src_small: object
    swap_send: object
    swap_recv: object
    coef_sem: object
    resid_sem: object
    load_sem: object
    wqkv: object
    picked: object
    rows: object


LATE_LOADS = 8


def backward_kernel(*refs):
    ref = BackInputs(*refs[: len(BackInputs._fields)])
    late_refs = refs[-LATE_LOADS:]
    refs = refs[:-LATE_LOADS]
    late = slice(7, 7 + LATE_LOADS)
    waiting = ref[late]
    ref = ref._replace(**dict(zip(ref._fields[late], late_refs)))
    rest = refs[len(BackInputs._fields) :]
    outs, layer_out = rest[:9], rest[9]
    rest = rest[10:]
    held = FIRST_ITEMS + 4 * len(SCATTER_ITEMS)
    buffers, rest = rest[:held], rest[held:]
    sems = ScatterSems(*rest[: len(ScatterSems._fields)])
    own = BackWork(*rest[len(ScatterSems._fields) :])
    sources = (
        own.src_qkv.at[0],
        own.src_qkv.at[1],
        own.src_qkv.at[2],
        ref.output,
        ref.gate,
        ref.up,
        ref.down,
        own.src_table,
        own.src_small,
    )
    scatter = Scatter(sources, outs, ref.layer, layer_out, buffers, sems)
    stages = scatter.stages()
    width, tokens = ref.qt.shape
    pairs = width // 128
    bias = own.one_hot.at[0 : ref.kt.shape[1], 0:tokens]
    scatter.meet()
    for item in range(FIRST_ITEMS):
        scatter.stage_begin(item)

    queue = [[functools.partial(stages[stage], item) for stage, item in group] for group in SCHEDULE]

    def tick():
        for task in queue.pop(0):
            task()

    loads = []
    for k in range(LATE_LOADS):
        loads.append(pltpu.make_async_copy(waiting[k], late_refs[k], own.load_sem.at[k]))
        loads[k].start()
    for k, weight in enumerate((ref.wq, ref.wk, ref.wv)):
        part = own.wqkv.at[k * width : (k + 1) * width]
        loads.append(pltpu.make_async_copy(weight, part, own.load_sem.at[LATE_LOADS + k]))
        loads[-1].start()
    scatter.layer_start()
    tick()
    fill_bias(bias, ref.key_marks, ref.key_marks.at[:, 0:tokens])
    for load in loads[:5]:
        load.wait()

    def swap(i, which):
        rows = pl.ds(pl.multiple_of(which * width + 128 * i, 128), 128)
        return remote(
            own.away.at[rows],
            own.came.at[rows],
            own.swap_send.at[which, i],
            own.swap_recv.at[which, i],
            scatter.twin,
            scatter.place,
        )

    ticks = [queue.pop(0) for _ in range(pairs)]

    def pair_step(i, carry):
        at = pl.ds(pl.multiple_of(128 * i, 128), 128)
        attend_backward_pair(
            ref.qt.at[at],
            ref.kt.at[at],
            ref.vt.at[at],
            ref.got.at[at],
            ref.out.at[at],
            ref.lse.at[i],
            bias,
            own.grads.at[at],
            own.grads.at[pl.ds(pl.multiple_of(width + 128 * i, 128), 128)],
            own.grads.at[pl.ds(pl.multiple_of(2 * width + 128 * i, 128), 128)],
            own.away.at[at],
            own.away.at[pl.ds(pl.multiple_of(width + 128 * i, 128), 128)],
        )
        swap(i, 0).start()
        swap(i, 1).start()
        for k, group in enumerate(ticks):
            if group:

                @pl.when(i == k)
                def _():
                    for task in group:
                        task()

        return carry

    lax.fori_loop(0, pairs, pair_step, 0)

    for load in loads[5:]:
        load.wait()
    wide = own.wide
    normed_t = own.one_hot.at[0:width, 0:tokens]
    normed_t[...] = ref.normed[...].T
    coef = own.came.at[0 : KW * VOCAB]

    def coef_copy():
        return pltpu.make_async_copy(ref.coef, coef, own.coef_sem)

    def hand_out(source):
        lines, _, _, count, size, _ = source.shape
        total = lines * 4 * count

        if size % 8:
            for o in range(total):
                where = (o // (4 * count), o // (2 * count) % 2, o // count % 2, o % count)
                source[where] = wide[size * o : size * (o + 1)].astype(source.dtype)
        else:

            def step(o, carry):
                where = (o // (4 * count), o // (2 * count) % 2, o // count % 2, o % count)
                source[where] = wide[pl.ds(pl.multiple_of(size * o, 8), size)].astype(source.dtype)
                return carry

            lax.fori_loop(0, total, step, 0)

    def take(count):
        groups = [queue.pop(0) for _ in range(count)]

        def run(i):
            for k, group in enumerate(groups):
                if group:

                    @pl.when(i == k)
                    def _():
                        for task in group:
                            task()

        return run

    def third(i):
        return pl.ds(pl.multiple_of(i * width, width), width)

    def add_halves():
        def add_half(j, carry):
            which, i = j // pairs, j % pairs
            swap(i, which).wait_recv()
            rows = pl.ds(pl.multiple_of(which * width + 128 * i, 128), 128)
            at = pl.ds(pl.multiple_of((which + 1) * width + 128 * i, 128), 128)
            own.grads[at] = plus(own.grads[at], own.came[rows])
            return carry

        lax.fori_loop(0, 2 * pairs, add_half, 0)
        coef_copy().start()

    weight_tasks = take(3)

    def weight_step(i, carry):
        pl.when(i == 1)(add_halves)
        wide[...] = mm_nt(normed_t[...], own.grads[third(i)])
        hand_out(own.src_qkv.at[i])
        for k in range(3):
            pl.when(i == k)(functools.partial(scatter.stage_begin, FIRST_ITEMS + k))
        weight_tasks(i)
        return carry

    lax.fori_loop(0, 3, weight_step, 0)

    norm_tasks = take(1)
    wide[:, 0:tokens] = jnp.zeros((width, tokens), jnp.float32)

    def norm_step(i, carry):
        wide[:, 0:tokens] += mm(own.wqkv[third(i)], own.grads[third(i)])
        norm_tasks(i - 1)
        return carry

    lax.fori_loop(0, 3, norm_step, 0)
    normed_grad = wide[:, 0:tokens].T
    resid_copy = pltpu.make_async_copy(ref.resid, wide.at[0:tokens], own.resid_sem)
    resid_copy.start()
    stream = ref.stream[...]
    gain = ref.small[KW + 1 : KW + 2]
    scale = lax.rsqrt(jnp.mean(stream * stream, axis=-1, keepdims=True) + 1e-06)
    gain_grad = jnp.sum(normed_grad * stream * scale, axis=0, keepdims=True)
    scaled = normed_grad * gain
    inner = jnp.mean(scaled * stream, axis=-1, keepdims=True)
    resid_copy.wait()
    grad16 = (wide[0:tokens] + scale * scaled - stream * (scale * scale * scale * inner)).astype(jnp.bfloat16)
    tick()
    coef_copy().wait()
    tok_backward_body(grad16, coef, ref, own, tick, take)
    hand_out(own.src_table)
    scatter.stage_begin(FIRST_ITEMS + 3)
    rows = jnp.concatenate([own.rows[0 : KW + 1], gain_grad, ref.gain_two[...]], axis=0)
    source = own.src_small
    lines, _, _, count, _, _ = source.shape
    total = lines * 4 * count
    for o in range(total):
        where = (o // (4 * count), o // (2 * count) % 2, o // count % 2, o % count)
        source[where] = lane_shift(rows, o * (width // total))[:, 0:128]
    scatter.stage_begin(FIRST_ITEMS + 4)
    while queue:
        tick()
    scatter.finish()

    def drain(i, carry):
        swap(i, 0).wait_send()
        swap(i, 1).wait_send()
        return carry

    lax.fori_loop(0, pairs, drain, 0)


def backward_all(arrays, shapes):
    count = lax.axis_size("seq")
    lines = lax.axis_size("dp") // 4
    total = lines * 4 * count
    vmem = pl.BlockSpec(memory_space=pltpu.VMEM)
    hbm = pl.BlockSpec(memory_space=pltpu.HBM)
    layer = arrays.layer
    width, tokens = arrays.qt.shape
    out_shape = [jax.ShapeDtypeStruct(shape[:2], jnp.float32) for shape in shapes]
    out_shape.append(jax.ShapeDtypeStruct(layer.shape, layer.dtype))
    buffers, sems = scatter_scratch(shapes, lines, count, layer.shape[0])
    views = list(arrays)
    for k in range(4):
        grad = arrays[k]
        views[k] = grad.reshape(lines, 2, 2, count, grad.shape[0] // total, grad.shape[1])

    def source(index):
        rows, cols, kind = shapes[index]
        return pltpu.VMEM((lines, 2, 2, count, rows, cols), kind)

    half = jnp.bfloat16
    own = [
        pltpu.VMEM((3 * width, tokens), half),
        pltpu.VMEM((2 * width, tokens), half),
        pltpu.VMEM((2 * width, tokens), half),
        pltpu.VMEM((width, width), jnp.float32),
        pltpu.VMEM((KW * VOCAB, arrays.idm.shape[1]), half),
        pltpu.VMEM((3,) + source(0).shape, half),
        source(7),
        source(8),
        pltpu.SemaphoreType.DMA((2, width // 128)),
        pltpu.SemaphoreType.DMA((2, width // 128)),
        pltpu.SemaphoreType.DMA,
        pltpu.SemaphoreType.DMA,
        pltpu.SemaphoreType.DMA((LATE_LOADS + 3,)),
        pltpu.VMEM((3 * width, width), half),
        pltpu.VMEM((KW * VOCAB, 1), jnp.float32),
        pltpu.VMEM((8, width), jnp.float32),
    ]
    return pl.pallas_call(
        backward_kernel,
        name="backward_all",
        out_shape=out_shape,
        in_specs=[hbm] * (10 + LATE_LOADS) + [vmem] * (len(views) - 10 - LATE_LOADS),
        out_specs=[vmem] * 9 + [hbm],
        scratch_shapes=buffers + sems + own + [pltpu.VMEM(a.shape, a.dtype) for a in arrays[7 : 7 + LATE_LOADS]],
        compiler_params=pltpu.CompilerParams(
            collective_id=1, has_side_effects=True, vmem_limit_bytes=63 * 1024 * 1024
        ),
    )(*views)


def tok_forward_body(own, core, tokens, tick):
    ids_ref, marks_ref, table_ref, small_ref = own.ids_pad, own.marks_pad, own.table, own.small
    stream_ref, normed_ref, coef_ref, tap_ref = own.stream, own.normed, own.coef, own.tap
    rows_ref, idm_ref, one_hot = own.rows, own.idm, own.one_hot
    half_bytes = 2 * tokens
    span = one_hot.shape[1]
    wide = span + 2 * LEFT
    first = pl.ds(pl.multiple_of(core * half_bytes, 128), wide)
    ids = ids_ref[:, first]
    marks = marks_ref[:, first]
    for tap in range(KW):
        by = tap - KW // 2
        same = (lane_shift(marks, by) == marks) & (marks > 0)
        idm_ref[tap : tap + 1] = jnp.where(same, lane_shift(ids, by), -1)[0:1, LEFT : LEFT + span]
    tick()
    fill_one_hot(one_hot, idm_ref)

    tick()
    score = jnp.broadcast_to(small_ref[KW : KW + 1], (8, small_ref.shape[1])).astype(jnp.bfloat16)

    def step(tap, carry):
        product = table_ref[...].astype(jnp.float32) * small_ref[pl.ds(tap, 1)]
        high, low = split_two(product)
        tap_ref[tap_rows(tap)] = high
        own.scored[:, tap_rows(tap)] = mm_nt(score, high) + mm_nt(score, low)
        return carry

    lax.fori_loop(0, KW, step, 0)
    tick()
    high, low = split_two(own.scored[...])
    u_row = mm(high, one_hot[...]) + mm(low, one_hot[...])

    tick()
    high = u_row.astype(jnp.bfloat16).astype(jnp.float32)
    marks_here = marks[:, LEFT : LEFT + span].astype(jnp.float32)
    away = marks_ref[:, pl.ds(pl.multiple_of((1 - core) * half_bytes, 128), wide)][:, LEFT : LEFT + span]
    away = away.astype(jnp.float32)
    packed = jnp.concatenate([marks_here, high, u_row - high, away], axis=0).astype(jnp.bfloat16)
    shape = (span, wide // 2)
    twice = 2 * lax.broadcasted_iota(jnp.int32, shape, 1) - lax.broadcasted_iota(jnp.int32, shape, 0) - LEFT
    marks_of, u_of = [], []
    for e in range(2):
        pick = (twice == -e).astype(jnp.float32).astype(jnp.bfloat16)
        apart = mm(packed, pick)
        marks_of.append(apart[0:8])
        u_of.append(apart[8:16] + apart[16:24])
        if e == 0:
            kept = slice(LEFT, LEFT + tokens)
            both = jnp.concatenate([apart[0:1, kept], apart[24:25, kept]], axis=1)
            own.marks[...] = both.astype(jnp.int32)

    tick()
    inside, inverse = pool_rows(marks_of, core, half_bytes)
    prob = {}
    for e in range(2):
        shifted = {}
        for s in range(1 - MAXBLOCK, MAXBLOCK):
            f = (e + s) % 2
            shifted[s] = lane_shift(u_of[f], (e + s - f) // 2)
        scores = [u_of[e]]
        for b in range(2, MAXBLOCK + 1):
            total = u_of[e]
            for s in range(1 - b, b):
                if s != 0:
                    total = total + inside[b, e, s] * shifted[s]
            scores.append(total * inverse[b, e])
        top = scores[0]
        for value in scores[1:]:
            top = jnp.maximum(top, value)
        expo = [jnp.exp(value - top) for value in scores]
        whole = expo[0] + expo[1] + expo[2] + expo[3]
        for b in range(1, MAXBLOCK + 1):
            prob[b, e] = expo[b - 1] / whole
            rows_ref[2 * b + e : 2 * b + e + 1] = prob[b, e][0:1]
        rows_ref[e : e + 1] = marks_of[e][0:1]
    coefs = band_coefs({key: 0.5 * value for key, value in prob.items()}, inside, inverse)
    gain = small_ref[KW + 1 : KW + 2]
    tick()
    for i in range(tokens // BAND):
        matrix = band_matrix(coefs, i).astype(jnp.bfloat16)
        lanes = slice(i * BAND, (i + 1) * BAND)
        part = mm(one_hot[:, 2 * i * BAND : (2 * i + 3) * BAND], matrix).astype(jnp.bfloat16)
        coef_ref[:, lanes] = part
        stream = mm_tn(part, tap_ref[...])
        stream_ref[lanes] = stream
        scale = lax.rsqrt(jnp.mean(stream * stream, axis=-1, keepdims=True) + 1e-06)
        normed_ref[lanes] = (stream * scale * gain).astype(jnp.bfloat16)
        if i < tokens // BAND - 1:
            tick()


FUSED_ITEMS = (
    (7, 0, 1, 0, 0),
    (8, 0, 1, 0, 0),
    (0, 0, 1, 1, 1),
    (1, 0, 1, 0, 1),
    (2, 0, 1, 1, 1),
    (3, 0, 1, 0, 1),
    (6, 0, 2, 0, 2),
    (4, 1, 2, 0, 2),
    (6, 1, 2, 1, 3),
    (5, 0, 2, 1, 3),
    (4, 0, 2, 1, 4),
    (5, 1, 2, 0, 4),
)
FUSED_SCHEDULE = (
    (
        (0, 0, 0), (1, 0, 0), (0, 1, 0), (1, 1, 0), (2, 0, 1), (3, 0, 0),
        (3, 1, 0), (2, 0, 2), (4, 0, 0), (3, 0, 1), (2, 0, 3), (2, 1, 1),
        (0, 2, 0), (3, 0, 2), (4, 1, 0), (3, 0, 3), (2, 1, 2), (4, 0, 1),
        (3, 1, 1), (4, 0, 2), (4, 0, 3), (2, 1, 3), (1, 2, 0), (2, 2, 1),
        (0, 3, 0),
    ),
    (),
    (),
    (
        (2, 2, 2), (3, 1, 2),
    ),
    ((4, 1, 1),),
    ((3, 1, 3),),
    (),
    (
        (2, 2, 3), (1, 3, 0), (2, 3, 1), (0, 4, 0), (3, 2, 0),
    ),
    (
        (3, 2, 1), (3, 2, 2), (2, 3, 2), (4, 1, 2), (4, 1, 3),
    ),
    (
        (2, 3, 3), (1, 4, 0), (2, 4, 1), (3, 2, 3),
    ),
    (),
    (
        (2, 4, 2), (3, 3, 0),
    ),
    (
        (3, 3, 1), (4, 2, 0),
    ),
    (
        (2, 4, 3), (5, 0, 0),
    ),
    (),
    ((4, 2, 1),),
    (
        (3, 3, 2), (3, 3, 3), (4, 2, 2), (4, 3, 0),
    ),
    ((3, 4, 0),),
    (
        (3, 4, 1), (4, 2, 3), (4, 3, 1), (4, 3, 2),
    ),
    (
        (3, 4, 2), (3, 4, 3), (4, 3, 3), (4, 4, 0),
    ),
    (
        (4, 4, 1), (4, 4, 2), (4, 4, 3),
    ),
)


class Gather:
    def __init__(self, ins, outs, cells_in, cells_out, cot_in, cot_out, sems):
        self.ins, self.outs, self.sems = ins, outs, sems
        self.cells_in, self.cells_out, self.cot_in, self.cot_out = cells_in, cells_out, cot_in, cot_out
        self.y, self.x, self.core, self.place, self.lines, self.count = position()
        y, x, core = self.y, self.x, self.core
        self.group = y * 2 + x
        self.dp = dp_of(y, x, core)
        self.twin = dp_of(y, x, 1 - core)
        self.side = dp_of(y, 1 - x, core)
        self.ahead = [(y + k) % self.lines for k in range(1, self.lines)]
        self.phases = {}
        for item, entry in enumerate(FUSED_ITEMS):
            self.phases.setdefault(entry[4], []).append(item)

    def meet(self):
        targets = [(self.twin, self.place), (self.side, self.place)]
        for k in range(1, self.count):
            other = (self.place + k) % self.count
            targets += [(self.dp, other), (self.twin, other)]
        for other_y in self.ahead:
            targets.append((dp_of(other_y, self.x, self.core), self.place))
        meet(targets)

    def lanes(self, item):
        array, part, parts, _, _ = FUSED_ITEMS[item]
        cols = self.ins[array].shape[1] // parts
        return pl.ds(part * cols, cols)

    def shard(self, item):
        return self.ins[FUSED_ITEMS[item][0]].at[:, self.lanes(item)]

    def rows(self, item, first, blocks):
        array = FUSED_ITEMS[item][0]
        size = self.ins[array].shape[0]
        start = pl.multiple_of(first * size, 8)
        return self.outs[array].at[pl.ds(start, blocks * size), self.lanes(item)]

    def block(self, item, g, z):
        return self.rows(item, (g * 2 + self.core) * self.count + z, 1)

    def group_block(self, item, g, core):
        return self.rows(item, (g * 2 + core) * self.count, self.count)

    def came(self, item, g, z):
        return self.sems.recv.at[item, g * self.count + z]

    def arrived(self, item, g, z):
        dst = self.block(item, g, z)
        remote(dst, dst, self.sems.x.at[item], self.came(item, g, z), self.twin, self.place).wait_recv()

    def to_side(self, item, src, g, z):
        remote(
            src, self.block(item, g, z), self.sems.x.at[item], self.came(item, g, z), self.side, self.place
        ).start()

    def to_lines(self, item, src, g, z):
        for other_y in self.ahead:
            remote(
                src,
                self.block(item, g, z),
                self.sems.y.at[item],
                self.came(item, g, z),
                dp_of(other_y, self.x, self.core),
                self.place,
            ).start()

    def to_z(self, item, src, z, way):
        return remote(
            src,
            self.block(item, self.group, z),
            self.sems.z.at[item, z, way],
            self.came(item, self.group, z),
            self.dp,
            self.place + 1 - 2 * way,
        )

    def to_twin(self, item, g):
        src = self.group_block(item, g, self.core)
        remote(
            src, src, self.sems.twin.at[item], self.sems.twin_recv.at[item, g], self.twin, self.place
        ).start()

    def own_copy(self, item):
        return pltpu.make_async_copy(
            self.shard(item), self.block(item, self.group, self.place), self.sems.own.at[item]
        )

    def task_own(self, phase):
        for item in self.phases[phase]:
            src = self.shard(item)

            @pl.when(self.place < self.count - 1)
            def _():
                self.to_z(item, src, self.place, 0).start()

            @pl.when(self.place > 0)
            def _():
                self.to_z(item, src, self.place, 1).start()

            self.own_copy(item).start()

    def task_sides(self, phase):
        for item in self.phases[phase]:
            src = self.shard(item)
            self.to_side(item, src, self.group, self.place)
            self.to_lines(item, src, self.group, self.place)

    def both_ways(self, step, body):
        def way_step(way, carry):
            z = self.place + step * (2 * way - 1)

            @pl.when((z >= 0) & (z < self.count))
            def _():
                body(z, way)

            return carry

        lax.fori_loop(0, 2, way_step, 0)

    def steps(self, step, body):
        if step < 3:
            body(step)
            return

        def loop(s, carry):
            body(s)
            return carry

        lax.fori_loop(3, self.count, loop, 0)

    def task_first(self, phase, step):
        items = self.phases[phase]

        def receive(z, way):
            for item in items:
                self.arrived(item, self.group, z)
                src = self.block(item, self.group, z)
                then = self.place + 1 - 2 * way
                onward = (then >= 0) & (then < self.count)

                @pl.when(onward)
                def _():
                    self.to_z(item, src, z, way).start()

                self.to_side(item, src, self.group, z)
                self.to_lines(item, src, self.group, z)

        self.steps(step, lambda s: self.both_ways(s, receive))
        if step == 3:
            for item in items:
                self.own_copy(item).wait()
                self.to_twin(item, self.group)

    def at_distance(self, step, body):
        if step == 0:
            body(self.place, 0)
        else:
            self.steps(step, lambda s: self.both_ways(s, body))

    def task_second(self, phase, step):
        items = self.phases[phase]

        def receive(z, way):
            for item in items:
                if FUSED_ITEMS[item][3] == 0:
                    g = self.y * 2 + (1 - self.x)
                    self.arrived(item, g, z)
                    self.to_lines(item, self.block(item, g, z), g, z)
                else:
                    for other_y in self.ahead:
                        g = other_y * 2 + self.x
                        self.arrived(item, g, z)
                        self.to_side(item, self.block(item, g, z), g, z)

        self.at_distance(step, receive)
        if step == 3:
            for item in items:
                if FUSED_ITEMS[item][3] == 0:
                    self.to_twin(item, self.y * 2 + (1 - self.x))
                else:
                    for other_y in self.ahead:
                        self.to_twin(item, other_y * 2 + self.x)

    def task_third(self, phase, step):
        items = self.phases[phase]

        def rest(item):
            if FUSED_ITEMS[item][3] == 0:
                return [other_y * 2 + x for other_y in self.ahead for x in (self.x, 1 - self.x)]
            return [other_y * 2 + (1 - self.x) for other_y in [self.y] + self.ahead]

        def receive(z, way):
            for item in items:
                for g in rest(item):
                    self.arrived(item, g, z)

        self.at_distance(step, receive)
        if step == 3:
            for item in items:
                for g in rest(item):
                    self.to_twin(item, g)

    def full(self, item):
        def step(g, carry):
            dst = self.group_block(item, g, 1 - self.core)
            remote(
                dst, dst, self.sems.twin.at[item], self.sems.twin_recv.at[item, g], self.twin, self.place
            ).wait_recv()
            return carry

        lax.fori_loop(0, self.lines * 2, step, 0)

    def cell_copies(self, fn_remote, fn_local):
        seqs = self.cells_in.shape[0]
        for r in range(seqs):
            chip = seqs * self.core + r
            for c in range(2):
                home = (chip == self.place) & (self.core == c)

                @pl.when(home)
                def _():
                    fn_local(r)

                @pl.when(jnp.logical_not(home))
                def _():
                    fn_remote(r, c, chip)

    def cell_remote(self, r, c, chip):
        return remote(
            self.cells_in.at[r],
            self.cells_out.at[self.place],
            self.sems.cell_send.at[r, c],
            self.sems.cell_recv.at[self.place],
            dp_of(self.y, self.x, c),
            chip,
        )

    def cells_start(self):
        self.cell_copies(
            lambda r, c, chip: self.cell_remote(r, c, chip).start(),
            lambda r: pltpu.make_async_copy(
                self.cells_in.at[r], self.cells_out.at[self.place], self.sems.cell_recv.at[self.place]
            ).start(),
        )

    def cells_wait(self):
        for q in range(self.count):
            dst = self.cells_out.at[q]
            remote(
                dst, dst, self.sems.cell_send.at[0, 0], self.sems.cell_recv.at[q], self.twin, self.place
            ).wait_recv()

    def cot_copies(self, fn_remote, fn_local):
        seqs = self.cot_in.shape[0]
        for r in range(seqs):
            chip = seqs * self.core + r
            home = (chip == self.place) & (self.core == self.place // seqs)

            @pl.when(home)
            def _():
                fn_local(r)

            @pl.when(jnp.logical_not(home))
            def _():
                fn_remote(r, chip)

    def cot_remote(self, r, chip):
        seqs = self.cot_in.shape[0]
        slot = self.place % seqs
        return remote(
            self.cot_in.at[r],
            self.cot_out.at[slot],
            self.sems.cot_send.at[r],
            self.sems.cot_recv.at[slot],
            dp_of(self.y, self.x, self.place // seqs),
            chip,
        )

    def task_cot(self):
        slot = self.place % self.cot_in.shape[0]
        self.cot_copies(
            lambda r, chip: self.cot_remote(r, chip).start(),
            lambda r: pltpu.make_async_copy(
                self.cot_in.at[r], self.cot_out.at[slot], self.sems.cot_recv.at[slot]
            ).start(),
        )

    def task(self, kind, phase, step):
        if kind == 0:
            self.task_own(phase)
        elif kind == 1:
            self.task_sides(phase)
        elif kind == 2:
            self.task_first(phase, step)
        elif kind == 3:
            self.task_second(phase, step)
        elif kind == 4:
            self.task_third(phase, step)
        else:
            self.task_cot()

    def finish(self, waited):
        count, groups = self.count, self.lines * 2
        for item in range(len(FUSED_ITEMS)):
            if item not in waited:
                self.full(item)
            tree = FUSED_ITEMS[item][3]

            def sent(blocks, sem):
                src = self.rows(item, 0, blocks)
                remote(src, src, sem, self.came(item, 0, 0), self.twin, self.place).wait_send()

            sent(count * (1 if tree == 0 else self.lines), self.sems.x.at[item])
            sent(count * (self.lines - 1) * (2 if tree == 0 else 1), self.sems.y.at[item])
            sent(count * groups, self.sems.twin.at[item])

            def drain(z, carry):
                @pl.when((z <= self.place) & (self.place < count - 1))
                def _():
                    self.to_z(item, self.block(item, self.group, z), z, 0).wait_send()

                @pl.when((z >= self.place) & (self.place > 0))
                def _():
                    self.to_z(item, self.block(item, self.group, z), z, 1).wait_send()

                return carry

            lax.fori_loop(0, count, drain, 0)
        for q in range(self.cot_in.shape[0]):
            dst = self.cot_out.at[q]
            remote(
                dst, dst, self.sems.cot_send.at[0], self.sems.cot_recv.at[q], self.twin, self.place
            ).wait_recv()
        self.cell_copies(lambda r, c, chip: self.cell_remote(r, c, chip).wait_send(), lambda r: None)
        self.cot_copies(lambda r, chip: self.cot_remote(r, chip).wait_send(), lambda r: None)


class GatherSems(NamedTuple):
    recv: object
    twin_recv: object
    z: object
    x: object
    y: object
    twin: object
    own: object
    cell_recv: object
    cell_send: object
    cot_recv: object
    cot_send: object
class FrontOuts(NamedTuple):
    cot: object
    stream: object
    normed: object
    coef: object
    tap: object
    rows: object
    idm: object
    qt: object
    kt: object
    vt: object
    out: object
    lse: object
    marks: object
    small: object
    resid: object
    normed_two: object


class FrontWork(NamedTuple):
    stream: object
    normed: object
    coef: object
    tap: object
    rows: object
    idm: object
    qt: object
    kt: object
    vt: object
    out: object
    lse: object
    marks: object
    small: object
    resid: object
    normed_two: object
    cells: object
    ids_pad: object
    marks_pad: object
    table: object
    blocks: object
    wq: object
    wk: object
    wv: object
    wo: object
    other: object
    one_hot: object
    bias: object
    scores: object
    out_sem: object
    load_sem: object
    swap_send: object
    swap_recv: object
    small_in: object
    cells_in: object
    scored: object
    pair: object
    wkv: object
    kv: object


def attend_forward_pair(qt, kt, vt, bias, scores, out, lse):
    keys = kt[...].T
    chunks = keys.shape[0] // CHUNK
    for h in range(2):
        query = pair_rows(qt, h)
        own = slice(h * HEAD_DIM, (h + 1) * HEAD_DIM)
        top = None
        for c in range(chunks):
            rows = slice(c * CHUNK, (c + 1) * CHUNK)
            part = mm(keys[rows], query) + bias[rows]
            scores[h, rows] = part
            high = jnp.max(part, axis=0, keepdims=True)
            top = high if top is None else jnp.maximum(top, high)
        total = None
        summed = None
        for c in range(chunks):
            rows = slice(c * CHUNK, (c + 1) * CHUNK)
            expo = jnp.exp(scores[h, rows] - top)
            part = jnp.sum(expo, axis=0, keepdims=True)
            total = part if total is None else total + part
            part = mm(vt[own, rows], expo.astype(jnp.bfloat16))
            summed = part if summed is None else summed + part
        out[own] = (summed / total).astype(jnp.bfloat16)
        lse[h : h + 1] = top + jnp.log(total)


def forward_kernel(*refs):
    arrays = 9
    byte_ids, segments, taps, vectors = refs[arrays - 1 : arrays + 3]
    cot_in, rest = refs[arrays + 3], refs[arrays + 4 :]
    full, cells_out = rest[:arrays], rest[arrays]
    kept = len(FrontOuts._fields)
    to = FrontOuts(*rest[arrays + 1 : arrays + 1 + kept])
    rest = rest[arrays + 1 + kept :]
    sems = GatherSems(*rest[: len(GatherSems._fields)])
    own = FrontWork(*rest[len(GatherSems._fields) :])
    small_in, cells_in = own.small_in, own.cells_in
    tokens, width = own.stream.shape
    own = own._replace(
        normed=own.pair.at[0:tokens],
        other=own.pair.at[tokens : 2 * tokens],
        wk=own.wkv.at[0:width],
        wv=own.wkv.at[width : 2 * width],
        kt=own.kv.at[0:width],
        vt=own.kv.at[width : 2 * width],
    )
    ins = refs[: arrays - 1] + (small_in,)
    gather = Gather(ins, full, cells_in, cells_out, cot_in, to.cot, sems)
    which = {}
    for item, entry in enumerate(FUSED_ITEMS):
        which[entry[0]] = item
    queue = [list(group) for group in FUSED_SCHEDULE]

    def tick():
        for entry in queue.pop(0):
            gather.task(*entry)

    saved = []

    def save(src, dst):
        copy = pltpu.make_async_copy(src, dst, own.out_sem.at[len(saved)])
        copy.start()
        saved.append(copy)

    def load(array, dst):
        gather.full(which[array])
        copy = pltpu.make_async_copy(full[array], dst, own.load_sem.at[array])
        copy.start()
        return copy

    small_in[...] = jnp.zeros_like(small_in)
    small_in[0:KW, 0 : taps.shape[1]] = taps[...].astype(jnp.float32)
    small_in[KW:8, 0 : taps.shape[1]] = vectors[...]
    per_part = byte_ids.shape[1] // 128
    for r in range(byte_ids.shape[0]):
        for k in range(per_part):
            lanes = slice(128 * k, 128 * (k + 1))
            cells_in[r, k : k + 1] = byte_ids[r : r + 1, lanes]
            cells_in[r, per_part + k : per_part + k + 1] = segments[r : r + 1, lanes] + 1
    gather.meet()
    gather.cells_start()
    tick()

    core, place = gather.core, gather.place
    tokens, width = own.stream.shape
    half_bytes = 2 * tokens
    span = own.one_hot.shape[1]
    wide = span + 2 * LEFT
    gather.cells_wait()
    cell_copy = pltpu.make_async_copy(cells_out, own.cells, own.load_sem.at[4])
    cell_copy.start()
    load_table = load(7, own.table)
    load_blocks = load(8, own.blocks)
    cell_copy.wait()
    ids_pad, marks_pad = own.ids_pad, own.marks_pad
    ids_pad[:, 0 : 2 * LEFT] = jnp.full((8, 2 * LEFT), -1, jnp.int32)
    marks_pad[:, 0 : 2 * LEFT] = jnp.zeros((8, 2 * LEFT), jnp.int32)
    end = 2 * LEFT + 2 * half_bytes
    ids_pad[:, end : end + 2 * LEFT] = jnp.full((8, 2 * LEFT), -1, jnp.int32)
    marks_pad[:, end : end + 2 * LEFT] = jnp.zeros((8, 2 * LEFT), jnp.int32)
    parts, per_part = own.cells.shape[0], own.cells.shape[1] // 2
    for q in range(parts):
        for r in range(per_part):
            at = slice(2 * LEFT + (q * per_part + r) * 128, 2 * LEFT + (q * per_part + r + 1) * 128)
            ids_pad[:, at] = jnp.broadcast_to(own.cells[q, r : r + 1], (8, 128))
            marks_pad[:, at] = jnp.broadcast_to(own.cells[q, per_part + r : per_part + r + 1], (8, 128))
    load_blocks.wait()
    total = gather.lines * 4 * gather.count
    chan = width // total
    lane = lax.broadcasted_iota(jnp.int32, (8, 128), 1)
    columns = [jnp.zeros((8, 128), jnp.float32) for _ in range(width // 128)]
    for o in range(total):
        piece = jnp.where(lane < chan, own.blocks[8 * o : 8 * o + 8], 0.0)
        at, by = divmod(o * chan, 128)
        turned = piece if by == 0 else pltpu.roll(piece, by, 1)
        columns[at] = columns[at] + jnp.where(lane >= by, turned, 0.0)
        if by + chan > 128:
            columns[at + 1] = columns[at + 1] + jnp.where(lane < by, turned, 0.0)
    own.small[...] = jnp.concatenate(columns, axis=1)
    save(own.small, to.small)
    load_table.wait()
    tok_forward_body(own, core, tokens, tick)
    save(own.stream, to.stream)
    save(own.normed, to.normed)
    save(own.coef, to.coef)
    save(own.tap, to.tap)
    save(own.rows, to.rows)
    save(own.idm, to.idm)
    save(own.marks, to.marks)

    swap = remote(own.normed, own.other, own.swap_send, own.swap_recv, gather.twin, place)
    swap.start()
    tick()
    load_wq = load(0, own.wq)
    load_wk = load(1, own.wk)
    load_wv = load(2, own.wv)

    def project(rows, weight):
        return mm(rows[...], weight[...]).astype(jnp.bfloat16)

    load_wq.wait()
    own.qt[...] = (project(own.normed, own.wq) * HEAD_DIM ** (-0.5)).astype(jnp.bfloat16).T
    save(own.qt, to.qt)
    tick()
    load_wk.wait()
    load_wv.wait()
    groups = [queue.pop(0) for _ in range(4)]

    def project_step(i, carry):
        which, part = i % 2, i // 2

        @pl.when(i == 2)
        def _():
            swap.wait_recv()

        rows = own.pair.at[pl.ds(pl.multiple_of(part * tokens, tokens), tokens)]
        weight = own.wkv.at[pl.ds(pl.multiple_of(which * width, width), width)]
        to_rows = pl.ds(pl.multiple_of(which * width, width), width)
        own.kv[to_rows, pl.ds(pl.multiple_of(part * tokens, tokens), tokens)] = project(rows, weight).T
        for k, group in enumerate(groups):
            if group:

                @pl.when(i == k)
                def _():
                    for entry in group:
                        gather.task(*entry)

        return carry

    lax.fori_loop(0, 4, project_step, 0)
    save(own.kt, to.kt)
    save(own.vt, to.vt)
    load_wo = load(3, own.wo)
    fill_bias(own.bias, own.marks, own.marks.at[:, 0:tokens])
    pairs = width // 128
    ticks = [queue.pop(0) for _ in range(pairs)]

    def pair_step(i, carry):
        at = pl.ds(pl.multiple_of(128 * i, 128), 128)
        attend_forward_pair(
            own.qt.at[at],
            own.kt.at[at],
            own.vt.at[at],
            own.bias,
            own.scores,
            own.out.at[at],
            own.lse.at[i],
        )
        for k, group in enumerate(ticks):
            if group:

                @pl.when(i == k)
                def _():
                    for entry in group:
                        gather.task(*entry)

        return carry

    lax.fori_loop(0, pairs, pair_step, 0)
    save(own.out, to.out)
    save(own.lse, to.lse)
    load_wo.wait()
    resid = own.stream[...] + mm(own.out[...].T, own.wo[...])
    own.resid[...] = resid
    save(own.resid, to.resid)
    scale = lax.rsqrt(jnp.mean(resid * resid, axis=-1, keepdims=True) + 1e-06)
    own.normed_two[...] = (resid * scale * own.small[KW + 2 : KW + 3]).astype(jnp.bfloat16)
    save(own.normed_two, to.normed_two)
    while queue:
        tick()
    gather.finish([which[a] for a in (0, 1, 2, 3, 7, 8)])
    for copy in saved:
        copy.wait()
    swap.wait_send()


def forward_all(shards, byte_ids, segments, taps, vectors, cot, tokens):
    count = lax.axis_size("seq")
    group_count = lax.axis_size(ALL)
    groups = group_count // (2 * count)
    items = len(FUSED_ITEMS)
    seqs = byte_ids.shape[0]
    cells = jax.ShapeDtypeStruct((seqs, byte_ids.shape[1] // 64, 128), jnp.int32)
    width = shards[0].shape[1]
    span = 2 * tokens + 2 * LEFT
    half, single = jnp.bfloat16, jnp.float32
    vmem = pl.BlockSpec(memory_space=pltpu.VMEM)
    hbm = pl.BlockSpec(memory_space=pltpu.HBM)
    pairs = width // 128
    held = (
        ((tokens, width), single),
        ((tokens, width), half),
        ((KW * VOCAB, tokens), half),
        ((KW * VOCAB, width), half),
        ((16, (span + 2 * LEFT) // 2), single),
        ((8, span), jnp.int32),
        ((width, tokens), half),
        ((width, 2 * tokens), half),
        ((width, 2 * tokens), half),
        ((width, tokens), half),
        ((pairs, 2, tokens), single),
        ((1, 2 * tokens), jnp.int32),
        ((8, width), single),
        ((tokens, width), single),
        ((tokens, width), half),
    )
    small = jax.ShapeDtypeStruct((8, 128), single)
    shapes = [jax.ShapeDtypeStruct((a.shape[0] * group_count, a.shape[1]), a.dtype) for a in shards + (small,)]
    shapes.append(jax.ShapeDtypeStruct((count,) + cells.shape[1:], cells.dtype))
    shapes.append(jax.ShapeDtypeStruct(cot.shape, cot.dtype))
    shapes += [jax.ShapeDtypeStruct(*entry) for entry in held]
    dma = pltpu.SemaphoreType.DMA
    scratch = [
        dma((items, groups * count)),
        dma((items, groups)),
        dma((items, count, 2)),
        dma((items,)),
        dma((items,)),
        dma((items,)),
        dma((items,)),
        dma((count,)),
        dma((seqs, 2)),
        dma((seqs,)),
        dma((seqs,)),
    ]
    scratch += [pltpu.VMEM(*entry) for entry in held]
    scratch += [
        pltpu.VMEM((count,) + cells.shape[1:], cells.dtype),
        pltpu.VMEM((8, 4 * tokens + 4 * LEFT), jnp.int32),
        pltpu.VMEM((8, 4 * tokens + 4 * LEFT), jnp.int32),
        pltpu.VMEM((VOCAB, width), half),
        pltpu.VMEM((8 * group_count, 128), single),
        pltpu.VMEM((width, width), half),
        pltpu.VMEM((width, width), half),
        pltpu.VMEM((width, width), half),
        pltpu.VMEM((width, width), half),
        pltpu.VMEM((tokens, width), half),
        pltpu.VMEM((KW * VOCAB, span), half),
        pltpu.VMEM((2 * tokens, tokens), single),
        pltpu.VMEM((2, 2 * tokens, tokens), single),
        dma((len(held),)),
        dma((9,)),
        dma,
        dma,
        pltpu.VMEM((8, 128), single),
        pltpu.VMEM(cells.shape, cells.dtype),
        pltpu.VMEM((8, KW * VOCAB), single),
        pltpu.VMEM((2 * tokens, width), half),
        pltpu.VMEM((2 * width, width), half),
        pltpu.VMEM((2 * width, 2 * tokens), half),
    ]
    out = pl.pallas_call(
        forward_kernel,
        name="forward_all",
        out_shape=shapes,
        in_specs=[vmem] * (len(shards) + 5),
        out_specs=[hbm] * len(shapes),
        scratch_shapes=scratch,
        compiler_params=pltpu.CompilerParams(
            collective_id=0, has_side_effects=True, vmem_limit_bytes=60 * 1024 * 1024
        ),
    )(*shards, byte_ids, segments, taps, vectors, cot)
    return list(out[:9]), FrontOuts(*out[10:])

FF_BLOCK = 512


def feed_kernel(
    normed,
    cot,
    resid,
    small,
    out_t,
    w_gate,
    w_up,
    w_down,
    w_output,
    gate_grad,
    up_grad,
    down_grad,
    layer,
    output_grad,
    got,
    resid_grad,
    gain_grad,
    normed_t,
    total,
    normed_grad,
):
    step = pl.program_id(0)

    @pl.when(step == 0)
    def _():
        normed_t[...] = normed[...].T
        total[...] = jnp.zeros_like(total)
        normed_grad[...] = jnp.zeros_like(normed_grad)

    gate = mm(normed[...], w_gate[...])
    up = mm(normed[...], w_up[...])
    root = 0.7978845608028654
    square = gate * gate
    bent = jnp.tanh(root * gate * (1.0 + 0.044715 * square))
    half = 0.5 * (1.0 + bent)
    act = gate * half
    slope = half + 0.5 * gate * (1.0 - bent * bent) * (root * (1.0 + 3 * 0.044715 * square))
    hidden = (act * up).astype(jnp.bfloat16)
    total[...] += mm(hidden, w_down[...])
    hidden_grad = mm_nt(cot[...], w_down[...])
    up_part = (hidden_grad * act).astype(jnp.bfloat16)
    gate_part = (hidden_grad * up * slope).astype(jnp.bfloat16)
    down_grad[...] = mm(hidden.T, cot[...]).astype(jnp.bfloat16)
    gate_grad[...] = mm(normed_t[...], gate_part).astype(jnp.bfloat16)
    up_grad[...] = mm(normed_t[...], up_part).astype(jnp.bfloat16)
    normed_grad[...] += mm_nt(gate_part, w_gate[...]) + mm_nt(up_part, w_up[...])

    @pl.when(step == pl.num_programs(0) - 1)
    def _():
        stream = resid[...]
        layer[...] = (stream + total[...]).astype(jnp.bfloat16)
        scale = lax.rsqrt(jnp.mean(stream * stream, axis=-1, keepdims=True) + 1e-06)
        grad = normed_grad[...]
        gain_grad[...] = jnp.sum(grad * stream * scale, axis=0, keepdims=True)
        scaled = grad * small[KW + 2 : KW + 3]
        inner = jnp.mean(scaled * stream, axis=-1, keepdims=True)
        whole = cot[...].astype(jnp.float32) + scale * scaled - stream * (scale * scale * scale * inner)
        resid_grad[...] = whole
        proj = whole.astype(jnp.bfloat16)
        output_grad[...] = mm(out_t[...], proj).astype(jnp.bfloat16)
        got[...] = mm_nt(w_output[...], proj).astype(jnp.bfloat16)


def feed_forward(normed, cot, resid, small, out_t, w_gate, w_up, w_down, w_output):
    tokens, width = normed.shape
    wide = w_gate.shape[1]
    whole = lambda shape: pl.BlockSpec(shape, lambda f: (0, 0))
    columns = pl.BlockSpec((width, FF_BLOCK), lambda f: (0, f))
    rows = pl.BlockSpec((FF_BLOCK, width), lambda f: (f, 0))
    half, single = jnp.bfloat16, jnp.float32
    return pl.pallas_call(
        feed_kernel,
        name="feed_forward",
        grid=(wide // FF_BLOCK,),
        in_specs=[
            whole((tokens, width)),
            whole((tokens, width)),
            whole((tokens, width)),
            whole(small.shape),
            whole((width, tokens)),
            columns,
            columns,
            rows,
            whole((width, width)),
        ],
        out_specs=[
            columns,
            columns,
            rows,
            whole((tokens, width)),
            whole((width, width)),
            whole((width, tokens)),
            whole((tokens, width)),
            whole((1, width)),
        ],
        out_shape=[
            jax.ShapeDtypeStruct((width, wide), half),
            jax.ShapeDtypeStruct((width, wide), half),
            jax.ShapeDtypeStruct((wide, width), half),
            jax.ShapeDtypeStruct((tokens, width), half),
            jax.ShapeDtypeStruct((width, width), half),
            jax.ShapeDtypeStruct((width, tokens), half),
            jax.ShapeDtypeStruct((tokens, width), single),
            jax.ShapeDtypeStruct((1, width), single),
        ],
        scratch_shapes=[
            pltpu.VMEM((width, tokens), half),
            pltpu.VMEM((tokens, width), single),
            pltpu.VMEM((tokens, width), single),
        ],
        compiler_params=pltpu.CompilerParams(vmem_limit_bytes=VMEM_BYTES),
    )(normed, cot, resid, small, out_t, w_gate, w_up, w_down, w_output)


def result_kernel(count, chan, *refs):
    ins, outs, sem = refs[:count], refs[count:-1], refs[-1]
    small = ins[-1]
    copies = [pltpu.make_async_copy(ins[k], outs[k], sem.at[k]) for k in range(count - 1)]
    for copy in copies:
        copy.start()
    outs[count - 1][...] = small[0:KW, 0:chan]
    for k in range(3):
        outs[count + k][...] = small[KW + k : KW + k + 1, 0:chan]
    for copy in copies:
        copy.wait()


def results(arrays, small, chan):
    vmem = pl.BlockSpec(memory_space=pltpu.VMEM)
    hbm = pl.BlockSpec(memory_space=pltpu.HBM)
    count = len(arrays) + 1
    shapes = [jax.ShapeDtypeStruct(a.shape, a.dtype) for a in arrays]
    shapes.append(jax.ShapeDtypeStruct((KW, chan), jnp.float32))
    shapes += [jax.ShapeDtypeStruct((1, chan), jnp.float32)] * 3
    return pl.pallas_call(
        functools.partial(result_kernel, count, chan),
        name="results",
        out_shape=shapes,
        in_specs=[vmem] * count,
        out_specs=[hbm] * len(arrays) + [vmem] * 4,
        scratch_shapes=[pltpu.SemaphoreType.DMA((count,))],
    )(*arrays, small)


def per_device(
    byte_ids,
    segments,
    embed_table,
    conv_weight,
    score_vector,
    first_gain,
    w_query,
    w_key,
    w_value,
    w_output,
    second_gain,
    w_gate,
    w_up,
    w_down,
    out_grad,
):
    seqs, part_bytes = byte_ids.shape
    count = lax.axis_size("seq")
    seq_len = part_bytes * count
    width = w_query.shape[1]
    wide = w_gate.shape[1]
    half_bytes = seq_len // 2
    half = half_bytes // 2
    core = lax.axis_index("dp") % 2
    place = lax.axis_index("seq")

    chan = conv_weight.shape[0]
    shards = (w_query, w_key, w_value, w_output, w_gate, w_up, w_down, embed_table)
    vectors = jnp.stack([score_vector, first_gain, second_gain]).astype(jnp.float32)
    if all(shard.shape[0] % 8 == 0 for shard in shards):
        full, held = forward_all(shards, byte_ids, segments, conv_weight.T, vectors, out_grad, half)
        wq, wk, wv, wo, wg, wu, wd, table, _ = full
        cot = held.cot.reshape(half, width)
        small_full, stream, normed_one, resid_one = held.small, held.stream, held.normed, held.resid
        coef, tap_table, rows, idm = held.coef, held.tap, held.rows, held.idm
        queries, keys, vals, attn_out, lse = held.qt, held.kt, held.vt, held.out, held.lse
        key_marks = held.marks[0]
        normed_two = held.normed_two
    else:
        small = jnp.concatenate([conv_weight.T.astype(jnp.float32), vectors], axis=0)
        small = jnp.pad(small, ((0, 0), (0, 128 - chan)))
        cells = jnp.stack([byte_ids, segments + 1], axis=1).reshape(seqs, -1, 128)
        wq, wk, wv, wo, wg, wu, wd, table, small_full, cells, cot = gather_all(shards + (small,), cells, out_grad)
        cells = cells.reshape(count, 2, part_bytes).transpose(1, 0, 2).reshape(2, seq_len)
        ids_row, marks_row = cells[0], cells[1]
        cot = cot.reshape(half, width)
        small_full = small_full.reshape(lax.axis_size(ALL), 8, 128)[:, :, :chan].transpose(1, 0, 2).reshape(8, width)
        gain_two = small_full[KW + 2 : KW + 3]

        stream, normed_one, coef, tap_table, rows, idm = tok_forward(ids_row, marks_row, table, small_full, half)

        twins = [(i, i ^ 1) for i in range(lax.axis_size("dp"))]
        normed_other = lax.ppermute(normed_one, "dp", twins)
        token_marks = marks_row[::2]
        query_marks = lax.dynamic_slice_in_dim(token_marks, core * half, half, axis=0)
        other_marks = lax.dynamic_slice_in_dim(token_marks, (1 - core) * half, half, axis=0)
        key_marks = jnp.concatenate([query_marks, other_marks])
        queries = (mm_tt(wq, normed_one).astype(jnp.bfloat16) * HEAD_DIM ** (-0.5)).astype(jnp.bfloat16)
        normed_keys = jnp.concatenate([normed_one, normed_other], axis=0)
        keys = mm_tt(wk, normed_keys).astype(jnp.bfloat16)
        vals = mm_tt(wv, normed_keys).astype(jnp.bfloat16)
        attn_out, lse = attend_forward(queries, keys, vals, key_marks, query_marks)

        resid_one = stream + mm_tn(attn_out, wo)
        normed_two = rms_scale(resid_one, gain_two).astype(jnp.bfloat16)
    grad_gate, grad_up, grad_down, layer_rows, grad_output, attn_grad, resid_grad, gain_two_grad = feed_forward(
        normed_two, cot, resid_one, small_full, attn_out, wg, wu, wd, wo
    )
    layer_rows = layer_rows.reshape(seqs, part_bytes // 2, width)
    shapes = [(w.shape[0], w.shape[1], jnp.bfloat16) for w in shards] + [(8, 128, jnp.float32)]
    out = backward_all(
        BackInputs(
            gate=grad_gate,
            up=grad_up,
            down=grad_down,
            output=grad_output,
            coef=coef,
            resid=resid_grad,
            qt=queries,
            kt=keys,
            vt=vals,
            got=attn_grad,
            out=attn_out,
            lse=lse,
            key_marks=key_marks[None],
            normed=normed_one,
            stream=stream,
            wq=wq,
            wk=wk,
            wv=wv,
            small=small_full,
            gain_two=gain_two_grad,
            table=table,
            tap=tap_table,
            rows=rows,
            idm=idm,
            layer=layer_rows,
        ),
        shapes,
    )
    done = results([out[9]] + list(out[:8]), out[8], chan)
    return (
        done[0],
        done[8],
        done[9].T,
        done[10][0],
        done[11][0],
        done[1],
        done[2],
        done[3],
        done[4],
        done[12][0],
        done[5],
        done[6],
        done[7],
    )


def solution(mesh):
    flat = P(ALL)
    rows = P(ALL, None)
    in_specs = (
        P("dp", "seq"),
        P("dp", "seq"),
        rows,
        rows,
        flat,
        flat,
        rows,
        rows,
        rows,
        rows,
        flat,
        rows,
        rows,
        rows,
        P("dp", "seq", None),
    )
    out_specs = (
        P("dp", "seq", None),
        rows,
        rows,
        flat,
        flat,
        rows,
        rows,
        rows,
        rows,
        flat,
        rows,
        rows,
        rows,
    )
    return jax.shard_map(
        per_device, mesh=mesh, in_specs=in_specs, out_specs=out_specs, check_vma=False
    )
```

```python
import functools
from typing import NamedTuple

import jax
import jax.numpy as jnp
from jax import lax
from jax.experimental import pallas as pl
from jax.experimental.pallas import tpu as pltpu
from jax.sharding import PartitionSpec as P

HEADS = 12
HEAD_DIM = 64
VOCAB = 256
MAXBLOCK = 4
KW = 5
DOCS = 8
ALL = ("dp", "seq")
VMEM_BYTES = 56 * 1024 * 1024


def mm(left, right):
    return jnp.dot(left, right, preferred_element_type=jnp.float32)


def mm_nt(left, right):
    return lax.dot_general(left, right, (((1,), (1,)), ((), ())), preferred_element_type=jnp.float32)


def mm_tn(left, right):
    return lax.dot_general(left, right, (((0,), (0,)), ((), ())), preferred_element_type=jnp.float32)


def mm_tt(left, right):
    return lax.dot_general(left, right, (((0,), (1,)), ((), ())), preferred_element_type=jnp.float32)


def rms_scale(values, gain):
    return values * lax.rsqrt(jnp.mean(values * values, axis=-1, keepdims=True) + 1e-06) * gain


def gelu_tanh(values):
    return jax.nn.gelu(values, approximate=True)


MESH = pl.DeviceIdType.MESH


def position():
    dp = lax.axis_index("dp")
    place = lax.axis_index("seq")
    lines = lax.axis_size("dp") // 4
    group = dp // 2
    return group // 2, group % 2, dp % 2, place, lines, lax.axis_size("seq")


def dp_of(y, x, core):
    return (y * 2 + x) * 2 + core


def meet(targets):
    barrier = pltpu.get_barrier_semaphore()
    for dp, place in targets:
        pl.semaphore_signal(barrier, inc=1, device_id=(dp, place), device_id_type=MESH)
    pl.semaphore_wait(barrier, len(targets))


def remote(src, dst, send_sem, recv_sem, dp, place):
    return pltpu.make_async_remote_copy(
        src_ref=src,
        dst_ref=dst,
        send_sem=send_sem,
        recv_sem=recv_sem,
        device_id=(dp, place),
        device_id_type=MESH,
    )


GATHER_ITEMS = (
    (7, 0, 0, 0),
    (8, 0, 0, 0),
    (0, 0, 0, 0),
    (2, 0, 0, 1),
    (1, 0, 0, 0),
    (3, 0, 0, 1),
    (4, 0, 0, 0),
    (5, 0, 0, 1),
    (6, 0, 1, 0),
    (6, 1, 1, 1),
)
GATHER_PHASES = ((0, 1), (2, 3, 4, 5), (6, 7), (8, 9))


def gather_kernel(arrays, *refs):
    ins = refs[:arrays]
    cells_in, cot_in = refs[arrays], refs[arrays + 1]
    outs = refs[arrays + 2 : 2 * arrays + 2]
    cells_out, cot_out = refs[2 * arrays + 2], refs[2 * arrays + 3]
    recv, recv_sib, send_z, send_x, send_y, send_sib, own_sem, cell_recv, cell_send, cot_recv, cot_send = refs[
        2 * arrays + 4 :
    ]
    y, x, core, place, lines, count = position()
    seqs = cells_in.shape[0]
    groups = lines * 2
    group = y * 2 + x
    dp = dp_of(y, x, core)
    twin = dp_of(y, x, 1 - core)
    side = dp_of(y, 1 - x, core)
    ahead = [(y + k) % lines for k in range(1, lines)]

    targets = [(twin, place), (side, place)]
    for k in range(1, count):
        targets += [(dp, (place + k) % count), (twin, (place + k) % count)]
    for other_y in ahead:
        targets.append((dp_of(other_y, x, core), place))
    meet(targets)

    def cell_copies(fn_remote, fn_local):
        for r in range(seqs):
            chip = seqs * core + r
            for c in range(2):
                home = (chip == place) & (core == c)

                @pl.when(home)
                def _():
                    fn_local(r, c)

                @pl.when(jnp.logical_not(home))
                def _():
                    fn_remote(r, c, chip)

    def cell_remote(r, c, chip):
        return remote(
            cells_in.at[r],
            cells_out.at[place],
            cell_send.at[r, c],
            cell_recv.at[place],
            dp_of(y, x, c),
            chip,
        )

    cell_copies(
        lambda r, c, chip: cell_remote(r, c, chip).start(),
        lambda r, c: pltpu.make_async_copy(
            cells_in.at[r], cells_out.at[place], cell_recv.at[place]
        ).start(),
    )

    def view(item):
        array, first, columns, _ = GATHER_ITEMS[item]
        in_ref, out_ref = ins[array], outs[array]
        if columns:
            cols = in_ref.shape[1] // 2
            lanes = pl.ds(first * cols, cols)
        else:
            lanes = pl.ds(0, in_ref.shape[1])
        return in_ref.at[:, lanes], out_ref, lanes

    def block(item, g, z):
        _, out_ref, lanes = view(item)
        return out_ref.at[(g * 2 + core) * count + z, :, lanes]

    def group_block(item, g, c):
        _, out_ref, lanes = view(item)
        return out_ref.at[pl.ds((g * 2 + c) * count, count), :, lanes]

    def many(item, blocks):
        _, out_ref, lanes = view(item)
        return out_ref.at[pl.ds(0, blocks), :, lanes]

    def arrived(item, g, z):
        dst = block(item, g, z)
        remote(dst, dst, send_x.at[item], recv.at[item, g * count + z], twin, place).wait_recv()

    def to_side(item, src, g, z):
        remote(src, block(item, g, z), send_x.at[item], recv.at[item, g * count + z], side, place).start()

    def to_lines(item, src, g, z):
        for other_y in ahead:
            remote(
                src,
                block(item, g, z),
                send_y.at[item],
                recv.at[item, g * count + z],
                dp_of(other_y, x, core),
                place,
            ).start()

    def to_z(item, src, z, step):
        return remote(
            src,
            block(item, group, z),
            send_z.at[item, z, step],
            recv.at[item, group * count + z],
            dp,
            place + 1 - 2 * step,
        )

    def to_twin(item, g):
        src = group_block(item, g, core)
        remote(src, src, send_sib.at[item], recv_sib.at[item, g], twin, place).start()

    def own_copy(item):
        return pltpu.make_async_copy(view(item)[0], block(item, group, place), own_sem.at[item])

    def first_own(items):
        for item in items:
            src = view(item)[0]

            @pl.when(place < count - 1)
            def _():
                to_z(item, src, place, 0).start()

            @pl.when(place > 0)
            def _():
                to_z(item, src, place, 1).start()

            own_copy(item).start()

    def first_sides(items):
        for item in items:
            src = view(item)[0]
            to_side(item, src, group, place)
            to_lines(item, src, group, place)

    def first_level(items):
        def step(s, carry):
            low = place - s
            high = place + s
            for item in items:

                @pl.when(low >= 0)
                def _():
                    arrived(item, group, low)
                    src = block(item, group, low)

                    @pl.when(place < count - 1)
                    def _():
                        to_z(item, src, low, 0).start()

                    to_side(item, src, group, low)
                    to_lines(item, src, group, low)

                @pl.when(high < count)
                def _():
                    arrived(item, group, high)
                    src = block(item, group, high)

                    @pl.when(place > 0)
                    def _():
                        to_z(item, src, high, 1).start()

                    to_side(item, src, group, high)
                    to_lines(item, src, group, high)

            return carry

        lax.fori_loop(1, count, step, 0)
        for item in items:
            own_copy(item).wait()
            to_twin(item, group)

    def second_level(items):
        def step(s, carry):
            z = (place + s) % count
            for item in items:
                if GATHER_ITEMS[item][3] == 0:
                    g = y * 2 + (1 - x)
                    arrived(item, g, z)
                    to_lines(item, block(item, g, z), g, z)
                else:
                    for other_y in ahead:
                        g = other_y * 2 + x
                        arrived(item, g, z)
                        to_side(item, block(item, g, z), g, z)
            return carry

        lax.fori_loop(0, count, step, 0)
        for item in items:
            if GATHER_ITEMS[item][3] == 0:
                to_twin(item, y * 2 + (1 - x))
            else:
                for other_y in ahead:
                    to_twin(item, other_y * 2 + x)

    def third_level(items):
        def rest(item):
            if GATHER_ITEMS[item][3] == 0:
                return [other_y * 2 + other_x for other_y in ahead for other_x in (x, 1 - x)]
            return [other_y * 2 + (1 - x) for other_y in [y] + ahead]

        def step(s, carry):
            z = (place + s) % count
            for item in items:
                for g in rest(item):
                    arrived(item, g, z)
            return carry

        lax.fori_loop(0, count, step, 0)
        for item in items:
            for g in rest(item):
                to_twin(item, g)

    def cot_copies(fn_remote, fn_local):
        for r in range(seqs):
            chip = seqs * core + r
            home = (chip == place) & (core == place // seqs)

            @pl.when(home)
            def _():
                fn_local(r)

            @pl.when(jnp.logical_not(home))
            def _():
                fn_remote(r, chip)

    def cot_remote(r, chip):
        return remote(
            cot_in.at[r],
            cot_out.at[place % seqs],
            cot_send.at[r],
            cot_recv.at[place % seqs],
            dp_of(y, x, place // seqs),
            chip,
        )

    phases = GATHER_PHASES
    for items in phases:
        first_own(items)
    first_sides(phases[0])
    first_level(phases[0])
    for k in range(1, len(phases)):
        first_sides(phases[k])
        first_level(phases[k])
        second_level(phases[k - 1])
        if k == 1:
            cot_copies(
                lambda r, chip: cot_remote(r, chip).start(),
                lambda r: pltpu.make_async_copy(
                    cot_in.at[r], cot_out.at[place % seqs], cot_recv.at[place % seqs]
                ).start(),
            )
        if k > 1:
            third_level(phases[k - 2])
    second_level(phases[-1])
    third_level(phases[-2])
    third_level(phases[-1])

    for item in range(len(GATHER_ITEMS)):
        for g in range(groups):
            dst = group_block(item, g, 1 - core)
            remote(dst, dst, send_sib.at[item], recv_sib.at[item, g], twin, place).wait_recv()
        tree = GATHER_ITEMS[item][3]

        def sent(blocks, sem):
            src = many(item, blocks)
            remote(src, src, sem, recv.at[item, 0], twin, place).wait_send()

        sent(count * (1 if tree == 0 else lines), send_x.at[item])
        sent(count * (lines - 1) * (2 if tree == 0 else 1), send_y.at[item])
        sent(count * groups, send_sib.at[item])

        def drain(z, carry):
            @pl.when((z <= place) & (place < count - 1))
            def _():
                to_z(item, block(item, group, z), z, 0).wait_send()

            @pl.when((z >= place) & (place > 0))
            def _():
                to_z(item, block(item, group, z), z, 1).wait_send()

            return carry

        lax.fori_loop(0, count, drain, 0)
    for q in range(count):
        dst = cells_out.at[q]
        remote(dst, dst, cell_send.at[0, 0], cell_recv.at[q], twin, place).wait_recv()
    for q in range(seqs):
        dst = cot_out.at[q]
        remote(dst, dst, cot_send.at[0], cot_recv.at[q], twin, place).wait_recv()
    cell_copies(lambda r, c, chip: cell_remote(r, c, chip).wait_send(), lambda r, c: None)
    cot_copies(lambda r, chip: cot_remote(r, chip).wait_send(), lambda r: None)


def gather_all(shards, cells, cot):
    count = lax.axis_size("seq")
    group_count = lax.axis_size(ALL)
    groups = group_count // (2 * count)
    items = len(GATHER_ITEMS)
    seqs = cells.shape[0]
    vmem = pl.BlockSpec(memory_space=pltpu.VMEM)
    hbm = pl.BlockSpec(memory_space=pltpu.HBM)
    shapes = [jax.ShapeDtypeStruct((group_count,) + s.shape, s.dtype) for s in shards]
    shapes.append(jax.ShapeDtypeStruct((count,) + cells.shape[1:], cells.dtype))
    shapes.append(jax.ShapeDtypeStruct(cot.shape, cot.dtype))
    dma = pltpu.SemaphoreType.DMA
    out = pl.pallas_call(
        functools.partial(gather_kernel, len(shards)),
        name="gather_all",
        out_shape=shapes,
        in_specs=[vmem] * (len(shards) + 2),
        out_specs=[hbm] * len(shapes),
        scratch_shapes=[
            dma((items, groups * count)),
            dma((items, groups)),
            dma((items, count, 2)),
            dma((items,)),
            dma((items,)),
            dma((items,)),
            dma((items,)),
            dma((count,)),
            dma((seqs, 2)),
            dma((seqs,)),
            dma((seqs,)),
        ],
        compiler_params=pltpu.CompilerParams(collective_id=0, has_side_effects=True),
    )(*shards, cells, cot)
    full = [o.reshape(-1, o.shape[2]) for o in out[: len(shards)]]
    return full + list(out[len(shards) :])


LEFT = 128
BAND = 256


def split_two(values):
    high = values.astype(jnp.bfloat16)
    return high, (values - high.astype(jnp.float32)).astype(jnp.bfloat16)


def lane_shift(row, by):
    by = by % row.shape[1]
    return row if by == 0 else pltpu.roll(row, row.shape[1] - by, 1)


def pool_rows(marks, core, half_bytes):
    lanes = lax.broadcasted_iota(jnp.int32, marks[0].shape, 1)
    inside, inverse = {}, {}
    for e in range(2):
        place = core * half_bytes + 2 * (lanes - LEFT) + e + 768
        third = lax.shift_right_logical(place * 21846, 16)
        remains = {2: place & 1, 3: place - 3 * third, 4: place & 3}
        shifted = {}
        for s in range(1 - MAXBLOCK, MAXBLOCK):
            f = (e + s) % 2
            shifted[s] = lane_shift(marks[f], (e + s - f) // 2) == marks[e]
        for b in range(2, MAXBLOCK + 1):
            number = jnp.ones(marks[0].shape, jnp.float32)
            for s in range(1 - b, b):
                if s == 0:
                    continue
                at = remains[b] + s
                on = (shifted[s] & (at >= 0) & (at < b)).astype(jnp.float32)
                inside[b, e, s] = on
                number = number + on
            inverse[b, e] = 1.0 / number
    return inside, inverse


def band_coefs(per_byte, inside, inverse):
    coefs = {}
    for o in range(1 - MAXBLOCK, MAXBLOCK + 1):
        total = None
        for e in range(2):
            s = o - e
            if not 1 - MAXBLOCK <= s < MAXBLOCK:
                continue
            for b in range(1, MAXBLOCK + 1):
                if b == 1:
                    if s != 0:
                        continue
                    term = per_byte[b, e]
                elif s == 0:
                    term = per_byte[b, e] * inverse[b, e]
                elif (b, e, s) in inside:
                    term = per_byte[b, e] * inverse[b, e] * inside[b, e, s]
                else:
                    continue
                total = term if total is None else total + term
        coefs[o] = total
    return coefs


def band_matrix(coefs, block):
    shape = (3 * BAND, BAND)
    delta = lax.broadcasted_iota(jnp.int32, shape, 0) - LEFT - 2 * lax.broadcasted_iota(jnp.int32, shape, 1)
    out = jnp.zeros(shape, jnp.float32)
    for o, row in coefs.items():
        part = row[0:1, LEFT + BAND * block : LEFT + BAND * (block + 1)]
        out = jnp.where(delta == o, part, out)
    return out


def tap_rows(tap):
    return pl.ds(pl.multiple_of(tap * VOCAB, VOCAB), VOCAB)


def fill_one_hot(one_hot, idm_ref):
    vocab = lax.broadcasted_iota(jnp.int32, (VOCAB, one_hot.shape[1]), 0)

    def step(tap, carry):
        hit = vocab == idm_ref[pl.ds(tap, 1)]
        one_hot[tap_rows(tap)] = hit.astype(jnp.float32).astype(jnp.bfloat16)
        return carry

    lax.fori_loop(0, KW, step, 0)


def tok_forward_kernel(ids_ref, marks_ref, table_ref, small_ref, stream_ref, normed_ref, coef_ref, tap_ref, rows_ref, idm_ref, one_hot):
    core = lax.axis_index("dp") % 2
    tokens = stream_ref.shape[0]
    half_bytes = 2 * tokens
    span = one_hot.shape[1]
    wide = span + 2 * LEFT
    first = pl.ds(pl.multiple_of(core * half_bytes, 128), wide)
    ids = ids_ref[:, first]
    marks = marks_ref[:, first]
    for tap in range(KW):
        by = tap - KW // 2
        same = (lane_shift(marks, by) == marks) & (marks > 0)
        idm_ref[tap : tap + 1] = jnp.where(same, lane_shift(ids, by), -1)[0:1, LEFT : LEFT + span]
    fill_one_hot(one_hot, idm_ref)

    score = jnp.broadcast_to(small_ref[KW : KW + 1], (8, small_ref.shape[1])).astype(jnp.bfloat16)
    scored = []
    for tap in range(KW):
        product = table_ref[...].astype(jnp.float32) * small_ref[tap : tap + 1]
        high, low = split_two(product)
        tap_ref[tap * VOCAB : (tap + 1) * VOCAB] = high
        scored.append(mm_nt(score, high) + mm_nt(score, low))
    high, low = split_two(jnp.concatenate(scored, axis=1))
    u_row = mm(high, one_hot[...]) + mm(low, one_hot[...])

    high = u_row.astype(jnp.bfloat16).astype(jnp.float32)
    marks_here = marks[:, LEFT : LEFT + span].astype(jnp.float32)
    packed = jnp.concatenate([marks_here, high, u_row - high, jnp.zeros_like(high)], axis=0).astype(jnp.bfloat16)
    shape = (span, wide // 2)
    twice = 2 * lax.broadcasted_iota(jnp.int32, shape, 1) - lax.broadcasted_iota(jnp.int32, shape, 0) - LEFT
    marks_of, u_of = [], []
    for e in range(2):
        pick = (twice == -e).astype(jnp.float32).astype(jnp.bfloat16)
        apart = mm(packed, pick)
        marks_of.append(apart[0:8])
        u_of.append(apart[8:16] + apart[16:24])

    inside, inverse = pool_rows(marks_of, core, half_bytes)
    prob = {}
    for e in range(2):
        shifted = {}
        for s in range(1 - MAXBLOCK, MAXBLOCK):
            f = (e + s) % 2
            shifted[s] = lane_shift(u_of[f], (e + s - f) // 2)
        scores = [u_of[e]]
        for b in range(2, MAXBLOCK + 1):
            total = u_of[e]
            for s in range(1 - b, b):
                if s != 0:
                    total = total + inside[b, e, s] * shifted[s]
            scores.append(total * inverse[b, e])
        top = scores[0]
        for value in scores[1:]:
            top = jnp.maximum(top, value)
        expo = [jnp.exp(value - top) for value in scores]
        whole = expo[0] + expo[1] + expo[2] + expo[3]
        for b in range(1, MAXBLOCK + 1):
            prob[b, e] = expo[b - 1] / whole
            rows_ref[2 * b + e : 2 * b + e + 1] = prob[b, e][0:1]
        rows_ref[e : e + 1] = marks_of[e][0:1]
    coefs = band_coefs({key: 0.5 * value for key, value in prob.items()}, inside, inverse)
    gain = small_ref[KW + 1 : KW + 2]
    for i in range(tokens // BAND):
        matrix = band_matrix(coefs, i).astype(jnp.bfloat16)
        lanes = slice(i * BAND, (i + 1) * BAND)
        part = mm(one_hot[:, 2 * i * BAND : (2 * i + 3) * BAND], matrix).astype(jnp.bfloat16)
        coef_ref[:, lanes] = part
        stream = mm_tn(part, tap_ref[...])
        stream_ref[lanes] = stream
        scale = lax.rsqrt(jnp.mean(stream * stream, axis=-1, keepdims=True) + 1e-06)
        normed_ref[lanes] = (stream * scale * gain).astype(jnp.bfloat16)


def tok_forward(ids_row, marks_row, table, small, tokens):
    width = table.shape[1]
    span = 2 * tokens + 2 * LEFT
    wide = span + 2 * LEFT

    def padded(row, fill):
        row = jnp.pad(row, (2 * LEFT, 2 * LEFT), constant_values=fill)
        return jnp.broadcast_to(row[None], (8, row.shape[0]))

    return pl.pallas_call(
        tok_forward_kernel,
        name="tok_forward",
        out_shape=[
            jax.ShapeDtypeStruct((tokens, width), jnp.float32),
            jax.ShapeDtypeStruct((tokens, width), jnp.bfloat16),
            jax.ShapeDtypeStruct((KW * VOCAB, tokens), jnp.bfloat16),
            jax.ShapeDtypeStruct((KW * VOCAB, width), jnp.bfloat16),
            jax.ShapeDtypeStruct((16, wide // 2), jnp.float32),
            jax.ShapeDtypeStruct((8, span), jnp.int32),
        ],
        scratch_shapes=[pltpu.VMEM((KW * VOCAB, span), jnp.bfloat16)],
        compiler_params=pltpu.CompilerParams(vmem_limit_bytes=VMEM_BYTES),
    )(padded(ids_row, -1), padded(marks_row, 0), table, small)


def tok_backward_body(grad16, coef_ref, ref, own, tick, take):
    tap_ref, rows_ref, idm_ref, table_ref, small_ref = ref.tap, ref.rows, ref.idm, ref.table, ref.small
    one_hot = own.one_hot
    core = lax.axis_index("dp") % 2
    tokens = grad16.shape[0]
    fill_one_hot(one_hot, idm_ref)
    tick()

    def whole_row(k):
        return jnp.broadcast_to(rows_ref[k : k + 1], (8, rows_ref.shape[1]))

    marks_of = [whole_row(0), whole_row(1)]
    inside, inverse = pool_rows(marks_of, core, 2 * tokens)
    shape = (3 * BAND, BAND)
    delta = lax.broadcasted_iota(jnp.int32, shape, 0) - LEFT - 2 * lax.broadcasted_iota(jnp.int32, shape, 1)
    through = mm_nt(tap_ref[...], grad16).astype(jnp.bfloat16)
    tick()
    diag = {o: [] for o in range(1 - MAXBLOCK, MAXBLOCK + 1)}
    edge = jnp.zeros((8, LEFT), jnp.float32)
    for i in range(tokens // BAND):
        near = mm_tn(one_hot[:, 2 * i * BAND : (2 * i + 3) * BAND], through[:, i * BAND : (i + 1) * BAND])
        for o in diag:
            total = jnp.sum(jnp.where(delta == o, near, 0.0), axis=0, keepdims=True)
            diag[o].append(jnp.broadcast_to(total, (8, BAND)))
        tick()
    diag = {o: jnp.concatenate([edge] + parts + [edge], axis=1) for o, parts in diag.items()}
    size_grad = {}
    for e in range(2):
        grads = [0.5 * diag[e]]
        for b in range(2, MAXBLOCK + 1):
            total = diag[e]
            for s in range(1 - b, b):
                if s != 0:
                    total = total + inside[b, e, s] * diag[s + e]
            grads.append(0.5 * total * inverse[b, e])
        probs = [whole_row(2 * b + e) for b in range(1, MAXBLOCK + 1)]
        mean = probs[0] * grads[0]
        for p, g in zip(probs[1:], grads[1:]):
            mean = mean + p * g
        for b in range(1, MAXBLOCK + 1):
            size_grad[b, e] = probs[b - 1] * (grads[b - 1] - mean)
    coefs = band_coefs(size_grad, inside, inverse)
    picked = None
    for i in range(tokens // BAND):
        matrix = band_matrix(coefs, i).astype(jnp.bfloat16)
        part = mm(one_hot[:, 2 * i * BAND : (2 * i + 3) * BAND], matrix)
        part = jnp.sum(part, axis=1, keepdims=True)
        picked = part if picked is None else picked + part
        tick()
    own.picked[...] = picked
    score = small_ref[KW : KW + 1]
    table_grad = own.wide.at[0:VOCAB]
    table_grad[...] = jnp.zeros(table_grad.shape, jnp.float32)
    own.rows[...] = jnp.zeros_like(own.rows)
    tap_tasks = take(KW - 1)

    def step(tap, carry):
        here = own.picked[tap_rows(tap)]
        table = table_ref[:, 0 : score.shape[1]].astype(jnp.float32)
        part = mm(coef_ref[tap_rows(tap)], grad16) + here * score
        taps = small_ref[pl.ds(tap, 1)]
        table_grad[...] += part * taps
        own.rows[pl.ds(tap, 1)] = jnp.sum(part * table, axis=0, keepdims=True)
        own.rows[KW : KW + 1] += jnp.sum(table * here, axis=0, keepdims=True) * taps
        tap_tasks(tap)
        return carry

    lax.fori_loop(0, KW, step, 0)


CHUNK = 256


def pair_rows(ref, h):
    values = ref[...]
    rows = lax.broadcasted_iota(jnp.int32, values.shape, 0)
    return jnp.where((rows // HEAD_DIM) == h, values, jnp.zeros_like(values))


def fill_bias(bias, key_marks, query_marks):
    def apart(marks):
        rows = lax.broadcasted_iota(jnp.int32, (2 * DOCS, marks.shape[1]), 0)
        return (rows == marks[...]).astype(jnp.float32).astype(jnp.bfloat16)

    queries = apart(query_marks)
    for c in range(key_marks.shape[1] // CHUNK):
        keys = slice(c * CHUNK, (c + 1) * CHUNK)
        same = mm_tn(apart(key_marks.at[:, keys]), queries)
        bias[keys] = jnp.where(same > 0.5, 0.0, -1e30).astype(bias.dtype)


def attend_forward_kernel(qt_ref, kt_ref, vt_ref, key_marks, query_marks, out_ref, lse_ref, bias, scores):
    @pl.when(pl.program_id(0) == 0)
    def _():
        fill_bias(bias, key_marks, query_marks)

    keys = kt_ref[...].T
    chunks = keys.shape[0] // CHUNK
    for h in range(2):
        query = pair_rows(qt_ref, h)
        top = None
        for c in range(chunks):
            rows = slice(c * CHUNK, (c + 1) * CHUNK)
            part = mm(keys[rows], query) + bias[rows]
            scores[h, rows] = part
            high = jnp.max(part, axis=0, keepdims=True)
            top = high if top is None else jnp.maximum(top, high)
        total = None
        out = None
        for c in range(chunks):
            rows = slice(c * CHUNK, (c + 1) * CHUNK)
            expo = jnp.exp(scores[h, rows] - top)
            part = jnp.sum(expo, axis=0, keepdims=True)
            total = part if total is None else total + part
            part = mm(vt_ref[h * HEAD_DIM : (h + 1) * HEAD_DIM, rows], expo.astype(jnp.bfloat16))
            out = part if out is None else out + part
        out_ref[h * HEAD_DIM : (h + 1) * HEAD_DIM] = (out / total).astype(jnp.bfloat16)
        lse_ref[0, h : h + 1] = top + jnp.log(total)


def attend_forward(qt, kt, vt, key_marks, query_marks):
    width, tokens = qt.shape
    keys = kt.shape[1]
    pairs = width // 128
    rows = lambda size: pl.BlockSpec((128, size), lambda i: (i, 0))
    whole = lambda shape: pl.BlockSpec(shape, lambda i: (0, 0))
    return pl.pallas_call(
        attend_forward_kernel,
        name="attend_forward",
        grid=(pairs,),
        in_specs=[rows(tokens), rows(keys), rows(keys), whole((1, keys)), whole((1, tokens))],
        out_specs=[rows(tokens), pl.BlockSpec((1, 2, tokens), lambda i: (i, 0, 0))],
        out_shape=[
            jax.ShapeDtypeStruct((width, tokens), jnp.bfloat16),
            jax.ShapeDtypeStruct((pairs, 2, tokens), jnp.float32),
        ],
        scratch_shapes=[
            pltpu.VMEM((keys, tokens), jnp.float32),
            pltpu.VMEM((2, keys, tokens), jnp.float32),
        ],
        compiler_params=pltpu.CompilerParams(vmem_limit_bytes=VMEM_BYTES),
    )(qt, kt, vt, key_marks[None], query_marks[None])


def attend_backward_pair(qt, kt, vt, got_ref, out, lse_ref, bias, dq, dk_own, dv_own, dk_away, dv_away, tasks):
    keys = kt[...].T
    vals = vt[...].T
    chunks = keys.shape[0] // CHUNK
    for h in range(2):
        own = slice(h * HEAD_DIM, (h + 1) * HEAD_DIM)
        query = pair_rows(qt, h)
        got = pair_rows(got_ref, h)
        dots = jnp.sum(
            got_ref[own].astype(jnp.float32) * out[own].astype(jnp.float32), axis=0, keepdims=True
        )
        lse = lse_ref[h : h + 1]
        query_grad = None
        for c in range(chunks):
            rows = slice(c * CHUNK, (c + 1) * CHUNK)
            soft = jnp.exp(mm(keys[rows], query) + (bias[rows].astype(jnp.float32) - lse))
            change = soft * (mm(vals[rows], got) - dots)
            soft16 = soft.astype(jnp.bfloat16)
            change16 = change.astype(jnp.bfloat16)
            first = c < chunks // 2
            to = slice((c % (chunks // 2)) * CHUNK, (c % (chunks // 2) + 1) * CHUNK)
            (dv_own if first else dv_away)[own, to] = mm_nt(got_ref[own], soft16).astype(jnp.bfloat16)
            (dk_own if first else dk_away)[own, to] = mm_nt(qt[own], change16).astype(jnp.bfloat16)
            part = mm(kt[own, rows], change16)
            query_grad = part if query_grad is None else query_grad + part
        dq[own] = (query_grad * HEAD_DIM ** (-0.5)).astype(jnp.bfloat16)
        if h == 0:
            tasks()


SCATTER_ITEMS = (
    (4, 1, 2, 0),
    (6, 1, 2, 1),
    (5, 0, 2, 0),
    (5, 1, 2, 0),
    (3, 0, 1, 1),
    (6, 0, 2, 0),
    (4, 0, 2, 1),
    (0, 0, 1, 1),
    (1, 0, 1, 0),
    (2, 0, 1, 1),
    (7, 0, 1, 1),
    (8, 0, 1, 1),
)
FIRST_ITEMS = 7
SCHEDULE = (
    (
        (0, 0), (0, 1), (0, 2),
    ),
    (
        (0, 3), (0, 4),
    ),
    (
        (0, 5), (0, 6),
    ),
    (),
    (
        (1, 0), (1, 1),
    ),
    (),
    (),
    ((1, 4),),
    ((1, 2),),
    (),
    (),
    (),
    (
        (1, 3), (1, 6),
    ),
    (),
    (
        (2, 0), (0, 7),
    ),
    ((0, 8),),
    (
        (3, 0), (2, 2), (1, 5), (0, 9),
    ),
    (
        (4, 0), (2, 1), (2, 3),
    ),
    ((3, 2),),
    (
        (5, 0), (2, 4),
    ),
    (
        (4, 2), (1, 7),
    ),
    (
        (3, 1), (2, 6),
    ),
    (
        (5, 2), (3, 3),
    ),
    (
        (2, 5), (4, 1), (3, 4),
    ),
    (),
    (),
    (
        (4, 3), (5, 1), (1, 8), (3, 6),
    ),
    ((4, 4),),
    (
        (1, 9), (5, 3), (2, 7), (3, 5), (0, 10), (5, 4),
        (0, 11), (4, 6), (2, 8), (3, 7), (4, 5), (5, 6),
        (2, 9), (1, 10), (1, 11), (4, 7), (5, 5), (3, 8),
        (2, 10), (2, 11), (5, 7), (3, 9), (4, 8), (3, 10),
        (3, 11), (4, 9), (5, 8), (4, 10), (4, 11), (5, 9),
        (5, 10), (5, 11),
    ),
)


class Scatter:
    def __init__(self, sources, outs, layer_in, layer_out, buffers, sems):
        items = len(SCATTER_ITEMS)
        self.sources, self.outs = sources, outs
        self.layer_in, self.layer_out = layer_in, layer_out
        self.sems = sems
        self.y, self.x, self.core, self.place, self.lines, self.count = position()
        y, x, core = self.y, self.x, self.core
        self.own = list(buffers[:FIRST_ITEMS])
        for array, _, _, _ in SCATTER_ITEMS[FIRST_ITEMS:]:
            self.own.append(sources[array].at[:, :, core])
        buffers = buffers[FIRST_ITEMS:]
        self.from_twin, self.first_in, self.second_in, self.line_in = [
            buffers[k * items : (k + 1) * items] for k in range(4)
        ]
        self.dp = dp_of(y, x, core)
        self.twin = dp_of(y, x, 1 - core)
        self.side = dp_of(y, 1 - x, core)
        self.ahead = [(y + k) % self.lines for k in range(1, self.lines)]

    def meet(self):
        targets = [(self.twin, self.place), (self.side, self.place)]
        for k in range(1, self.count):
            other = (self.place + k) % self.count
            targets += [(self.dp, other), (self.twin, other)]
        for other_y in self.ahead:
            targets.append((dp_of(other_y, self.x, self.core), self.place))
        meet(targets)

    def order(self, item):
        return SCATTER_ITEMS[item][3]

    def columns(self, item):
        array, part, parts, _ = SCATTER_ITEMS[item]
        cols = self.sources[array].shape[-1] // parts
        return pl.ds(part * cols, cols)

    def to_twin(self, item):
        src = self.sources[SCATTER_ITEMS[item][0]].at[:, :, 1 - self.core, :, :, self.columns(item)]
        sems = self.sems
        return remote(
            src, self.from_twin[item], sems.twin_send.at[item], sems.twin_recv.at[item], self.twin, self.place
        )

    def own_in(self, item):
        src = self.sources[SCATTER_ITEMS[item][0]].at[:, :, self.core, :, :, self.columns(item)]
        return pltpu.make_async_copy(src, self.own[item], self.sems.own.at[item])

    def x_copy(self, item):
        own = self.own[item]
        if self.order(item) == 0:
            src, dst = own.at[self.y, 1 - self.x], self.second_in[item].at[0]
        else:
            src, dst = own.at[:, 1 - self.x], self.first_in[item]
        return remote(
            src, dst, self.sems.x_send.at[item], self.sems.x_recv.at[item], self.side, self.place
        )

    def y_copy(self, item, k):
        other_y = self.ahead[k]
        own = self.own[item]
        if self.order(item) == 0:
            src, dst = own.at[other_y], self.first_in[item].at[k]
        else:
            src, dst = own.at[other_y, self.x], self.second_in[item].at[k]
        return remote(
            src,
            dst,
            self.sems.y_send.at[item, k],
            self.sems.y_recv.at[item, k],
            dp_of(other_y, self.x, self.core),
            self.place,
        )

    def stage_begin(self, item):
        self.to_twin(item).start()
        if item < FIRST_ITEMS:
            self.own_in(item).start()

    def stage_core(self, item):
        if item < FIRST_ITEMS:
            self.own_in(item).wait()
        self.to_twin(item).wait_recv()
        own, came = self.own[item], self.from_twin[item]

        def step(i, carry):
            a, b, z = i // (2 * self.count), i // self.count % 2, i % self.count
            own[a, b, z] = plus(own[a, b, z], came[a, b, z])
            return carry

        lax.fori_loop(0, 2 * self.lines * self.count, step, 0)
        if self.order(item) == 0:
            for k in range(self.lines - 1):
                self.y_copy(item, k).start()
        else:
            self.x_copy(item).start()

    def stage_first(self, item):
        own, came = self.own[item], self.first_in[item]
        y, x, lines = self.y, self.x, self.lines
        if self.order(item) == 0:
            for k in range(lines - 1):
                self.y_copy(item, k).wait_recv()

            def step(i, carry):
                b, z = i // self.count, i % self.count
                total = own[y, b, z]
                for k in range(lines - 1):
                    total = plus(total, came[k, b, z])
                own[y, b, z] = total
                return carry

            lax.fori_loop(0, 2 * self.count, step, 0)
            self.x_copy(item).start()
        else:
            self.x_copy(item).wait_recv()

            def step(i, carry):
                a, z = i // self.count, i % self.count
                own[a, x, z] = plus(own[a, x, z], came[a, z])
                return carry

            lax.fori_loop(0, lines * self.count, step, 0)
            for k in range(lines - 1):
                self.y_copy(item, k).start()

    def mine(self, item, z):
        return self.own[item].at[self.y, self.x, z]

    def z_copy(self, item, z, way):
        return remote(
            self.mine(item, z),
            self.line_in[item].at[way, z],
            self.sems.z_send.at[item, z],
            self.sems.z_recv.at[item, way, z],
            self.dp,
            self.place + 1 - 2 * way,
        )

    def z_forward(self, item, way, first):
        def step(z, carry):
            @pl.when((z - self.place) * (1 - 2 * way) > 0)
            def _():
                if not first:
                    self.z_copy(item, z, way).wait_recv()
                    ref = self.mine(item, z)
                    ref[...] = plus(ref[...], self.line_in[item][way, z])
                self.z_copy(item, z, way).start()

            return carry

        lax.fori_loop(0, self.count, step, 0)

    def stage_second(self, item):
        own, came = self.own[item], self.second_in[item]
        y, x = self.y, self.x
        if self.order(item) == 0:
            self.x_copy(item).wait_recv()
        else:
            for k in range(self.lines - 1):
                self.y_copy(item, k).wait_recv()

        def step(z, carry):
            total = own[y, x, z]
            for k in range(came.shape[0]):
                total = plus(total, came[k, z])
            own[y, x, z] = total
            return carry

        lax.fori_loop(0, self.count, step, 0)

        self.each_way(lambda way, depth: pl.when(depth == 0)(lambda: self.z_forward(item, way, True)))

    def each_way(self, body):
        def step(way, carry):
            body(way, self.place + way * (self.count - 1 - 2 * self.place))
            return carry

        lax.fori_loop(0, 2, step, 0)

    def stage_hop(self, hop, item):
        self.each_way(lambda way, depth: pl.when(depth == hop)(lambda: self.z_forward(item, way, False)))

    def stage_last(self, item):
        out = self.outs[SCATTER_ITEMS[item][0]]
        columns = self.columns(item)
        place = self.place
        out[:, columns] = self.mine(item, place)[...].astype(jnp.float32)

        def add(way):
            self.z_copy(item, place, way).wait_recv()
            out[:, columns] += self.line_in[item][way, place].astype(jnp.float32)

        self.each_way(lambda way, depth: pl.when(depth > 0)(lambda: add(way)))

    def layer_copies(self, fn_remote, fn_local):
        seqs = self.layer_in.shape[0]
        for k in range(seqs):
            chip = seqs * self.core + k
            home = (chip == self.place) & (self.core == self.place // seqs)

            @pl.when(home)
            def _():
                fn_local(k)

            @pl.when(jnp.logical_not(home))
            def _():
                fn_remote(k, chip)

    def layer_remote(self, k, chip):
        seqs = self.layer_in.shape[0]
        row = self.place % seqs
        return remote(
            self.layer_in.at[k],
            self.layer_out.at[row],
            self.sems.layer_send.at[k],
            self.sems.layer_recv.at[row],
            dp_of(self.y, self.x, self.place // seqs),
            chip,
        )

    def layer_start(self):
        row = self.place % self.layer_in.shape[0]
        self.layer_copies(
            lambda k, chip: self.layer_remote(k, chip).start(),
            lambda k: pltpu.make_async_copy(
                self.layer_in.at[k], self.layer_out.at[row], self.sems.layer_recv.at[row]
            ).start(),
        )

    def stage_hop_one(self, item):
        self.stage_hop(1, item)

    def stage_hops(self, item):
        for hop in range(2, self.count - 1):
            self.stage_hop(hop, item)

    def stages(self):
        return (
            self.stage_core,
            self.stage_first,
            self.stage_second,
            self.stage_hop_one,
            self.stage_hops,
            self.stage_last,
        )

    def finish(self):
        for item in range(len(SCATTER_ITEMS)):
            self.to_twin(item).wait_send()
            self.x_copy(item).wait_send()
            for k in range(self.lines - 1):
                self.y_copy(item, k).wait_send()

            def drain(z, carry):
                @pl.when(z > self.place)
                def _():
                    self.z_copy(item, z, 0).wait_send()

                @pl.when(z < self.place)
                def _():
                    self.z_copy(item, z, 1).wait_send()

                return carry

            lax.fori_loop(0, self.count, drain, 0)
        for r in range(self.layer_in.shape[0]):
            dst = self.layer_out.at[r]
            remote(
                dst, dst, self.sems.layer_send.at[0], self.sems.layer_recv.at[r], self.twin, self.place
            ).wait_recv()
        self.layer_copies(lambda k, chip: self.layer_remote(k, chip).wait_send(), lambda k: None)


class ScatterSems(NamedTuple):
    own: object
    twin_send: object
    twin_recv: object
    x_send: object
    x_recv: object
    y_send: object
    y_recv: object
    z_send: object
    z_recv: object
    layer_send: object
    layer_recv: object


def plus(left, right):
    return left + right


def scatter_scratch(shapes, lines, count, seqs):
    items = len(SCATTER_ITEMS)
    own, first_in, second_in, line_in = [], [], [], []
    for array, _, parts, order in SCATTER_ITEMS:
        rows, cols, kind = shapes[array]
        cols = cols // parts
        own.append(pltpu.VMEM((lines, 2, count, rows, cols), kind))
        if order == 0:
            first_in.append(pltpu.VMEM((lines - 1, 2, count, rows, cols), kind))
            second_in.append(pltpu.VMEM((1, count, rows, cols), kind))
        else:
            first_in.append(pltpu.VMEM((lines, count, rows, cols), kind))
            second_in.append(pltpu.VMEM((lines - 1, count, rows, cols), kind))
        line_in.append(pltpu.VMEM((2, count, rows, cols), kind))
    dma = pltpu.SemaphoreType.DMA
    sems = [dma((FIRST_ITEMS,))] + [dma((items,))] * 4
    sems += [dma((items, lines - 1))] * 2 + [dma((items, count)), dma((items, 2, count))]
    sems += [dma((seqs,))] * 2
    return own[:FIRST_ITEMS] + own + first_in + second_in + line_in, sems


class BackInputs(NamedTuple):
    gate: object
    up: object
    down: object
    output: object
    coef: object
    resid: object
    layer: object
    qt: object
    kt: object
    vt: object
    got: object
    out: object
    normed: object
    stream: object
    tap: object
    attend: object
    lse: object
    key_marks: object
    small: object
    gain_two: object
    table: object
    rows: object
    idm: object


class BackWork(NamedTuple):
    grads: object
    away: object
    came: object
    wide: object
    one_hot: object
    src_qkv: object
    src_table: object
    src_small: object
    swap_send: object
    swap_recv: object
    coef_sem: object
    resid_sem: object
    load_sem: object
    wqkv: object
    picked: object
    rows: object


LATE_LOADS = 8


def backward_kernel(*refs):
    ref = BackInputs(*refs[: len(BackInputs._fields)])
    late_refs = refs[-LATE_LOADS:]
    refs = refs[:-LATE_LOADS]
    late = slice(7, 7 + LATE_LOADS)
    waiting = ref[late]
    ref = ref._replace(**dict(zip(ref._fields[late], late_refs)))
    rest = refs[len(BackInputs._fields) :]
    outs, layer_out = rest[:9], rest[9]
    rest = rest[10:]
    held = FIRST_ITEMS + 4 * len(SCATTER_ITEMS)
    buffers, rest = rest[:held], rest[held:]
    sems = ScatterSems(*rest[: len(ScatterSems._fields)])
    own = BackWork(*rest[len(ScatterSems._fields) :])
    sources = (
        own.src_qkv.at[0],
        own.src_qkv.at[1],
        own.src_qkv.at[2],
        ref.output,
        ref.gate,
        ref.up,
        ref.down,
        own.src_table,
        own.src_small,
    )
    scatter = Scatter(sources, outs, ref.layer, layer_out, buffers, sems)
    stages = scatter.stages()
    width, tokens = ref.qt.shape
    pairs = width // 128
    bias = own.one_hot.at[0 : ref.kt.shape[1], 0:tokens]
    scatter.meet()
    for item in range(FIRST_ITEMS):
        scatter.stage_begin(item)

    queue = [[functools.partial(stages[stage], item) for stage, item in group] for group in SCHEDULE]

    def tick():
        for task in queue.pop(0):
            task()

    loads = []
    for k in range(LATE_LOADS):
        loads.append(pltpu.make_async_copy(waiting[k], late_refs[k], own.load_sem.at[k]))
        loads[k].start()
    for k in range(3):
        weight = ref.attend.at[:, k * width : (k + 1) * width]
        part = own.wqkv.at[k * width : (k + 1) * width]
        loads.append(pltpu.make_async_copy(weight, part, own.load_sem.at[LATE_LOADS + k]))
        loads[-1].start()
    scatter.layer_start()
    tick()
    fill_bias(bias, ref.key_marks, ref.key_marks.at[:, 0:tokens])
    for load in loads[:5]:
        load.wait()

    def swap(i, which):
        rows = pl.ds(pl.multiple_of(which * width + 128 * i, 128), 128)
        return remote(
            own.away.at[rows],
            own.came.at[rows],
            own.swap_send.at[which, i],
            own.swap_recv.at[which, i],
            scatter.twin,
            scatter.place,
        )

    ticks = [queue.pop(0) for _ in range(2 * pairs)]

    def pair_tasks(groups, i):
        for k, group in enumerate(groups):
            if group:

                @pl.when(i == k)
                def _():
                    for task in group:
                        task()

    def pair_step(i, carry):
        at = pl.ds(pl.multiple_of(128 * i, 128), 128)
        attend_backward_pair(
            ref.qt.at[at],
            ref.kt.at[at],
            ref.vt.at[at],
            ref.got.at[at],
            ref.out.at[at],
            ref.lse.at[i],
            bias,
            own.grads.at[at],
            own.grads.at[pl.ds(pl.multiple_of(width + 128 * i, 128), 128)],
            own.grads.at[pl.ds(pl.multiple_of(2 * width + 128 * i, 128), 128)],
            own.away.at[at],
            own.away.at[pl.ds(pl.multiple_of(width + 128 * i, 128), 128)],
            lambda: pair_tasks(ticks[0::2], i),
        )
        swap(i, 0).start()
        swap(i, 1).start()
        pair_tasks(ticks[1::2], i)
        return carry

    lax.fori_loop(0, pairs, pair_step, 0)

    for load in loads[5:]:
        load.wait()
    wide = own.wide
    normed_t = own.one_hot.at[0:width, 0:tokens]
    normed_t[...] = ref.normed[...].T
    coef = own.came.at[0 : KW * VOCAB]

    def coef_copy():
        return pltpu.make_async_copy(ref.coef, coef, own.coef_sem)

    def hand_out(source):
        lines, _, _, count, size, _ = source.shape
        total = lines * 4 * count

        if size % 8:
            for o in range(total):
                where = (o // (4 * count), o // (2 * count) % 2, o // count % 2, o % count)
                source[where] = wide[size * o : size * (o + 1)].astype(source.dtype)
        else:

            def step(o, carry):
                where = (o // (4 * count), o // (2 * count) % 2, o // count % 2, o % count)
                source[where] = wide[pl.ds(pl.multiple_of(size * o, 8), size)].astype(source.dtype)
                return carry

            lax.fori_loop(0, total, step, 0)

    def take(count):
        groups = [queue.pop(0) for _ in range(count)]

        def run(i):
            for k, group in enumerate(groups):
                if group:

                    @pl.when(i == k)
                    def _():
                        for task in group:
                            task()

        return run

    def third(i):
        return pl.ds(pl.multiple_of(i * width, width), width)

    def add_halves():
        def add_half(j, carry):
            which, i = j // pairs, j % pairs
            swap(i, which).wait_recv()
            rows = pl.ds(pl.multiple_of(which * width + 128 * i, 128), 128)
            at = pl.ds(pl.multiple_of((which + 1) * width + 128 * i, 128), 128)
            own.grads[at] = plus(own.grads[at], own.came[rows])
            return carry

        lax.fori_loop(0, 2 * pairs, add_half, 0)
        coef_copy().start()

    weight_tasks = take(3)

    def weight_step(i, carry):
        pl.when(i == 1)(add_halves)
        wide[...] = mm_nt(normed_t[...], own.grads[third(i)])
        hand_out(own.src_qkv.at[i])
        for k in range(3):
            pl.when(i == k)(functools.partial(scatter.stage_begin, FIRST_ITEMS + k))
        weight_tasks(i)
        return carry

    lax.fori_loop(0, 3, weight_step, 0)

    norm_tasks = take(1)
    wide[:, 0:tokens] = jnp.zeros((width, tokens), jnp.float32)

    def norm_step(i, carry):
        wide[:, 0:tokens] += mm(own.wqkv[third(i)], own.grads[third(i)])
        norm_tasks(i - 1)
        return carry

    lax.fori_loop(0, 3, norm_step, 0)
    normed_grad = wide[:, 0:tokens].T
    resid_copy = pltpu.make_async_copy(ref.resid, wide.at[0:tokens], own.resid_sem)
    resid_copy.start()
    stream = ref.stream[...]
    gain = ref.small[KW + 1 : KW + 2]
    scale = lax.rsqrt(jnp.mean(stream * stream, axis=-1, keepdims=True) + 1e-06)
    gain_grad = jnp.sum(normed_grad * stream * scale, axis=0, keepdims=True)
    scaled = normed_grad * gain
    inner = jnp.mean(scaled * stream, axis=-1, keepdims=True)
    resid_copy.wait()
    grad16 = (wide[0:tokens] + scale * scaled - stream * (scale * scale * scale * inner)).astype(jnp.bfloat16)
    tick()
    coef_copy().wait()
    tok_backward_body(grad16, coef, ref, own, tick, take)
    hand_out(own.src_table)
    scatter.stage_begin(FIRST_ITEMS + 3)
    rows = jnp.concatenate([own.rows[0 : KW + 1], gain_grad, ref.gain_two[...]], axis=0)
    source = own.src_small
    lines, _, _, count, _, _ = source.shape
    total = lines * 4 * count
    for o in range(total):
        where = (o // (4 * count), o // (2 * count) % 2, o // count % 2, o % count)
        source[where] = lane_shift(rows, o * (width // total))[:, 0:128]
    scatter.stage_begin(FIRST_ITEMS + 4)
    while queue:
        tick()
    scatter.finish()

    def drain(i, carry):
        swap(i, 0).wait_send()
        swap(i, 1).wait_send()
        return carry

    lax.fori_loop(0, pairs, drain, 0)


def backward_all(arrays, shapes):
    count = lax.axis_size("seq")
    lines = lax.axis_size("dp") // 4
    total = lines * 4 * count
    vmem = pl.BlockSpec(memory_space=pltpu.VMEM)
    hbm = pl.BlockSpec(memory_space=pltpu.HBM)
    layer = arrays.layer
    width, tokens = arrays.qt.shape
    out_shape = [jax.ShapeDtypeStruct(shape[:2], jnp.float32) for shape in shapes]
    out_shape.append(jax.ShapeDtypeStruct(layer.shape, layer.dtype))
    buffers, sems = scatter_scratch(shapes, lines, count, layer.shape[0])
    views = list(arrays)
    for k in range(4):
        grad = arrays[k]
        views[k] = grad.reshape(lines, 2, 2, count, grad.shape[0] // total, grad.shape[1])

    def source(index):
        rows, cols, kind = shapes[index]
        return pltpu.VMEM((lines, 2, 2, count, rows, cols), kind)

    half = jnp.bfloat16
    own = [
        pltpu.VMEM((3 * width, tokens), half),
        pltpu.VMEM((2 * width, tokens), half),
        pltpu.VMEM((2 * width, tokens), half),
        pltpu.VMEM((width, width), jnp.float32),
        pltpu.VMEM((KW * VOCAB, arrays.idm.shape[1]), half),
        pltpu.VMEM((3,) + source(0).shape, half),
        source(7),
        source(8),
        pltpu.SemaphoreType.DMA((2, width // 128)),
        pltpu.SemaphoreType.DMA((2, width // 128)),
        pltpu.SemaphoreType.DMA,
        pltpu.SemaphoreType.DMA,
        pltpu.SemaphoreType.DMA((LATE_LOADS + 3,)),
        pltpu.VMEM((3 * width, width), half),
        pltpu.VMEM((KW * VOCAB, 1), jnp.float32),
        pltpu.VMEM((8, width), jnp.float32),
    ]
    return pl.pallas_call(
        backward_kernel,
        name="backward_all",
        out_shape=out_shape,
        in_specs=[hbm] * (8 + LATE_LOADS) + [vmem] * (len(views) - 8 - LATE_LOADS),
        out_specs=[vmem] * 9 + [hbm],
        scratch_shapes=buffers + sems + own + [pltpu.VMEM(a.shape, a.dtype) for a in arrays[7 : 7 + LATE_LOADS]],
        compiler_params=pltpu.CompilerParams(
            collective_id=1, has_side_effects=True, vmem_limit_bytes=63 * 1024 * 1024
        ),
    )(*views)


def tok_forward_body(own, core, tokens, tick):
    ids_ref, marks_ref, table_ref, small_ref = own.ids_pad, own.marks_pad, own.table, own.small
    table_ref = table_ref.at[:, 0 : own.stream.shape[1]]
    stream_ref, normed_ref, coef_ref, tap_ref = own.stream, own.normed, own.coef, own.tap
    rows_ref, idm_ref, one_hot = own.rows, own.idm, own.one_hot
    half_bytes = 2 * tokens
    span = one_hot.shape[1]
    wide = span + 2 * LEFT
    first = pl.ds(pl.multiple_of(core * half_bytes, 128), wide)
    ids = ids_ref[:, first]
    marks = marks_ref[:, first]
    for tap in range(KW):
        by = tap - KW // 2
        same = (lane_shift(marks, by) == marks) & (marks > 0)
        idm_ref[tap : tap + 1] = jnp.where(same, lane_shift(ids, by), -1)[0:1, LEFT : LEFT + span]
    tick()
    fill_one_hot(one_hot, idm_ref)

    tick()
    score = jnp.broadcast_to(small_ref[KW : KW + 1], (8, small_ref.shape[1])).astype(jnp.bfloat16)

    def step(tap, carry):
        product = table_ref[...].astype(jnp.float32) * small_ref[pl.ds(tap, 1)]
        high, low = split_two(product)
        tap_ref[tap_rows(tap)] = high
        own.scored[:, tap_rows(tap)] = mm_nt(score, high) + mm_nt(score, low)
        return carry

    lax.fori_loop(0, KW, step, 0)
    tick()
    high, low = split_two(own.scored[...])
    u_row = mm(high, one_hot[...]) + mm(low, one_hot[...])

    tick()
    high = u_row.astype(jnp.bfloat16).astype(jnp.float32)
    marks_here = marks[:, LEFT : LEFT + span].astype(jnp.float32)
    away = marks_ref[:, pl.ds(pl.multiple_of((1 - core) * half_bytes, 128), wide)][:, LEFT : LEFT + span]
    away = away.astype(jnp.float32)
    packed = jnp.concatenate([marks_here, high, u_row - high, away], axis=0).astype(jnp.bfloat16)
    shape = (span, wide // 2)
    twice = 2 * lax.broadcasted_iota(jnp.int32, shape, 1) - lax.broadcasted_iota(jnp.int32, shape, 0) - LEFT
    marks_of, u_of = [], []
    for e in range(2):
        pick = (twice == -e).astype(jnp.float32).astype(jnp.bfloat16)
        apart = mm(packed, pick)
        marks_of.append(apart[0:8])
        u_of.append(apart[8:16] + apart[16:24])
        if e == 0:
            kept = slice(LEFT, LEFT + tokens)
            both = jnp.concatenate([apart[0:1, kept], apart[24:25, kept]], axis=1)
            own.marks[...] = both.astype(jnp.int32)

    tick()
    inside, inverse = pool_rows(marks_of, core, half_bytes)
    prob = {}
    for e in range(2):
        shifted = {}
        for s in range(1 - MAXBLOCK, MAXBLOCK):
            f = (e + s) % 2
            shifted[s] = lane_shift(u_of[f], (e + s - f) // 2)
        scores = [u_of[e]]
        for b in range(2, MAXBLOCK + 1):
            total = u_of[e]
            for s in range(1 - b, b):
                if s != 0:
                    total = total + inside[b, e, s] * shifted[s]
            scores.append(total * inverse[b, e])
        top = scores[0]
        for value in scores[1:]:
            top = jnp.maximum(top, value)
        expo = [jnp.exp(value - top) for value in scores]
        whole = expo[0] + expo[1] + expo[2] + expo[3]
        for b in range(1, MAXBLOCK + 1):
            prob[b, e] = expo[b - 1] / whole
            rows_ref[2 * b + e : 2 * b + e + 1] = prob[b, e][0:1]
        rows_ref[e : e + 1] = marks_of[e][0:1]
    coefs = band_coefs({key: 0.5 * value for key, value in prob.items()}, inside, inverse)
    gain = small_ref[KW + 1 : KW + 2]
    tick()
    for i in range(tokens // BAND):
        matrix = band_matrix(coefs, i).astype(jnp.bfloat16)
        lanes = slice(i * BAND, (i + 1) * BAND)
        part = mm(one_hot[:, 2 * i * BAND : (2 * i + 3) * BAND], matrix).astype(jnp.bfloat16)
        coef_ref[:, lanes] = part
        stream = mm_tn(part, tap_ref[...])
        stream_ref[lanes] = stream
        scale = lax.rsqrt(jnp.mean(stream * stream, axis=-1, keepdims=True) + 1e-06)
        normed_ref[lanes] = (stream * scale * gain).astype(jnp.bfloat16)
        if i < tokens // BAND - 1:
            tick()


FUSED_ITEMS = (
    (4, 0, 1, 0, 0),
    (0, 0, 2, 1, 1),
    (0, 1, 2, 0, 1),
    (2, 1, 2, 1, 2),
    (3, 0, 1, 0, 3),
    (2, 0, 2, 0, 4),
    (1, 0, 1, 1, 5),
)
FUSED_SCHEDULE = (
    (
        (0, 0, 0), (1, 0, 0), (0, 1, 0), (1, 1, 0), (2, 0, 1), (3, 0, 0),
        (3, 1, 0), (2, 0, 2), (4, 0, 0), (3, 0, 1), (2, 0, 3), (2, 1, 1),
        (0, 2, 0), (3, 0, 2), (4, 1, 0), (3, 0, 3), (2, 1, 2), (4, 0, 1),
        (3, 1, 1), (2, 1, 3), (1, 2, 0), (2, 2, 1), (0, 3, 0), (4, 0, 2),
        (4, 0, 3), (2, 2, 2),
    ),
    (),
    (
        (2, 2, 3), (1, 3, 0), (2, 3, 1), (0, 4, 0), (3, 1, 2),
    ),
    (
        (2, 3, 2), (3, 1, 3), (3, 2, 0), (4, 1, 1),
    ),
    ((3, 2, 1),),
    (
        (2, 3, 3), (1, 4, 0), (2, 4, 1), (0, 5, 0), (3, 2, 2),
    ),
    ((3, 2, 3),),
    (
        (2, 4, 2), (3, 3, 0),
    ),
    (
        (2, 4, 3), (1, 5, 0), (2, 5, 1), (3, 3, 1), (4, 1, 2), (4, 1, 3),
        (2, 5, 2),
    ),
    (
        (3, 3, 2), (4, 2, 0),
    ),
    (
        (2, 5, 3), (5, 0, 0), (3, 3, 3), (4, 2, 1),
    ),
    (
        (3, 4, 0), (3, 4, 1),
    ),
    (
        (3, 4, 2), (4, 2, 2), (4, 2, 3), (4, 3, 0),
    ),
    (),
    ((3, 4, 3),),
    (),
    ((3, 5, 0),),
    ((3, 5, 1),),
    (),
    ((4, 3, 1),),
    (
        (3, 5, 2), (4, 5, 0),
    ),
    ((3, 5, 3),),
    (
        (4, 3, 2), (4, 3, 3), (4, 5, 1),
    ),
    ((4, 4, 0),),
    (
        (4, 4, 1), (4, 5, 2),
    ),
    (
        (4, 4, 2), (4, 4, 3), (4, 5, 3),
    ),
    (),
)


class Gather:
    def __init__(self, ins, outs, cells_in, cells_out, cot_in, cot_out, sems):
        self.ins, self.outs, self.sems = ins, outs, sems
        self.cells_in, self.cells_out, self.cot_in, self.cot_out = cells_in, cells_out, cot_in, cot_out
        self.y, self.x, self.core, self.place, self.lines, self.count = position()
        y, x, core = self.y, self.x, self.core
        self.group = y * 2 + x
        self.dp = dp_of(y, x, core)
        self.twin = dp_of(y, x, 1 - core)
        self.side = dp_of(y, 1 - x, core)
        self.ahead = [(y + k) % self.lines for k in range(1, self.lines)]
        self.phases = {}
        for item, entry in enumerate(FUSED_ITEMS):
            self.phases.setdefault(entry[4], []).append(item)

    def meet(self):
        targets = [(self.twin, self.place), (self.side, self.place)]
        for k in range(1, self.count):
            other = (self.place + k) % self.count
            targets += [(self.dp, other), (self.twin, other)]
        for other_y in self.ahead:
            targets.append((dp_of(other_y, self.x, self.core), self.place))
        meet(targets)

    def lanes(self, item):
        array, part, parts, _, _ = FUSED_ITEMS[item]
        cols = self.ins[array].shape[1] // parts
        return pl.ds(part * cols, cols)

    def shard(self, item):
        return self.ins[FUSED_ITEMS[item][0]].at[:, self.lanes(item)]

    def rows(self, item, first, blocks):
        array = FUSED_ITEMS[item][0]
        size = self.ins[array].shape[0]
        start = pl.multiple_of(first * size, 8)
        return self.outs[array].at[pl.ds(start, blocks * size), self.lanes(item)]

    def block(self, item, g, z):
        return self.rows(item, (g * 2 + self.core) * self.count + z, 1)

    def group_block(self, item, g, core):
        return self.rows(item, (g * 2 + core) * self.count, self.count)

    def came(self, item, g, z):
        return self.sems.recv.at[item, g * self.count + z]

    def arrived(self, item, g, z):
        dst = self.block(item, g, z)
        remote(dst, dst, self.sems.x.at[item], self.came(item, g, z), self.twin, self.place).wait_recv()

    def to_side(self, item, src, g, z):
        remote(
            src, self.block(item, g, z), self.sems.x.at[item], self.came(item, g, z), self.side, self.place
        ).start()

    def to_lines(self, item, src, g, z):
        for other_y in self.ahead:
            remote(
                src,
                self.block(item, g, z),
                self.sems.y.at[item],
                self.came(item, g, z),
                dp_of(other_y, self.x, self.core),
                self.place,
            ).start()

    def to_z(self, item, src, z, way):
        return remote(
            src,
            self.block(item, self.group, z),
            self.sems.z.at[item, z, way],
            self.came(item, self.group, z),
            self.dp,
            self.place + 1 - 2 * way,
        )

    def to_twin(self, item, g):
        src = self.group_block(item, g, self.core)
        remote(
            src, src, self.sems.twin.at[item], self.sems.twin_recv.at[item, g], self.twin, self.place
        ).start()

    def own_copy(self, item):
        return pltpu.make_async_copy(
            self.shard(item), self.block(item, self.group, self.place), self.sems.own.at[item]
        )

    def task_own(self, phase):
        for item in self.phases[phase]:
            src = self.shard(item)

            @pl.when(self.place < self.count - 1)
            def _():
                self.to_z(item, src, self.place, 0).start()

            @pl.when(self.place > 0)
            def _():
                self.to_z(item, src, self.place, 1).start()

            self.own_copy(item).start()

    def task_sides(self, phase):
        for item in self.phases[phase]:
            src = self.shard(item)
            self.to_side(item, src, self.group, self.place)
            self.to_lines(item, src, self.group, self.place)

    def both_ways(self, step, body):
        def way_step(way, carry):
            z = self.place + step * (2 * way - 1)

            @pl.when((z >= 0) & (z < self.count))
            def _():
                body(z, way)

            return carry

        lax.fori_loop(0, 2, way_step, 0)

    def steps(self, step, body):
        if step < 3:
            body(step)
            return

        def loop(s, carry):
            body(s)
            return carry

        lax.fori_loop(3, self.count, loop, 0)

    def task_first(self, phase, step):
        items = self.phases[phase]

        def receive(z, way):
            for item in items:
                self.arrived(item, self.group, z)
                src = self.block(item, self.group, z)
                then = self.place + 1 - 2 * way
                onward = (then >= 0) & (then < self.count)

                @pl.when(onward)
                def _():
                    self.to_z(item, src, z, way).start()

                self.to_side(item, src, self.group, z)
                self.to_lines(item, src, self.group, z)

        self.steps(step, lambda s: self.both_ways(s, receive))
        if step == 3:
            for item in items:
                self.own_copy(item).wait()
                self.to_twin(item, self.group)

    def at_distance(self, step, body):
        if step == 0:
            body(self.place, 0)
        else:
            self.steps(step, lambda s: self.both_ways(s, body))

    def task_second(self, phase, step):
        items = self.phases[phase]

        def receive(z, way):
            for item in items:
                if FUSED_ITEMS[item][3] == 0:
                    g = self.y * 2 + (1 - self.x)
                    self.arrived(item, g, z)
                    self.to_lines(item, self.block(item, g, z), g, z)
                else:
                    for other_y in self.ahead:
                        g = other_y * 2 + self.x
                        self.arrived(item, g, z)
                        self.to_side(item, self.block(item, g, z), g, z)

        self.at_distance(step, receive)
        if step == 3:
            for item in items:
                if FUSED_ITEMS[item][3] == 0:
                    self.to_twin(item, self.y * 2 + (1 - self.x))
                else:
                    for other_y in self.ahead:
                        self.to_twin(item, other_y * 2 + self.x)

    def task_third(self, phase, step):
        items = self.phases[phase]

        def rest(item):
            if FUSED_ITEMS[item][3] == 0:
                return [other_y * 2 + x for other_y in self.ahead for x in (self.x, 1 - self.x)]
            return [other_y * 2 + (1 - self.x) for other_y in [self.y] + self.ahead]

        def receive(z, way):
            for item in items:
                for g in rest(item):
                    self.arrived(item, g, z)

        self.at_distance(step, receive)
        if step == 3:
            for item in items:
                for g in rest(item):
                    self.to_twin(item, g)

    def full(self, item):
        def step(g, carry):
            dst = self.group_block(item, g, 1 - self.core)
            remote(
                dst, dst, self.sems.twin.at[item], self.sems.twin_recv.at[item, g], self.twin, self.place
            ).wait_recv()
            return carry

        lax.fori_loop(0, self.lines * 2, step, 0)

    def cell_copies(self, fn_remote, fn_local):
        seqs = self.cells_in.shape[0]
        for r in range(seqs):
            chip = seqs * self.core + r
            for c in range(2):
                home = (chip == self.place) & (self.core == c)

                @pl.when(home)
                def _():
                    fn_local(r)

                @pl.when(jnp.logical_not(home))
                def _():
                    fn_remote(r, c, chip)

    def cell_remote(self, r, c, chip):
        return remote(
            self.cells_in.at[r],
            self.cells_out.at[self.place],
            self.sems.cell_send.at[r, c],
            self.sems.cell_recv.at[self.place],
            dp_of(self.y, self.x, c),
            chip,
        )

    def cells_start(self):
        self.cell_copies(
            lambda r, c, chip: self.cell_remote(r, c, chip).start(),
            lambda r: pltpu.make_async_copy(
                self.cells_in.at[r], self.cells_out.at[self.place], self.sems.cell_recv.at[self.place]
            ).start(),
        )

    def cells_wait(self):
        for q in range(self.count):
            dst = self.cells_out.at[q]
            remote(
                dst, dst, self.sems.cell_send.at[0, 0], self.sems.cell_recv.at[q], self.twin, self.place
            ).wait_recv()

    def cot_copies(self, fn_remote, fn_local):
        seqs = self.cot_in.shape[0]
        for r in range(seqs):
            chip = seqs * self.core + r
            home = (chip == self.place) & (self.core == self.place // seqs)

            @pl.when(home)
            def _():
                fn_local(r)

            @pl.when(jnp.logical_not(home))
            def _():
                fn_remote(r, chip)

    def cot_remote(self, r, chip):
        seqs = self.cot_in.shape[0]
        slot = self.place % seqs
        return remote(
            self.cot_in.at[r],
            self.cot_out.at[slot],
            self.sems.cot_send.at[r],
            self.sems.cot_recv.at[slot],
            dp_of(self.y, self.x, self.place // seqs),
            chip,
        )

    def task_cot(self):
        slot = self.place % self.cot_in.shape[0]
        self.cot_copies(
            lambda r, chip: self.cot_remote(r, chip).start(),
            lambda r: pltpu.make_async_copy(
                self.cot_in.at[r], self.cot_out.at[slot], self.sems.cot_recv.at[slot]
            ).start(),
        )

    def task(self, kind, phase, step):
        if kind == 0:
            self.task_own(phase)
        elif kind == 1:
            self.task_sides(phase)
        elif kind == 2:
            self.task_first(phase, step)
        elif kind == 3:
            self.task_second(phase, step)
        elif kind == 4:
            self.task_third(phase, step)
        else:
            self.task_cot()

    def finish(self, waited):
        count, groups = self.count, self.lines * 2
        for item in range(len(FUSED_ITEMS)):
            if item not in waited:
                self.full(item)
            tree = FUSED_ITEMS[item][3]

            def sent(blocks, sem):
                src = self.rows(item, 0, blocks)
                remote(src, src, sem, self.came(item, 0, 0), self.twin, self.place).wait_send()

            sent(count * (1 if tree == 0 else self.lines), self.sems.x.at[item])
            sent(count * (self.lines - 1) * (2 if tree == 0 else 1), self.sems.y.at[item])
            sent(count * groups, self.sems.twin.at[item])

            def drain(z, carry):
                @pl.when((z <= self.place) & (self.place < count - 1))
                def _():
                    self.to_z(item, self.block(item, self.group, z), z, 0).wait_send()

                @pl.when((z >= self.place) & (self.place > 0))
                def _():
                    self.to_z(item, self.block(item, self.group, z), z, 1).wait_send()

                return carry

            lax.fori_loop(0, count, drain, 0)
        for q in range(self.cot_in.shape[0]):
            dst = self.cot_out.at[q]
            remote(
                dst, dst, self.sems.cot_send.at[0], self.sems.cot_recv.at[q], self.twin, self.place
            ).wait_recv()
        self.cell_copies(lambda r, c, chip: self.cell_remote(r, c, chip).wait_send(), lambda r: None)
        self.cot_copies(lambda r, chip: self.cot_remote(r, chip).wait_send(), lambda r: None)


class GatherSems(NamedTuple):
    recv: object
    twin_recv: object
    z: object
    x: object
    y: object
    twin: object
    own: object
    cell_recv: object
    cell_send: object
    cot_recv: object
    cot_send: object
class FrontOuts(NamedTuple):
    cot: object
    stream: object
    normed: object
    coef: object
    tap: object
    rows: object
    idm: object
    qt: object
    kt: object
    vt: object
    out: object
    lse: object
    marks: object
    small: object
    resid: object
    normed_two: object


class FrontWork(NamedTuple):
    stream: object
    normed: object
    coef: object
    tap: object
    rows: object
    idm: object
    qt: object
    kt: object
    vt: object
    out: object
    lse: object
    marks: object
    small: object
    resid: object
    normed_two: object
    cells: object
    ids_pad: object
    marks_pad: object
    table: object
    blocks: object
    wq: object
    wk: object
    wv: object
    wo: object
    other: object
    one_hot: object
    bias: object
    scores: object
    out_sem: object
    load_sem: object
    swap_send: object
    swap_recv: object
    small_in: object
    cells_in: object
    scored: object
    pair: object
    wkv: object
    kv: object
    attend_in: object
    table_in: object


def attend_forward_pair(qt, kt, vt, bias, scores, out, lse, tasks):
    keys = kt[...].T
    chunks = keys.shape[0] // CHUNK
    for h in range(2):
        query = pair_rows(qt, h)
        own = slice(h * HEAD_DIM, (h + 1) * HEAD_DIM)
        top = None
        for c in range(chunks):
            rows = slice(c * CHUNK, (c + 1) * CHUNK)
            part = mm(keys[rows], query) + bias[rows]
            scores[h, rows] = part
            high = jnp.max(part, axis=0, keepdims=True)
            top = high if top is None else jnp.maximum(top, high)
        total = None
        summed = None
        for c in range(chunks):
            rows = slice(c * CHUNK, (c + 1) * CHUNK)
            expo = jnp.exp(scores[h, rows] - top)
            part = jnp.sum(expo, axis=0, keepdims=True)
            total = part if total is None else total + part
            part = mm(vt[own, rows], expo.astype(jnp.bfloat16))
            summed = part if summed is None else summed + part
        out[own] = (summed / total).astype(jnp.bfloat16)
        lse[h : h + 1] = top + jnp.log(total)
        if h == 0:
            tasks()


def forward_kernel(*refs):
    arrays = 5
    attend_parts, feed_parts, embed_table = refs[:4], refs[4:7], refs[7]
    byte_ids, segments, taps, vectors, cot_in = refs[8:13]
    rest = refs[13:]
    full, cells_out = rest[:arrays], rest[arrays]
    kept = len(FrontOuts._fields)
    to = FrontOuts(*rest[arrays + 1 : arrays + 1 + kept])
    rest = rest[arrays + 1 + kept :]
    sems = GatherSems(*rest[: len(GatherSems._fields)])
    own = FrontWork(*rest[len(GatherSems._fields) :])
    small_in, cells_in = own.small_in, own.cells_in
    tokens, width = own.stream.shape
    own = own._replace(
        normed=own.pair.at[0:tokens],
        other=own.pair.at[tokens : 2 * tokens],
        wk=own.wkv.at[0:width],
        wv=own.wkv.at[width : 2 * width],
        kt=own.kv.at[0:width],
        vt=own.kv.at[width : 2 * width],
    )
    ins = (own.attend_in,) + tuple(feed_parts) + (own.table_in,)
    gather = Gather(ins, full, cells_in, cells_out, cot_in, to.cot, sems)
    which = {}
    for item, entry in enumerate(FUSED_ITEMS):
        which[entry[0], entry[1]] = item
    queue = [list(group) for group in FUSED_SCHEDULE]

    def tick():
        for entry in queue.pop(0):
            gather.task(*entry)

    saved = []

    def save(src, dst):
        copy = pltpu.make_async_copy(src, dst, own.out_sem.at[len(saved)])
        copy.start()
        saved.append(copy)

    def load(k, dst):
        if k % 2 == 0:
            gather.full(which[0, k // 2])
        copy = pltpu.make_async_copy(full[0].at[:, k * width : (k + 1) * width], dst, own.load_sem.at[k])
        copy.start()
        return copy

    small_in[...] = jnp.zeros_like(small_in)
    small_in[0:KW, 0 : taps.shape[1]] = taps[...].astype(jnp.float32)
    small_in[KW:8, 0 : taps.shape[1]] = vectors[...]
    own.table_in[:, 0:width] = embed_table[...]
    own.table_in[:, width : width + 128] = small_in[...].astype(jnp.bfloat16)
    for k in range(4):
        own.attend_in[:, k * width : (k + 1) * width] = attend_parts[k][...]
    per_part = byte_ids.shape[1] // 128
    for r in range(byte_ids.shape[0]):
        for k in range(per_part):
            lanes = slice(128 * k, 128 * (k + 1))
            cells_in[r, k : k + 1] = byte_ids[r : r + 1, lanes]
            cells_in[r, per_part + k : per_part + k + 1] = segments[r : r + 1, lanes] + 1
    gather.meet()
    gather.cells_start()
    tick()

    core, place = gather.core, gather.place
    tokens, width = own.stream.shape
    half_bytes = 2 * tokens
    span = own.one_hot.shape[1]
    wide = span + 2 * LEFT
    gather.cells_wait()
    cell_copy = pltpu.make_async_copy(cells_out, own.cells, own.load_sem.at[4])
    cell_copy.start()
    gather.full(which[4, 0])
    load_table = pltpu.make_async_copy(full[4], own.table, own.load_sem.at[5])
    load_table.start()
    cell_copy.wait()
    ids_pad, marks_pad = own.ids_pad, own.marks_pad
    ids_pad[:, 0 : 2 * LEFT] = jnp.full((8, 2 * LEFT), -1, jnp.int32)
    marks_pad[:, 0 : 2 * LEFT] = jnp.zeros((8, 2 * LEFT), jnp.int32)
    end = 2 * LEFT + 2 * half_bytes
    ids_pad[:, end : end + 2 * LEFT] = jnp.full((8, 2 * LEFT), -1, jnp.int32)
    marks_pad[:, end : end + 2 * LEFT] = jnp.zeros((8, 2 * LEFT), jnp.int32)
    parts, per_part = own.cells.shape[0], own.cells.shape[1] // 2
    for q in range(parts):
        for r in range(per_part):
            at = slice(2 * LEFT + (q * per_part + r) * 128, 2 * LEFT + (q * per_part + r + 1) * 128)
            ids_pad[:, at] = jnp.broadcast_to(own.cells[q, r : r + 1], (8, 128))
            marks_pad[:, at] = jnp.broadcast_to(own.cells[q, per_part + r : per_part + r + 1], (8, 128))
    load_table.wait()
    own.blocks[...] = own.table[:, width : width + 128].astype(jnp.float32)
    total = gather.lines * 4 * gather.count
    chan = width // total
    lane = lax.broadcasted_iota(jnp.int32, (8, 128), 1)
    columns = [jnp.zeros((8, 128), jnp.float32) for _ in range(width // 128)]
    for o in range(total):
        piece = jnp.where(lane < chan, own.blocks[8 * o : 8 * o + 8], 0.0)
        at, by = divmod(o * chan, 128)
        turned = piece if by == 0 else pltpu.roll(piece, by, 1)
        columns[at] = columns[at] + jnp.where(lane >= by, turned, 0.0)
        if by + chan > 128:
            columns[at + 1] = columns[at + 1] + jnp.where(lane < by, turned, 0.0)
    own.small[...] = jnp.concatenate(columns, axis=1)
    save(own.small, to.small)
    tok_forward_body(own, core, tokens, tick)
    save(own.stream, to.stream)
    save(own.normed, to.normed)
    save(own.coef, to.coef)
    save(own.tap, to.tap)
    save(own.rows, to.rows)
    save(own.idm, to.idm)
    save(own.marks, to.marks)

    swap = remote(own.normed, own.other, own.swap_send, own.swap_recv, gather.twin, place)
    swap.start()
    tick()
    load_wq = load(0, own.wq)
    load_wk = load(1, own.wk)
    load_wv = load(2, own.wv)

    def project(rows, weight):
        return mm(rows[...], weight[...]).astype(jnp.bfloat16)

    load_wq.wait()
    own.qt[...] = (project(own.normed, own.wq) * HEAD_DIM ** (-0.5)).astype(jnp.bfloat16).T
    save(own.qt, to.qt)
    tick()
    load_wk.wait()
    load_wv.wait()
    groups = [queue.pop(0) for _ in range(4)]

    def project_step(i, carry):
        which, part = i % 2, i // 2

        @pl.when(i == 2)
        def _():
            swap.wait_recv()

        rows = own.pair.at[pl.ds(pl.multiple_of(part * tokens, tokens), tokens)]
        weight = own.wkv.at[pl.ds(pl.multiple_of(which * width, width), width)]
        to_rows = pl.ds(pl.multiple_of(which * width, width), width)
        own.kv[to_rows, pl.ds(pl.multiple_of(part * tokens, tokens), tokens)] = project(rows, weight).T
        for k, group in enumerate(groups):
            if group:

                @pl.when(i == k)
                def _():
                    for entry in group:
                        gather.task(*entry)

        return carry

    lax.fori_loop(0, 4, project_step, 0)
    save(own.kt, to.kt)
    save(own.vt, to.vt)
    load_wo = load(3, own.wo)
    fill_bias(own.bias, own.marks, own.marks.at[:, 0:tokens])
    pairs = width // 128
    ticks = [queue.pop(0) for _ in range(2 * pairs)]

    def pair_tasks(groups, i):
        for k, group in enumerate(groups):
            if group:

                @pl.when(i == k)
                def _():
                    for entry in group:
                        gather.task(*entry)

    def pair_step(i, carry):
        at = pl.ds(pl.multiple_of(128 * i, 128), 128)
        attend_forward_pair(
            own.qt.at[at],
            own.kt.at[at],
            own.vt.at[at],
            own.bias,
            own.scores,
            own.out.at[at],
            own.lse.at[i],
            lambda: pair_tasks(ticks[0::2], i),
        )
        pair_tasks(ticks[1::2], i)
        return carry

    lax.fori_loop(0, pairs, pair_step, 0)
    save(own.out, to.out)
    save(own.lse, to.lse)
    load_wo.wait()
    resid = own.stream[...] + mm(own.out[...].T, own.wo[...])
    own.resid[...] = resid
    save(own.resid, to.resid)
    scale = lax.rsqrt(jnp.mean(resid * resid, axis=-1, keepdims=True) + 1e-06)
    own.normed_two[...] = (resid * scale * own.small[KW + 2 : KW + 3]).astype(jnp.bfloat16)
    save(own.normed_two, to.normed_two)
    while queue:
        tick()
    gather.finish([which[0, 0], which[0, 1], which[4, 0]])
    for copy in saved:
        copy.wait()
    swap.wait_send()


def forward_all(shards, byte_ids, segments, taps, vectors, cot, tokens):
    count = lax.axis_size("seq")
    group_count = lax.axis_size(ALL)
    groups = group_count // (2 * count)
    items = len(FUSED_ITEMS)
    seqs = byte_ids.shape[0]
    cells = jax.ShapeDtypeStruct((seqs, byte_ids.shape[1] // 64, 128), jnp.int32)
    width = shards[0].shape[1]
    span = 2 * tokens + 2 * LEFT
    half, single = jnp.bfloat16, jnp.float32
    vmem = pl.BlockSpec(memory_space=pltpu.VMEM)
    hbm = pl.BlockSpec(memory_space=pltpu.HBM)
    pairs = width // 128
    held = (
        ((tokens, width), single),
        ((tokens, width), half),
        ((KW * VOCAB, tokens), half),
        ((KW * VOCAB, width), half),
        ((16, (span + 2 * LEFT) // 2), single),
        ((8, span), jnp.int32),
        ((width, tokens), half),
        ((width, 2 * tokens), half),
        ((width, 2 * tokens), half),
        ((width, tokens), half),
        ((pairs, 2, tokens), single),
        ((1, 2 * tokens), jnp.int32),
        ((8, width), single),
        ((tokens, width), single),
        ((tokens, width), half),
    )
    size = shards[0].shape[0]
    sent = [(size, 4 * width)] + [shard.shape for shard in shards[4:7]] + [(8, width + 128)]
    shapes = [jax.ShapeDtypeStruct((rows * group_count, cols), half) for rows, cols in sent]
    shapes.append(jax.ShapeDtypeStruct((count,) + cells.shape[1:], cells.dtype))
    shapes.append(jax.ShapeDtypeStruct(cot.shape, cot.dtype))
    shapes += [jax.ShapeDtypeStruct(*entry) for entry in held]
    dma = pltpu.SemaphoreType.DMA
    scratch = [
        dma((items, groups * count)),
        dma((items, groups)),
        dma((items, count, 2)),
        dma((items,)),
        dma((items,)),
        dma((items,)),
        dma((items,)),
        dma((count,)),
        dma((seqs, 2)),
        dma((seqs,)),
        dma((seqs,)),
    ]
    scratch += [pltpu.VMEM(*entry) for entry in held]
    scratch += [
        pltpu.VMEM((count,) + cells.shape[1:], cells.dtype),
        pltpu.VMEM((8, 4 * tokens + 4 * LEFT), jnp.int32),
        pltpu.VMEM((8, 4 * tokens + 4 * LEFT), jnp.int32),
        pltpu.VMEM((VOCAB, width + 128), half),
        pltpu.VMEM((8 * group_count, 128), single),
        pltpu.VMEM((width, width), half),
        pltpu.VMEM((width, width), half),
        pltpu.VMEM((width, width), half),
        pltpu.VMEM((width, width), half),
        pltpu.VMEM((tokens, width), half),
        pltpu.VMEM((KW * VOCAB, span), half),
        pltpu.VMEM((2 * tokens, tokens), single),
        pltpu.VMEM((2, 2 * tokens, tokens), single),
        dma((len(held),)),
        dma((9,)),
        dma,
        dma,
        pltpu.VMEM((8, 128), single),
        pltpu.VMEM(cells.shape, cells.dtype),
        pltpu.VMEM((8, KW * VOCAB), single),
        pltpu.VMEM((2 * tokens, width), half),
        pltpu.VMEM((2 * width, width), half),
        pltpu.VMEM((2 * width, 2 * tokens), half),
        pltpu.VMEM((shards[0].shape[0], 4 * width), half),
        pltpu.VMEM((8, width + 128), half),
    ]
    out = pl.pallas_call(
        forward_kernel,
        name="forward_all",
        out_shape=shapes,
        in_specs=[vmem] * (len(shards) + 5),
        out_specs=[hbm] * len(shapes),
        scratch_shapes=scratch,
        compiler_params=pltpu.CompilerParams(
            collective_id=0, has_side_effects=True, vmem_limit_bytes=60 * 1024 * 1024
        ),
    )(*shards, byte_ids, segments, taps, vectors, cot)
    return list(out[:5]), FrontOuts(*out[6:])

FF_BLOCK = 512


def feed_kernel(
    normed,
    cot,
    resid,
    small,
    out_t,
    w_gate,
    w_up,
    w_down,
    attend,
    gate_grad,
    up_grad,
    down_grad,
    layer,
    output_grad,
    got,
    resid_grad,
    gain_grad,
    normed_t,
    total,
    normed_grad,
    stream_here,
    out_here,
    output_here,
    late_sem,
):
    step = pl.program_id(0)
    width = resid.shape[1]
    w_output = attend.at[:, 3 * width : 4 * width]
    late = ((resid, stream_here), (out_t, out_here), (w_output, output_here))
    late = [pltpu.make_async_copy(src, dst, late_sem.at[k]) for k, (src, dst) in enumerate(late)]

    @pl.when(step == 0)
    def _():
        for copy in late:
            copy.start()
        normed_t[...] = normed[...].T
        total[...] = jnp.zeros_like(total)
        normed_grad[...] = jnp.zeros_like(normed_grad)

    gate = mm(normed[...], w_gate[...])
    up = mm(normed[...], w_up[...])
    root = 0.7978845608028654
    square = gate * gate
    bent = jnp.tanh(root * gate * (1.0 + 0.044715 * square))
    half = 0.5 * (1.0 + bent)
    act = gate * half
    slope = half + 0.5 * gate * (1.0 - bent * bent) * (root * (1.0 + 3 * 0.044715 * square))
    hidden = (act * up).astype(jnp.bfloat16)
    total[...] += mm(hidden, w_down[...])
    hidden_grad = mm_nt(cot[...], w_down[...])
    up_part = (hidden_grad * act).astype(jnp.bfloat16)
    gate_part = (hidden_grad * up * slope).astype(jnp.bfloat16)
    down_grad[...] = mm(hidden.T, cot[...]).astype(jnp.bfloat16)
    gate_grad[...] = mm(normed_t[...], gate_part).astype(jnp.bfloat16)
    up_grad[...] = mm(normed_t[...], up_part).astype(jnp.bfloat16)
    normed_grad[...] += mm_nt(gate_part, w_gate[...]) + mm_nt(up_part, w_up[...])

    @pl.when(step == pl.num_programs(0) - 1)
    def _():
        for copy in late:
            copy.wait()
        stream = stream_here[...]
        layer[...] = (stream + total[...]).astype(jnp.bfloat16)
        scale = lax.rsqrt(jnp.mean(stream * stream, axis=-1, keepdims=True) + 1e-06)
        grad = normed_grad[...]
        gain_grad[...] = jnp.sum(grad * stream * scale, axis=0, keepdims=True)
        scaled = grad * small[KW + 2 : KW + 3]
        inner = jnp.mean(scaled * stream, axis=-1, keepdims=True)
        whole = cot[...].astype(jnp.float32) + scale * scaled - stream * (scale * scale * scale * inner)
        resid_grad[...] = whole
        proj = whole.astype(jnp.bfloat16)
        output_grad[...] = mm(out_here[...], proj).astype(jnp.bfloat16)
        got[...] = mm_nt(output_here[...], proj).astype(jnp.bfloat16)


def feed_forward(normed, cot, resid, small, out_t, w_gate, w_up, w_down, attend):
    tokens, width = normed.shape
    wide = w_gate.shape[1]
    whole = lambda shape: pl.BlockSpec(shape, lambda f: (0, 0))
    hbm = pl.BlockSpec(memory_space=pltpu.HBM)
    columns = pl.BlockSpec((width, FF_BLOCK), lambda f: (0, f))
    rows = pl.BlockSpec((FF_BLOCK, width), lambda f: (f, 0))
    half, single = jnp.bfloat16, jnp.float32
    return pl.pallas_call(
        feed_kernel,
        name="feed_forward",
        grid=(wide // FF_BLOCK,),
        in_specs=[
            whole((tokens, width)),
            whole((tokens, width)),
            hbm,
            whole(small.shape),
            hbm,
            columns,
            columns,
            rows,
            hbm,
        ],
        out_specs=[
            columns,
            columns,
            rows,
            whole((tokens, width)),
            whole((width, width)),
            whole((width, tokens)),
            whole((tokens, width)),
            whole((1, width)),
        ],
        out_shape=[
            jax.ShapeDtypeStruct((width, wide), half),
            jax.ShapeDtypeStruct((width, wide), half),
            jax.ShapeDtypeStruct((wide, width), half),
            jax.ShapeDtypeStruct((tokens, width), half),
            jax.ShapeDtypeStruct((width, width), half),
            jax.ShapeDtypeStruct((width, tokens), half),
            jax.ShapeDtypeStruct((tokens, width), single),
            jax.ShapeDtypeStruct((1, width), single),
        ],
        scratch_shapes=[
            pltpu.VMEM((width, tokens), half),
            pltpu.VMEM((tokens, width), single),
            pltpu.VMEM((tokens, width), single),
            pltpu.VMEM((tokens, width), single),
            pltpu.VMEM((width, tokens), half),
            pltpu.VMEM((width, width), half),
            pltpu.SemaphoreType.DMA((3,)),
        ],
        compiler_params=pltpu.CompilerParams(vmem_limit_bytes=VMEM_BYTES),
    )(normed, cot, resid, small, out_t, w_gate, w_up, w_down, attend)


def result_kernel(count, chan, *refs):
    ins, outs, sem = refs[:count], refs[count:-1], refs[-1]
    small = ins[-1]
    copies = [pltpu.make_async_copy(ins[k], outs[k], sem.at[k]) for k in range(count - 1)]
    for copy in copies:
        copy.start()
    outs[count - 1][...] = small[0:KW, 0:chan]
    for k in range(3):
        outs[count + k][...] = small[KW + k : KW + k + 1, 0:chan]
    for copy in copies:
        copy.wait()


def results(arrays, small, chan):
    vmem = pl.BlockSpec(memory_space=pltpu.VMEM)
    hbm = pl.BlockSpec(memory_space=pltpu.HBM)
    count = len(arrays) + 1
    shapes = [jax.ShapeDtypeStruct(a.shape, a.dtype) for a in arrays]
    shapes.append(jax.ShapeDtypeStruct((KW, chan), jnp.float32))
    shapes += [jax.ShapeDtypeStruct((1, chan), jnp.float32)] * 3
    return pl.pallas_call(
        functools.partial(result_kernel, count, chan),
        name="results",
        out_shape=shapes,
        in_specs=[vmem] * count,
        out_specs=[hbm] * len(arrays) + [vmem] * 4,
        scratch_shapes=[pltpu.SemaphoreType.DMA((count,))],
    )(*arrays, small)


def per_device(
    byte_ids,
    segments,
    embed_table,
    conv_weight,
    score_vector,
    first_gain,
    w_query,
    w_key,
    w_value,
    w_output,
    second_gain,
    w_gate,
    w_up,
    w_down,
    out_grad,
):
    seqs, part_bytes = byte_ids.shape
    count = lax.axis_size("seq")
    seq_len = part_bytes * count
    width = w_query.shape[1]
    wide = w_gate.shape[1]
    half_bytes = seq_len // 2
    half = half_bytes // 2
    core = lax.axis_index("dp") % 2
    place = lax.axis_index("seq")

    chan = conv_weight.shape[0]
    shards = (w_query, w_key, w_value, w_output, w_gate, w_up, w_down, embed_table)
    vectors = jnp.stack([score_vector, first_gain, second_gain]).astype(jnp.float32)
    if all(shard.shape[0] % 8 == 0 for shard in shards):
        full, held = forward_all(shards, byte_ids, segments, conv_weight.T, vectors, out_grad, half)
        attend, wg, wu, wd, table = full
        cot = held.cot.reshape(half, width)
        small_full, stream, normed_one, resid_one = held.small, held.stream, held.normed, held.resid
        coef, tap_table, rows, idm = held.coef, held.tap, held.rows, held.idm
        queries, keys, vals, attn_out, lse = held.qt, held.kt, held.vt, held.out, held.lse
        key_marks = held.marks[0]
        normed_two = held.normed_two
    else:
        small = jnp.concatenate([conv_weight.T.astype(jnp.float32), vectors], axis=0)
        small = jnp.pad(small, ((0, 0), (0, 128 - chan)))
        cells = jnp.stack([byte_ids, segments + 1], axis=1).reshape(seqs, -1, 128)
        wq, wk, wv, wo, wg, wu, wd, table, small_full, cells, cot = gather_all(shards + (small,), cells, out_grad)
        attend = jnp.concatenate([wq, wk, wv, wo], axis=1)
        cells = cells.reshape(count, 2, part_bytes).transpose(1, 0, 2).reshape(2, seq_len)
        ids_row, marks_row = cells[0], cells[1]
        cot = cot.reshape(half, width)
        small_full = small_full.reshape(lax.axis_size(ALL), 8, 128)[:, :, :chan].transpose(1, 0, 2).reshape(8, width)
        gain_two = small_full[KW + 2 : KW + 3]

        stream, normed_one, coef, tap_table, rows, idm = tok_forward(ids_row, marks_row, table, small_full, half)

        twins = [(i, i ^ 1) for i in range(lax.axis_size("dp"))]
        normed_other = lax.ppermute(normed_one, "dp", twins)
        token_marks = marks_row[::2]
        query_marks = lax.dynamic_slice_in_dim(token_marks, core * half, half, axis=0)
        other_marks = lax.dynamic_slice_in_dim(token_marks, (1 - core) * half, half, axis=0)
        key_marks = jnp.concatenate([query_marks, other_marks])
        queries = (mm_tt(wq, normed_one).astype(jnp.bfloat16) * HEAD_DIM ** (-0.5)).astype(jnp.bfloat16)
        normed_keys = jnp.concatenate([normed_one, normed_other], axis=0)
        keys = mm_tt(wk, normed_keys).astype(jnp.bfloat16)
        vals = mm_tt(wv, normed_keys).astype(jnp.bfloat16)
        attn_out, lse = attend_forward(queries, keys, vals, key_marks, query_marks)

        resid_one = stream + mm_tn(attn_out, wo)
        normed_two = rms_scale(resid_one, gain_two).astype(jnp.bfloat16)
    grad_gate, grad_up, grad_down, layer_rows, grad_output, attn_grad, resid_grad, gain_two_grad = feed_forward(
        normed_two, cot, resid_one, small_full, attn_out, wg, wu, wd, attend
    )
    layer_rows = layer_rows.reshape(seqs, part_bytes // 2, width)
    shapes = [(w.shape[0], w.shape[1], jnp.bfloat16) for w in shards] + [(8, 128, jnp.float32)]
    out = backward_all(
        BackInputs(
            gate=grad_gate,
            up=grad_up,
            down=grad_down,
            output=grad_output,
            coef=coef,
            resid=resid_grad,
            qt=queries,
            kt=keys,
            vt=vals,
            got=attn_grad,
            out=attn_out,
            lse=lse,
            key_marks=key_marks[None],
            normed=normed_one,
            stream=stream,
            attend=attend,
            small=small_full,
            gain_two=gain_two_grad,
            table=table,
            tap=tap_table,
            rows=rows,
            idm=idm,
            layer=layer_rows,
        ),
        shapes,
    )
    done = results([out[9]] + list(out[:8]), out[8], chan)
    return (
        done[0],
        done[8],
        done[9].T,
        done[10][0],
        done[11][0],
        done[1],
        done[2],
        done[3],
        done[4],
        done[12][0],
        done[5],
        done[6],
        done[7],
    )


def solution(mesh):
    flat = P(ALL)
    rows = P(ALL, None)
    in_specs = (
        P("dp", "seq"),
        P("dp", "seq"),
        rows,
        rows,
        flat,
        flat,
        rows,
        rows,
        rows,
        rows,
        flat,
        rows,
        rows,
        rows,
        P("dp", "seq", None),
    )
    out_specs = (
        P("dp", "seq", None),
        rows,
        rows,
        flat,
        flat,
        rows,
        rows,
        rows,
        rows,
        flat,
        rows,
        rows,
        rows,
    )
    return jax.shard_map(
        per_device, mesh=mesh, in_specs=in_specs, out_specs=out_specs, check_vma=False
    )
```

```python
import functools
from typing import NamedTuple

import jax
import jax.numpy as jnp
from jax import lax
from jax.experimental import pallas as pl
from jax.experimental.pallas import tpu as pltpu
from jax.sharding import PartitionSpec as P

HEADS = 12
HEAD_DIM = 64
VOCAB = 256
MAXBLOCK = 4
KW = 5
DOCS = 8
ALL = ("dp", "seq")
VMEM_BYTES = 56 * 1024 * 1024


def mm(left, right):
    return jnp.dot(left, right, preferred_element_type=jnp.float32)


def mm_nt(left, right):
    return lax.dot_general(left, right, (((1,), (1,)), ((), ())), preferred_element_type=jnp.float32)


def mm_tn(left, right):
    return lax.dot_general(left, right, (((0,), (0,)), ((), ())), preferred_element_type=jnp.float32)


def mm_tt(left, right):
    return lax.dot_general(left, right, (((0,), (1,)), ((), ())), preferred_element_type=jnp.float32)


def rms_scale(values, gain):
    return values * lax.rsqrt(jnp.mean(values * values, axis=-1, keepdims=True) + 1e-06) * gain


def gelu_tanh(values):
    return jax.nn.gelu(values, approximate=True)


MESH = pl.DeviceIdType.MESH


def position():
    dp = lax.axis_index("dp")
    place = lax.axis_index("seq")
    lines = lax.axis_size("dp") // 4
    group = dp // 2
    return group // 2, group % 2, dp % 2, place, lines, lax.axis_size("seq")


def dp_of(y, x, core):
    return (y * 2 + x) * 2 + core


def meet(targets):
    barrier = pltpu.get_barrier_semaphore()
    for dp, place in targets:
        pl.semaphore_signal(barrier, inc=1, device_id=(dp, place), device_id_type=MESH)
    pl.semaphore_wait(barrier, len(targets))


def remote(src, dst, send_sem, recv_sem, dp, place):
    return pltpu.make_async_remote_copy(
        src_ref=src,
        dst_ref=dst,
        send_sem=send_sem,
        recv_sem=recv_sem,
        device_id=(dp, place),
        device_id_type=MESH,
    )


GATHER_ITEMS = (
    (7, 0, 0, 0),
    (8, 0, 0, 0),
    (0, 0, 0, 0),
    (2, 0, 0, 1),
    (1, 0, 0, 0),
    (3, 0, 0, 1),
    (4, 0, 0, 0),
    (5, 0, 0, 1),
    (6, 0, 1, 0),
    (6, 1, 1, 1),
)
GATHER_PHASES = ((0, 1), (2, 3, 4, 5), (6, 7), (8, 9))


def gather_kernel(arrays, *refs):
    ins = refs[:arrays]
    cells_in, cot_in = refs[arrays], refs[arrays + 1]
    outs = refs[arrays + 2 : 2 * arrays + 2]
    cells_out, cot_out = refs[2 * arrays + 2], refs[2 * arrays + 3]
    recv, recv_sib, send_z, send_x, send_y, send_sib, own_sem, cell_recv, cell_send, cot_recv, cot_send = refs[
        2 * arrays + 4 :
    ]
    y, x, core, place, lines, count = position()
    seqs = cells_in.shape[0]
    groups = lines * 2
    group = y * 2 + x
    dp = dp_of(y, x, core)
    twin = dp_of(y, x, 1 - core)
    side = dp_of(y, 1 - x, core)
    ahead = [(y + k) % lines for k in range(1, lines)]

    targets = [(twin, place), (side, place)]
    for k in range(1, count):
        targets += [(dp, (place + k) % count), (twin, (place + k) % count)]
    for other_y in ahead:
        targets.append((dp_of(other_y, x, core), place))
    meet(targets)

    def cell_copies(fn_remote, fn_local):
        for r in range(seqs):
            chip = seqs * core + r
            for c in range(2):
                home = (chip == place) & (core == c)

                @pl.when(home)
                def _():
                    fn_local(r, c)

                @pl.when(jnp.logical_not(home))
                def _():
                    fn_remote(r, c, chip)

    def cell_remote(r, c, chip):
        return remote(
            cells_in.at[r],
            cells_out.at[place],
            cell_send.at[r, c],
            cell_recv.at[place],
            dp_of(y, x, c),
            chip,
        )

    cell_copies(
        lambda r, c, chip: cell_remote(r, c, chip).start(),
        lambda r, c: pltpu.make_async_copy(
            cells_in.at[r], cells_out.at[place], cell_recv.at[place]
        ).start(),
    )

    def view(item):
        array, first, columns, _ = GATHER_ITEMS[item]
        in_ref, out_ref = ins[array], outs[array]
        if columns:
            cols = in_ref.shape[1] // 2
            lanes = pl.ds(first * cols, cols)
        else:
            lanes = pl.ds(0, in_ref.shape[1])
        return in_ref.at[:, lanes], out_ref, lanes

    def block(item, g, z):
        _, out_ref, lanes = view(item)
        return out_ref.at[(g * 2 + core) * count + z, :, lanes]

    def group_block(item, g, c):
        _, out_ref, lanes = view(item)
        return out_ref.at[pl.ds((g * 2 + c) * count, count), :, lanes]

    def many(item, blocks):
        _, out_ref, lanes = view(item)
        return out_ref.at[pl.ds(0, blocks), :, lanes]

    def arrived(item, g, z):
        dst = block(item, g, z)
        remote(dst, dst, send_x.at[item], recv.at[item, g * count + z], twin, place).wait_recv()

    def to_side(item, src, g, z):
        remote(src, block(item, g, z), send_x.at[item], recv.at[item, g * count + z], side, place).start()

    def to_lines(item, src, g, z):
        for other_y in ahead:
            remote(
                src,
                block(item, g, z),
                send_y.at[item],
                recv.at[item, g * count + z],
                dp_of(other_y, x, core),
                place,
            ).start()

    def to_z(item, src, z, step):
        return remote(
            src,
            block(item, group, z),
            send_z.at[item, z, step],
            recv.at[item, group * count + z],
            dp,
            place + 1 - 2 * step,
        )

    def to_twin(item, g):
        src = group_block(item, g, core)
        remote(src, src, send_sib.at[item], recv_sib.at[item, g], twin, place).start()

    def own_copy(item):
        return pltpu.make_async_copy(view(item)[0], block(item, group, place), own_sem.at[item])

    def first_own(items):
        for item in items:
            src = view(item)[0]

            @pl.when(place < count - 1)
            def _():
                to_z(item, src, place, 0).start()

            @pl.when(place > 0)
            def _():
                to_z(item, src, place, 1).start()

            own_copy(item).start()

    def first_sides(items):
        for item in items:
            src = view(item)[0]
            to_side(item, src, group, place)
            to_lines(item, src, group, place)

    def first_level(items):
        def step(s, carry):
            low = place - s
            high = place + s
            for item in items:

                @pl.when(low >= 0)
                def _():
                    arrived(item, group, low)
                    src = block(item, group, low)

                    @pl.when(place < count - 1)
                    def _():
                        to_z(item, src, low, 0).start()

                    to_side(item, src, group, low)
                    to_lines(item, src, group, low)

                @pl.when(high < count)
                def _():
                    arrived(item, group, high)
                    src = block(item, group, high)

                    @pl.when(place > 0)
                    def _():
                        to_z(item, src, high, 1).start()

                    to_side(item, src, group, high)
                    to_lines(item, src, group, high)

            return carry

        lax.fori_loop(1, count, step, 0)
        for item in items:
            own_copy(item).wait()
            to_twin(item, group)

    def second_level(items):
        def step(s, carry):
            z = (place + s) % count
            for item in items:
                if GATHER_ITEMS[item][3] == 0:
                    g = y * 2 + (1 - x)
                    arrived(item, g, z)
                    to_lines(item, block(item, g, z), g, z)
                else:
                    for other_y in ahead:
                        g = other_y * 2 + x
                        arrived(item, g, z)
                        to_side(item, block(item, g, z), g, z)
            return carry

        lax.fori_loop(0, count, step, 0)
        for item in items:
            if GATHER_ITEMS[item][3] == 0:
                to_twin(item, y * 2 + (1 - x))
            else:
                for other_y in ahead:
                    to_twin(item, other_y * 2 + x)

    def third_level(items):
        def rest(item):
            if GATHER_ITEMS[item][3] == 0:
                return [other_y * 2 + other_x for other_y in ahead for other_x in (x, 1 - x)]
            return [other_y * 2 + (1 - x) for other_y in [y] + ahead]

        def step(s, carry):
            z = (place + s) % count
            for item in items:
                for g in rest(item):
                    arrived(item, g, z)
            return carry

        lax.fori_loop(0, count, step, 0)
        for item in items:
            for g in rest(item):
                to_twin(item, g)

    def cot_copies(fn_remote, fn_local):
        for r in range(seqs):
            chip = seqs * core + r
            home = (chip == place) & (core == place // seqs)

            @pl.when(home)
            def _():
                fn_local(r)

            @pl.when(jnp.logical_not(home))
            def _():
                fn_remote(r, chip)

    def cot_remote(r, chip):
        return remote(
            cot_in.at[r],
            cot_out.at[place % seqs],
            cot_send.at[r],
            cot_recv.at[place % seqs],
            dp_of(y, x, place // seqs),
            chip,
        )

    phases = GATHER_PHASES
    for items in phases:
        first_own(items)
    first_sides(phases[0])
    first_level(phases[0])
    for k in range(1, len(phases)):
        first_sides(phases[k])
        first_level(phases[k])
        second_level(phases[k - 1])
        if k == 1:
            cot_copies(
                lambda r, chip: cot_remote(r, chip).start(),
                lambda r: pltpu.make_async_copy(
                    cot_in.at[r], cot_out.at[place % seqs], cot_recv.at[place % seqs]
                ).start(),
            )
        if k > 1:
            third_level(phases[k - 2])
    second_level(phases[-1])
    third_level(phases[-2])
    third_level(phases[-1])

    for item in range(len(GATHER_ITEMS)):
        for g in range(groups):
            dst = group_block(item, g, 1 - core)
            remote(dst, dst, send_sib.at[item], recv_sib.at[item, g], twin, place).wait_recv()
        tree = GATHER_ITEMS[item][3]

        def sent(blocks, sem):
            src = many(item, blocks)
            remote(src, src, sem, recv.at[item, 0], twin, place).wait_send()

        sent(count * (1 if tree == 0 else lines), send_x.at[item])
        sent(count * (lines - 1) * (2 if tree == 0 else 1), send_y.at[item])
        sent(count * groups, send_sib.at[item])

        def drain(z, carry):
            @pl.when((z <= place) & (place < count - 1))
            def _():
                to_z(item, block(item, group, z), z, 0).wait_send()

            @pl.when((z >= place) & (place > 0))
            def _():
                to_z(item, block(item, group, z), z, 1).wait_send()

            return carry

        lax.fori_loop(0, count, drain, 0)
    for q in range(count):
        dst = cells_out.at[q]
        remote(dst, dst, cell_send.at[0, 0], cell_recv.at[q], twin, place).wait_recv()
    for q in range(seqs):
        dst = cot_out.at[q]
        remote(dst, dst, cot_send.at[0], cot_recv.at[q], twin, place).wait_recv()
    cell_copies(lambda r, c, chip: cell_remote(r, c, chip).wait_send(), lambda r, c: None)
    cot_copies(lambda r, chip: cot_remote(r, chip).wait_send(), lambda r: None)


def gather_all(shards, cells, cot):
    count = lax.axis_size("seq")
    group_count = lax.axis_size(ALL)
    groups = group_count // (2 * count)
    items = len(GATHER_ITEMS)
    seqs = cells.shape[0]
    vmem = pl.BlockSpec(memory_space=pltpu.VMEM)
    hbm = pl.BlockSpec(memory_space=pltpu.HBM)
    shapes = [jax.ShapeDtypeStruct((group_count,) + s.shape, s.dtype) for s in shards]
    shapes.append(jax.ShapeDtypeStruct((count,) + cells.shape[1:], cells.dtype))
    shapes.append(jax.ShapeDtypeStruct(cot.shape, cot.dtype))
    dma = pltpu.SemaphoreType.DMA
    out = pl.pallas_call(
        functools.partial(gather_kernel, len(shards)),
        name="gather_all",
        out_shape=shapes,
        in_specs=[vmem] * (len(shards) + 2),
        out_specs=[hbm] * len(shapes),
        scratch_shapes=[
            dma((items, groups * count)),
            dma((items, groups)),
            dma((items, count, 2)),
            dma((items,)),
            dma((items,)),
            dma((items,)),
            dma((items,)),
            dma((count,)),
            dma((seqs, 2)),
            dma((seqs,)),
            dma((seqs,)),
        ],
        compiler_params=pltpu.CompilerParams(collective_id=0, has_side_effects=True),
    )(*shards, cells, cot)
    full = [o.reshape(-1, o.shape[2]) for o in out[: len(shards)]]
    return full + list(out[len(shards) :])


LEFT = 128
BAND = 256


def split_two(values):
    high = values.astype(jnp.bfloat16)
    return high, (values - high.astype(jnp.float32)).astype(jnp.bfloat16)


def lane_shift(row, by):
    by = by % row.shape[1]
    return row if by == 0 else pltpu.roll(row, row.shape[1] - by, 1)


def pool_rows(marks, core, half_bytes):
    lanes = lax.broadcasted_iota(jnp.int32, marks[0].shape, 1)
    inside, inverse = {}, {}
    for e in range(2):
        place = core * half_bytes + 2 * (lanes - LEFT) + e + 768
        third = lax.shift_right_logical(place * 21846, 16)
        remains = {2: place & 1, 3: place - 3 * third, 4: place & 3}
        shifted = {}
        for s in range(1 - MAXBLOCK, MAXBLOCK):
            f = (e + s) % 2
            shifted[s] = lane_shift(marks[f], (e + s - f) // 2) == marks[e]
        for b in range(2, MAXBLOCK + 1):
            number = jnp.ones(marks[0].shape, jnp.float32)
            for s in range(1 - b, b):
                if s == 0:
                    continue
                at = remains[b] + s
                on = (shifted[s] & (at >= 0) & (at < b)).astype(jnp.float32)
                inside[b, e, s] = on
                number = number + on
            inverse[b, e] = 1.0 / number
    return inside, inverse


def band_coefs(per_byte, inside, inverse):
    coefs = {}
    for o in range(1 - MAXBLOCK, MAXBLOCK + 1):
        total = None
        for e in range(2):
            s = o - e
            if not 1 - MAXBLOCK <= s < MAXBLOCK:
                continue
            for b in range(1, MAXBLOCK + 1):
                if b == 1:
                    if s != 0:
                        continue
                    term = per_byte[b, e]
                elif s == 0:
                    term = per_byte[b, e] * inverse[b, e]
                elif (b, e, s) in inside:
                    term = per_byte[b, e] * inverse[b, e] * inside[b, e, s]
                else:
                    continue
                total = term if total is None else total + term
        coefs[o] = total
    return coefs


def band_matrix(coefs, block):
    shape = (3 * BAND, BAND)
    delta = lax.broadcasted_iota(jnp.int32, shape, 0) - LEFT - 2 * lax.broadcasted_iota(jnp.int32, shape, 1)
    out = jnp.zeros(shape, jnp.float32)
    for o, row in coefs.items():
        part = row[0:1, LEFT + BAND * block : LEFT + BAND * (block + 1)]
        out = jnp.where(delta == o, part, out)
    return out


def tap_rows(tap):
    return pl.ds(pl.multiple_of(tap * VOCAB, VOCAB), VOCAB)


def fill_one_hot(one_hot, idm_ref):
    vocab = lax.broadcasted_iota(jnp.int32, (VOCAB, one_hot.shape[1]), 0)

    def step(tap, carry):
        hit = vocab == idm_ref[pl.ds(tap, 1)]
        one_hot[tap_rows(tap)] = hit.astype(jnp.float32).astype(jnp.bfloat16)
        return carry

    lax.fori_loop(0, KW, step, 0)


def tok_forward_kernel(ids_ref, marks_ref, table_ref, small_ref, stream_ref, normed_ref, coef_ref, tap_ref, rows_ref, idm_ref, one_hot):
    core = lax.axis_index("dp") % 2
    tokens = stream_ref.shape[0]
    half_bytes = 2 * tokens
    span = one_hot.shape[1]
    wide = span + 2 * LEFT
    first = pl.ds(pl.multiple_of(core * half_bytes, 128), wide)
    ids = ids_ref[:, first]
    marks = marks_ref[:, first]
    for tap in range(KW):
        by = tap - KW // 2
        same = (lane_shift(marks, by) == marks) & (marks > 0)
        idm_ref[tap : tap + 1] = jnp.where(same, lane_shift(ids, by), -1)[0:1, LEFT : LEFT + span]
    fill_one_hot(one_hot, idm_ref)

    score = jnp.broadcast_to(small_ref[KW : KW + 1], (8, small_ref.shape[1])).astype(jnp.bfloat16)
    scored = []
    for tap in range(KW):
        product = table_ref[...].astype(jnp.float32) * small_ref[tap : tap + 1]
        high, low = split_two(product)
        tap_ref[tap * VOCAB : (tap + 1) * VOCAB] = high
        scored.append(mm_nt(score, high) + mm_nt(score, low))
    high, low = split_two(jnp.concatenate(scored, axis=1))
    u_row = mm(high, one_hot[...]) + mm(low, one_hot[...])

    high = u_row.astype(jnp.bfloat16).astype(jnp.float32)
    marks_here = marks[:, LEFT : LEFT + span].astype(jnp.float32)
    packed = jnp.concatenate([marks_here, high, u_row - high, jnp.zeros_like(high)], axis=0).astype(jnp.bfloat16)
    shape = (span, wide // 2)
    twice = 2 * lax.broadcasted_iota(jnp.int32, shape, 1) - lax.broadcasted_iota(jnp.int32, shape, 0) - LEFT
    marks_of, u_of = [], []
    for e in range(2):
        pick = (twice == -e).astype(jnp.float32).astype(jnp.bfloat16)
        apart = mm(packed, pick)
        marks_of.append(apart[0:8])
        u_of.append(apart[8:16] + apart[16:24])

    inside, inverse = pool_rows(marks_of, core, half_bytes)
    prob = {}
    for e in range(2):
        shifted = {}
        for s in range(1 - MAXBLOCK, MAXBLOCK):
            f = (e + s) % 2
            shifted[s] = lane_shift(u_of[f], (e + s - f) // 2)
        scores = [u_of[e]]
        for b in range(2, MAXBLOCK + 1):
            total = u_of[e]
            for s in range(1 - b, b):
                if s != 0:
                    total = total + inside[b, e, s] * shifted[s]
            scores.append(total * inverse[b, e])
        top = scores[0]
        for value in scores[1:]:
            top = jnp.maximum(top, value)
        expo = [jnp.exp(value - top) for value in scores]
        whole = expo[0] + expo[1] + expo[2] + expo[3]
        for b in range(1, MAXBLOCK + 1):
            prob[b, e] = expo[b - 1] / whole
            rows_ref[2 * b + e : 2 * b + e + 1] = prob[b, e][0:1]
        rows_ref[e : e + 1] = marks_of[e][0:1]
    coefs = band_coefs({key: 0.5 * value for key, value in prob.items()}, inside, inverse)
    gain = small_ref[KW + 1 : KW + 2]
    for i in range(tokens // BAND):
        matrix = band_matrix(coefs, i).astype(jnp.bfloat16)
        lanes = slice(i * BAND, (i + 1) * BAND)
        part = mm(one_hot[:, 2 * i * BAND : (2 * i + 3) * BAND], matrix).astype(jnp.bfloat16)
        coef_ref[:, lanes] = part
        stream = mm_tn(part, tap_ref[...])
        stream_ref[lanes] = stream
        scale = lax.rsqrt(jnp.mean(stream * stream, axis=-1, keepdims=True) + 1e-06)
        normed_ref[lanes] = (stream * scale * gain).astype(jnp.bfloat16)


def tok_forward(ids_row, marks_row, table, small, tokens):
    width = table.shape[1]
    span = 2 * tokens + 2 * LEFT
    wide = span + 2 * LEFT

    def padded(row, fill):
        row = jnp.pad(row, (2 * LEFT, 2 * LEFT), constant_values=fill)
        return jnp.broadcast_to(row[None], (8, row.shape[0]))

    return pl.pallas_call(
        tok_forward_kernel,
        name="tok_forward",
        out_shape=[
            jax.ShapeDtypeStruct((tokens, width), jnp.float32),
            jax.ShapeDtypeStruct((tokens, width), jnp.bfloat16),
            jax.ShapeDtypeStruct((KW * VOCAB, tokens), jnp.bfloat16),
            jax.ShapeDtypeStruct((KW * VOCAB, width), jnp.bfloat16),
            jax.ShapeDtypeStruct((16, wide // 2), jnp.float32),
            jax.ShapeDtypeStruct((8, span), jnp.int32),
        ],
        scratch_shapes=[pltpu.VMEM((KW * VOCAB, span), jnp.bfloat16)],
        compiler_params=pltpu.CompilerParams(vmem_limit_bytes=VMEM_BYTES),
    )(padded(ids_row, -1), padded(marks_row, 0), table, small)


def tok_backward_body(grad16, coef_ref, ref, own, tick, take):
    tap_ref, rows_ref, idm_ref, table_ref, small_ref = ref.tap, ref.rows, ref.idm, ref.table, ref.small
    one_hot = own.one_hot
    core = lax.axis_index("dp") % 2
    tokens = grad16.shape[0]
    fill_one_hot(one_hot, idm_ref)
    tick()

    def whole_row(k):
        return jnp.broadcast_to(rows_ref[k : k + 1], (8, rows_ref.shape[1]))

    marks_of = [whole_row(0), whole_row(1)]
    inside, inverse = pool_rows(marks_of, core, 2 * tokens)
    shape = (3 * BAND, BAND)
    delta = lax.broadcasted_iota(jnp.int32, shape, 0) - LEFT - 2 * lax.broadcasted_iota(jnp.int32, shape, 1)
    through = mm_nt(tap_ref[...], grad16).astype(jnp.bfloat16)
    tick()
    diag = {o: [] for o in range(1 - MAXBLOCK, MAXBLOCK + 1)}
    edge = jnp.zeros((8, LEFT), jnp.float32)
    for i in range(tokens // BAND):
        near = mm_tn(one_hot[:, 2 * i * BAND : (2 * i + 3) * BAND], through[:, i * BAND : (i + 1) * BAND])
        for o in diag:
            total = jnp.sum(jnp.where(delta == o, near, 0.0), axis=0, keepdims=True)
            diag[o].append(jnp.broadcast_to(total, (8, BAND)))
        tick()
    diag = {o: jnp.concatenate([edge] + parts + [edge], axis=1) for o, parts in diag.items()}
    size_grad = {}
    for e in range(2):
        grads = [0.5 * diag[e]]
        for b in range(2, MAXBLOCK + 1):
            total = diag[e]
            for s in range(1 - b, b):
                if s != 0:
                    total = total + inside[b, e, s] * diag[s + e]
            grads.append(0.5 * total * inverse[b, e])
        probs = [whole_row(2 * b + e) for b in range(1, MAXBLOCK + 1)]
        mean = probs[0] * grads[0]
        for p, g in zip(probs[1:], grads[1:]):
            mean = mean + p * g
        for b in range(1, MAXBLOCK + 1):
            size_grad[b, e] = probs[b - 1] * (grads[b - 1] - mean)
    coefs = band_coefs(size_grad, inside, inverse)
    picked = None
    for i in range(tokens // BAND):
        matrix = band_matrix(coefs, i).astype(jnp.bfloat16)
        part = mm(one_hot[:, 2 * i * BAND : (2 * i + 3) * BAND], matrix)
        part = jnp.sum(part, axis=1, keepdims=True)
        picked = part if picked is None else picked + part
        tick()
    own.picked[...] = picked
    score = small_ref[KW : KW + 1]
    table_grad = own.wide.at[0:VOCAB]
    table_grad[...] = jnp.zeros(table_grad.shape, jnp.float32)
    own.rows[...] = jnp.zeros_like(own.rows)
    tap_tasks = take(KW - 1)

    def step(tap, carry):
        here = own.picked[tap_rows(tap)]
        table = table_ref[:, 0 : score.shape[1]].astype(jnp.float32)
        part = mm(coef_ref[tap_rows(tap)], grad16) + here * score
        taps = small_ref[pl.ds(tap, 1)]
        table_grad[...] += part * taps
        own.rows[pl.ds(tap, 1)] = jnp.sum(part * table, axis=0, keepdims=True)
        own.rows[KW : KW + 1] += jnp.sum(table * here, axis=0, keepdims=True) * taps
        tap_tasks(tap)
        return carry

    lax.fori_loop(0, KW, step, 0)


CHUNK = 256


def pair_rows(ref, h):
    values = ref[...]
    rows = lax.broadcasted_iota(jnp.int32, values.shape, 0)
    return jnp.where((rows // HEAD_DIM) == h, values, jnp.zeros_like(values))


def fill_bias(bias, key_marks, query_marks):
    def apart(marks):
        rows = lax.broadcasted_iota(jnp.int32, (2 * DOCS, marks.shape[1]), 0)
        return (rows == marks[...]).astype(jnp.float32).astype(jnp.bfloat16)

    queries = apart(query_marks)
    for c in range(key_marks.shape[1] // CHUNK):
        keys = slice(c * CHUNK, (c + 1) * CHUNK)
        same = mm_tn(apart(key_marks.at[:, keys]), queries)
        bias[keys] = jnp.where(same > 0.5, 0.0, -1e30).astype(bias.dtype)


def attend_forward_kernel(qt_ref, kt_ref, vt_ref, key_marks, query_marks, out_ref, lse_ref, bias, scores):
    @pl.when(pl.program_id(0) == 0)
    def _():
        fill_bias(bias, key_marks, query_marks)

    keys = kt_ref[...].T
    chunks = keys.shape[0] // CHUNK
    for h in range(2):
        query = pair_rows(qt_ref, h)
        top = None
        for c in range(chunks):
            rows = slice(c * CHUNK, (c + 1) * CHUNK)
            part = mm(keys[rows], query) + bias[rows]
            scores[h, rows] = part
            high = jnp.max(part, axis=0, keepdims=True)
            top = high if top is None else jnp.maximum(top, high)
        total = None
        out = None
        for c in range(chunks):
            rows = slice(c * CHUNK, (c + 1) * CHUNK)
            expo = jnp.exp(scores[h, rows] - top)
            part = jnp.sum(expo, axis=0, keepdims=True)
            total = part if total is None else total + part
            part = mm(vt_ref[h * HEAD_DIM : (h + 1) * HEAD_DIM, rows], expo.astype(jnp.bfloat16))
            out = part if out is None else out + part
        out_ref[h * HEAD_DIM : (h + 1) * HEAD_DIM] = (out / total).astype(jnp.bfloat16)
        lse_ref[0, h : h + 1] = top + jnp.log(total)


def attend_forward(qt, kt, vt, key_marks, query_marks):
    width, tokens = qt.shape
    keys = kt.shape[1]
    pairs = width // 128
    rows = lambda size: pl.BlockSpec((128, size), lambda i: (i, 0))
    whole = lambda shape: pl.BlockSpec(shape, lambda i: (0, 0))
    return pl.pallas_call(
        attend_forward_kernel,
        name="attend_forward",
        grid=(pairs,),
        in_specs=[rows(tokens), rows(keys), rows(keys), whole((1, keys)), whole((1, tokens))],
        out_specs=[rows(tokens), pl.BlockSpec((1, 2, tokens), lambda i: (i, 0, 0))],
        out_shape=[
            jax.ShapeDtypeStruct((width, tokens), jnp.bfloat16),
            jax.ShapeDtypeStruct((pairs, 2, tokens), jnp.float32),
        ],
        scratch_shapes=[
            pltpu.VMEM((keys, tokens), jnp.float32),
            pltpu.VMEM((2, keys, tokens), jnp.float32),
        ],
        compiler_params=pltpu.CompilerParams(vmem_limit_bytes=VMEM_BYTES),
    )(qt, kt, vt, key_marks[None], query_marks[None])


def attend_backward_pair(qt, kt, vt, got_ref, out, lse_ref, bias, dq, dk_own, dv_own, dk_away, dv_away, tasks):
    keys = kt[...].T
    vals = vt[...].T
    chunks = keys.shape[0] // CHUNK
    for h in range(2):
        own = slice(h * HEAD_DIM, (h + 1) * HEAD_DIM)
        query = pair_rows(qt, h)
        got = pair_rows(got_ref, h)
        dots = jnp.sum(
            got_ref[own].astype(jnp.float32) * out[own].astype(jnp.float32), axis=0, keepdims=True
        )
        lse = lse_ref[h : h + 1]
        query_grad = None
        for c in range(chunks):
            rows = slice(c * CHUNK, (c + 1) * CHUNK)
            soft = jnp.exp(mm(keys[rows], query) + (bias[rows].astype(jnp.float32) - lse))
            change = soft * (mm(vals[rows], got) - dots)
            soft16 = soft.astype(jnp.bfloat16)
            change16 = change.astype(jnp.bfloat16)
            first = c < chunks // 2
            to = slice((c % (chunks // 2)) * CHUNK, (c % (chunks // 2) + 1) * CHUNK)
            (dv_own if first else dv_away)[own, to] = mm_nt(got_ref[own], soft16).astype(jnp.bfloat16)
            (dk_own if first else dk_away)[own, to] = mm_nt(qt[own], change16).astype(jnp.bfloat16)
            part = mm(kt[own, rows], change16)
            query_grad = part if query_grad is None else query_grad + part
        dq[own] = (query_grad * HEAD_DIM ** (-0.5)).astype(jnp.bfloat16)
        if h == 0:
            tasks()


SCATTER_ITEMS = (
    (4, 1, 2, 0),
    (6, 1, 2, 1),
    (5, 0, 2, 0),
    (5, 1, 2, 0),
    (3, 0, 1, 1),
    (6, 0, 2, 0),
    (4, 0, 2, 1),
    (0, 0, 1, 1),
    (1, 0, 1, 0),
    (2, 0, 1, 1),
    (7, 0, 1, 1),
    (8, 0, 1, 1),
)
FIRST_ITEMS = 7
SCHEDULE = (
    (
        (0, 0), (0, 1), (0, 2),
    ),
    (
        (0, 3), (0, 4),
    ),
    (
        (0, 5), (0, 6),
    ),
    (),
    (
        (1, 0), (1, 1),
    ),
    (),
    (),
    ((1, 4),),
    ((1, 2),),
    (),
    (),
    (),
    (
        (1, 3), (1, 6),
    ),
    (),
    (
        (2, 0), (0, 7),
    ),
    ((0, 8),),
    (
        (3, 0), (2, 2), (1, 5), (0, 9),
    ),
    (
        (4, 0), (2, 1), (2, 3),
    ),
    ((3, 2),),
    (
        (5, 0), (2, 4),
    ),
    (
        (4, 2), (1, 7),
    ),
    (
        (3, 1), (2, 6),
    ),
    (
        (5, 2), (3, 3),
    ),
    (
        (2, 5), (4, 1), (3, 4),
    ),
    (),
    (),
    (
        (4, 3), (5, 1), (1, 8), (3, 6),
    ),
    ((4, 4),),
    (
        (1, 9), (5, 3), (2, 7), (3, 5), (0, 10), (5, 4),
        (0, 11), (4, 6), (2, 8), (3, 7), (4, 5), (5, 6),
        (2, 9), (1, 10), (1, 11), (4, 7), (5, 5), (3, 8),
        (2, 10), (2, 11), (5, 7), (3, 9), (4, 8), (3, 10),
        (3, 11), (4, 9), (5, 8), (4, 10), (4, 11), (5, 9),
        (5, 10), (5, 11),
    ),
)


LATE_SOURCES = (4, 5, 6)


class Scatter:
    def __init__(self, sources, outs, layer_in, layer_out, buffers, sems):
        items = len(SCATTER_ITEMS)
        self.sources, self.outs = sources, outs
        self.layer_in, self.layer_out = layer_in, layer_out
        self.sems = sems
        self.y, self.x, self.core, self.place, self.lines, self.count = position()
        y, x, core = self.y, self.x, self.core
        self.own, taken = [], 0
        for array, _, _, _ in SCATTER_ITEMS:
            if array in LATE_SOURCES:
                self.own.append(buffers[taken])
                taken += 1
            else:
                self.own.append(sources[array].at[:, :, core])
        buffers = buffers[taken:]
        self.from_twin, self.first_in, self.second_in, self.line_in = [
            buffers[k * items : (k + 1) * items] for k in range(4)
        ]
        self.dp = dp_of(y, x, core)
        self.twin = dp_of(y, x, 1 - core)
        self.side = dp_of(y, 1 - x, core)
        self.ahead = [(y + k) % self.lines for k in range(1, self.lines)]

    def meet(self):
        targets = [(self.twin, self.place), (self.side, self.place)]
        for k in range(1, self.count):
            other = (self.place + k) % self.count
            targets += [(self.dp, other), (self.twin, other)]
        for other_y in self.ahead:
            targets.append((dp_of(other_y, self.x, self.core), self.place))
        meet(targets)

    def order(self, item):
        return SCATTER_ITEMS[item][3]

    def columns(self, item):
        array, part, parts, _ = SCATTER_ITEMS[item]
        cols = self.sources[array].shape[-1] // parts
        return pl.ds(part * cols, cols)

    def to_twin(self, item):
        src = self.sources[SCATTER_ITEMS[item][0]].at[:, :, 1 - self.core, :, :, self.columns(item)]
        sems = self.sems
        return remote(
            src, self.from_twin[item], sems.twin_send.at[item], sems.twin_recv.at[item], self.twin, self.place
        )

    def own_in(self, item):
        src = self.sources[SCATTER_ITEMS[item][0]].at[:, :, self.core, :, :, self.columns(item)]
        return pltpu.make_async_copy(src, self.own[item], self.sems.own.at[item])

    def x_copy(self, item):
        own = self.own[item]
        if self.order(item) == 0:
            src, dst = own.at[self.y, 1 - self.x], self.second_in[item].at[0]
        else:
            src, dst = own.at[:, 1 - self.x], self.first_in[item]
        return remote(
            src, dst, self.sems.x_send.at[item], self.sems.x_recv.at[item], self.side, self.place
        )

    def y_copy(self, item, k):
        other_y = self.ahead[k]
        own = self.own[item]
        if self.order(item) == 0:
            src, dst = own.at[other_y], self.first_in[item].at[k]
        else:
            src, dst = own.at[other_y, self.x], self.second_in[item].at[k]
        return remote(
            src,
            dst,
            self.sems.y_send.at[item, k],
            self.sems.y_recv.at[item, k],
            dp_of(other_y, self.x, self.core),
            self.place,
        )

    def stage_begin(self, item):
        self.to_twin(item).start()
        if SCATTER_ITEMS[item][0] in LATE_SOURCES:
            self.own_in(item).start()

    def stage_core(self, item):
        if SCATTER_ITEMS[item][0] in LATE_SOURCES:
            self.own_in(item).wait()
        self.to_twin(item).wait_recv()
        own, came = self.own[item], self.from_twin[item]

        def step(i, carry):
            a, b, z = i // (2 * self.count), i // self.count % 2, i % self.count
            own[a, b, z] = plus(own[a, b, z], came[a, b, z])
            return carry

        lax.fori_loop(0, 2 * self.lines * self.count, step, 0)
        if self.order(item) == 0:
            for k in range(self.lines - 1):
                self.y_copy(item, k).start()
        else:
            self.x_copy(item).start()

    def stage_first(self, item):
        own, came = self.own[item], self.first_in[item]
        y, x, lines = self.y, self.x, self.lines
        if self.order(item) == 0:
            for k in range(lines - 1):
                self.y_copy(item, k).wait_recv()

            def step(i, carry):
                b, z = i // self.count, i % self.count
                total = own[y, b, z]
                for k in range(lines - 1):
                    total = plus(total, came[k, b, z])
                own[y, b, z] = total
                return carry

            lax.fori_loop(0, 2 * self.count, step, 0)
            self.x_copy(item).start()
        else:
            self.x_copy(item).wait_recv()

            def step(i, carry):
                a, z = i // self.count, i % self.count
                own[a, x, z] = plus(own[a, x, z], came[a, z])
                return carry

            lax.fori_loop(0, lines * self.count, step, 0)
            for k in range(lines - 1):
                self.y_copy(item, k).start()

    def mine(self, item, z):
        return self.own[item].at[self.y, self.x, z]

    def z_copy(self, item, z, way):
        return remote(
            self.mine(item, z),
            self.line_in[item].at[way, z],
            self.sems.z_send.at[item, z],
            self.sems.z_recv.at[item, way, z],
            self.dp,
            self.place + 1 - 2 * way,
        )

    def z_forward(self, item, way, first):
        def step(z, carry):
            @pl.when((z - self.place) * (1 - 2 * way) > 0)
            def _():
                if not first:
                    self.z_copy(item, z, way).wait_recv()
                    ref = self.mine(item, z)
                    ref[...] = plus(ref[...], self.line_in[item][way, z])
                self.z_copy(item, z, way).start()

            return carry

        lax.fori_loop(0, self.count, step, 0)

    def stage_second(self, item):
        own, came = self.own[item], self.second_in[item]
        y, x = self.y, self.x
        if self.order(item) == 0:
            self.x_copy(item).wait_recv()
        else:
            for k in range(self.lines - 1):
                self.y_copy(item, k).wait_recv()

        def step(z, carry):
            total = own[y, x, z]
            for k in range(came.shape[0]):
                total = plus(total, came[k, z])
            own[y, x, z] = total
            return carry

        lax.fori_loop(0, self.count, step, 0)

        self.each_way(lambda way, depth: pl.when(depth == 0)(lambda: self.z_forward(item, way, True)))

    def each_way(self, body):
        def step(way, carry):
            body(way, self.place + way * (self.count - 1 - 2 * self.place))
            return carry

        lax.fori_loop(0, 2, step, 0)

    def stage_hop(self, hop, item):
        self.each_way(lambda way, depth: pl.when(depth == hop)(lambda: self.z_forward(item, way, False)))

    def stage_last(self, item):
        out = self.outs[SCATTER_ITEMS[item][0]]
        columns = self.columns(item)
        place = self.place
        out[:, columns] = self.mine(item, place)[...].astype(jnp.float32)

        def add(way):
            self.z_copy(item, place, way).wait_recv()
            out[:, columns] += self.line_in[item][way, place].astype(jnp.float32)

        self.each_way(lambda way, depth: pl.when(depth > 0)(lambda: add(way)))

    def layer_copies(self, fn_remote, fn_local):
        seqs = self.layer_in.shape[0]
        for k in range(seqs):
            chip = seqs * self.core + k
            home = (chip == self.place) & (self.core == self.place // seqs)

            @pl.when(home)
            def _():
                fn_local(k)

            @pl.when(jnp.logical_not(home))
            def _():
                fn_remote(k, chip)

    def layer_remote(self, k, chip):
        seqs = self.layer_in.shape[0]
        row = self.place % seqs
        return remote(
            self.layer_in.at[k],
            self.layer_out.at[row],
            self.sems.layer_send.at[k],
            self.sems.layer_recv.at[row],
            dp_of(self.y, self.x, self.place // seqs),
            chip,
        )

    def layer_start(self):
        row = self.place % self.layer_in.shape[0]
        self.layer_copies(
            lambda k, chip: self.layer_remote(k, chip).start(),
            lambda k: pltpu.make_async_copy(
                self.layer_in.at[k], self.layer_out.at[row], self.sems.layer_recv.at[row]
            ).start(),
        )

    def stage_hop_one(self, item):
        self.stage_hop(1, item)

    def stage_hops(self, item):
        for hop in range(2, self.count - 1):
            self.stage_hop(hop, item)

    def stages(self):
        return (
            self.stage_core,
            self.stage_first,
            self.stage_second,
            self.stage_hop_one,
            self.stage_hops,
            self.stage_last,
        )

    def finish(self):
        for item in range(len(SCATTER_ITEMS)):
            self.to_twin(item).wait_send()
            self.x_copy(item).wait_send()
            for k in range(self.lines - 1):
                self.y_copy(item, k).wait_send()

            def drain(z, carry):
                @pl.when(z > self.place)
                def _():
                    self.z_copy(item, z, 0).wait_send()

                @pl.when(z < self.place)
                def _():
                    self.z_copy(item, z, 1).wait_send()

                return carry

            lax.fori_loop(0, self.count, drain, 0)
        for r in range(self.layer_in.shape[0]):
            dst = self.layer_out.at[r]
            remote(
                dst, dst, self.sems.layer_send.at[0], self.sems.layer_recv.at[r], self.twin, self.place
            ).wait_recv()
        self.layer_copies(lambda k, chip: self.layer_remote(k, chip).wait_send(), lambda k: None)


class ScatterSems(NamedTuple):
    own: object
    twin_send: object
    twin_recv: object
    x_send: object
    x_recv: object
    y_send: object
    y_recv: object
    z_send: object
    z_recv: object
    layer_send: object
    layer_recv: object


def plus(left, right):
    return left + right


def scatter_scratch(shapes, lines, count, seqs):
    items = len(SCATTER_ITEMS)
    own, first_in, second_in, line_in = [], [], [], []
    for array, _, parts, order in SCATTER_ITEMS:
        rows, cols, kind = shapes[array]
        cols = cols // parts
        own.append(pltpu.VMEM((lines, 2, count, rows, cols), kind))
        if order == 0:
            first_in.append(pltpu.VMEM((lines - 1, 2, count, rows, cols), kind))
            second_in.append(pltpu.VMEM((1, count, rows, cols), kind))
        else:
            first_in.append(pltpu.VMEM((lines, count, rows, cols), kind))
            second_in.append(pltpu.VMEM((lines - 1, count, rows, cols), kind))
        line_in.append(pltpu.VMEM((2, count, rows, cols), kind))
    dma = pltpu.SemaphoreType.DMA
    sems = [dma((FIRST_ITEMS,))] + [dma((items,))] * 4
    sems += [dma((items, lines - 1))] * 2 + [dma((items, count)), dma((items, 2, count))]
    sems += [dma((seqs,))] * 2
    kept = [own[k] for k, entry in enumerate(SCATTER_ITEMS) if entry[0] in LATE_SOURCES]
    return kept + own + first_in + second_in + line_in, sems


class BackInputs(NamedTuple):
    gate: object
    up: object
    down: object
    coef: object
    resid: object
    layer: object
    qt: object
    kt: object
    vt: object
    out: object
    normed: object
    stream: object
    tap: object
    attend: object
    lse: object
    key_marks: object
    small: object
    gain_two: object
    table: object
    rows: object
    idm: object


class BackWork(NamedTuple):
    grads: object
    away: object
    came: object
    wide: object
    one_hot: object
    src_qkv: object
    src_table: object
    src_small: object
    swap_send: object
    swap_recv: object
    coef_sem: object
    resid_sem: object
    load_sem: object
    wqkv: object
    picked: object
    rows: object
    src_output: object
    got: object


LATE_LOADS = 7


def backward_kernel(*refs):
    ref = BackInputs(*refs[: len(BackInputs._fields)])
    late_refs = refs[-LATE_LOADS:]
    refs = refs[:-LATE_LOADS]
    late = slice(6, 6 + LATE_LOADS)
    waiting = ref[late]
    ref = ref._replace(**dict(zip(ref._fields[late], late_refs)))
    rest = refs[len(BackInputs._fields) :]
    outs, layer_out = rest[:9], rest[9]
    rest = rest[10:]
    held = 4 * len(SCATTER_ITEMS) + sum(entry[0] in LATE_SOURCES for entry in SCATTER_ITEMS)
    buffers, rest = rest[:held], rest[held:]
    sems = ScatterSems(*rest[: len(ScatterSems._fields)])
    own = BackWork(*rest[len(ScatterSems._fields) :])
    sources = (
        own.src_qkv.at[0],
        own.src_qkv.at[1],
        own.src_qkv.at[2],
        own.src_output,
        ref.gate,
        ref.up,
        ref.down,
        own.src_table,
        own.src_small,
    )
    scatter = Scatter(sources, outs, ref.layer, layer_out, buffers, sems)
    stages = scatter.stages()
    width, tokens = ref.qt.shape
    pairs = width // 128
    bias = own.one_hot.at[0 : ref.kt.shape[1], 0:tokens]
    scatter.meet()
    for item in range(FIRST_ITEMS):
        if SCATTER_ITEMS[item][0] in LATE_SOURCES:
            scatter.stage_begin(item)

    queue = [[functools.partial(stages[stage], item) for stage, item in group] for group in SCHEDULE]

    def tick():
        for task in queue.pop(0):
            task()

    loads = []
    for k in range(LATE_LOADS):
        loads.append(pltpu.make_async_copy(waiting[k], late_refs[k], own.load_sem.at[k]))
        loads[k].start()

    def weight_load(k, at):
        weight = ref.attend.at[:, k * width : (k + 1) * width]
        return pltpu.make_async_copy(weight, own.wqkv.at[at * width : (at + 1) * width], own.load_sem.at[LATE_LOADS + at])

    def resid_load():
        return pltpu.make_async_copy(ref.resid, own.wide.at[0:tokens], own.resid_sem)

    weight_load(3, 0).start()
    resid_load().start()
    scatter.layer_start()
    tick()
    wide = own.wide

    def hand_out(source):
        lines, _, _, count, size, _ = source.shape
        total = lines * 4 * count

        if size % 8:
            for o in range(total):
                where = (o // (4 * count), o // (2 * count) % 2, o // count % 2, o % count)
                source[where] = wide[size * o : size * (o + 1)].astype(source.dtype)
        else:

            def step(o, carry):
                where = (o // (4 * count), o // (2 * count) % 2, o // count % 2, o % count)
                source[where] = wide[pl.ds(pl.multiple_of(size * o, 8), size)].astype(source.dtype)
                return carry

            lax.fori_loop(0, total, step, 0)

    fill_bias(bias, ref.key_marks, ref.key_marks.at[:, 0:tokens])
    for load in loads[:4]:
        load.wait()
    weight_load(3, 0).wait()
    resid_load().wait()
    proj = wide[0:tokens].astype(jnp.bfloat16)
    own.got[...] = mm_nt(own.wqkv[0:width], proj).astype(jnp.bfloat16)
    wide[...] = mm(ref.out[...], proj)
    hand_out(own.src_output)
    for item in range(FIRST_ITEMS):
        if SCATTER_ITEMS[item][0] == 3:
            scatter.stage_begin(item)
    for k in range(3):
        weight_load(k, k).start()

    def swap(i, which):
        rows = pl.ds(pl.multiple_of(which * width + 128 * i, 128), 128)
        return remote(
            own.away.at[rows],
            own.came.at[rows],
            own.swap_send.at[which, i],
            own.swap_recv.at[which, i],
            scatter.twin,
            scatter.place,
        )

    ticks = [queue.pop(0) for _ in range(2 * pairs)]

    def pair_tasks(groups, i):
        for k, group in enumerate(groups):
            if group:

                @pl.when(i == k)
                def _():
                    for task in group:
                        task()

    def pair_step(i, carry):
        at = pl.ds(pl.multiple_of(128 * i, 128), 128)
        attend_backward_pair(
            ref.qt.at[at],
            ref.kt.at[at],
            ref.vt.at[at],
            own.got.at[at],
            ref.out.at[at],
            ref.lse.at[i],
            bias,
            own.grads.at[at],
            own.grads.at[pl.ds(pl.multiple_of(width + 128 * i, 128), 128)],
            own.grads.at[pl.ds(pl.multiple_of(2 * width + 128 * i, 128), 128)],
            own.away.at[at],
            own.away.at[pl.ds(pl.multiple_of(width + 128 * i, 128), 128)],
            lambda: pair_tasks(ticks[0::2], i),
        )
        swap(i, 0).start()
        swap(i, 1).start()
        pair_tasks(ticks[1::2], i)
        return carry

    lax.fori_loop(0, pairs, pair_step, 0)

    for load in loads[4:]:
        load.wait()
    for k in range(3):
        weight_load(k, k).wait()
    normed_t = own.one_hot.at[0:width, 0:tokens]
    normed_t[...] = ref.normed[...].T
    coef = own.came.at[0 : KW * VOCAB]

    def coef_copy():
        return pltpu.make_async_copy(ref.coef, coef, own.coef_sem)

    def take(count):
        groups = [queue.pop(0) for _ in range(count)]

        def run(i):
            for k, group in enumerate(groups):
                if group:

                    @pl.when(i == k)
                    def _():
                        for task in group:
                            task()

        return run

    def third(i):
        return pl.ds(pl.multiple_of(i * width, width), width)

    def add_halves():
        def add_half(j, carry):
            which, i = j // pairs, j % pairs
            swap(i, which).wait_recv()
            rows = pl.ds(pl.multiple_of(which * width + 128 * i, 128), 128)
            at = pl.ds(pl.multiple_of((which + 1) * width + 128 * i, 128), 128)
            own.grads[at] = plus(own.grads[at], own.came[rows])
            return carry

        lax.fori_loop(0, 2 * pairs, add_half, 0)
        coef_copy().start()

    weight_tasks = take(3)

    def weight_step(i, carry):
        pl.when(i == 1)(add_halves)
        wide[...] = mm_nt(normed_t[...], own.grads[third(i)])
        hand_out(own.src_qkv.at[i])
        for k in range(3):
            pl.when(i == k)(functools.partial(scatter.stage_begin, FIRST_ITEMS + k))
        weight_tasks(i)
        return carry

    lax.fori_loop(0, 3, weight_step, 0)

    norm_tasks = take(1)
    wide[:, 0:tokens] = jnp.zeros((width, tokens), jnp.float32)

    def norm_step(i, carry):
        wide[:, 0:tokens] += mm(own.wqkv[third(i)], own.grads[third(i)])
        norm_tasks(i - 1)
        return carry

    lax.fori_loop(0, 3, norm_step, 0)
    normed_grad = wide[:, 0:tokens].T
    resid_load().start()
    stream = ref.stream[...]
    gain = ref.small[KW + 1 : KW + 2]
    scale = lax.rsqrt(jnp.mean(stream * stream, axis=-1, keepdims=True) + 1e-06)
    gain_grad = jnp.sum(normed_grad * stream * scale, axis=0, keepdims=True)
    scaled = normed_grad * gain
    inner = jnp.mean(scaled * stream, axis=-1, keepdims=True)
    resid_load().wait()
    grad16 = (wide[0:tokens] + scale * scaled - stream * (scale * scale * scale * inner)).astype(jnp.bfloat16)
    tick()
    coef_copy().wait()
    tok_backward_body(grad16, coef, ref, own, tick, take)
    hand_out(own.src_table)
    scatter.stage_begin(FIRST_ITEMS + 3)
    rows = jnp.concatenate([own.rows[0 : KW + 1], gain_grad, ref.gain_two[...]], axis=0)
    source = own.src_small
    lines, _, _, count, _, _ = source.shape
    total = lines * 4 * count
    for o in range(total):
        where = (o // (4 * count), o // (2 * count) % 2, o // count % 2, o % count)
        source[where] = lane_shift(rows, o * (width // total))[:, 0:128]
    scatter.stage_begin(FIRST_ITEMS + 4)
    while queue:
        tick()
    scatter.finish()

    def drain(i, carry):
        swap(i, 0).wait_send()
        swap(i, 1).wait_send()
        return carry

    lax.fori_loop(0, pairs, drain, 0)


def backward_all(arrays, shapes):
    count = lax.axis_size("seq")
    lines = lax.axis_size("dp") // 4
    total = lines * 4 * count
    vmem = pl.BlockSpec(memory_space=pltpu.VMEM)
    hbm = pl.BlockSpec(memory_space=pltpu.HBM)
    layer = arrays.layer
    width, tokens = arrays.qt.shape
    out_shape = [jax.ShapeDtypeStruct(shape[:2], jnp.float32) for shape in shapes]
    out_shape.append(jax.ShapeDtypeStruct(layer.shape, layer.dtype))
    buffers, sems = scatter_scratch(shapes, lines, count, layer.shape[0])
    views = list(arrays)
    for k in range(3):
        grad = arrays[k]
        views[k] = grad.reshape(lines, 2, 2, count, grad.shape[0] // total, grad.shape[1])

    def source(index):
        rows, cols, kind = shapes[index]
        return pltpu.VMEM((lines, 2, 2, count, rows, cols), kind)

    half = jnp.bfloat16
    own = [
        pltpu.VMEM((3 * width, tokens), half),
        pltpu.VMEM((2 * width, tokens), half),
        pltpu.VMEM((2 * width, tokens), half),
        pltpu.VMEM((width, width), jnp.float32),
        pltpu.VMEM((KW * VOCAB, arrays.idm.shape[1]), half),
        pltpu.VMEM((3,) + source(0).shape, half),
        source(7),
        source(8),
        pltpu.SemaphoreType.DMA((2, width // 128)),
        pltpu.SemaphoreType.DMA((2, width // 128)),
        pltpu.SemaphoreType.DMA,
        pltpu.SemaphoreType.DMA,
        pltpu.SemaphoreType.DMA((LATE_LOADS + 3,)),
        pltpu.VMEM((3 * width, width), half),
        pltpu.VMEM((KW * VOCAB, 1), jnp.float32),
        pltpu.VMEM((8, width), jnp.float32),
        source(3),
        pltpu.VMEM((width, tokens), half),
    ]
    return pl.pallas_call(
        backward_kernel,
        name="backward_all",
        out_shape=out_shape,
        in_specs=[hbm] * (7 + LATE_LOADS) + [vmem] * (len(views) - 7 - LATE_LOADS),
        out_specs=[vmem] * 9 + [hbm],
        scratch_shapes=buffers + sems + own + [pltpu.VMEM(a.shape, a.dtype) for a in arrays[6 : 6 + LATE_LOADS]],
        compiler_params=pltpu.CompilerParams(
            collective_id=1, has_side_effects=True, vmem_limit_bytes=63 * 1024 * 1024
        ),
    )(*views)


def tok_forward_body(own, core, tokens, tick):
    ids_ref, marks_ref, table_ref, small_ref = own.ids_pad, own.marks_pad, own.table, own.small
    table_ref = table_ref.at[:, 0 : own.stream.shape[1]]
    stream_ref, normed_ref, coef_ref, tap_ref = own.stream, own.normed, own.coef, own.tap
    rows_ref, idm_ref, one_hot = own.rows, own.idm, own.one_hot
    half_bytes = 2 * tokens
    span = one_hot.shape[1]
    wide = span + 2 * LEFT
    first = pl.ds(pl.multiple_of(core * half_bytes, 128), wide)
    ids = ids_ref[:, first]
    marks = marks_ref[:, first]
    for tap in range(KW):
        by = tap - KW // 2
        same = (lane_shift(marks, by) == marks) & (marks > 0)
        idm_ref[tap : tap + 1] = jnp.where(same, lane_shift(ids, by), -1)[0:1, LEFT : LEFT + span]
    tick()
    fill_one_hot(one_hot, idm_ref)

    tick()
    score = jnp.broadcast_to(small_ref[KW : KW + 1], (8, small_ref.shape[1])).astype(jnp.bfloat16)

    def step(tap, carry):
        product = table_ref[...].astype(jnp.float32) * small_ref[pl.ds(tap, 1)]
        high, low = split_two(product)
        tap_ref[tap_rows(tap)] = high
        own.scored[:, tap_rows(tap)] = mm_nt(score, high) + mm_nt(score, low)
        return carry

    lax.fori_loop(0, KW, step, 0)
    tick()
    high, low = split_two(own.scored[...])
    u_row = mm(high, one_hot[...]) + mm(low, one_hot[...])

    tick()
    high = u_row.astype(jnp.bfloat16).astype(jnp.float32)
    marks_here = marks[:, LEFT : LEFT + span].astype(jnp.float32)
    away = marks_ref[:, pl.ds(pl.multiple_of((1 - core) * half_bytes, 128), wide)][:, LEFT : LEFT + span]
    away = away.astype(jnp.float32)
    packed = jnp.concatenate([marks_here, high, u_row - high, away], axis=0).astype(jnp.bfloat16)
    shape = (span, wide // 2)
    twice = 2 * lax.broadcasted_iota(jnp.int32, shape, 1) - lax.broadcasted_iota(jnp.int32, shape, 0) - LEFT
    marks_of, u_of = [], []
    for e in range(2):
        pick = (twice == -e).astype(jnp.float32).astype(jnp.bfloat16)
        apart = mm(packed, pick)
        marks_of.append(apart[0:8])
        u_of.append(apart[8:16] + apart[16:24])
        if e == 0:
            kept = slice(LEFT, LEFT + tokens)
            both = jnp.concatenate([apart[0:1, kept], apart[24:25, kept]], axis=1)
            own.marks[...] = both.astype(jnp.int32)

    tick()
    inside, inverse = pool_rows(marks_of, core, half_bytes)
    prob = {}
    for e in range(2):
        shifted = {}
        for s in range(1 - MAXBLOCK, MAXBLOCK):
            f = (e + s) % 2
            shifted[s] = lane_shift(u_of[f], (e + s - f) // 2)
        scores = [u_of[e]]
        for b in range(2, MAXBLOCK + 1):
            total = u_of[e]
            for s in range(1 - b, b):
                if s != 0:
                    total = total + inside[b, e, s] * shifted[s]
            scores.append(total * inverse[b, e])
        top = scores[0]
        for value in scores[1:]:
            top = jnp.maximum(top, value)
        expo = [jnp.exp(value - top) for value in scores]
        whole = expo[0] + expo[1] + expo[2] + expo[3]
        for b in range(1, MAXBLOCK + 1):
            prob[b, e] = expo[b - 1] / whole
            rows_ref[2 * b + e : 2 * b + e + 1] = prob[b, e][0:1]
        rows_ref[e : e + 1] = marks_of[e][0:1]
    coefs = band_coefs({key: 0.5 * value for key, value in prob.items()}, inside, inverse)
    gain = small_ref[KW + 1 : KW + 2]
    tick()
    for i in range(tokens // BAND):
        matrix = band_matrix(coefs, i).astype(jnp.bfloat16)
        lanes = slice(i * BAND, (i + 1) * BAND)
        part = mm(one_hot[:, 2 * i * BAND : (2 * i + 3) * BAND], matrix).astype(jnp.bfloat16)
        coef_ref[:, lanes] = part
        stream = mm_tn(part, tap_ref[...])
        stream_ref[lanes] = stream
        scale = lax.rsqrt(jnp.mean(stream * stream, axis=-1, keepdims=True) + 1e-06)
        normed_ref[lanes] = (stream * scale * gain).astype(jnp.bfloat16)
        if i < tokens // BAND - 1:
            tick()


FUSED_ITEMS = (
    (4, 0, 1, 0, 0),
    (0, 0, 2, 1, 1),
    (0, 1, 2, 0, 1),
    (2, 1, 2, 1, 2),
    (3, 0, 1, 0, 3),
    (2, 0, 2, 0, 4),
    (1, 0, 1, 1, 5),
)
FUSED_SCHEDULE = (
    (
        (0, 0, 0), (1, 0, 0), (0, 1, 0), (1, 1, 0), (2, 0, 1), (3, 0, 0),
        (3, 1, 0), (2, 0, 2), (4, 0, 0), (3, 0, 1), (2, 0, 3), (2, 1, 1),
        (0, 2, 0), (3, 0, 2), (4, 1, 0), (3, 0, 3), (2, 1, 2), (4, 0, 1),
        (3, 1, 1), (2, 1, 3), (1, 2, 0), (2, 2, 1), (0, 3, 0), (4, 0, 2),
        (4, 0, 3), (2, 2, 2),
    ),
    (),
    (
        (2, 2, 3), (1, 3, 0), (2, 3, 1), (0, 4, 0), (3, 1, 2),
    ),
    (
        (2, 3, 2), (3, 1, 3), (3, 2, 0), (4, 1, 1),
    ),
    ((3, 2, 1),),
    (
        (2, 3, 3), (1, 4, 0), (2, 4, 1), (0, 5, 0), (3, 2, 2),
    ),
    ((3, 2, 3),),
    (
        (2, 4, 2), (3, 3, 0),
    ),
    (
        (2, 4, 3), (1, 5, 0), (2, 5, 1), (3, 3, 1), (4, 1, 2), (4, 1, 3),
        (2, 5, 2),
    ),
    (
        (3, 3, 2), (4, 2, 0),
    ),
    (
        (2, 5, 3), (5, 0, 0), (3, 3, 3), (4, 2, 1),
    ),
    (
        (3, 4, 0), (3, 4, 1),
    ),
    (
        (3, 4, 2), (4, 2, 2), (4, 2, 3), (4, 3, 0),
    ),
    (),
    ((3, 4, 3),),
    (),
    ((3, 5, 0),),
    ((3, 5, 1),),
    (),
    ((4, 3, 1),),
    (
        (3, 5, 2), (4, 5, 0),
    ),
    ((3, 5, 3),),
    (
        (4, 3, 2), (4, 3, 3), (4, 5, 1),
    ),
    ((4, 4, 0),),
    (
        (4, 4, 1), (4, 5, 2),
    ),
    (
        (4, 4, 2), (4, 4, 3), (4, 5, 3),
    ),
    (),
)


class Gather:
    def __init__(self, ins, outs, cells_in, cells_out, cot_in, cot_out, sems):
        self.ins, self.outs, self.sems = ins, outs, sems
        self.cells_in, self.cells_out, self.cot_in, self.cot_out = cells_in, cells_out, cot_in, cot_out
        self.y, self.x, self.core, self.place, self.lines, self.count = position()
        y, x, core = self.y, self.x, self.core
        self.group = y * 2 + x
        self.dp = dp_of(y, x, core)
        self.twin = dp_of(y, x, 1 - core)
        self.side = dp_of(y, 1 - x, core)
        self.ahead = [(y + k) % self.lines for k in range(1, self.lines)]
        self.phases = {}
        for item, entry in enumerate(FUSED_ITEMS):
            self.phases.setdefault(entry[4], []).append(item)

    def meet(self):
        targets = [(self.twin, self.place), (self.side, self.place)]
        for k in range(1, self.count):
            other = (self.place + k) % self.count
            targets += [(self.dp, other), (self.twin, other)]
        for other_y in self.ahead:
            targets.append((dp_of(other_y, self.x, self.core), self.place))
        meet(targets)

    def lanes(self, item):
        array, part, parts, _, _ = FUSED_ITEMS[item]
        cols = self.ins[array].shape[1] // parts
        return pl.ds(part * cols, cols)

    def shard(self, item):
        return self.ins[FUSED_ITEMS[item][0]].at[:, self.lanes(item)]

    def rows(self, item, first, blocks):
        array = FUSED_ITEMS[item][0]
        size = self.ins[array].shape[0]
        start = pl.multiple_of(first * size, 8)
        return self.outs[array].at[pl.ds(start, blocks * size), self.lanes(item)]

    def block(self, item, g, z):
        return self.rows(item, (g * 2 + self.core) * self.count + z, 1)

    def group_block(self, item, g, core):
        return self.rows(item, (g * 2 + core) * self.count, self.count)

    def came(self, item, g, z):
        return self.sems.recv.at[item, g * self.count + z]

    def arrived(self, item, g, z):
        dst = self.block(item, g, z)
        remote(dst, dst, self.sems.x.at[item], self.came(item, g, z), self.twin, self.place).wait_recv()

    def to_side(self, item, src, g, z):
        remote(
            src, self.block(item, g, z), self.sems.x.at[item], self.came(item, g, z), self.side, self.place
        ).start()

    def to_lines(self, item, src, g, z):
        for other_y in self.ahead:
            remote(
                src,
                self.block(item, g, z),
                self.sems.y.at[item],
                self.came(item, g, z),
                dp_of(other_y, self.x, self.core),
                self.place,
            ).start()

    def to_z(self, item, src, z, way):
        return remote(
            src,
            self.block(item, self.group, z),
            self.sems.z.at[item, z, way],
            self.came(item, self.group, z),
            self.dp,
            self.place + 1 - 2 * way,
        )

    def to_twin(self, item, g):
        src = self.group_block(item, g, self.core)
        remote(
            src, src, self.sems.twin.at[item], self.sems.twin_recv.at[item, g], self.twin, self.place
        ).start()

    def own_copy(self, item):
        return pltpu.make_async_copy(
            self.shard(item), self.block(item, self.group, self.place), self.sems.own.at[item]
        )

    def task_own(self, phase):
        for item in self.phases[phase]:
            src = self.shard(item)

            @pl.when(self.place < self.count - 1)
            def _():
                self.to_z(item, src, self.place, 0).start()

            @pl.when(self.place > 0)
            def _():
                self.to_z(item, src, self.place, 1).start()

            self.own_copy(item).start()

    def task_sides(self, phase):
        for item in self.phases[phase]:
            src = self.shard(item)
            self.to_side(item, src, self.group, self.place)
            self.to_lines(item, src, self.group, self.place)

    def both_ways(self, step, body):
        def way_step(way, carry):
            z = self.place + step * (2 * way - 1)

            @pl.when((z >= 0) & (z < self.count))
            def _():
                body(z, way)

            return carry

        lax.fori_loop(0, 2, way_step, 0)

    def steps(self, step, body):
        if step < 3:
            body(step)
            return

        def loop(s, carry):
            body(s)
            return carry

        lax.fori_loop(3, self.count, loop, 0)

    def task_first(self, phase, step):
        items = self.phases[phase]

        def receive(z, way):
            for item in items:
                self.arrived(item, self.group, z)
                src = self.block(item, self.group, z)
                then = self.place + 1 - 2 * way
                onward = (then >= 0) & (then < self.count)

                @pl.when(onward)
                def _():
                    self.to_z(item, src, z, way).start()

                self.to_side(item, src, self.group, z)
                self.to_lines(item, src, self.group, z)

        self.steps(step, lambda s: self.both_ways(s, receive))
        if step == 3:
            for item in items:
                self.own_copy(item).wait()
                self.to_twin(item, self.group)

    def at_distance(self, step, body):
        if step == 0:
            body(self.place, 0)
        else:
            self.steps(step, lambda s: self.both_ways(s, body))

    def task_second(self, phase, step):
        items = self.phases[phase]

        def receive(z, way):
            for item in items:
                if FUSED_ITEMS[item][3] == 0:
                    g = self.y * 2 + (1 - self.x)
                    self.arrived(item, g, z)
                    self.to_lines(item, self.block(item, g, z), g, z)
                else:
                    for other_y in self.ahead:
                        g = other_y * 2 + self.x
                        self.arrived(item, g, z)
                        self.to_side(item, self.block(item, g, z), g, z)

        self.at_distance(step, receive)
        if step == 3:
            for item in items:
                if FUSED_ITEMS[item][3] == 0:
                    self.to_twin(item, self.y * 2 + (1 - self.x))
                else:
                    for other_y in self.ahead:
                        self.to_twin(item, other_y * 2 + self.x)

    def task_third(self, phase, step):
        items = self.phases[phase]

        def rest(item):
            if FUSED_ITEMS[item][3] == 0:
                return [other_y * 2 + x for other_y in self.ahead for x in (self.x, 1 - self.x)]
            return [other_y * 2 + (1 - self.x) for other_y in [self.y] + self.ahead]

        def receive(z, way):
            for item in items:
                for g in rest(item):
                    self.arrived(item, g, z)

        self.at_distance(step, receive)
        if step == 3:
            for item in items:
                for g in rest(item):
                    self.to_twin(item, g)

    def full(self, item):
        def step(g, carry):
            dst = self.group_block(item, g, 1 - self.core)
            remote(
                dst, dst, self.sems.twin.at[item], self.sems.twin_recv.at[item, g], self.twin, self.place
            ).wait_recv()
            return carry

        lax.fori_loop(0, self.lines * 2, step, 0)

    def cell_copies(self, fn_remote, fn_local):
        seqs = self.cells_in.shape[0]
        for r in range(seqs):
            chip = seqs * self.core + r
            for c in range(2):
                home = (chip == self.place) & (self.core == c)

                @pl.when(home)
                def _():
                    fn_local(r)

                @pl.when(jnp.logical_not(home))
                def _():
                    fn_remote(r, c, chip)

    def cell_remote(self, r, c, chip):
        return remote(
            self.cells_in.at[r],
            self.cells_out.at[self.place],
            self.sems.cell_send.at[r, c],
            self.sems.cell_recv.at[self.place],
            dp_of(self.y, self.x, c),
            chip,
        )

    def cells_start(self):
        self.cell_copies(
            lambda r, c, chip: self.cell_remote(r, c, chip).start(),
            lambda r: pltpu.make_async_copy(
                self.cells_in.at[r], self.cells_out.at[self.place], self.sems.cell_recv.at[self.place]
            ).start(),
        )

    def cells_wait(self):
        for q in range(self.count):
            dst = self.cells_out.at[q]
            remote(
                dst, dst, self.sems.cell_send.at[0, 0], self.sems.cell_recv.at[q], self.twin, self.place
            ).wait_recv()

    def cot_copies(self, fn_remote, fn_local):
        seqs = self.cot_in.shape[0]
        for r in range(seqs):
            chip = seqs * self.core + r
            home = (chip == self.place) & (self.core == self.place // seqs)

            @pl.when(home)
            def _():
                fn_local(r)

            @pl.when(jnp.logical_not(home))
            def _():
                fn_remote(r, chip)

    def cot_remote(self, r, chip):
        seqs = self.cot_in.shape[0]
        slot = self.place % seqs
        return remote(
            self.cot_in.at[r],
            self.cot_out.at[slot],
            self.sems.cot_send.at[r],
            self.sems.cot_recv.at[slot],
            dp_of(self.y, self.x, self.place // seqs),
            chip,
        )

    def task_cot(self):
        slot = self.place % self.cot_in.shape[0]
        self.cot_copies(
            lambda r, chip: self.cot_remote(r, chip).start(),
            lambda r: pltpu.make_async_copy(
                self.cot_in.at[r], self.cot_out.at[slot], self.sems.cot_recv.at[slot]
            ).start(),
        )

    def task(self, kind, phase, step):
        if kind == 0:
            self.task_own(phase)
        elif kind == 1:
            self.task_sides(phase)
        elif kind == 2:
            self.task_first(phase, step)
        elif kind == 3:
            self.task_second(phase, step)
        elif kind == 4:
            self.task_third(phase, step)
        else:
            self.task_cot()

    def finish(self, waited):
        count, groups = self.count, self.lines * 2
        for item in range(len(FUSED_ITEMS)):
            if item not in waited:
                self.full(item)
            tree = FUSED_ITEMS[item][3]

            def sent(blocks, sem):
                src = self.rows(item, 0, blocks)
                remote(src, src, sem, self.came(item, 0, 0), self.twin, self.place).wait_send()

            sent(count * (1 if tree == 0 else self.lines), self.sems.x.at[item])
            sent(count * (self.lines - 1) * (2 if tree == 0 else 1), self.sems.y.at[item])
            sent(count * groups, self.sems.twin.at[item])

            def drain(z, carry):
                @pl.when((z <= self.place) & (self.place < count - 1))
                def _():
                    self.to_z(item, self.block(item, self.group, z), z, 0).wait_send()

                @pl.when((z >= self.place) & (self.place > 0))
                def _():
                    self.to_z(item, self.block(item, self.group, z), z, 1).wait_send()

                return carry

            lax.fori_loop(0, count, drain, 0)
        for q in range(self.cot_in.shape[0]):
            dst = self.cot_out.at[q]
            remote(
                dst, dst, self.sems.cot_send.at[0], self.sems.cot_recv.at[q], self.twin, self.place
            ).wait_recv()
        self.cell_copies(lambda r, c, chip: self.cell_remote(r, c, chip).wait_send(), lambda r: None)
        self.cot_copies(lambda r, chip: self.cot_remote(r, chip).wait_send(), lambda r: None)


class GatherSems(NamedTuple):
    recv: object
    twin_recv: object
    z: object
    x: object
    y: object
    twin: object
    own: object
    cell_recv: object
    cell_send: object
    cot_recv: object
    cot_send: object
class FrontOuts(NamedTuple):
    cot: object
    stream: object
    normed: object
    coef: object
    tap: object
    rows: object
    idm: object
    qt: object
    kt: object
    vt: object
    out: object
    lse: object
    marks: object
    small: object
    resid: object
    normed_two: object


class FrontWork(NamedTuple):
    stream: object
    normed: object
    coef: object
    tap: object
    rows: object
    idm: object
    qt: object
    kt: object
    vt: object
    out: object
    lse: object
    marks: object
    small: object
    resid: object
    normed_two: object
    cells: object
    ids_pad: object
    marks_pad: object
    table: object
    blocks: object
    wq: object
    wk: object
    wv: object
    wo: object
    other: object
    one_hot: object
    bias: object
    scores: object
    out_sem: object
    load_sem: object
    swap_send: object
    swap_recv: object
    small_in: object
    cells_in: object
    scored: object
    pair: object
    wkv: object
    kv: object
    attend_in: object
    table_in: object


def attend_forward_pair(qt, kt, vt, bias, scores, out, lse, tasks):
    keys = kt[...].T
    chunks = keys.shape[0] // CHUNK
    for h in range(2):
        query = pair_rows(qt, h)
        own = slice(h * HEAD_DIM, (h + 1) * HEAD_DIM)
        top = None
        for c in range(chunks):
            rows = slice(c * CHUNK, (c + 1) * CHUNK)
            part = mm(keys[rows], query) + bias[rows]
            scores[h, rows] = part
            high = jnp.max(part, axis=0, keepdims=True)
            top = high if top is None else jnp.maximum(top, high)
        total = None
        summed = None
        for c in range(chunks):
            rows = slice(c * CHUNK, (c + 1) * CHUNK)
            expo = jnp.exp(scores[h, rows] - top)
            part = jnp.sum(expo, axis=0, keepdims=True)
            total = part if total is None else total + part
            part = mm(vt[own, rows], expo.astype(jnp.bfloat16))
            summed = part if summed is None else summed + part
        out[own] = (summed / total).astype(jnp.bfloat16)
        lse[h : h + 1] = top + jnp.log(total)
        if h == 0:
            tasks()


def forward_kernel(*refs):
    arrays = 5
    attend_parts, feed_parts, embed_table = refs[:4], refs[4:7], refs[7]
    byte_ids, segments, taps, vectors, cot_in = refs[8:13]
    rest = refs[13:]
    full, cells_out = rest[:arrays], rest[arrays]
    kept = len(FrontOuts._fields)
    to = FrontOuts(*rest[arrays + 1 : arrays + 1 + kept])
    rest = rest[arrays + 1 + kept :]
    sems = GatherSems(*rest[: len(GatherSems._fields)])
    own = FrontWork(*rest[len(GatherSems._fields) :])
    small_in, cells_in = own.small_in, own.cells_in
    tokens, width = own.stream.shape
    own = own._replace(
        normed=own.pair.at[0:tokens],
        other=own.pair.at[tokens : 2 * tokens],
        wk=own.wkv.at[0:width],
        wv=own.wkv.at[width : 2 * width],
        kt=own.kv.at[0:width],
        vt=own.kv.at[width : 2 * width],
    )
    ins = (own.attend_in,) + tuple(feed_parts) + (own.table_in,)
    gather = Gather(ins, full, cells_in, cells_out, cot_in, to.cot, sems)
    which = {}
    for item, entry in enumerate(FUSED_ITEMS):
        which[entry[0], entry[1]] = item
    queue = [list(group) for group in FUSED_SCHEDULE]

    def tick():
        for entry in queue.pop(0):
            gather.task(*entry)

    saved = []

    def save(src, dst):
        copy = pltpu.make_async_copy(src, dst, own.out_sem.at[len(saved)])
        copy.start()
        saved.append(copy)

    def load(k, dst):
        if k % 2 == 0:
            gather.full(which[0, k // 2])
        copy = pltpu.make_async_copy(full[0].at[:, k * width : (k + 1) * width], dst, own.load_sem.at[k])
        copy.start()
        return copy

    small_in[...] = jnp.zeros_like(small_in)
    small_in[0:KW, 0 : taps.shape[1]] = taps[...].astype(jnp.float32)
    small_in[KW:8, 0 : taps.shape[1]] = vectors[...]
    own.table_in[:, 0:width] = embed_table[...]
    own.table_in[:, width : width + 128] = small_in[...].astype(jnp.bfloat16)
    for k in range(4):
        own.attend_in[:, k * width : (k + 1) * width] = attend_parts[k][...]
    per_part = byte_ids.shape[1] // 128
    for r in range(byte_ids.shape[0]):
        for k in range(per_part):
            lanes = slice(128 * k, 128 * (k + 1))
            cells_in[r, k : k + 1] = byte_ids[r : r + 1, lanes]
            cells_in[r, per_part + k : per_part + k + 1] = segments[r : r + 1, lanes] + 1
    gather.meet()
    gather.cells_start()
    tick()

    core, place = gather.core, gather.place
    tokens, width = own.stream.shape
    half_bytes = 2 * tokens
    span = own.one_hot.shape[1]
    wide = span + 2 * LEFT
    gather.cells_wait()
    cell_copy = pltpu.make_async_copy(cells_out, own.cells, own.load_sem.at[4])
    cell_copy.start()
    gather.full(which[4, 0])
    load_table = pltpu.make_async_copy(full[4], own.table, own.load_sem.at[5])
    load_table.start()
    cell_copy.wait()
    ids_pad, marks_pad = own.ids_pad, own.marks_pad
    ids_pad[:, 0 : 2 * LEFT] = jnp.full((8, 2 * LEFT), -1, jnp.int32)
    marks_pad[:, 0 : 2 * LEFT] = jnp.zeros((8, 2 * LEFT), jnp.int32)
    end = 2 * LEFT + 2 * half_bytes
    ids_pad[:, end : end + 2 * LEFT] = jnp.full((8, 2 * LEFT), -1, jnp.int32)
    marks_pad[:, end : end + 2 * LEFT] = jnp.zeros((8, 2 * LEFT), jnp.int32)
    parts, per_part = own.cells.shape[0], own.cells.shape[1] // 2
    for q in range(parts):
        for r in range(per_part):
            at = slice(2 * LEFT + (q * per_part + r) * 128, 2 * LEFT + (q * per_part + r + 1) * 128)
            ids_pad[:, at] = jnp.broadcast_to(own.cells[q, r : r + 1], (8, 128))
            marks_pad[:, at] = jnp.broadcast_to(own.cells[q, per_part + r : per_part + r + 1], (8, 128))
    load_table.wait()
    own.blocks[...] = own.table[:, width : width + 128].astype(jnp.float32)
    total = gather.lines * 4 * gather.count
    chan = width // total
    lane = lax.broadcasted_iota(jnp.int32, (8, 128), 1)
    columns = [jnp.zeros((8, 128), jnp.float32) for _ in range(width // 128)]
    for o in range(total):
        piece = jnp.where(lane < chan, own.blocks[8 * o : 8 * o + 8], 0.0)
        at, by = divmod(o * chan, 128)
        turned = piece if by == 0 else pltpu.roll(piece, by, 1)
        columns[at] = columns[at] + jnp.where(lane >= by, turned, 0.0)
        if by + chan > 128:
            columns[at + 1] = columns[at + 1] + jnp.where(lane < by, turned, 0.0)
    own.small[...] = jnp.concatenate(columns, axis=1)
    save(own.small, to.small)
    tok_forward_body(own, core, tokens, tick)
    save(own.stream, to.stream)
    save(own.normed, to.normed)
    save(own.coef, to.coef)
    save(own.tap, to.tap)
    save(own.rows, to.rows)
    save(own.idm, to.idm)
    save(own.marks, to.marks)

    swap = remote(own.normed, own.other, own.swap_send, own.swap_recv, gather.twin, place)
    swap.start()
    tick()
    load_wq = load(0, own.wq)
    load_wk = load(1, own.wk)
    load_wv = load(2, own.wv)

    def project(rows, weight):
        return mm(rows[...], weight[...]).astype(jnp.bfloat16)

    load_wq.wait()
    own.qt[...] = (project(own.normed, own.wq) * HEAD_DIM ** (-0.5)).astype(jnp.bfloat16).T
    save(own.qt, to.qt)
    tick()
    load_wk.wait()
    load_wv.wait()
    groups = [queue.pop(0) for _ in range(4)]

    def project_step(i, carry):
        which, part = i % 2, i // 2

        @pl.when(i == 2)
        def _():
            swap.wait_recv()

        rows = own.pair.at[pl.ds(pl.multiple_of(part * tokens, tokens), tokens)]
        weight = own.wkv.at[pl.ds(pl.multiple_of(which * width, width), width)]
        to_rows = pl.ds(pl.multiple_of(which * width, width), width)
        own.kv[to_rows, pl.ds(pl.multiple_of(part * tokens, tokens), tokens)] = project(rows, weight).T
        for k, group in enumerate(groups):
            if group:

                @pl.when(i == k)
                def _():
                    for entry in group:
                        gather.task(*entry)

        return carry

    lax.fori_loop(0, 4, project_step, 0)
    save(own.kt, to.kt)
    save(own.vt, to.vt)
    load_wo = load(3, own.wo)
    fill_bias(own.bias, own.marks, own.marks.at[:, 0:tokens])
    pairs = width // 128
    ticks = [queue.pop(0) for _ in range(2 * pairs)]

    def pair_tasks(groups, i):
        for k, group in enumerate(groups):
            if group:

                @pl.when(i == k)
                def _():
                    for entry in group:
                        gather.task(*entry)

    def pair_step(i, carry):
        at = pl.ds(pl.multiple_of(128 * i, 128), 128)
        attend_forward_pair(
            own.qt.at[at],
            own.kt.at[at],
            own.vt.at[at],
            own.bias,
            own.scores,
            own.out.at[at],
            own.lse.at[i],
            lambda: pair_tasks(ticks[0::2], i),
        )
        pair_tasks(ticks[1::2], i)
        return carry

    lax.fori_loop(0, pairs, pair_step, 0)
    save(own.out, to.out)
    save(own.lse, to.lse)
    load_wo.wait()
    resid = own.stream[...] + mm(own.out[...].T, own.wo[...])
    own.resid[...] = resid
    save(own.resid, to.resid)
    scale = lax.rsqrt(jnp.mean(resid * resid, axis=-1, keepdims=True) + 1e-06)
    own.normed_two[...] = (resid * scale * own.small[KW + 2 : KW + 3]).astype(jnp.bfloat16)
    save(own.normed_two, to.normed_two)
    while queue:
        tick()
    gather.finish([which[0, 0], which[0, 1], which[4, 0]])
    for copy in saved:
        copy.wait()
    swap.wait_send()


def forward_all(shards, byte_ids, segments, taps, vectors, cot, tokens):
    count = lax.axis_size("seq")
    group_count = lax.axis_size(ALL)
    groups = group_count // (2 * count)
    items = len(FUSED_ITEMS)
    seqs = byte_ids.shape[0]
    cells = jax.ShapeDtypeStruct((seqs, byte_ids.shape[1] // 64, 128), jnp.int32)
    width = shards[0].shape[1]
    span = 2 * tokens + 2 * LEFT
    half, single = jnp.bfloat16, jnp.float32
    vmem = pl.BlockSpec(memory_space=pltpu.VMEM)
    hbm = pl.BlockSpec(memory_space=pltpu.HBM)
    pairs = width // 128
    held = (
        ((tokens, width), single),
        ((tokens, width), half),
        ((KW * VOCAB, tokens), half),
        ((KW * VOCAB, width), half),
        ((16, (span + 2 * LEFT) // 2), single),
        ((8, span), jnp.int32),
        ((width, tokens), half),
        ((width, 2 * tokens), half),
        ((width, 2 * tokens), half),
        ((width, tokens), half),
        ((pairs, 2, tokens), single),
        ((1, 2 * tokens), jnp.int32),
        ((8, width), single),
        ((tokens, width), single),
        ((tokens, width), half),
    )
    size = shards[0].shape[0]
    sent = [(size, 4 * width)] + [shard.shape for shard in shards[4:7]] + [(8, width + 128)]
    shapes = [jax.ShapeDtypeStruct((rows * group_count, cols), half) for rows, cols in sent]
    shapes.append(jax.ShapeDtypeStruct((count,) + cells.shape[1:], cells.dtype))
    shapes.append(jax.ShapeDtypeStruct(cot.shape, cot.dtype))
    shapes += [jax.ShapeDtypeStruct(*entry) for entry in held]
    dma = pltpu.SemaphoreType.DMA
    scratch = [
        dma((items, groups * count)),
        dma((items, groups)),
        dma((items, count, 2)),
        dma((items,)),
        dma((items,)),
        dma((items,)),
        dma((items,)),
        dma((count,)),
        dma((seqs, 2)),
        dma((seqs,)),
        dma((seqs,)),
    ]
    scratch += [pltpu.VMEM(*entry) for entry in held]
    scratch += [
        pltpu.VMEM((count,) + cells.shape[1:], cells.dtype),
        pltpu.VMEM((8, 4 * tokens + 4 * LEFT), jnp.int32),
        pltpu.VMEM((8, 4 * tokens + 4 * LEFT), jnp.int32),
        pltpu.VMEM((VOCAB, width + 128), half),
        pltpu.VMEM((8 * group_count, 128), single),
        pltpu.VMEM((width, width), half),
        pltpu.VMEM((width, width), half),
        pltpu.VMEM((width, width), half),
        pltpu.VMEM((width, width), half),
        pltpu.VMEM((tokens, width), half),
        pltpu.VMEM((KW * VOCAB, span), half),
        pltpu.VMEM((2 * tokens, tokens), single),
        pltpu.VMEM((2, 2 * tokens, tokens), single),
        dma((len(held),)),
        dma((9,)),
        dma,
        dma,
        pltpu.VMEM((8, 128), single),
        pltpu.VMEM(cells.shape, cells.dtype),
        pltpu.VMEM((8, KW * VOCAB), single),
        pltpu.VMEM((2 * tokens, width), half),
        pltpu.VMEM((2 * width, width), half),
        pltpu.VMEM((2 * width, 2 * tokens), half),
        pltpu.VMEM((shards[0].shape[0], 4 * width), half),
        pltpu.VMEM((8, width + 128), half),
    ]
    out = pl.pallas_call(
        forward_kernel,
        name="forward_all",
        out_shape=shapes,
        in_specs=[vmem] * (len(shards) + 5),
        out_specs=[hbm] * len(shapes),
        scratch_shapes=scratch,
        compiler_params=pltpu.CompilerParams(
            collective_id=0, has_side_effects=True, vmem_limit_bytes=60 * 1024 * 1024
        ),
    )(*shards, byte_ids, segments, taps, vectors, cot)
    return list(out[:5]), FrontOuts(*out[6:])

FF_BLOCK = 512


def feed_kernel(
    normed,
    cot,
    resid,
    small,
    w_gate,
    w_up,
    w_down,
    gate_grad,
    up_grad,
    down_grad,
    layer,
    resid_grad,
    gain_grad,
    normed_t,
    total,
    normed_grad,
    stream_here,
    late_sem,
):
    step = pl.program_id(0)
    late = [pltpu.make_async_copy(resid, stream_here, late_sem.at[0])]

    @pl.when(step == 0)
    def _():
        for copy in late:
            copy.start()
        normed_t[...] = normed[...].T
        total[...] = jnp.zeros_like(total)
        normed_grad[...] = jnp.zeros_like(normed_grad)

    gate = mm(normed[...], w_gate[...])
    up = mm(normed[...], w_up[...])
    root = 0.7978845608028654
    square = gate * gate
    bent = jnp.tanh(root * gate * (1.0 + 0.044715 * square))
    half = 0.5 * (1.0 + bent)
    act = gate * half
    slope = half + 0.5 * gate * (1.0 - bent * bent) * (root * (1.0 + 3 * 0.044715 * square))
    hidden = (act * up).astype(jnp.bfloat16)
    total[...] += mm(hidden, w_down[...])
    hidden_grad = mm_nt(cot[...], w_down[...])
    up_part = (hidden_grad * act).astype(jnp.bfloat16)
    gate_part = (hidden_grad * up * slope).astype(jnp.bfloat16)
    down_grad[...] = mm(hidden.T, cot[...]).astype(jnp.bfloat16)
    gate_grad[...] = mm(normed_t[...], gate_part).astype(jnp.bfloat16)
    up_grad[...] = mm(normed_t[...], up_part).astype(jnp.bfloat16)
    normed_grad[...] += mm_nt(gate_part, w_gate[...]) + mm_nt(up_part, w_up[...])

    @pl.when(step == pl.num_programs(0) - 1)
    def _():
        for copy in late:
            copy.wait()
        stream = stream_here[...]
        layer[...] = (stream + total[...]).astype(jnp.bfloat16)
        scale = lax.rsqrt(jnp.mean(stream * stream, axis=-1, keepdims=True) + 1e-06)
        grad = normed_grad[...]
        gain_grad[...] = jnp.sum(grad * stream * scale, axis=0, keepdims=True)
        scaled = grad * small[KW + 2 : KW + 3]
        inner = jnp.mean(scaled * stream, axis=-1, keepdims=True)
        whole = cot[...].astype(jnp.float32) + scale * scaled - stream * (scale * scale * scale * inner)
        resid_grad[...] = whole


def feed_forward(normed, cot, resid, small, w_gate, w_up, w_down):
    tokens, width = normed.shape
    wide = w_gate.shape[1]
    whole = lambda shape: pl.BlockSpec(shape, lambda f: (0, 0))
    hbm = pl.BlockSpec(memory_space=pltpu.HBM)
    columns = pl.BlockSpec((width, FF_BLOCK), lambda f: (0, f))
    rows = pl.BlockSpec((FF_BLOCK, width), lambda f: (f, 0))
    half, single = jnp.bfloat16, jnp.float32
    return pl.pallas_call(
        feed_kernel,
        name="feed_forward",
        grid=(wide // FF_BLOCK,),
        in_specs=[
            whole((tokens, width)),
            whole((tokens, width)),
            hbm,
            whole(small.shape),
            columns,
            columns,
            rows,
        ],
        out_specs=[
            columns,
            columns,
            rows,
            whole((tokens, width)),
            whole((tokens, width)),
            whole((1, width)),
        ],
        out_shape=[
            jax.ShapeDtypeStruct((width, wide), half),
            jax.ShapeDtypeStruct((width, wide), half),
            jax.ShapeDtypeStruct((wide, width), half),
            jax.ShapeDtypeStruct((tokens, width), half),
            jax.ShapeDtypeStruct((tokens, width), single),
            jax.ShapeDtypeStruct((1, width), single),
        ],
        scratch_shapes=[
            pltpu.VMEM((width, tokens), half),
            pltpu.VMEM((tokens, width), single),
            pltpu.VMEM((tokens, width), single),
            pltpu.VMEM((tokens, width), single),
            pltpu.SemaphoreType.DMA((3,)),
        ],
        compiler_params=pltpu.CompilerParams(vmem_limit_bytes=VMEM_BYTES),
    )(normed, cot, resid, small, w_gate, w_up, w_down)


def result_kernel(count, chan, *refs):
    ins, outs, sem = refs[:count], refs[count:-1], refs[-1]
    small = ins[-1]
    copies = [pltpu.make_async_copy(ins[k], outs[k], sem.at[k]) for k in range(count - 1)]
    for copy in copies:
        copy.start()
    outs[count - 1][...] = small[0:KW, 0:chan]
    for k in range(3):
        outs[count + k][...] = small[KW + k : KW + k + 1, 0:chan]
    for copy in copies:
        copy.wait()


def results(arrays, small, chan):
    vmem = pl.BlockSpec(memory_space=pltpu.VMEM)
    hbm = pl.BlockSpec(memory_space=pltpu.HBM)
    count = len(arrays) + 1
    shapes = [jax.ShapeDtypeStruct(a.shape, a.dtype) for a in arrays]
    shapes.append(jax.ShapeDtypeStruct((KW, chan), jnp.float32))
    shapes += [jax.ShapeDtypeStruct((1, chan), jnp.float32)] * 3
    return pl.pallas_call(
        functools.partial(result_kernel, count, chan),
        name="results",
        out_shape=shapes,
        in_specs=[vmem] * count,
        out_specs=[hbm] * len(arrays) + [vmem] * 4,
        scratch_shapes=[pltpu.SemaphoreType.DMA((count,))],
    )(*arrays, small)


def per_device(
    byte_ids,
    segments,
    embed_table,
    conv_weight,
    score_vector,
    first_gain,
    w_query,
    w_key,
    w_value,
    w_output,
    second_gain,
    w_gate,
    w_up,
    w_down,
    out_grad,
):
    seqs, part_bytes = byte_ids.shape
    count = lax.axis_size("seq")
    seq_len = part_bytes * count
    width = w_query.shape[1]
    wide = w_gate.shape[1]
    half_bytes = seq_len // 2
    half = half_bytes // 2
    core = lax.axis_index("dp") % 2
    place = lax.axis_index("seq")

    chan = conv_weight.shape[0]
    shards = (w_query, w_key, w_value, w_output, w_gate, w_up, w_down, embed_table)
    vectors = jnp.stack([score_vector, first_gain, second_gain]).astype(jnp.float32)
    if all(shard.shape[0] % 8 == 0 for shard in shards):
        full, held = forward_all(shards, byte_ids, segments, conv_weight.T, vectors, out_grad, half)
        attend, wg, wu, wd, table = full
        cot = held.cot.reshape(half, width)
        small_full, stream, normed_one, resid_one = held.small, held.stream, held.normed, held.resid
        coef, tap_table, rows, idm = held.coef, held.tap, held.rows, held.idm
        queries, keys, vals, attn_out, lse = held.qt, held.kt, held.vt, held.out, held.lse
        key_marks = held.marks[0]
        normed_two = held.normed_two
    else:
        small = jnp.concatenate([conv_weight.T.astype(jnp.float32), vectors], axis=0)
        small = jnp.pad(small, ((0, 0), (0, 128 - chan)))
        cells = jnp.stack([byte_ids, segments + 1], axis=1).reshape(seqs, -1, 128)
        wq, wk, wv, wo, wg, wu, wd, table, small_full, cells, cot = gather_all(shards + (small,), cells, out_grad)
        attend = jnp.concatenate([wq, wk, wv, wo], axis=1)
        cells = cells.reshape(count, 2, part_bytes).transpose(1, 0, 2).reshape(2, seq_len)
        ids_row, marks_row = cells[0], cells[1]
        cot = cot.reshape(half, width)
        small_full = small_full.reshape(lax.axis_size(ALL), 8, 128)[:, :, :chan].transpose(1, 0, 2).reshape(8, width)
        gain_two = small_full[KW + 2 : KW + 3]

        stream, normed_one, coef, tap_table, rows, idm = tok_forward(ids_row, marks_row, table, small_full, half)

        twins = [(i, i ^ 1) for i in range(lax.axis_size("dp"))]
        normed_other = lax.ppermute(normed_one, "dp", twins)
        token_marks = marks_row[::2]
        query_marks = lax.dynamic_slice_in_dim(token_marks, core * half, half, axis=0)
        other_marks = lax.dynamic_slice_in_dim(token_marks, (1 - core) * half, half, axis=0)
        key_marks = jnp.concatenate([query_marks, other_marks])
        queries = (mm_tt(wq, normed_one).astype(jnp.bfloat16) * HEAD_DIM ** (-0.5)).astype(jnp.bfloat16)
        normed_keys = jnp.concatenate([normed_one, normed_other], axis=0)
        keys = mm_tt(wk, normed_keys).astype(jnp.bfloat16)
        vals = mm_tt(wv, normed_keys).astype(jnp.bfloat16)
        attn_out, lse = attend_forward(queries, keys, vals, key_marks, query_marks)

        resid_one = stream + mm_tn(attn_out, wo)
        normed_two = rms_scale(resid_one, gain_two).astype(jnp.bfloat16)
    grad_gate, grad_up, grad_down, layer_rows, resid_grad, gain_two_grad = feed_forward(
        normed_two, cot, resid_one, small_full, wg, wu, wd
    )
    layer_rows = layer_rows.reshape(seqs, part_bytes // 2, width)
    shapes = [(w.shape[0], w.shape[1], jnp.bfloat16) for w in shards] + [(8, 128, jnp.float32)]
    out = backward_all(
        BackInputs(
            gate=grad_gate,
            up=grad_up,
            down=grad_down,
            coef=coef,
            resid=resid_grad,
            qt=queries,
            kt=keys,
            vt=vals,
            out=attn_out,
            lse=lse,
            key_marks=key_marks[None],
            normed=normed_one,
            stream=stream,
            attend=attend,
            small=small_full,
            gain_two=gain_two_grad,
            table=table,
            tap=tap_table,
            rows=rows,
            idm=idm,
            layer=layer_rows,
        ),
        shapes,
    )
    done = results([out[9]] + list(out[:8]), out[8], chan)
    return (
        done[0],
        done[8],
        done[9].T,
        done[10][0],
        done[11][0],
        done[1],
        done[2],
        done[3],
        done[4],
        done[12][0],
        done[5],
        done[6],
        done[7],
    )


def solution(mesh):
    flat = P(ALL)
    rows = P(ALL, None)
    in_specs = (
        P("dp", "seq"),
        P("dp", "seq"),
        rows,
        rows,
        flat,
        flat,
        rows,
        rows,
        rows,
        rows,
        flat,
        rows,
        rows,
        rows,
        P("dp", "seq", None),
    )
    out_specs = (
        P("dp", "seq", None),
        rows,
        rows,
        flat,
        flat,
        rows,
        rows,
        rows,
        rows,
        flat,
        rows,
        rows,
        rows,
    )
    return jax.shard_map(
        per_device, mesh=mesh, in_specs=in_specs, out_specs=out_specs, check_vma=False
    )
```

```python
import functools
from typing import NamedTuple

import jax
import jax.numpy as jnp
from jax import lax
from jax.experimental import pallas as pl
from jax.experimental.pallas import tpu as pltpu
from jax.sharding import PartitionSpec as P

HEADS = 12
HEAD_DIM = 64
VOCAB = 256
MAXBLOCK = 4
KW = 5
DOCS = 8
ALL = ("dp", "seq")
VMEM_BYTES = 56 * 1024 * 1024


def mm(left, right):
    return jnp.dot(left, right, preferred_element_type=jnp.float32)


def mm_nt(left, right):
    return lax.dot_general(left, right, (((1,), (1,)), ((), ())), preferred_element_type=jnp.float32)


def mm_tn(left, right):
    return lax.dot_general(left, right, (((0,), (0,)), ((), ())), preferred_element_type=jnp.float32)


def mm_tt(left, right):
    return lax.dot_general(left, right, (((0,), (1,)), ((), ())), preferred_element_type=jnp.float32)


def rms_scale(values, gain):
    return values * lax.rsqrt(jnp.mean(values * values, axis=-1, keepdims=True) + 1e-06) * gain


def gelu_tanh(values):
    return jax.nn.gelu(values, approximate=True)


MESH = pl.DeviceIdType.MESH


def position():
    dp = lax.axis_index("dp")
    place = lax.axis_index("seq")
    lines = lax.axis_size("dp") // 4
    group = dp // 2
    return group // 2, group % 2, dp % 2, place, lines, lax.axis_size("seq")


def dp_of(y, x, core):
    return (y * 2 + x) * 2 + core


def meet(targets):
    barrier = pltpu.get_barrier_semaphore()
    for dp, place in targets:
        pl.semaphore_signal(barrier, inc=1, device_id=(dp, place), device_id_type=MESH)
    pl.semaphore_wait(barrier, len(targets))


def remote(src, dst, send_sem, recv_sem, dp, place):
    return pltpu.make_async_remote_copy(
        src_ref=src,
        dst_ref=dst,
        send_sem=send_sem,
        recv_sem=recv_sem,
        device_id=(dp, place),
        device_id_type=MESH,
    )


GATHER_ITEMS = (
    (7, 0, 0, 0),
    (8, 0, 0, 0),
    (0, 0, 0, 0),
    (2, 0, 0, 1),
    (1, 0, 0, 0),
    (3, 0, 0, 1),
    (4, 0, 0, 0),
    (5, 0, 0, 1),
    (6, 0, 1, 0),
    (6, 1, 1, 1),
)
GATHER_PHASES = ((0, 1), (2, 3, 4, 5), (6, 7), (8, 9))


def gather_kernel(arrays, *refs):
    ins = refs[:arrays]
    cells_in, cot_in = refs[arrays], refs[arrays + 1]
    outs = refs[arrays + 2 : 2 * arrays + 2]
    cells_out, cot_out = refs[2 * arrays + 2], refs[2 * arrays + 3]
    recv, recv_sib, send_z, send_x, send_y, send_sib, own_sem, cell_recv, cell_send, cot_recv, cot_send = refs[
        2 * arrays + 4 :
    ]
    y, x, core, place, lines, count = position()
    seqs = cells_in.shape[0]
    groups = lines * 2
    group = y * 2 + x
    dp = dp_of(y, x, core)
    twin = dp_of(y, x, 1 - core)
    side = dp_of(y, 1 - x, core)
    ahead = [(y + k) % lines for k in range(1, lines)]

    targets = [(twin, place), (side, place)]
    for k in range(1, count):
        targets += [(dp, (place + k) % count), (twin, (place + k) % count)]
    for other_y in ahead:
        targets.append((dp_of(other_y, x, core), place))
    meet(targets)

    def cell_copies(fn_remote, fn_local):
        for r in range(seqs):
            chip = seqs * core + r
            for c in range(2):
                home = (chip == place) & (core == c)

                @pl.when(home)
                def _():
                    fn_local(r, c)

                @pl.when(jnp.logical_not(home))
                def _():
                    fn_remote(r, c, chip)

    def cell_remote(r, c, chip):
        return remote(
            cells_in.at[r],
            cells_out.at[place],
            cell_send.at[r, c],
            cell_recv.at[place],
            dp_of(y, x, c),
            chip,
        )

    cell_copies(
        lambda r, c, chip: cell_remote(r, c, chip).start(),
        lambda r, c: pltpu.make_async_copy(
            cells_in.at[r], cells_out.at[place], cell_recv.at[place]
        ).start(),
    )

    def view(item):
        array, first, columns, _ = GATHER_ITEMS[item]
        in_ref, out_ref = ins[array], outs[array]
        if columns:
            cols = in_ref.shape[1] // 2
            lanes = pl.ds(first * cols, cols)
        else:
            lanes = pl.ds(0, in_ref.shape[1])
        return in_ref.at[:, lanes], out_ref, lanes

    def block(item, g, z):
        _, out_ref, lanes = view(item)
        return out_ref.at[(g * 2 + core) * count + z, :, lanes]

    def group_block(item, g, c):
        _, out_ref, lanes = view(item)
        return out_ref.at[pl.ds((g * 2 + c) * count, count), :, lanes]

    def many(item, blocks):
        _, out_ref, lanes = view(item)
        return out_ref.at[pl.ds(0, blocks), :, lanes]

    def arrived(item, g, z):
        dst = block(item, g, z)
        remote(dst, dst, send_x.at[item], recv.at[item, g * count + z], twin, place).wait_recv()

    def to_side(item, src, g, z):
        remote(src, block(item, g, z), send_x.at[item], recv.at[item, g * count + z], side, place).start()

    def to_lines(item, src, g, z):
        for other_y in ahead:
            remote(
                src,
                block(item, g, z),
                send_y.at[item],
                recv.at[item, g * count + z],
                dp_of(other_y, x, core),
                place,
            ).start()

    def to_z(item, src, z, step):
        return remote(
            src,
            block(item, group, z),
            send_z.at[item, z, step],
            recv.at[item, group * count + z],
            dp,
            place + 1 - 2 * step,
        )

    def to_twin(item, g):
        src = group_block(item, g, core)
        remote(src, src, send_sib.at[item], recv_sib.at[item, g], twin, place).start()

    def own_copy(item):
        return pltpu.make_async_copy(view(item)[0], block(item, group, place), own_sem.at[item])

    def first_own(items):
        for item in items:
            src = view(item)[0]

            @pl.when(place < count - 1)
            def _():
                to_z(item, src, place, 0).start()

            @pl.when(place > 0)
            def _():
                to_z(item, src, place, 1).start()

            own_copy(item).start()

    def first_sides(items):
        for item in items:
            src = view(item)[0]
            to_side(item, src, group, place)
            to_lines(item, src, group, place)

    def first_level(items):
        def step(s, carry):
            low = place - s
            high = place + s
            for item in items:

                @pl.when(low >= 0)
                def _():
                    arrived(item, group, low)
                    src = block(item, group, low)

                    @pl.when(place < count - 1)
                    def _():
                        to_z(item, src, low, 0).start()

                    to_side(item, src, group, low)
                    to_lines(item, src, group, low)

                @pl.when(high < count)
                def _():
                    arrived(item, group, high)
                    src = block(item, group, high)

                    @pl.when(place > 0)
                    def _():
                        to_z(item, src, high, 1).start()

                    to_side(item, src, group, high)
                    to_lines(item, src, group, high)

            return carry

        lax.fori_loop(1, count, step, 0)
        for item in items:
            own_copy(item).wait()
            to_twin(item, group)

    def second_level(items):
        def step(s, carry):
            z = (place + s) % count
            for item in items:
                if GATHER_ITEMS[item][3] == 0:
                    g = y * 2 + (1 - x)
                    arrived(item, g, z)
                    to_lines(item, block(item, g, z), g, z)
                else:
                    for other_y in ahead:
                        g = other_y * 2 + x
                        arrived(item, g, z)
                        to_side(item, block(item, g, z), g, z)
            return carry

        lax.fori_loop(0, count, step, 0)
        for item in items:
            if GATHER_ITEMS[item][3] == 0:
                to_twin(item, y * 2 + (1 - x))
            else:
                for other_y in ahead:
                    to_twin(item, other_y * 2 + x)

    def third_level(items):
        def rest(item):
            if GATHER_ITEMS[item][3] == 0:
                return [other_y * 2 + other_x for other_y in ahead for other_x in (x, 1 - x)]
            return [other_y * 2 + (1 - x) for other_y in [y] + ahead]

        def step(s, carry):
            z = (place + s) % count
            for item in items:
                for g in rest(item):
                    arrived(item, g, z)
            return carry

        lax.fori_loop(0, count, step, 0)
        for item in items:
            for g in rest(item):
                to_twin(item, g)

    def cot_copies(fn_remote, fn_local):
        for r in range(seqs):
            chip = seqs * core + r
            home = (chip == place) & (core == place // seqs)

            @pl.when(home)
            def _():
                fn_local(r)

            @pl.when(jnp.logical_not(home))
            def _():
                fn_remote(r, chip)

    def cot_remote(r, chip):
        return remote(
            cot_in.at[r],
            cot_out.at[place % seqs],
            cot_send.at[r],
            cot_recv.at[place % seqs],
            dp_of(y, x, place // seqs),
            chip,
        )

    phases = GATHER_PHASES
    for items in phases:
        first_own(items)
    first_sides(phases[0])
    first_level(phases[0])
    for k in range(1, len(phases)):
        first_sides(phases[k])
        first_level(phases[k])
        second_level(phases[k - 1])
        if k == 1:
            cot_copies(
                lambda r, chip: cot_remote(r, chip).start(),
                lambda r: pltpu.make_async_copy(
                    cot_in.at[r], cot_out.at[place % seqs], cot_recv.at[place % seqs]
                ).start(),
            )
        if k > 1:
            third_level(phases[k - 2])
    second_level(phases[-1])
    third_level(phases[-2])
    third_level(phases[-1])

    for item in range(len(GATHER_ITEMS)):
        for g in range(groups):
            dst = group_block(item, g, 1 - core)
            remote(dst, dst, send_sib.at[item], recv_sib.at[item, g], twin, place).wait_recv()
        tree = GATHER_ITEMS[item][3]

        def sent(blocks, sem):
            src = many(item, blocks)
            remote(src, src, sem, recv.at[item, 0], twin, place).wait_send()

        sent(count * (1 if tree == 0 else lines), send_x.at[item])
        sent(count * (lines - 1) * (2 if tree == 0 else 1), send_y.at[item])
        sent(count * groups, send_sib.at[item])

        def drain(z, carry):
            @pl.when((z <= place) & (place < count - 1))
            def _():
                to_z(item, block(item, group, z), z, 0).wait_send()

            @pl.when((z >= place) & (place > 0))
            def _():
                to_z(item, block(item, group, z), z, 1).wait_send()

            return carry

        lax.fori_loop(0, count, drain, 0)
    for q in range(count):
        dst = cells_out.at[q]
        remote(dst, dst, cell_send.at[0, 0], cell_recv.at[q], twin, place).wait_recv()
    for q in range(seqs):
        dst = cot_out.at[q]
        remote(dst, dst, cot_send.at[0], cot_recv.at[q], twin, place).wait_recv()
    cell_copies(lambda r, c, chip: cell_remote(r, c, chip).wait_send(), lambda r, c: None)
    cot_copies(lambda r, chip: cot_remote(r, chip).wait_send(), lambda r: None)


def gather_all(shards, cells, cot):
    count = lax.axis_size("seq")
    group_count = lax.axis_size(ALL)
    groups = group_count // (2 * count)
    items = len(GATHER_ITEMS)
    seqs = cells.shape[0]
    vmem = pl.BlockSpec(memory_space=pltpu.VMEM)
    hbm = pl.BlockSpec(memory_space=pltpu.HBM)
    shapes = [jax.ShapeDtypeStruct((group_count,) + s.shape, s.dtype) for s in shards]
    shapes.append(jax.ShapeDtypeStruct((count,) + cells.shape[1:], cells.dtype))
    shapes.append(jax.ShapeDtypeStruct(cot.shape, cot.dtype))
    dma = pltpu.SemaphoreType.DMA
    out = pl.pallas_call(
        functools.partial(gather_kernel, len(shards)),
        name="gather_all",
        out_shape=shapes,
        in_specs=[vmem] * (len(shards) + 2),
        out_specs=[hbm] * len(shapes),
        scratch_shapes=[
            dma((items, groups * count)),
            dma((items, groups)),
            dma((items, count, 2)),
            dma((items,)),
            dma((items,)),
            dma((items,)),
            dma((items,)),
            dma((count,)),
            dma((seqs, 2)),
            dma((seqs,)),
            dma((seqs,)),
        ],
        compiler_params=pltpu.CompilerParams(collective_id=0, has_side_effects=True),
    )(*shards, cells, cot)
    full = [o.reshape(-1, o.shape[2]) for o in out[: len(shards)]]
    return full + list(out[len(shards) :])


LEFT = 128
BAND = 256


def split_two(values):
    high = values.astype(jnp.bfloat16)
    return high, (values - high.astype(jnp.float32)).astype(jnp.bfloat16)


def lane_shift(row, by):
    by = by % row.shape[1]
    return row if by == 0 else pltpu.roll(row, row.shape[1] - by, 1)


def pool_rows(marks, core, half_bytes):
    lanes = lax.broadcasted_iota(jnp.int32, marks[0].shape, 1)
    inside, inverse = {}, {}
    for e in range(2):
        place = core * half_bytes + 2 * (lanes - LEFT) + e + 768
        third = lax.shift_right_logical(place * 21846, 16)
        remains = {2: place & 1, 3: place - 3 * third, 4: place & 3}
        shifted = {}
        for s in range(1 - MAXBLOCK, MAXBLOCK):
            f = (e + s) % 2
            shifted[s] = lane_shift(marks[f], (e + s - f) // 2) == marks[e]
        for b in range(2, MAXBLOCK + 1):
            number = jnp.ones(marks[0].shape, jnp.float32)
            for s in range(1 - b, b):
                if s == 0:
                    continue
                at = remains[b] + s
                on = (shifted[s] & (at >= 0) & (at < b)).astype(jnp.float32)
                inside[b, e, s] = on
                number = number + on
            inverse[b, e] = 1.0 / number
    return inside, inverse


def band_coefs(per_byte, inside, inverse):
    coefs = {}
    for o in range(1 - MAXBLOCK, MAXBLOCK + 1):
        total = None
        for e in range(2):
            s = o - e
            if not 1 - MAXBLOCK <= s < MAXBLOCK:
                continue
            for b in range(1, MAXBLOCK + 1):
                if b == 1:
                    if s != 0:
                        continue
                    term = per_byte[b, e]
                elif s == 0:
                    term = per_byte[b, e] * inverse[b, e]
                elif (b, e, s) in inside:
                    term = per_byte[b, e] * inverse[b, e] * inside[b, e, s]
                else:
                    continue
                total = term if total is None else total + term
        coefs[o] = total
    return coefs


def band_matrix(coefs, block):
    shape = (3 * BAND, BAND)
    delta = lax.broadcasted_iota(jnp.int32, shape, 0) - LEFT - 2 * lax.broadcasted_iota(jnp.int32, shape, 1)
    out = jnp.zeros(shape, jnp.float32)
    for o, row in coefs.items():
        part = row[0:1, LEFT + BAND * block : LEFT + BAND * (block + 1)]
        out = jnp.where(delta == o, part, out)
    return out


def tap_rows(tap):
    return pl.ds(pl.multiple_of(tap * VOCAB, VOCAB), VOCAB)


def fill_one_hot(one_hot, idm_ref):
    vocab = lax.broadcasted_iota(jnp.int32, (VOCAB, one_hot.shape[1]), 0)

    def step(tap, carry):
        hit = vocab == idm_ref[pl.ds(tap, 1)]
        one_hot[tap_rows(tap)] = hit.astype(jnp.float32).astype(jnp.bfloat16)
        return carry

    lax.fori_loop(0, KW, step, 0)


def tok_forward_kernel(ids_ref, marks_ref, table_ref, small_ref, stream_ref, normed_ref, coef_ref, tap_ref, rows_ref, idm_ref, one_hot):
    core = lax.axis_index("dp") % 2
    tokens = stream_ref.shape[0]
    half_bytes = 2 * tokens
    span = one_hot.shape[1]
    wide = span + 2 * LEFT
    first = pl.ds(pl.multiple_of(core * half_bytes, 128), wide)
    ids = ids_ref[:, first]
    marks = marks_ref[:, first]
    for tap in range(KW):
        by = tap - KW // 2
        same = (lane_shift(marks, by) == marks) & (marks > 0)
        idm_ref[tap : tap + 1] = jnp.where(same, lane_shift(ids, by), -1)[0:1, LEFT : LEFT + span]
    fill_one_hot(one_hot, idm_ref)

    score = jnp.broadcast_to(small_ref[KW : KW + 1], (8, small_ref.shape[1])).astype(jnp.bfloat16)
    scored = []
    for tap in range(KW):
        product = table_ref[...].astype(jnp.float32) * small_ref[tap : tap + 1]
        high, low = split_two(product)
        tap_ref[tap * VOCAB : (tap + 1) * VOCAB] = high
        scored.append(mm_nt(score, high) + mm_nt(score, low))
    high, low = split_two(jnp.concatenate(scored, axis=1))
    u_row = mm(high, one_hot[...]) + mm(low, one_hot[...])

    high = u_row.astype(jnp.bfloat16).astype(jnp.float32)
    marks_here = marks[:, LEFT : LEFT + span].astype(jnp.float32)
    packed = jnp.concatenate([marks_here, high, u_row - high, jnp.zeros_like(high)], axis=0).astype(jnp.bfloat16)
    shape = (span, wide // 2)
    twice = 2 * lax.broadcasted_iota(jnp.int32, shape, 1) - lax.broadcasted_iota(jnp.int32, shape, 0) - LEFT
    marks_of, u_of = [], []
    for e in range(2):
        pick = (twice == -e).astype(jnp.float32).astype(jnp.bfloat16)
        apart = mm(packed, pick)
        marks_of.append(apart[0:8])
        u_of.append(apart[8:16] + apart[16:24])

    inside, inverse = pool_rows(marks_of, core, half_bytes)
    prob = {}
    for e in range(2):
        shifted = {}
        for s in range(1 - MAXBLOCK, MAXBLOCK):
            f = (e + s) % 2
            shifted[s] = lane_shift(u_of[f], (e + s - f) // 2)
        scores = [u_of[e]]
        for b in range(2, MAXBLOCK + 1):
            total = u_of[e]
            for s in range(1 - b, b):
                if s != 0:
                    total = total + inside[b, e, s] * shifted[s]
            scores.append(total * inverse[b, e])
        top = scores[0]
        for value in scores[1:]:
            top = jnp.maximum(top, value)
        expo = [jnp.exp(value - top) for value in scores]
        whole = expo[0] + expo[1] + expo[2] + expo[3]
        for b in range(1, MAXBLOCK + 1):
            prob[b, e] = expo[b - 1] / whole
            rows_ref[2 * b + e : 2 * b + e + 1] = prob[b, e][0:1]
        rows_ref[e : e + 1] = marks_of[e][0:1]
    coefs = band_coefs({key: 0.5 * value for key, value in prob.items()}, inside, inverse)
    gain = small_ref[KW + 1 : KW + 2]
    for i in range(tokens // BAND):
        matrix = band_matrix(coefs, i).astype(jnp.bfloat16)
        lanes = slice(i * BAND, (i + 1) * BAND)
        part = mm(one_hot[:, 2 * i * BAND : (2 * i + 3) * BAND], matrix).astype(jnp.bfloat16)
        coef_ref[:, lanes] = part
        stream = mm_tn(part, tap_ref[...])
        stream_ref[lanes] = stream
        scale = lax.rsqrt(jnp.mean(stream * stream, axis=-1, keepdims=True) + 1e-06)
        normed_ref[lanes] = (stream * scale * gain).astype(jnp.bfloat16)


def tok_forward(ids_row, marks_row, table, small, tokens):
    width = table.shape[1]
    span = 2 * tokens + 2 * LEFT
    wide = span + 2 * LEFT

    def padded(row, fill):
        row = jnp.pad(row, (2 * LEFT, 2 * LEFT), constant_values=fill)
        return jnp.broadcast_to(row[None], (8, row.shape[0]))

    return pl.pallas_call(
        tok_forward_kernel,
        name="tok_forward",
        out_shape=[
            jax.ShapeDtypeStruct((tokens, width), jnp.float32),
            jax.ShapeDtypeStruct((tokens, width), jnp.bfloat16),
            jax.ShapeDtypeStruct((KW * VOCAB, tokens), jnp.bfloat16),
            jax.ShapeDtypeStruct((KW * VOCAB, width), jnp.bfloat16),
            jax.ShapeDtypeStruct((16, wide // 2), jnp.float32),
            jax.ShapeDtypeStruct((8, span), jnp.int32),
        ],
        scratch_shapes=[pltpu.VMEM((KW * VOCAB, span), jnp.bfloat16)],
        compiler_params=pltpu.CompilerParams(vmem_limit_bytes=VMEM_BYTES),
    )(padded(ids_row, -1), padded(marks_row, 0), table, small)


def tok_backward_body(grad16, coef_ref, ref, own, tick, take):
    tap_ref, rows_ref, idm_ref, table_ref, small_ref = ref.tap, ref.rows, ref.idm, ref.table, ref.small
    one_hot = own.one_hot
    core = lax.axis_index("dp") % 2
    tokens = grad16.shape[0]
    fill_one_hot(one_hot, idm_ref)
    tick()

    def whole_row(k):
        return jnp.broadcast_to(rows_ref[k : k + 1], (8, rows_ref.shape[1]))

    marks_of = [whole_row(0), whole_row(1)]
    inside, inverse = pool_rows(marks_of, core, 2 * tokens)
    shape = (3 * BAND, BAND)
    delta = lax.broadcasted_iota(jnp.int32, shape, 0) - LEFT - 2 * lax.broadcasted_iota(jnp.int32, shape, 1)
    through = mm_nt(tap_ref[...], grad16).astype(jnp.bfloat16)
    tick()
    diag = {o: [] for o in range(1 - MAXBLOCK, MAXBLOCK + 1)}
    edge = jnp.zeros((8, LEFT), jnp.float32)
    for i in range(tokens // BAND):
        near = mm_tn(one_hot[:, 2 * i * BAND : (2 * i + 3) * BAND], through[:, i * BAND : (i + 1) * BAND])
        for o in diag:
            total = jnp.sum(jnp.where(delta == o, near, 0.0), axis=0, keepdims=True)
            diag[o].append(jnp.broadcast_to(total, (8, BAND)))
        tick()
    diag = {o: jnp.concatenate([edge] + parts + [edge], axis=1) for o, parts in diag.items()}
    size_grad = {}
    for e in range(2):
        grads = [0.5 * diag[e]]
        for b in range(2, MAXBLOCK + 1):
            total = diag[e]
            for s in range(1 - b, b):
                if s != 0:
                    total = total + inside[b, e, s] * diag[s + e]
            grads.append(0.5 * total * inverse[b, e])
        probs = [whole_row(2 * b + e) for b in range(1, MAXBLOCK + 1)]
        mean = probs[0] * grads[0]
        for p, g in zip(probs[1:], grads[1:]):
            mean = mean + p * g
        for b in range(1, MAXBLOCK + 1):
            size_grad[b, e] = probs[b - 1] * (grads[b - 1] - mean)
    coefs = band_coefs(size_grad, inside, inverse)
    picked = None
    for i in range(tokens // BAND):
        matrix = band_matrix(coefs, i).astype(jnp.bfloat16)
        part = mm(one_hot[:, 2 * i * BAND : (2 * i + 3) * BAND], matrix)
        part = jnp.sum(part, axis=1, keepdims=True)
        picked = part if picked is None else picked + part
        tick()
    own.picked[...] = picked
    score = small_ref[KW : KW + 1]
    table_grad = own.wide.at[0:VOCAB]
    table_grad[...] = jnp.zeros(table_grad.shape, jnp.float32)
    own.rows[...] = jnp.zeros_like(own.rows)
    tap_tasks = take(KW - 1)

    def step(tap, carry):
        here = own.picked[tap_rows(tap)]
        table = table_ref[:, 0 : score.shape[1]].astype(jnp.float32)
        part = mm(coef_ref[tap_rows(tap)], grad16) + here * score
        taps = small_ref[pl.ds(tap, 1)]
        table_grad[...] += part * taps
        own.rows[pl.ds(tap, 1)] = jnp.sum(part * table, axis=0, keepdims=True)
        own.rows[KW : KW + 1] += jnp.sum(table * here, axis=0, keepdims=True) * taps
        tap_tasks(tap)
        return carry

    lax.fori_loop(0, KW, step, 0)


CHUNK = 256


def pair_rows(ref, h):
    values = ref[...]
    rows = lax.broadcasted_iota(jnp.int32, values.shape, 0)
    return jnp.where((rows // HEAD_DIM) == h, values, jnp.zeros_like(values))


def fill_bias(bias, key_marks, query_marks):
    def apart(marks):
        rows = lax.broadcasted_iota(jnp.int32, (2 * DOCS, marks.shape[1]), 0)
        return (rows == marks[...]).astype(jnp.float32).astype(jnp.bfloat16)

    queries = apart(query_marks)
    for c in range(key_marks.shape[1] // CHUNK):
        keys = slice(c * CHUNK, (c + 1) * CHUNK)
        same = mm_tn(apart(key_marks.at[:, keys]), queries)
        bias[keys] = jnp.where(same > 0.5, 0.0, -1e30).astype(bias.dtype)


def attend_forward_kernel(qt_ref, kt_ref, vt_ref, key_marks, query_marks, out_ref, lse_ref, bias, scores):
    @pl.when(pl.program_id(0) == 0)
    def _():
        fill_bias(bias, key_marks, query_marks)

    keys = kt_ref[...].T
    chunks = keys.shape[0] // CHUNK
    for h in range(2):
        query = pair_rows(qt_ref, h)
        top = None
        for c in range(chunks):
            rows = slice(c * CHUNK, (c + 1) * CHUNK)
            part = mm(keys[rows], query) + bias[rows]
            scores[h, rows] = part
            high = jnp.max(part, axis=0, keepdims=True)
            top = high if top is None else jnp.maximum(top, high)
        total = None
        out = None
        for c in range(chunks):
            rows = slice(c * CHUNK, (c + 1) * CHUNK)
            expo = jnp.exp(scores[h, rows] - top)
            part = jnp.sum(expo, axis=0, keepdims=True)
            total = part if total is None else total + part
            part = mm(vt_ref[h * HEAD_DIM : (h + 1) * HEAD_DIM, rows], expo.astype(jnp.bfloat16))
            out = part if out is None else out + part
        out_ref[h * HEAD_DIM : (h + 1) * HEAD_DIM] = (out / total).astype(jnp.bfloat16)
        lse_ref[0, h : h + 1] = top + jnp.log(total)


def attend_forward(qt, kt, vt, key_marks, query_marks):
    width, tokens = qt.shape
    keys = kt.shape[1]
    pairs = width // 128
    rows = lambda size: pl.BlockSpec((128, size), lambda i: (i, 0))
    whole = lambda shape: pl.BlockSpec(shape, lambda i: (0, 0))
    return pl.pallas_call(
        attend_forward_kernel,
        name="attend_forward",
        grid=(pairs,),
        in_specs=[rows(tokens), rows(keys), rows(keys), whole((1, keys)), whole((1, tokens))],
        out_specs=[rows(tokens), pl.BlockSpec((1, 2, tokens), lambda i: (i, 0, 0))],
        out_shape=[
            jax.ShapeDtypeStruct((width, tokens), jnp.bfloat16),
            jax.ShapeDtypeStruct((pairs, 2, tokens), jnp.float32),
        ],
        scratch_shapes=[
            pltpu.VMEM((keys, tokens), jnp.float32),
            pltpu.VMEM((2, keys, tokens), jnp.float32),
        ],
        compiler_params=pltpu.CompilerParams(vmem_limit_bytes=VMEM_BYTES),
    )(qt, kt, vt, key_marks[None], query_marks[None])


def attend_backward_pair(qt, kt, vt, got_ref, out, lse_ref, bias, dq, dk_own, dv_own, dk_away, dv_away, tasks):
    keys = kt[...].T
    vals = vt[...].T
    chunks = keys.shape[0] // CHUNK
    for h in range(2):
        own = slice(h * HEAD_DIM, (h + 1) * HEAD_DIM)
        query = pair_rows(qt, h)
        got = pair_rows(got_ref, h)
        dots = jnp.sum(
            got_ref[own].astype(jnp.float32) * out[own].astype(jnp.float32), axis=0, keepdims=True
        )
        lse = lse_ref[h : h + 1]
        query_grad = None
        for c in range(chunks):
            rows = slice(c * CHUNK, (c + 1) * CHUNK)
            soft = jnp.exp(mm(keys[rows], query) + (bias[rows].astype(jnp.float32) - lse))
            change = soft * (mm(vals[rows], got) - dots)
            soft16 = soft.astype(jnp.bfloat16)
            change16 = change.astype(jnp.bfloat16)
            first = c < chunks // 2
            to = slice((c % (chunks // 2)) * CHUNK, (c % (chunks // 2) + 1) * CHUNK)
            (dv_own if first else dv_away)[own, to] = mm_nt(got_ref[own], soft16).astype(jnp.bfloat16)
            (dk_own if first else dk_away)[own, to] = mm_nt(qt[own], change16).astype(jnp.bfloat16)
            part = mm(kt[own, rows], change16)
            query_grad = part if query_grad is None else query_grad + part
        dq[own] = (query_grad * HEAD_DIM ** (-0.5)).astype(jnp.bfloat16)
        if h == 0:
            tasks()


SCATTER_ITEMS = (
    (4, 1, 2, 0),
    (6, 1, 2, 1),
    (5, 0, 2, 0),
    (5, 1, 2, 0),
    (3, 0, 1, 1),
    (6, 0, 2, 0),
    (4, 0, 2, 1),
    (0, 0, 1, 1),
    (1, 0, 1, 0),
    (2, 0, 1, 1),
    (7, 0, 1, 1),
    (8, 0, 1, 1),
)
FIRST_ITEMS = 7
SCHEDULE = (
    (
        (0, 0), (0, 1), (0, 2),
    ),
    (
        (0, 3), (0, 4),
    ),
    (
        (0, 5), (0, 6),
    ),
    (),
    (
        (1, 0), (1, 1),
    ),
    (),
    (),
    ((1, 4),),
    ((1, 2),),
    (),
    (),
    (),
    (
        (1, 3), (1, 6),
    ),
    (),
    (
        (2, 0), (0, 7),
    ),
    ((0, 8),),
    (
        (3, 0), (2, 2), (1, 5), (0, 9),
    ),
    (
        (4, 0), (2, 1), (2, 3),
    ),
    ((3, 2),),
    (
        (5, 0), (2, 4),
    ),
    (
        (4, 2), (1, 7),
    ),
    (
        (3, 1), (2, 6),
    ),
    (
        (5, 2), (3, 3),
    ),
    (
        (2, 5), (4, 1), (3, 4),
    ),
    (),
    (),
    (
        (4, 3), (5, 1), (1, 8), (3, 6),
    ),
    ((4, 4),),
    (
        (1, 9), (5, 3), (2, 7), (3, 5), (0, 10), (5, 4),
        (0, 11), (4, 6), (2, 8), (3, 7), (4, 5), (5, 6),
        (2, 9), (1, 10), (1, 11), (4, 7), (5, 5), (3, 8),
        (2, 10), (2, 11), (5, 7), (3, 9), (4, 8), (3, 10),
        (3, 11), (4, 9), (5, 8), (4, 10), (4, 11), (5, 9),
        (5, 10), (5, 11),
    ),
)


LATE_SOURCES = (4, 5, 6)


class Scatter:
    def __init__(self, sources, outs, layer_in, layer_out, buffers, sems):
        items = len(SCATTER_ITEMS)
        self.sources, self.outs = sources, outs
        self.layer_in, self.layer_out = layer_in, layer_out
        self.sems = sems
        self.y, self.x, self.core, self.place, self.lines, self.count = position()
        y, x, core = self.y, self.x, self.core
        self.own, taken = [], 0
        for array, _, _, _ in SCATTER_ITEMS:
            if array in LATE_SOURCES:
                self.own.append(buffers[taken])
                taken += 1
            else:
                self.own.append(sources[array].at[:, :, core])
        buffers = buffers[taken:]
        self.from_twin, self.first_in, self.second_in, self.line_in = [
            buffers[k * items : (k + 1) * items] for k in range(4)
        ]
        self.dp = dp_of(y, x, core)
        self.twin = dp_of(y, x, 1 - core)
        self.side = dp_of(y, 1 - x, core)
        self.ahead = [(y + k) % self.lines for k in range(1, self.lines)]

    def meet(self):
        targets = [(self.twin, self.place), (self.side, self.place)]
        for k in range(1, self.count):
            other = (self.place + k) % self.count
            targets += [(self.dp, other), (self.twin, other)]
        for other_y in self.ahead:
            targets.append((dp_of(other_y, self.x, self.core), self.place))
        meet(targets)

    def order(self, item):
        return SCATTER_ITEMS[item][3]

    def columns(self, item):
        array, part, parts, _ = SCATTER_ITEMS[item]
        cols = self.sources[array].shape[-1] // parts
        return pl.ds(part * cols, cols)

    def to_twin(self, item):
        src = self.sources[SCATTER_ITEMS[item][0]].at[:, :, 1 - self.core, :, :, self.columns(item)]
        sems = self.sems
        return remote(
            src, self.from_twin[item], sems.twin_send.at[item], sems.twin_recv.at[item], self.twin, self.place
        )

    def own_in(self, item):
        src = self.sources[SCATTER_ITEMS[item][0]].at[:, :, self.core, :, :, self.columns(item)]
        return pltpu.make_async_copy(src, self.own[item], self.sems.own.at[item])

    def x_copy(self, item):
        own = self.own[item]
        if self.order(item) == 0:
            src, dst = own.at[self.y, 1 - self.x], self.second_in[item].at[0]
        else:
            src, dst = own.at[:, 1 - self.x], self.first_in[item]
        return remote(
            src, dst, self.sems.x_send.at[item], self.sems.x_recv.at[item], self.side, self.place
        )

    def y_copy(self, item, k):
        other_y = self.ahead[k]
        own = self.own[item]
        if self.order(item) == 0:
            src, dst = own.at[other_y], self.first_in[item].at[k]
        else:
            src, dst = own.at[other_y, self.x], self.second_in[item].at[k]
        return remote(
            src,
            dst,
            self.sems.y_send.at[item, k],
            self.sems.y_recv.at[item, k],
            dp_of(other_y, self.x, self.core),
            self.place,
        )

    def stage_begin(self, item):
        self.to_twin(item).start()
        if SCATTER_ITEMS[item][0] in LATE_SOURCES:
            self.own_in(item).start()

    def stage_core(self, item):
        if SCATTER_ITEMS[item][0] in LATE_SOURCES:
            self.own_in(item).wait()
        self.to_twin(item).wait_recv()
        own, came = self.own[item], self.from_twin[item]

        def step(i, carry):
            a, b, z = i // (2 * self.count), i // self.count % 2, i % self.count
            own[a, b, z] = plus(own[a, b, z], came[a, b, z])
            return carry

        lax.fori_loop(0, 2 * self.lines * self.count, step, 0)
        if self.order(item) == 0:
            for k in range(self.lines - 1):
                self.y_copy(item, k).start()
        else:
            self.x_copy(item).start()

    def stage_first(self, item):
        own, came = self.own[item], self.first_in[item]
        y, x, lines = self.y, self.x, self.lines
        if self.order(item) == 0:
            for k in range(lines - 1):
                self.y_copy(item, k).wait_recv()

            def step(i, carry):
                b, z = i // self.count, i % self.count
                total = own[y, b, z]
                for k in range(lines - 1):
                    total = plus(total, came[k, b, z])
                own[y, b, z] = total
                return carry

            lax.fori_loop(0, 2 * self.count, step, 0)
            self.x_copy(item).start()
        else:
            self.x_copy(item).wait_recv()

            def step(i, carry):
                a, z = i // self.count, i % self.count
                own[a, x, z] = plus(own[a, x, z], came[a, z])
                return carry

            lax.fori_loop(0, lines * self.count, step, 0)
            for k in range(lines - 1):
                self.y_copy(item, k).start()

    def mine(self, item, z):
        return self.own[item].at[self.y, self.x, z]

    def z_copy(self, item, z, way):
        return remote(
            self.mine(item, z),
            self.line_in[item].at[way, z],
            self.sems.z_send.at[item, z],
            self.sems.z_recv.at[item, way, z],
            self.dp,
            self.place + 1 - 2 * way,
        )

    def z_forward(self, item, way, first):
        def step(z, carry):
            @pl.when((z - self.place) * (1 - 2 * way) > 0)
            def _():
                if not first:
                    self.z_copy(item, z, way).wait_recv()
                    ref = self.mine(item, z)
                    ref[...] = plus(ref[...], self.line_in[item][way, z])
                self.z_copy(item, z, way).start()

            return carry

        lax.fori_loop(0, self.count, step, 0)

    def stage_second(self, item):
        own, came = self.own[item], self.second_in[item]
        y, x = self.y, self.x
        if self.order(item) == 0:
            self.x_copy(item).wait_recv()
        else:
            for k in range(self.lines - 1):
                self.y_copy(item, k).wait_recv()

        def step(z, carry):
            total = own[y, x, z]
            for k in range(came.shape[0]):
                total = plus(total, came[k, z])
            own[y, x, z] = total
            return carry

        lax.fori_loop(0, self.count, step, 0)

        self.each_way(lambda way, depth: pl.when(depth == 0)(lambda: self.z_forward(item, way, True)))

    def each_way(self, body):
        def step(way, carry):
            body(way, self.place + way * (self.count - 1 - 2 * self.place))
            return carry

        lax.fori_loop(0, 2, step, 0)

    def stage_hop(self, hop, item):
        self.each_way(lambda way, depth: pl.when(depth == hop)(lambda: self.z_forward(item, way, False)))

    def stage_last(self, item):
        out = self.outs[SCATTER_ITEMS[item][0]]
        columns = self.columns(item)
        place = self.place
        out[:, columns] = self.mine(item, place)[...].astype(jnp.float32)

        def add(way):
            self.z_copy(item, place, way).wait_recv()
            out[:, columns] += self.line_in[item][way, place].astype(jnp.float32)

        self.each_way(lambda way, depth: pl.when(depth > 0)(lambda: add(way)))

    def layer_copies(self, fn_remote, fn_local):
        seqs = self.layer_in.shape[0]
        for k in range(seqs):
            chip = seqs * self.core + k
            home = (chip == self.place) & (self.core == self.place // seqs)

            @pl.when(home)
            def _():
                fn_local(k)

            @pl.when(jnp.logical_not(home))
            def _():
                fn_remote(k, chip)

    def layer_remote(self, k, chip):
        seqs = self.layer_in.shape[0]
        row = self.place % seqs
        return remote(
            self.layer_in.at[k],
            self.layer_out.at[row],
            self.sems.layer_send.at[k],
            self.sems.layer_recv.at[row],
            dp_of(self.y, self.x, self.place // seqs),
            chip,
        )

    def layer_start(self):
        row = self.place % self.layer_in.shape[0]
        self.layer_copies(
            lambda k, chip: self.layer_remote(k, chip).start(),
            lambda k: pltpu.make_async_copy(
                self.layer_in.at[k], self.layer_out.at[row], self.sems.layer_recv.at[row]
            ).start(),
        )

    def stage_hop_one(self, item):
        self.stage_hop(1, item)

    def stage_hops(self, item):
        for hop in range(2, self.count - 1):
            self.stage_hop(hop, item)

    def stages(self):
        return (
            self.stage_core,
            self.stage_first,
            self.stage_second,
            self.stage_hop_one,
            self.stage_hops,
            self.stage_last,
        )

    def finish(self):
        for item in range(len(SCATTER_ITEMS)):
            self.to_twin(item).wait_send()
            self.x_copy(item).wait_send()
            for k in range(self.lines - 1):
                self.y_copy(item, k).wait_send()

            def drain(z, carry):
                @pl.when(z > self.place)
                def _():
                    self.z_copy(item, z, 0).wait_send()

                @pl.when(z < self.place)
                def _():
                    self.z_copy(item, z, 1).wait_send()

                return carry

            lax.fori_loop(0, self.count, drain, 0)
        for r in range(self.layer_in.shape[0]):
            dst = self.layer_out.at[r]
            remote(
                dst, dst, self.sems.layer_send.at[0], self.sems.layer_recv.at[r], self.twin, self.place
            ).wait_recv()
        self.layer_copies(lambda k, chip: self.layer_remote(k, chip).wait_send(), lambda k: None)


class ScatterSems(NamedTuple):
    own: object
    twin_send: object
    twin_recv: object
    x_send: object
    x_recv: object
    y_send: object
    y_recv: object
    z_send: object
    z_recv: object
    layer_send: object
    layer_recv: object


def plus(left, right):
    return left + right


def scatter_scratch(shapes, lines, count, seqs):
    items = len(SCATTER_ITEMS)
    own, first_in, second_in, line_in = [], [], [], []
    for array, _, parts, order in SCATTER_ITEMS:
        rows, cols, kind = shapes[array]
        cols = cols // parts
        own.append(pltpu.VMEM((lines, 2, count, rows, cols), kind))
        if order == 0:
            first_in.append(pltpu.VMEM((lines - 1, 2, count, rows, cols), kind))
            second_in.append(pltpu.VMEM((1, count, rows, cols), kind))
        else:
            first_in.append(pltpu.VMEM((lines, count, rows, cols), kind))
            second_in.append(pltpu.VMEM((lines - 1, count, rows, cols), kind))
        line_in.append(pltpu.VMEM((2, count, rows, cols), kind))
    dma = pltpu.SemaphoreType.DMA
    sems = [dma((FIRST_ITEMS,))] + [dma((items,))] * 4
    sems += [dma((items, lines - 1))] * 2 + [dma((items, count)), dma((items, 2, count))]
    sems += [dma((seqs,))] * 2
    kept = [own[k] for k, entry in enumerate(SCATTER_ITEMS) if entry[0] in LATE_SOURCES]
    return kept + own + first_in + second_in + line_in, sems


class BackInputs(NamedTuple):
    gate: object
    up: object
    down: object
    coef: object
    resid: object
    layer: object
    qt: object
    kt: object
    vt: object
    out: object
    normed: object
    stream: object
    tap: object
    attend: object
    lse: object
    key_marks: object
    small: object
    gain_two: object
    table: object
    rows: object
    idm: object


class BackWork(NamedTuple):
    grads: object
    away: object
    came: object
    wide: object
    one_hot: object
    src_qkv: object
    src_table: object
    src_small: object
    swap_send: object
    swap_recv: object
    coef_sem: object
    resid_sem: object
    load_sem: object
    wqkv: object
    picked: object
    rows: object
    src_output: object
    got: object


LATE_LOADS = 7


def backward_kernel(*refs):
    ref = BackInputs(*refs[: len(BackInputs._fields)])
    late_refs = refs[-LATE_LOADS:]
    refs = refs[:-LATE_LOADS]
    late = slice(6, 6 + LATE_LOADS)
    waiting = ref[late]
    ref = ref._replace(**dict(zip(ref._fields[late], late_refs)))
    rest = refs[len(BackInputs._fields) :]
    outs, layer_out = rest[:9], rest[9]
    rest = rest[10:]
    held = 4 * len(SCATTER_ITEMS) + sum(entry[0] in LATE_SOURCES for entry in SCATTER_ITEMS)
    buffers, rest = rest[:held], rest[held:]
    sems = ScatterSems(*rest[: len(ScatterSems._fields)])
    own = BackWork(*rest[len(ScatterSems._fields) :])
    sources = (
        own.src_qkv.at[0],
        own.src_qkv.at[1],
        own.src_qkv.at[2],
        own.src_output,
        ref.gate,
        ref.up,
        ref.down,
        own.src_table,
        own.src_small,
    )
    scatter = Scatter(sources, outs, ref.layer, layer_out, buffers, sems)
    stages = scatter.stages()
    width, tokens = ref.qt.shape
    pairs = width // 128
    bias = own.one_hot.at[0 : ref.kt.shape[1], 0:tokens]
    scatter.meet()
    for item in range(FIRST_ITEMS):
        if SCATTER_ITEMS[item][0] in LATE_SOURCES:
            scatter.stage_begin(item)

    queue = [[functools.partial(stages[stage], item) for stage, item in group] for group in SCHEDULE]

    def tick():
        for task in queue.pop(0):
            task()

    loads = []
    for k in range(LATE_LOADS):
        loads.append(pltpu.make_async_copy(waiting[k], late_refs[k], own.load_sem.at[k]))
        loads[k].start()

    def weight_load(k, at):
        weight = ref.attend.at[:, k * width : (k + 1) * width]
        return pltpu.make_async_copy(weight, own.wqkv.at[at * width : (at + 1) * width], own.load_sem.at[LATE_LOADS + at])

    def resid_load():
        return pltpu.make_async_copy(ref.resid, own.wide.at[0:tokens], own.resid_sem)

    weight_load(3, 0).start()
    resid_load().start()
    scatter.layer_start()
    tick()
    wide = own.wide

    def hand_out(source):
        lines, _, _, count, size, _ = source.shape
        total = lines * 4 * count

        if size % 8:
            for o in range(total):
                where = (o // (4 * count), o // (2 * count) % 2, o // count % 2, o % count)
                source[where] = wide[size * o : size * (o + 1)].astype(source.dtype)
        else:

            def step(o, carry):
                where = (o // (4 * count), o // (2 * count) % 2, o // count % 2, o % count)
                source[where] = wide[pl.ds(pl.multiple_of(size * o, 8), size)].astype(source.dtype)
                return carry

            lax.fori_loop(0, total, step, 0)

    fill_bias(bias, ref.key_marks, ref.key_marks.at[:, 0:tokens])
    for load in loads[:4]:
        load.wait()
    weight_load(3, 0).wait()
    resid_load().wait()
    proj = wide[0:tokens].astype(jnp.bfloat16)
    own.got[...] = mm_nt(own.wqkv[0:width], proj).astype(jnp.bfloat16)
    wide[...] = mm(ref.out[...], proj)
    hand_out(own.src_output)
    for item in range(FIRST_ITEMS):
        if SCATTER_ITEMS[item][0] == 3:
            scatter.stage_begin(item)
    for k in range(3):
        weight_load(k, k).start()

    def swap(i, which):
        rows = pl.ds(pl.multiple_of(which * width + 128 * i, 128), 128)
        return remote(
            own.away.at[rows],
            own.came.at[rows],
            own.swap_send.at[which, i],
            own.swap_recv.at[which, i],
            scatter.twin,
            scatter.place,
        )

    ticks = [queue.pop(0) for _ in range(2 * pairs)]

    def pair_tasks(groups, i):
        for k, group in enumerate(groups):
            if group:

                @pl.when(i == k)
                def _():
                    for task in group:
                        task()

    def pair_step(i, carry):
        at = pl.ds(pl.multiple_of(128 * i, 128), 128)
        attend_backward_pair(
            ref.qt.at[at],
            ref.kt.at[at],
            ref.vt.at[at],
            own.got.at[at],
            ref.out.at[at],
            ref.lse.at[i],
            bias,
            own.grads.at[at],
            own.grads.at[pl.ds(pl.multiple_of(width + 128 * i, 128), 128)],
            own.grads.at[pl.ds(pl.multiple_of(2 * width + 128 * i, 128), 128)],
            own.away.at[at],
            own.away.at[pl.ds(pl.multiple_of(width + 128 * i, 128), 128)],
            lambda: pair_tasks(ticks[0::2], i),
        )
        swap(i, 0).start()
        swap(i, 1).start()
        pair_tasks(ticks[1::2], i)
        return carry

    lax.fori_loop(0, pairs, pair_step, 0)

    for load in loads[4:]:
        load.wait()
    for k in range(3):
        weight_load(k, k).wait()
    normed_t = own.one_hot.at[0:width, 0:tokens]
    normed_t[...] = ref.normed[...].T
    coef = own.came.at[0 : KW * VOCAB]

    def coef_copy():
        return pltpu.make_async_copy(ref.coef, coef, own.coef_sem)

    def take(count):
        groups = [queue.pop(0) for _ in range(count)]

        def run(i):
            for k, group in enumerate(groups):
                if group:

                    @pl.when(i == k)
                    def _():
                        for task in group:
                            task()

        return run

    def third(i):
        return pl.ds(pl.multiple_of(i * width, width), width)

    def add_halves():
        def add_half(j, carry):
            which, i = j // pairs, j % pairs
            swap(i, which).wait_recv()
            rows = pl.ds(pl.multiple_of(which * width + 128 * i, 128), 128)
            at = pl.ds(pl.multiple_of((which + 1) * width + 128 * i, 128), 128)
            own.grads[at] = plus(own.grads[at], own.came[rows])
            return carry

        lax.fori_loop(0, 2 * pairs, add_half, 0)
        coef_copy().start()

    weight_tasks = take(3)

    def weight_step(i, carry):
        pl.when(i == 1)(add_halves)
        wide[...] = mm_nt(normed_t[...], own.grads[third(i)])
        hand_out(own.src_qkv.at[i])
        for k in range(3):
            pl.when(i == k)(functools.partial(scatter.stage_begin, FIRST_ITEMS + k))
        weight_tasks(i)
        return carry

    lax.fori_loop(0, 3, weight_step, 0)

    norm_tasks = take(1)
    wide[:, 0:tokens] = jnp.zeros((width, tokens), jnp.float32)

    def norm_step(i, carry):
        wide[:, 0:tokens] += mm(own.wqkv[third(i)], own.grads[third(i)])
        norm_tasks(i - 1)
        return carry

    lax.fori_loop(0, 3, norm_step, 0)
    normed_grad = wide[:, 0:tokens].T
    resid_load().start()
    stream = ref.stream[...]
    gain = ref.small[KW + 1 : KW + 2]
    scale = lax.rsqrt(jnp.mean(stream * stream, axis=-1, keepdims=True) + 1e-06)
    gain_grad = jnp.sum(normed_grad * stream * scale, axis=0, keepdims=True)
    scaled = normed_grad * gain
    inner = jnp.mean(scaled * stream, axis=-1, keepdims=True)
    resid_load().wait()
    grad16 = (wide[0:tokens] + scale * scaled - stream * (scale * scale * scale * inner)).astype(jnp.bfloat16)
    tick()
    coef_copy().wait()
    tok_backward_body(grad16, coef, ref, own, tick, take)
    hand_out(own.src_table)
    scatter.stage_begin(FIRST_ITEMS + 3)
    rows = jnp.concatenate([own.rows[0 : KW + 1], gain_grad, ref.gain_two[...]], axis=0)
    source = own.src_small
    lines, _, _, count, _, _ = source.shape
    total = lines * 4 * count
    for o in range(total):
        where = (o // (4 * count), o // (2 * count) % 2, o // count % 2, o % count)
        source[where] = lane_shift(rows, o * (width // total))[:, 0:128]
    scatter.stage_begin(FIRST_ITEMS + 4)
    while queue:
        tick()
    scatter.finish()

    def drain(i, carry):
        swap(i, 0).wait_send()
        swap(i, 1).wait_send()
        return carry

    lax.fori_loop(0, pairs, drain, 0)


def backward_all(arrays, shapes):
    count = lax.axis_size("seq")
    lines = lax.axis_size("dp") // 4
    total = lines * 4 * count
    vmem = pl.BlockSpec(memory_space=pltpu.VMEM)
    hbm = pl.BlockSpec(memory_space=pltpu.HBM)
    layer = arrays.layer
    width, tokens = arrays.qt.shape
    out_shape = [jax.ShapeDtypeStruct(shape[:2], jnp.float32) for shape in shapes]
    out_shape.append(jax.ShapeDtypeStruct(layer.shape, layer.dtype))
    buffers, sems = scatter_scratch(shapes, lines, count, layer.shape[0])
    views = list(arrays)
    for k in range(3):
        grad = arrays[k]
        views[k] = grad.reshape(lines, 2, 2, count, grad.shape[0] // total, grad.shape[1])

    def source(index):
        rows, cols, kind = shapes[index]
        return pltpu.VMEM((lines, 2, 2, count, rows, cols), kind)

    half = jnp.bfloat16
    own = [
        pltpu.VMEM((3 * width, tokens), half),
        pltpu.VMEM((2 * width, tokens), half),
        pltpu.VMEM((2 * width, tokens), half),
        pltpu.VMEM((width, width), jnp.float32),
        pltpu.VMEM((KW * VOCAB, arrays.idm.shape[1]), half),
        pltpu.VMEM((3,) + source(0).shape, half),
        source(7),
        source(8),
        pltpu.SemaphoreType.DMA((2, width // 128)),
        pltpu.SemaphoreType.DMA((2, width // 128)),
        pltpu.SemaphoreType.DMA,
        pltpu.SemaphoreType.DMA,
        pltpu.SemaphoreType.DMA((LATE_LOADS + 3,)),
        pltpu.VMEM((3 * width, width), half),
        pltpu.VMEM((KW * VOCAB, 1), jnp.float32),
        pltpu.VMEM((8, width), jnp.float32),
        source(3),
        pltpu.VMEM((width, tokens), half),
    ]
    return pl.pallas_call(
        backward_kernel,
        name="backward_all",
        out_shape=out_shape,
        in_specs=[hbm] * (7 + LATE_LOADS) + [vmem] * (len(views) - 7 - LATE_LOADS),
        out_specs=[vmem] * 9 + [hbm],
        scratch_shapes=buffers + sems + own + [pltpu.VMEM(a.shape, a.dtype) for a in arrays[6 : 6 + LATE_LOADS]],
        compiler_params=pltpu.CompilerParams(
            collective_id=1, has_side_effects=True, vmem_limit_bytes=63 * 1024 * 1024
        ),
    )(*views)


def tok_forward_body(own, core, tokens, tick):
    ids_ref, marks_ref, table_ref, small_ref = own.ids_pad, own.marks_pad, own.table, own.small
    table_ref = table_ref.at[:, 0 : own.stream.shape[1]]
    stream_ref, normed_ref, coef_ref, tap_ref = own.stream, own.normed, own.coef, own.tap
    rows_ref, idm_ref, one_hot = own.rows, own.idm, own.one_hot
    half_bytes = 2 * tokens
    span = one_hot.shape[1]
    wide = span + 2 * LEFT
    first = pl.ds(pl.multiple_of(core * half_bytes, 128), wide)
    ids = ids_ref[:, first]
    marks = marks_ref[:, first]
    for tap in range(KW):
        by = tap - KW // 2
        same = (lane_shift(marks, by) == marks) & (marks > 0)
        idm_ref[tap : tap + 1] = jnp.where(same, lane_shift(ids, by), -1)[0:1, LEFT : LEFT + span]
    tick()
    fill_one_hot(one_hot, idm_ref)

    tick()
    score = jnp.broadcast_to(small_ref[KW : KW + 1], (8, small_ref.shape[1])).astype(jnp.bfloat16)

    def step(tap, carry):
        product = table_ref[...].astype(jnp.float32) * small_ref[pl.ds(tap, 1)]
        high, low = split_two(product)
        tap_ref[tap_rows(tap)] = high
        own.scored[:, tap_rows(tap)] = mm_nt(score, high) + mm_nt(score, low)
        return carry

    lax.fori_loop(0, KW, step, 0)
    tick()
    high, low = split_two(own.scored[...])
    u_row = mm(high, one_hot[...]) + mm(low, one_hot[...])

    tick()
    high = u_row.astype(jnp.bfloat16).astype(jnp.float32)
    marks_here = marks[:, LEFT : LEFT + span].astype(jnp.float32)
    away = marks_ref[:, pl.ds(pl.multiple_of((1 - core) * half_bytes, 128), wide)][:, LEFT : LEFT + span]
    away = away.astype(jnp.float32)
    packed = jnp.concatenate([marks_here, high, u_row - high, away], axis=0).astype(jnp.bfloat16)
    shape = (span, wide // 2)
    twice = 2 * lax.broadcasted_iota(jnp.int32, shape, 1) - lax.broadcasted_iota(jnp.int32, shape, 0) - LEFT
    marks_of, u_of = [], []
    for e in range(2):
        pick = (twice == -e).astype(jnp.float32).astype(jnp.bfloat16)
        apart = mm(packed, pick)
        marks_of.append(apart[0:8])
        u_of.append(apart[8:16] + apart[16:24])
        if e == 0:
            kept = slice(LEFT, LEFT + tokens)
            both = jnp.concatenate([apart[0:1, kept], apart[24:25, kept]], axis=1)
            own.marks[...] = both.astype(jnp.int32)

    tick()
    inside, inverse = pool_rows(marks_of, core, half_bytes)
    prob = {}
    for e in range(2):
        shifted = {}
        for s in range(1 - MAXBLOCK, MAXBLOCK):
            f = (e + s) % 2
            shifted[s] = lane_shift(u_of[f], (e + s - f) // 2)
        scores = [u_of[e]]
        for b in range(2, MAXBLOCK + 1):
            total = u_of[e]
            for s in range(1 - b, b):
                if s != 0:
                    total = total + inside[b, e, s] * shifted[s]
            scores.append(total * inverse[b, e])
        top = scores[0]
        for value in scores[1:]:
            top = jnp.maximum(top, value)
        expo = [jnp.exp(value - top) for value in scores]
        whole = expo[0] + expo[1] + expo[2] + expo[3]
        for b in range(1, MAXBLOCK + 1):
            prob[b, e] = expo[b - 1] / whole
            rows_ref[2 * b + e : 2 * b + e + 1] = prob[b, e][0:1]
        rows_ref[e : e + 1] = marks_of[e][0:1]
    coefs = band_coefs({key: 0.5 * value for key, value in prob.items()}, inside, inverse)
    gain = small_ref[KW + 1 : KW + 2]
    tick()
    for i in range(tokens // BAND):
        matrix = band_matrix(coefs, i).astype(jnp.bfloat16)
        lanes = slice(i * BAND, (i + 1) * BAND)
        part = mm(one_hot[:, 2 * i * BAND : (2 * i + 3) * BAND], matrix).astype(jnp.bfloat16)
        coef_ref[:, lanes] = part
        stream = mm_tn(part, tap_ref[...])
        stream_ref[lanes] = stream
        scale = lax.rsqrt(jnp.mean(stream * stream, axis=-1, keepdims=True) + 1e-06)
        normed_ref[lanes] = (stream * scale * gain).astype(jnp.bfloat16)
        if i < tokens // BAND - 1:
            tick()


FUSED_ITEMS = (
    (4, 0, 1, 0, 0),
    (0, 0, 2, 1, 1),
    (0, 1, 2, 0, 1),
    (2, 1, 2, 1, 2),
    (3, 0, 1, 0, 3),
    (2, 0, 2, 0, 4),
    (1, 0, 1, 1, 5),
)
FUSED_SCHEDULE = (
    (
        (0, 0, 0), (1, 0, 0), (0, 1, 0), (1, 1, 0), (2, 0, 1), (3, 0, 0),
        (3, 1, 0), (2, 0, 2), (4, 0, 0), (3, 0, 1), (2, 0, 3), (2, 1, 1),
        (0, 2, 0), (3, 0, 2), (4, 1, 0), (3, 0, 3), (2, 1, 2), (4, 0, 1),
        (3, 1, 1), (2, 1, 3), (1, 2, 0), (2, 2, 1), (0, 3, 0), (4, 0, 2),
        (4, 0, 3), (2, 2, 2),
    ),
    (),
    (
        (2, 2, 3), (1, 3, 0), (2, 3, 1), (0, 4, 0), (3, 1, 2),
    ),
    (
        (2, 3, 2), (3, 1, 3), (3, 2, 0), (4, 1, 1),
    ),
    ((3, 2, 1),),
    (
        (2, 3, 3), (1, 4, 0), (2, 4, 1), (0, 5, 0), (3, 2, 2),
    ),
    ((3, 2, 3),),
    (
        (2, 4, 2), (3, 3, 0),
    ),
    (
        (2, 4, 3), (1, 5, 0), (2, 5, 1), (3, 3, 1), (4, 1, 2), (4, 1, 3),
        (2, 5, 2),
    ),
    (
        (3, 3, 2), (4, 2, 0),
    ),
    (
        (2, 5, 3), (5, 0, 0), (3, 3, 3), (4, 2, 1),
    ),
    (
        (3, 4, 0), (3, 4, 1),
    ),
    (
        (3, 4, 2), (4, 2, 2), (4, 2, 3), (4, 3, 0),
    ),
    (),
    ((3, 4, 3),),
    (),
    ((3, 5, 0),),
    ((3, 5, 1),),
    (),
    ((4, 3, 1),),
    (
        (3, 5, 2), (4, 5, 0),
    ),
    ((3, 5, 3),),
    (
        (4, 3, 2), (4, 3, 3), (4, 5, 1),
    ),
    ((4, 4, 0),),
    (
        (4, 4, 1), (4, 5, 2),
    ),
    (
        (4, 4, 2), (4, 4, 3), (4, 5, 3),
    ),
    (),
)


class Gather:
    def __init__(self, ins, outs, cells_in, cells_out, cot_in, cot_out, sems):
        self.ins, self.outs, self.sems = ins, outs, sems
        self.cells_in, self.cells_out, self.cot_in, self.cot_out = cells_in, cells_out, cot_in, cot_out
        self.y, self.x, self.core, self.place, self.lines, self.count = position()
        y, x, core = self.y, self.x, self.core
        self.group = y * 2 + x
        self.dp = dp_of(y, x, core)
        self.twin = dp_of(y, x, 1 - core)
        self.side = dp_of(y, 1 - x, core)
        self.ahead = [(y + k) % self.lines for k in range(1, self.lines)]
        self.phases = {}
        for item, entry in enumerate(FUSED_ITEMS):
            self.phases.setdefault(entry[4], []).append(item)

    def meet(self):
        targets = [(self.twin, self.place), (self.side, self.place)]
        for k in range(1, self.count):
            other = (self.place + k) % self.count
            targets += [(self.dp, other), (self.twin, other)]
        for other_y in self.ahead:
            targets.append((dp_of(other_y, self.x, self.core), self.place))
        meet(targets)

    def lanes(self, item):
        array, part, parts, _, _ = FUSED_ITEMS[item]
        cols = self.ins[array].shape[1] // parts
        return pl.ds(part * cols, cols)

    def shard(self, item):
        return self.ins[FUSED_ITEMS[item][0]].at[:, self.lanes(item)]

    def rows(self, item, first, blocks):
        array = FUSED_ITEMS[item][0]
        size = self.ins[array].shape[0]
        start = pl.multiple_of(first * size, 8)
        return self.outs[array].at[pl.ds(start, blocks * size), self.lanes(item)]

    def block(self, item, g, z):
        return self.rows(item, (g * 2 + self.core) * self.count + z, 1)

    def group_block(self, item, g, core):
        return self.rows(item, (g * 2 + core) * self.count, self.count)

    def came(self, item, g, z):
        return self.sems.recv.at[item, g * self.count + z]

    def arrived(self, item, g, z):
        dst = self.block(item, g, z)
        remote(dst, dst, self.sems.x.at[item], self.came(item, g, z), self.twin, self.place).wait_recv()

    def to_side(self, item, src, g, z):
        remote(
            src, self.block(item, g, z), self.sems.x.at[item], self.came(item, g, z), self.side, self.place
        ).start()

    def to_lines(self, item, src, g, z):
        for other_y in self.ahead:
            remote(
                src,
                self.block(item, g, z),
                self.sems.y.at[item],
                self.came(item, g, z),
                dp_of(other_y, self.x, self.core),
                self.place,
            ).start()

    def to_z(self, item, src, z, way):
        return remote(
            src,
            self.block(item, self.group, z),
            self.sems.z.at[item, z, way],
            self.came(item, self.group, z),
            self.dp,
            self.place + 1 - 2 * way,
        )

    def to_twin(self, item, g):
        src = self.group_block(item, g, self.core)
        remote(
            src, src, self.sems.twin.at[item], self.sems.twin_recv.at[item, g], self.twin, self.place
        ).start()

    def own_copy(self, item):
        return pltpu.make_async_copy(
            self.shard(item), self.block(item, self.group, self.place), self.sems.own.at[item]
        )

    def task_own(self, phase):
        for item in self.phases[phase]:
            src = self.shard(item)

            @pl.when(self.place < self.count - 1)
            def _():
                self.to_z(item, src, self.place, 0).start()

            @pl.when(self.place > 0)
            def _():
                self.to_z(item, src, self.place, 1).start()

            self.own_copy(item).start()

    def task_sides(self, phase):
        for item in self.phases[phase]:
            src = self.shard(item)
            self.to_side(item, src, self.group, self.place)
            self.to_lines(item, src, self.group, self.place)

    def both_ways(self, step, body):
        def way_step(way, carry):
            z = self.place + step * (2 * way - 1)

            @pl.when((z >= 0) & (z < self.count))
            def _():
                body(z, way)

            return carry

        lax.fori_loop(0, 2, way_step, 0)

    def steps(self, step, body):
        if step < 3:
            body(step)
            return

        def loop(s, carry):
            body(s)
            return carry

        lax.fori_loop(3, self.count, loop, 0)

    def task_first(self, phase, step):
        items = self.phases[phase]

        def receive(z, way):
            for item in items:
                self.arrived(item, self.group, z)
                src = self.block(item, self.group, z)
                then = self.place + 1 - 2 * way
                onward = (then >= 0) & (then < self.count)

                @pl.when(onward)
                def _():
                    self.to_z(item, src, z, way).start()

                self.to_side(item, src, self.group, z)
                self.to_lines(item, src, self.group, z)

        self.steps(step, lambda s: self.both_ways(s, receive))
        if step == 3:
            for item in items:
                self.own_copy(item).wait()
                self.to_twin(item, self.group)

    def at_distance(self, step, body):
        if step == 0:
            body(self.place, 0)
        else:
            self.steps(step, lambda s: self.both_ways(s, body))

    def task_second(self, phase, step):
        items = self.phases[phase]

        def receive(z, way):
            for item in items:
                if FUSED_ITEMS[item][3] == 0:
                    g = self.y * 2 + (1 - self.x)
                    self.arrived(item, g, z)
                    self.to_lines(item, self.block(item, g, z), g, z)
                else:
                    for other_y in self.ahead:
                        g = other_y * 2 + self.x
                        self.arrived(item, g, z)
                        self.to_side(item, self.block(item, g, z), g, z)

        self.at_distance(step, receive)
        if step == 3:
            for item in items:
                if FUSED_ITEMS[item][3] == 0:
                    self.to_twin(item, self.y * 2 + (1 - self.x))
                else:
                    for other_y in self.ahead:
                        self.to_twin(item, other_y * 2 + self.x)

    def task_third(self, phase, step):
        items = self.phases[phase]

        def rest(item):
            if FUSED_ITEMS[item][3] == 0:
                return [other_y * 2 + x for other_y in self.ahead for x in (self.x, 1 - self.x)]
            return [other_y * 2 + (1 - self.x) for other_y in [self.y] + self.ahead]

        def receive(z, way):
            for item in items:
                for g in rest(item):
                    self.arrived(item, g, z)

        self.at_distance(step, receive)
        if step == 3:
            for item in items:
                for g in rest(item):
                    self.to_twin(item, g)

    def full(self, item):
        def step(g, carry):
            dst = self.group_block(item, g, 1 - self.core)
            remote(
                dst, dst, self.sems.twin.at[item], self.sems.twin_recv.at[item, g], self.twin, self.place
            ).wait_recv()
            return carry

        lax.fori_loop(0, self.lines * 2, step, 0)

    def cell_copies(self, fn_remote, fn_local):
        seqs = self.cells_in.shape[0]
        for r in range(seqs):
            chip = seqs * self.core + r
            for c in range(2):
                home = (chip == self.place) & (self.core == c)

                @pl.when(home)
                def _():
                    fn_local(r)

                @pl.when(jnp.logical_not(home))
                def _():
                    fn_remote(r, c, chip)

    def cell_remote(self, r, c, chip):
        return remote(
            self.cells_in.at[r],
            self.cells_out.at[self.place],
            self.sems.cell_send.at[r, c],
            self.sems.cell_recv.at[self.place],
            dp_of(self.y, self.x, c),
            chip,
        )

    def cells_start(self):
        self.cell_copies(
            lambda r, c, chip: self.cell_remote(r, c, chip).start(),
            lambda r: pltpu.make_async_copy(
                self.cells_in.at[r], self.cells_out.at[self.place], self.sems.cell_recv.at[self.place]
            ).start(),
        )

    def cells_wait(self):
        for q in range(self.count):
            dst = self.cells_out.at[q]
            remote(
                dst, dst, self.sems.cell_send.at[0, 0], self.sems.cell_recv.at[q], self.twin, self.place
            ).wait_recv()

    def cot_copies(self, fn_remote, fn_local):
        seqs = self.cot_in.shape[0]
        for r in range(seqs):
            chip = seqs * self.core + r
            home = (chip == self.place) & (self.core == self.place // seqs)

            @pl.when(home)
            def _():
                fn_local(r)

            @pl.when(jnp.logical_not(home))
            def _():
                fn_remote(r, chip)

    def cot_remote(self, r, chip):
        seqs = self.cot_in.shape[0]
        slot = self.place % seqs
        return remote(
            self.cot_in.at[r],
            self.cot_out.at[slot],
            self.sems.cot_send.at[r],
            self.sems.cot_recv.at[slot],
            dp_of(self.y, self.x, self.place // seqs),
            chip,
        )

    def task_cot(self):
        slot = self.place % self.cot_in.shape[0]
        self.cot_copies(
            lambda r, chip: self.cot_remote(r, chip).start(),
            lambda r: pltpu.make_async_copy(
                self.cot_in.at[r], self.cot_out.at[slot], self.sems.cot_recv.at[slot]
            ).start(),
        )

    def task(self, kind, phase, step):
        if kind == 0:
            self.task_own(phase)
        elif kind == 1:
            self.task_sides(phase)
        elif kind == 2:
            self.task_first(phase, step)
        elif kind == 3:
            self.task_second(phase, step)
        elif kind == 4:
            self.task_third(phase, step)
        else:
            self.task_cot()

    def finish(self, waited):
        count, groups = self.count, self.lines * 2
        for item in range(len(FUSED_ITEMS)):
            if item not in waited:
                self.full(item)
            tree = FUSED_ITEMS[item][3]

            def sent(blocks, sem):
                src = self.rows(item, 0, blocks)
                remote(src, src, sem, self.came(item, 0, 0), self.twin, self.place).wait_send()

            sent(count * (1 if tree == 0 else self.lines), self.sems.x.at[item])
            sent(count * (self.lines - 1) * (2 if tree == 0 else 1), self.sems.y.at[item])
            sent(count * groups, self.sems.twin.at[item])

            def drain(z, carry):
                @pl.when((z <= self.place) & (self.place < count - 1))
                def _():
                    self.to_z(item, self.block(item, self.group, z), z, 0).wait_send()

                @pl.when((z >= self.place) & (self.place > 0))
                def _():
                    self.to_z(item, self.block(item, self.group, z), z, 1).wait_send()

                return carry

            lax.fori_loop(0, count, drain, 0)
        for q in range(self.cot_in.shape[0]):
            dst = self.cot_out.at[q]
            remote(
                dst, dst, self.sems.cot_send.at[0], self.sems.cot_recv.at[q], self.twin, self.place
            ).wait_recv()
        self.cell_copies(lambda r, c, chip: self.cell_remote(r, c, chip).wait_send(), lambda r: None)
        self.cot_copies(lambda r, chip: self.cot_remote(r, chip).wait_send(), lambda r: None)


class GatherSems(NamedTuple):
    recv: object
    twin_recv: object
    z: object
    x: object
    y: object
    twin: object
    own: object
    cell_recv: object
    cell_send: object
    cot_recv: object
    cot_send: object
class FrontOuts(NamedTuple):
    cot: object
    stream: object
    normed: object
    coef: object
    tap: object
    rows: object
    idm: object
    qt: object
    kt: object
    vt: object
    out: object
    lse: object
    marks: object
    small: object
    resid: object
    normed_two: object


class FrontWork(NamedTuple):
    stream: object
    normed: object
    coef: object
    tap: object
    rows: object
    idm: object
    qt: object
    kt: object
    vt: object
    out: object
    lse: object
    marks: object
    small: object
    resid: object
    normed_two: object
    cells: object
    ids_pad: object
    marks_pad: object
    table: object
    blocks: object
    wq: object
    wk: object
    wv: object
    wo: object
    other: object
    one_hot: object
    bias: object
    scores: object
    out_sem: object
    load_sem: object
    swap_send: object
    swap_recv: object
    small_in: object
    cells_in: object
    scored: object
    pair: object
    wkv: object
    kv: object
    attend_in: object
    table_in: object


def attend_forward_pair(qt, kt, vt, bias, scores, out, lse, tasks):
    keys = kt[...].T
    chunks = keys.shape[0] // CHUNK
    for h in range(2):
        query = pair_rows(qt, h)
        own = slice(h * HEAD_DIM, (h + 1) * HEAD_DIM)
        top = None
        for c in range(chunks):
            rows = slice(c * CHUNK, (c + 1) * CHUNK)
            part = mm(keys[rows], query) + bias[rows]
            scores[h, rows] = part
            high = jnp.max(part, axis=0, keepdims=True)
            top = high if top is None else jnp.maximum(top, high)
        total = None
        summed = None
        for c in range(chunks):
            rows = slice(c * CHUNK, (c + 1) * CHUNK)
            expo = jnp.exp(scores[h, rows] - top)
            part = jnp.sum(expo, axis=0, keepdims=True)
            total = part if total is None else total + part
            part = mm(vt[own, rows], expo.astype(jnp.bfloat16))
            summed = part if summed is None else summed + part
        out[own] = (summed / total).astype(jnp.bfloat16)
        lse[h : h + 1] = top + jnp.log(total)
        if h == 0:
            tasks()


def forward_kernel(*refs):
    arrays = 5
    attend_parts, feed_parts, embed_table = refs[:4], refs[4:7], refs[7]
    byte_ids, segments, taps, vectors, cot_in = refs[8:13]
    rest = refs[13:]
    full, cells_out = rest[:arrays], rest[arrays]
    kept = len(FrontOuts._fields)
    to = FrontOuts(*rest[arrays + 1 : arrays + 1 + kept])
    rest = rest[arrays + 1 + kept :]
    sems = GatherSems(*rest[: len(GatherSems._fields)])
    own = FrontWork(*rest[len(GatherSems._fields) :])
    small_in, cells_in = own.small_in, own.cells_in
    tokens, width = own.stream.shape
    own = own._replace(
        normed=own.pair.at[0:tokens],
        other=own.pair.at[tokens : 2 * tokens],
        wk=own.wkv.at[0:width],
        wv=own.wkv.at[width : 2 * width],
        kt=own.kv.at[0:width],
        vt=own.kv.at[width : 2 * width],
    )
    ins = (own.attend_in,) + tuple(feed_parts) + (own.table_in,)
    gather = Gather(ins, full, cells_in, cells_out, cot_in, to.cot, sems)
    which = {}
    for item, entry in enumerate(FUSED_ITEMS):
        which[entry[0], entry[1]] = item
    queue = [list(group) for group in FUSED_SCHEDULE]

    def tick():
        for entry in queue.pop(0):
            gather.task(*entry)

    saved = []

    def save(src, dst):
        copy = pltpu.make_async_copy(src, dst, own.out_sem.at[len(saved)])
        copy.start()
        saved.append(copy)

    def load(k, dst):
        if k % 2 == 0:
            gather.full(which[0, k // 2])
        copy = pltpu.make_async_copy(full[0].at[:, k * width : (k + 1) * width], dst, own.load_sem.at[k])
        copy.start()
        return copy

    small_in[...] = jnp.zeros_like(small_in)
    small_in[0:KW, 0 : taps.shape[1]] = taps[...].astype(jnp.float32)
    small_in[KW:8, 0 : taps.shape[1]] = vectors[...]
    own.table_in[:, 0:width] = embed_table[...]
    own.table_in[:, width : width + 128] = small_in[...].astype(jnp.bfloat16)
    for k in range(4):
        own.attend_in[:, k * width : (k + 1) * width] = attend_parts[k][...]
    per_part = byte_ids.shape[1] // 128
    for r in range(byte_ids.shape[0]):
        for k in range(per_part):
            lanes = slice(128 * k, 128 * (k + 1))
            cells_in[r, k : k + 1] = byte_ids[r : r + 1, lanes]
            cells_in[r, per_part + k : per_part + k + 1] = segments[r : r + 1, lanes] + 1
    gather.meet()
    gather.cells_start()
    tick()

    core, place = gather.core, gather.place
    tokens, width = own.stream.shape
    half_bytes = 2 * tokens
    span = own.one_hot.shape[1]
    wide = span + 2 * LEFT
    gather.cells_wait()
    cell_copy = pltpu.make_async_copy(cells_out, own.cells, own.load_sem.at[4])
    cell_copy.start()
    gather.full(which[4, 0])
    load_table = pltpu.make_async_copy(full[4], own.table, own.load_sem.at[5])
    load_table.start()
    cell_copy.wait()
    ids_pad, marks_pad = own.ids_pad, own.marks_pad
    ids_pad[:, 0 : 2 * LEFT] = jnp.full((8, 2 * LEFT), -1, jnp.int32)
    marks_pad[:, 0 : 2 * LEFT] = jnp.zeros((8, 2 * LEFT), jnp.int32)
    end = 2 * LEFT + 2 * half_bytes
    ids_pad[:, end : end + 2 * LEFT] = jnp.full((8, 2 * LEFT), -1, jnp.int32)
    marks_pad[:, end : end + 2 * LEFT] = jnp.zeros((8, 2 * LEFT), jnp.int32)
    parts, per_part = own.cells.shape[0], own.cells.shape[1] // 2
    for q in range(parts):
        for r in range(per_part):
            at = slice(2 * LEFT + (q * per_part + r) * 128, 2 * LEFT + (q * per_part + r + 1) * 128)
            ids_pad[:, at] = jnp.broadcast_to(own.cells[q, r : r + 1], (8, 128))
            marks_pad[:, at] = jnp.broadcast_to(own.cells[q, per_part + r : per_part + r + 1], (8, 128))
    load_table.wait()
    own.blocks[...] = own.table[:, width : width + 128].astype(jnp.float32)
    total = gather.lines * 4 * gather.count
    chan = width // total
    lane = lax.broadcasted_iota(jnp.int32, (8, 128), 1)
    columns = [jnp.zeros((8, 128), jnp.float32) for _ in range(width // 128)]
    for o in range(total):
        piece = jnp.where(lane < chan, own.blocks[8 * o : 8 * o + 8], 0.0)
        at, by = divmod(o * chan, 128)
        turned = piece if by == 0 else pltpu.roll(piece, by, 1)
        columns[at] = columns[at] + jnp.where(lane >= by, turned, 0.0)
        if by + chan > 128:
            columns[at + 1] = columns[at + 1] + jnp.where(lane < by, turned, 0.0)
    own.small[...] = jnp.concatenate(columns, axis=1)
    save(own.small, to.small)
    tok_forward_body(own, core, tokens, tick)
    save(own.stream, to.stream)
    save(own.normed, to.normed)
    save(own.coef, to.coef)
    save(own.tap, to.tap)
    save(own.rows, to.rows)
    save(own.idm, to.idm)
    save(own.marks, to.marks)

    swap = remote(own.normed, own.other, own.swap_send, own.swap_recv, gather.twin, place)
    swap.start()
    tick()
    load_wq = load(0, own.wq)
    load_wk = load(1, own.wk)
    load_wv = load(2, own.wv)

    def project(rows, weight):
        return mm(rows[...], weight[...]).astype(jnp.bfloat16)

    load_wq.wait()
    own.qt[...] = (project(own.normed, own.wq) * HEAD_DIM ** (-0.5)).astype(jnp.bfloat16).T
    save(own.qt, to.qt)
    tick()
    load_wk.wait()
    load_wv.wait()
    groups = [queue.pop(0) for _ in range(4)]

    def project_step(i, carry):
        which, part = i % 2, i // 2

        @pl.when(i == 2)
        def _():
            swap.wait_recv()

        rows = own.pair.at[pl.ds(pl.multiple_of(part * tokens, tokens), tokens)]
        weight = own.wkv.at[pl.ds(pl.multiple_of(which * width, width), width)]
        to_rows = pl.ds(pl.multiple_of(which * width, width), width)
        own.kv[to_rows, pl.ds(pl.multiple_of(part * tokens, tokens), tokens)] = project(rows, weight).T
        for k, group in enumerate(groups):
            if group:

                @pl.when(i == k)
                def _():
                    for entry in group:
                        gather.task(*entry)

        return carry

    lax.fori_loop(0, 4, project_step, 0)
    save(own.kt, to.kt)
    save(own.vt, to.vt)
    load_wo = load(3, own.wo)
    fill_bias(own.bias, own.marks, own.marks.at[:, 0:tokens])
    pairs = width // 128
    ticks = [queue.pop(0) for _ in range(2 * pairs)]

    def pair_tasks(groups, i):
        for k, group in enumerate(groups):
            if group:

                @pl.when(i == k)
                def _():
                    for entry in group:
                        gather.task(*entry)

    def pair_step(i, carry):
        at = pl.ds(pl.multiple_of(128 * i, 128), 128)
        attend_forward_pair(
            own.qt.at[at],
            own.kt.at[at],
            own.vt.at[at],
            own.bias,
            own.scores,
            own.out.at[at],
            own.lse.at[i],
            lambda: pair_tasks(ticks[0::2], i),
        )
        pair_tasks(ticks[1::2], i)
        return carry

    lax.fori_loop(0, pairs, pair_step, 0)
    save(own.out, to.out)
    save(own.lse, to.lse)
    load_wo.wait()
    resid = own.stream[...] + mm(own.out[...].T, own.wo[...])
    own.resid[...] = resid
    save(own.resid, to.resid)
    scale = lax.rsqrt(jnp.mean(resid * resid, axis=-1, keepdims=True) + 1e-06)
    own.normed_two[...] = (resid * scale * own.small[KW + 2 : KW + 3]).astype(jnp.bfloat16)
    save(own.normed_two, to.normed_two)
    while queue:
        tick()
    gather.finish([which[0, 0], which[0, 1], which[4, 0]])
    for copy in saved:
        copy.wait()
    swap.wait_send()


def forward_all(shards, byte_ids, segments, taps, vectors, cot, tokens):
    count = lax.axis_size("seq")
    group_count = lax.axis_size(ALL)
    groups = group_count // (2 * count)
    items = len(FUSED_ITEMS)
    seqs = byte_ids.shape[0]
    cells = jax.ShapeDtypeStruct((seqs, byte_ids.shape[1] // 64, 128), jnp.int32)
    width = shards[0].shape[1]
    span = 2 * tokens + 2 * LEFT
    half, single = jnp.bfloat16, jnp.float32
    vmem = pl.BlockSpec(memory_space=pltpu.VMEM)
    hbm = pl.BlockSpec(memory_space=pltpu.HBM)
    pairs = width // 128
    held = (
        ((tokens, width), single),
        ((tokens, width), half),
        ((KW * VOCAB, tokens), half),
        ((KW * VOCAB, width), half),
        ((16, (span + 2 * LEFT) // 2), single),
        ((8, span), jnp.int32),
        ((width, tokens), half),
        ((width, 2 * tokens), half),
        ((width, 2 * tokens), half),
        ((width, tokens), half),
        ((pairs, 2, tokens), single),
        ((1, 2 * tokens), jnp.int32),
        ((8, width), single),
        ((tokens, width), single),
        ((tokens, width), half),
    )
    size = shards[0].shape[0]
    sent = [(size, 4 * width)] + [shard.shape for shard in shards[4:7]] + [(8, width + 128)]
    shapes = [jax.ShapeDtypeStruct((rows * group_count, cols), half) for rows, cols in sent]
    shapes.append(jax.ShapeDtypeStruct((count,) + cells.shape[1:], cells.dtype))
    shapes.append(jax.ShapeDtypeStruct(cot.shape, cot.dtype))
    shapes += [jax.ShapeDtypeStruct(*entry) for entry in held]
    dma = pltpu.SemaphoreType.DMA
    scratch = [
        dma((items, groups * count)),
        dma((items, groups)),
        dma((items, count, 2)),
        dma((items,)),
        dma((items,)),
        dma((items,)),
        dma((items,)),
        dma((count,)),
        dma((seqs, 2)),
        dma((seqs,)),
        dma((seqs,)),
    ]
    scratch += [pltpu.VMEM(*entry) for entry in held]
    scratch += [
        pltpu.VMEM((count,) + cells.shape[1:], cells.dtype),
        pltpu.VMEM((8, 4 * tokens + 4 * LEFT), jnp.int32),
        pltpu.VMEM((8, 4 * tokens + 4 * LEFT), jnp.int32),
        pltpu.VMEM((VOCAB, width + 128), half),
        pltpu.VMEM((8 * group_count, 128), single),
        pltpu.VMEM((width, width), half),
        pltpu.VMEM((width, width), half),
        pltpu.VMEM((width, width), half),
        pltpu.VMEM((width, width), half),
        pltpu.VMEM((tokens, width), half),
        pltpu.VMEM((KW * VOCAB, span), half),
        pltpu.VMEM((2 * tokens, tokens), single),
        pltpu.VMEM((2, 2 * tokens, tokens), single),
        dma((len(held),)),
        dma((9,)),
        dma,
        dma,
        pltpu.VMEM((8, 128), single),
        pltpu.VMEM(cells.shape, cells.dtype),
        pltpu.VMEM((8, KW * VOCAB), single),
        pltpu.VMEM((2 * tokens, width), half),
        pltpu.VMEM((2 * width, width), half),
        pltpu.VMEM((2 * width, 2 * tokens), half),
        pltpu.VMEM((shards[0].shape[0], 4 * width), half),
        pltpu.VMEM((8, width + 128), half),
    ]
    out = pl.pallas_call(
        forward_kernel,
        name="forward_all",
        out_shape=shapes,
        in_specs=[vmem] * (len(shards) + 5),
        out_specs=[hbm] * len(shapes),
        scratch_shapes=scratch,
        compiler_params=pltpu.CompilerParams(
            collective_id=0, has_side_effects=True, vmem_limit_bytes=60 * 1024 * 1024
        ),
    )(*shards, byte_ids, segments, taps, vectors, cot)
    return list(out[:5]), FrontOuts(*out[6:])

FF_BLOCK = 512


def feed_kernel(
    normed,
    cot,
    resid,
    small,
    w_gate,
    w_up,
    w_down,
    gate_grad,
    up_grad,
    down_grad,
    layer,
    resid_grad,
    gain_grad,
    normed_t,
    total,
    normed_grad,
    stream_here,
    late_sem,
    hidden,
    up_part,
    gate_part,
):
    step = pl.program_id(0)
    late = [pltpu.make_async_copy(resid, stream_here, late_sem.at[0])]

    @pl.when(step == 0)
    def _():
        for copy in late:
            copy.start()
        normed_t[...] = normed[...].T
        total[...] = jnp.zeros_like(total)
        normed_grad[...] = jnp.zeros_like(normed_grad)

    root = 0.7978845608028654
    size = normed.shape[0] // 2
    for part in range(2):
        rows = slice(part * size, (part + 1) * size)
        gate = mm(normed[rows], w_gate[...])
        up = mm(normed[rows], w_up[...])
        hidden_grad = mm_nt(cot[rows], w_down[...])
        square = gate * gate
        bent = jnp.tanh(gate * (root + (root * 0.044715) * square))
        half = 0.5 + 0.5 * bent
        act = gate * half
        slope = half + act * (1.0 - bent) * (root + (3 * root * 0.044715) * square)
        hidden[rows] = (act * up).astype(jnp.bfloat16)
        up_part[rows] = (hidden_grad * act).astype(jnp.bfloat16)
        gate_part[rows] = (hidden_grad * up * slope).astype(jnp.bfloat16)
    total[...] += mm(hidden[...], w_down[...])
    down_grad[...] = mm(hidden[...].T, cot[...]).astype(jnp.bfloat16)
    gate_grad[...] = mm(normed_t[...], gate_part[...]).astype(jnp.bfloat16)
    up_grad[...] = mm(normed_t[...], up_part[...]).astype(jnp.bfloat16)
    normed_grad[...] += mm_nt(gate_part[...], w_gate[...]) + mm_nt(up_part[...], w_up[...])

    @pl.when(step == pl.num_programs(0) - 1)
    def _():
        for copy in late:
            copy.wait()
        stream = stream_here[...]
        layer[...] = (stream + total[...]).astype(jnp.bfloat16)
        scale = lax.rsqrt(jnp.mean(stream * stream, axis=-1, keepdims=True) + 1e-06)
        grad = normed_grad[...]
        gain_grad[...] = jnp.sum(grad * stream * scale, axis=0, keepdims=True)
        scaled = grad * small[KW + 2 : KW + 3]
        inner = jnp.mean(scaled * stream, axis=-1, keepdims=True)
        whole = cot[...].astype(jnp.float32) + scale * scaled - stream * (scale * scale * scale * inner)
        resid_grad[...] = whole


def feed_forward(normed, cot, resid, small, w_gate, w_up, w_down):
    tokens, width = normed.shape
    wide = w_gate.shape[1]
    whole = lambda shape: pl.BlockSpec(shape, lambda f: (0, 0))
    hbm = pl.BlockSpec(memory_space=pltpu.HBM)
    columns = pl.BlockSpec((width, FF_BLOCK), lambda f: (0, f))
    rows = pl.BlockSpec((FF_BLOCK, width), lambda f: (f, 0))
    half, single = jnp.bfloat16, jnp.float32
    return pl.pallas_call(
        feed_kernel,
        name="feed_forward",
        grid=(wide // FF_BLOCK,),
        in_specs=[
            whole((tokens, width)),
            whole((tokens, width)),
            hbm,
            whole(small.shape),
            columns,
            columns,
            rows,
        ],
        out_specs=[
            columns,
            columns,
            rows,
            whole((tokens, width)),
            whole((tokens, width)),
            whole((1, width)),
        ],
        out_shape=[
            jax.ShapeDtypeStruct((width, wide), half),
            jax.ShapeDtypeStruct((width, wide), half),
            jax.ShapeDtypeStruct((wide, width), half),
            jax.ShapeDtypeStruct((tokens, width), half),
            jax.ShapeDtypeStruct((tokens, width), single),
            jax.ShapeDtypeStruct((1, width), single),
        ],
        scratch_shapes=[
            pltpu.VMEM((width, tokens), half),
            pltpu.VMEM((tokens, width), single),
            pltpu.VMEM((tokens, width), single),
            pltpu.VMEM((tokens, width), single),
            pltpu.SemaphoreType.DMA((3,)),
            pltpu.VMEM((tokens, FF_BLOCK), half),
            pltpu.VMEM((tokens, FF_BLOCK), half),
            pltpu.VMEM((tokens, FF_BLOCK), half),
        ],
        compiler_params=pltpu.CompilerParams(vmem_limit_bytes=VMEM_BYTES),
    )(normed, cot, resid, small, w_gate, w_up, w_down)


def result_kernel(count, chan, *refs):
    ins, outs, sem = refs[:count], refs[count:-1], refs[-1]
    small = ins[-1]
    copies = [pltpu.make_async_copy(ins[k], outs[k], sem.at[k]) for k in range(count - 1)]
    for copy in copies:
        copy.start()
    outs[count - 1][...] = small[0:KW, 0:chan]
    for k in range(3):
        outs[count + k][...] = small[KW + k : KW + k + 1, 0:chan]
    for copy in copies:
        copy.wait()


def results(arrays, small, chan):
    vmem = pl.BlockSpec(memory_space=pltpu.VMEM)
    hbm = pl.BlockSpec(memory_space=pltpu.HBM)
    count = len(arrays) + 1
    shapes = [jax.ShapeDtypeStruct(a.shape, a.dtype) for a in arrays]
    shapes.append(jax.ShapeDtypeStruct((KW, chan), jnp.float32))
    shapes += [jax.ShapeDtypeStruct((1, chan), jnp.float32)] * 3
    return pl.pallas_call(
        functools.partial(result_kernel, count, chan),
        name="results",
        out_shape=shapes,
        in_specs=[vmem] * count,
        out_specs=[hbm] * len(arrays) + [vmem] * 4,
        scratch_shapes=[pltpu.SemaphoreType.DMA((count,))],
    )(*arrays, small)


def per_device(
    byte_ids,
    segments,
    embed_table,
    conv_weight,
    score_vector,
    first_gain,
    w_query,
    w_key,
    w_value,
    w_output,
    second_gain,
    w_gate,
    w_up,
    w_down,
    out_grad,
):
    seqs, part_bytes = byte_ids.shape
    count = lax.axis_size("seq")
    seq_len = part_bytes * count
    width = w_query.shape[1]
    wide = w_gate.shape[1]
    half_bytes = seq_len // 2
    half = half_bytes // 2
    core = lax.axis_index("dp") % 2
    place = lax.axis_index("seq")

    chan = conv_weight.shape[0]
    shards = (w_query, w_key, w_value, w_output, w_gate, w_up, w_down, embed_table)
    vectors = jnp.stack([score_vector, first_gain, second_gain]).astype(jnp.float32)
    if all(shard.shape[0] % 8 == 0 for shard in shards):
        full, held = forward_all(shards, byte_ids, segments, conv_weight.T, vectors, out_grad, half)
        attend, wg, wu, wd, table = full
        cot = held.cot.reshape(half, width)
        small_full, stream, normed_one, resid_one = held.small, held.stream, held.normed, held.resid
        coef, tap_table, rows, idm = held.coef, held.tap, held.rows, held.idm
        queries, keys, vals, attn_out, lse = held.qt, held.kt, held.vt, held.out, held.lse
        key_marks = held.marks[0]
        normed_two = held.normed_two
    else:
        small = jnp.concatenate([conv_weight.T.astype(jnp.float32), vectors], axis=0)
        small = jnp.pad(small, ((0, 0), (0, 128 - chan)))
        cells = jnp.stack([byte_ids, segments + 1], axis=1).reshape(seqs, -1, 128)
        wq, wk, wv, wo, wg, wu, wd, table, small_full, cells, cot = gather_all(shards + (small,), cells, out_grad)
        attend = jnp.concatenate([wq, wk, wv, wo], axis=1)
        cells = cells.reshape(count, 2, part_bytes).transpose(1, 0, 2).reshape(2, seq_len)
        ids_row, marks_row = cells[0], cells[1]
        cot = cot.reshape(half, width)
        small_full = small_full.reshape(lax.axis_size(ALL), 8, 128)[:, :, :chan].transpose(1, 0, 2).reshape(8, width)
        gain_two = small_full[KW + 2 : KW + 3]

        stream, normed_one, coef, tap_table, rows, idm = tok_forward(ids_row, marks_row, table, small_full, half)

        twins = [(i, i ^ 1) for i in range(lax.axis_size("dp"))]
        normed_other = lax.ppermute(normed_one, "dp", twins)
        token_marks = marks_row[::2]
        query_marks = lax.dynamic_slice_in_dim(token_marks, core * half, half, axis=0)
        other_marks = lax.dynamic_slice_in_dim(token_marks, (1 - core) * half, half, axis=0)
        key_marks = jnp.concatenate([query_marks, other_marks])
        queries = (mm_tt(wq, normed_one).astype(jnp.bfloat16) * HEAD_DIM ** (-0.5)).astype(jnp.bfloat16)
        normed_keys = jnp.concatenate([normed_one, normed_other], axis=0)
        keys = mm_tt(wk, normed_keys).astype(jnp.bfloat16)
        vals = mm_tt(wv, normed_keys).astype(jnp.bfloat16)
        attn_out, lse = attend_forward(queries, keys, vals, key_marks, query_marks)

        resid_one = stream + mm_tn(attn_out, wo)
        normed_two = rms_scale(resid_one, gain_two).astype(jnp.bfloat16)
    grad_gate, grad_up, grad_down, layer_rows, resid_grad, gain_two_grad = feed_forward(
        normed_two, cot, resid_one, small_full, wg, wu, wd
    )
    layer_rows = layer_rows.reshape(seqs, part_bytes // 2, width)
    shapes = [(w.shape[0], w.shape[1], jnp.bfloat16) for w in shards] + [(8, 128, jnp.float32)]
    out = backward_all(
        BackInputs(
            gate=grad_gate,
            up=grad_up,
            down=grad_down,
            coef=coef,
            resid=resid_grad,
            qt=queries,
            kt=keys,
            vt=vals,
            out=attn_out,
            lse=lse,
            key_marks=key_marks[None],
            normed=normed_one,
            stream=stream,
            attend=attend,
            small=small_full,
            gain_two=gain_two_grad,
            table=table,
            tap=tap_table,
            rows=rows,
            idm=idm,
            layer=layer_rows,
        ),
        shapes,
    )
    done = results([out[9]] + list(out[:8]), out[8], chan)
    return (
        done[0],
        done[8],
        done[9].T,
        done[10][0],
        done[11][0],
        done[1],
        done[2],
        done[3],
        done[4],
        done[12][0],
        done[5],
        done[6],
        done[7],
    )


def solution(mesh):
    flat = P(ALL)
    rows = P(ALL, None)
    in_specs = (
        P("dp", "seq"),
        P("dp", "seq"),
        rows,
        rows,
        flat,
        flat,
        rows,
        rows,
        rows,
        rows,
        flat,
        rows,
        rows,
        rows,
        P("dp", "seq", None),
    )
    out_specs = (
        P("dp", "seq", None),
        rows,
        rows,
        flat,
        flat,
        rows,
        rows,
        rows,
        rows,
        flat,
        rows,
        rows,
        rows,
    )
    return jax.shard_map(
        per_device, mesh=mesh, in_specs=in_specs, out_specs=out_specs, check_vma=False
    )
```
